128 devices in a mesh: px: 8 (over z_hi, x), py: 16 (over z_lo, y, core).
Axes of the slice: x: 4, y: 4, z: 4 (z_hi: 2, z_lo: 2; z = z_hi * 2 + z_lo), core: 2. Of those that a mesh axis runs over, the one named last changes fastest.
Arguments:
- rho_hat: float32 [2, 128, 768, 768], P(None, 'px', 'py'), may hold values from -6 to 6
Outputs:
- v_hat: float32 [2, 128, 768, 768], P(None, 'px', 'py')
The draws below stay inside these ranges and needn't reach their ends.
All inputs are finite; a program needn't handle non-finite values.
Results may differ from the reference program's by a relative error of at most 0.0003.
Values sent between devices are 32-bit elements; how exact they have to be, the bound alone decides.
No kernel may reach another device: no remote copies, remote signals or barrier semaphores. Data moves between devices by JAX's collectives and lax.ppermute only.
A program may use at most 192 MiB of HBM per device.

```python
import math
import jax
import jax.numpy as jnp

NX = 768
NY = 768
NZ = 128


def block_scale(key, extent, shards, low, top_value):
    factor_of = 1.0
    for axis_at, shards_of in shards:
        draws = jax.random.uniform(jax.random.fold_in(jax.random.fold_in(key, 6), axis_at), (shards_of,), jnp.float32, low / len(shards), top_value / len(shards))
        factor_of = factor_of * jnp.repeat(jnp.exp(draws), extent[axis_at] // shards_of).reshape((-1,) + (1,) * (len(extent) - 1 - axis_at))
    return factor_of


def gaussian(rng, shape, scale, most, split=(), kind=jnp.bfloat16):
    array = jax.random.normal(rng, shape, jnp.float32) * scale
    if len(split) > 0:
        array = block_scale(rng, shape, split, -0.22, 0.18) * array
    return jnp.clip(array, min=-most, max=most).astype(kind)


def setup_inputs(seed: int = 0) -> dict:
    seeds = jax.random.split(jax.random.key(seed), 2)
    return {
        "rho_hat": gaussian(seeds[0], (2, NZ, NX, NY), 1.0, 6.0, ((1, 8), (2, 16)), jnp.float32),
    }


grid_step = 0.25
density_floor = 0.02
density_scale = 0.2
kappa_value = 0.804
mu_value = 0.2195149727645171
beta_value = 0.06672455060314922
gamma_value = (1.0 - math.log(2.0)) / (math.pi * math.pi)
correlation_scale = 0.031091
correlation_alpha = 0.2137
correlation_terms = (7.5957, 3.5876, 1.6382, 0.49294)

def energy_density(rho, sigma):
    cube = jnp.cbrt(rho)
    k_fermi = (3.0 * math.pi * math.pi) ** (1.0 / 3.0) * cube
    exchange_unif = -0.75 * (3.0 / math.pi) ** (1.0 / 3.0) * cube * rho
    s_square = sigma / (4.0 * k_fermi * k_fermi * rho * rho)
    enhance = 1.0 + kappa_value - kappa_value / (1.0 + mu_value * s_square / kappa_value)
    radius = (3.0 / (4.0 * math.pi)) ** (1.0 / 3.0) / cube
    root = jnp.sqrt(radius)
    denom = 2.0 * correlation_scale * (correlation_terms[0] * root + correlation_terms[1] * radius + correlation_terms[2] * radius * root + correlation_terms[3] * radius * radius)
    uniform_corr = -2.0 * correlation_scale * (1.0 + correlation_alpha * radius) * jnp.log(1.0 + 1.0 / denom)
    screen_square = 4.0 * k_fermi / math.pi
    t_square = sigma / (4.0 * screen_square * rho * rho)
    coefficient = beta_value / gamma_value / (jnp.exp(-uniform_corr / gamma_value) - 1.0)
    scaled = coefficient * t_square
    gradient_term = gamma_value * jnp.log(1.0 + beta_value / gamma_value * t_square * (1.0 + scaled) / (1.0 + scaled + scaled * scaled))
    return exchange_unif * enhance + rho * (uniform_corr + gradient_term)

def clamp_depth(field):
    return jnp.concatenate([field[:1], field, field[-1:]], axis=0)

def smooth_depth(field):
    padded = clamp_depth(field)
    return 0.25 * padded[:-2] + 0.5 * padded[1:-1] + 0.25 * padded[2:]

def slope_depth(field):
    padded = clamp_depth(field)
    return (padded[2:] - padded[:-2]) / (2.0 * grid_step)

def roll_smooth(field, axis):
    return 0.25 * jnp.roll(field, 1, axis) + 0.5 * field + 0.25 * jnp.roll(field, -1, axis)

def roll_slope(field, axis):
    return (jnp.roll(field, -1, axis) - jnp.roll(field, 1, axis)) / (2.0 * grid_step)

def reference(rho_hat):
    spectrum = rho_hat[0] + 1j * rho_hat[1]
    field = jnp.real(jnp.fft.ifft2(spectrum, axes=(1, 2))) * math.sqrt(NX * NY)
    density = density_floor + density_scale * jax.nn.softplus(field)
    smooth = smooth_depth(roll_smooth(roll_smooth(density, 1), 2))
    grad_x = roll_slope(smooth, 1)
    grad_y = roll_slope(smooth, 2)
    grad_z = slope_depth(smooth)
    sigma = grad_x * grad_x + grad_y * grad_y + grad_z * grad_z
    energy, pullback = jax.vjp(energy_density, smooth, sigma)
    d_rho, d_sigma = pullback(jnp.ones_like(energy))
    flux_x = 2.0 * d_sigma * grad_x
    flux_y = 2.0 * d_sigma * grad_y
    flux_z = 2.0 * d_sigma * grad_z
    spread = roll_slope(flux_x, 1) + roll_slope(flux_y, 2) + slope_depth(flux_z)
    potential = d_rho - spread
    result = jnp.fft.fft2(potential, axes=(1, 2)) / math.sqrt(NX * NY)
    result = result.at[:, 0, 0].set(0.0)
    return jnp.stack([jnp.real(result), jnp.imag(result)], axis=0).astype(rho_hat.dtype)
```

```python
import math

import jax
import jax.numpy as jnp
import numpy as np
from jax import lax
from jax.experimental import pallas as pl
from jax.experimental.pallas import tpu as pltpu
from jax.sharding import PartitionSpec as P

grid_step = 0.25
density_floor = 0.02
density_scale = 0.2
kappa_value = 0.804
mu_value = 0.2195149727645171
beta_value = 0.06672455060314922
gamma_value = (1.0 - math.log(2.0)) / (math.pi * math.pi)
correlation_scale = 0.031091
correlation_alpha = 0.2137
correlation_terms = (7.5957, 3.5876, 1.6382, 0.49294)

f32 = jnp.float32
bf16 = jnp.bfloat16
reach = 3
lead = 9


def params(mib):
    return pltpu.CompilerParams(vmem_limit_bytes=mib << 20)


def call(body, out, mib, **options):
    return pl.pallas_call(body, out_shape=out, compiler_params=params(mib), **options)


def split(value):
    high = value.astype(bf16)
    return high, (value - high.astype(f32)).astype(bf16)


def dot_nt(left, right):
    return lax.dot_general(left, right, (((1,), (1,)), ((), ())), preferred_element_type=f32)


def dot_nn(left, right):
    return lax.dot_general(left, right, (((1,), (0,)), ((), ())), preferred_element_type=f32)


def triple(dot, left_high, left_low, right_high, right_low):
    return dot(left_high, right_high) + (dot(left_low, right_high) + dot(left_high, right_low))


def tables_body(stride, coarse_ref, fine_ref, ch_ref, cl_ref, sh_ref, sl_ref):
    fine_cos, fine_sin = fine_ref[0], fine_ref[1]
    for a in range(coarse_ref.shape[1]):
        cos_a, sin_a = coarse_ref[0, a : a + 1], coarse_ref[1, a : a + 1]
        rows = slice(stride * a, stride * (a + 1))
        ch_ref[rows], cl_ref[rows] = split(cos_a * fine_cos - sin_a * fine_sin)
        sh_ref[rows], sl_ref[rows] = split(sin_a * fine_cos + cos_a * fine_sin)


def phase_tables(length, stride):
    def waves(rows, scale):
        angle = (np.outer(rows, np.arange(length)) % length) * (2.0 * math.pi / length)
        return np.stack([np.cos(angle), np.sin(angle)]).astype(np.float32) * np.float32(scale)

    coarse = waves(np.arange(0, length, stride), 1.0)
    fine = waves(np.arange(stride), 1.0 / math.sqrt(length))
    out = [jax.ShapeDtypeStruct((length, length), bf16)] * 4
    body = lambda *refs: tables_body(stride, *refs)
    return call(body, out, 32, name="tables")(jnp.asarray(coarse), jnp.asarray(fine))


def inverse_rows_body(x_ref, ch_ref, cl_ref, sh_ref, sl_ref, out_ref, high_ref, low_ref):
    rows = high_ref.shape[1]
    width = x_ref.shape[3]
    for c in range(2):
        high_ref[c], low_ref[c] = split(x_ref[c].reshape(rows, width))
    group = 4
    block = out_ref.shape[2]

    def step(m, carry):
        at = pl.ds(pl.multiple_of(m * group * block, group * block), group * block)
        ch, cl, sh, sl = ch_ref[at], cl_ref[at], sh_ref[at], sl_ref[at]
        real = (high_ref[0], low_ref[0])
        imag = (high_ref[1], low_ref[1])
        out_re = triple(dot_nt, ch, cl, *real) - triple(dot_nt, sh, sl, *imag)
        out_im = triple(dot_nt, sh, sl, *real) + triple(dot_nt, ch, cl, *imag)
        to = pl.ds(m * group, group)
        out_ref[to, 0] = out_re.reshape(group, block, rows)
        out_ref[to, 1] = out_im.reshape(group, block, rows)
        return carry

    lax.fori_loop(0, out_ref.shape[0] // group, step, 0)


def whole(shape):
    return pl.BlockSpec(shape, lambda *_: (0,) * len(shape))


def inverse_rows(rho_hat, tables, parts, steps):
    _, depth, local, width = rho_hat.shape
    planes = depth // steps
    block = width // parts
    rows = planes * local
    return call(
        inverse_rows_body,
        jax.ShapeDtypeStruct((parts, 2, block, depth * local), f32),
        48,
        grid=(steps,),
        in_specs=[pl.BlockSpec((2, planes, local, width), lambda i: (0, i, 0, 0))]
        + [whole((width, width))] * 4,
        out_specs=pl.BlockSpec((parts, 2, block, rows), lambda i: (0, 0, 0, i)),
        scratch_shapes=[pltpu.VMEM((2, rows, width), bf16), pltpu.VMEM((2, rows, width), bf16)],
        name="inverse_rows",
    )(rho_hat, *tables)


def gather_blocks(in_ref, high_ref, low_ref):
    parts, _, rows, lanes = in_ref.shape
    local = high_ref.shape[2] // parts
    for z in range(lanes // local):
        at = slice(z * local, (z + 1) * local)
        to = slice(z * rows, (z + 1) * rows)
        for c in range(2):
            joined = jnp.concatenate([in_ref[s, c, :, at] for s in range(parts)], axis=-1)
            high_ref[c, to], low_ref[c, to] = split(joined)


def inverse_columns_body(in_ref, ch_ref, cl_ref, sh_ref, sl_ref, out_ref, high_ref, low_ref):
    gather_blocks(in_ref, high_ref, low_ref)
    planes, rows, width = out_ref.shape
    group = planes // 2

    def step(m, carry):
        at = pl.ds(pl.multiple_of(m * group * rows, group * rows), group * rows)
        field = triple(dot_nn, high_ref[0, at], low_ref[0, at], ch_ref[...], cl_ref[...])
        field = field - triple(dot_nn, high_ref[1, at], low_ref[1, at], sh_ref[...], sl_ref[...])
        soft = jnp.maximum(field, 0.0) + jnp.log1p(jnp.exp(-jnp.abs(field)))
        density = density_floor + density_scale * soft
        out_ref[pl.ds(m * group, group)] = density.reshape(group, rows, width)
        return carry

    lax.fori_loop(0, 2, step, 0)


def inverse_columns(blocks, tables, steps):
    parts, _, rows, lanes = blocks.shape
    width = tables[0].shape[0]
    depth = lanes * parts // width
    planes = depth // steps
    scratch = pltpu.VMEM((2, planes * rows, width), bf16)
    return call(
        inverse_columns_body,
        jax.ShapeDtypeStruct((depth, rows, width), f32),
        48,
        grid=(steps,),
        in_specs=[pl.BlockSpec((parts, 2, rows, lanes // steps), lambda i: (0, 0, 0, i))]
        + [whole((width, width))] * 4,
        out_specs=pl.BlockSpec((planes, rows, width), lambda i: (i, 0, 0)),
        scratch_shapes=[scratch, scratch],
        name="inverse_columns",
    )(blocks, *tables)


def shift(value, axis, up):
    count = lax.axis_size(axis)
    pairs = [(i, (i + 1) % count) for i in range(count)]
    return lax.ppermute(value, axis, pairs if up else [(b, a) for a, b in pairs])


def edges_body(low_ref, first_ref, last_ref, high_ref, head_ref, tail_ref):
    depth = first_ref.shape[0]
    rows = low_ref.shape[1]
    for z in range(depth + 2 * reach):
        to = slice(reach * z, reach * (z + 1))
        if z < reach:
            head, tail = low_ref[z, :reach], low_ref[z, rows - reach :]
        elif z < depth + reach:
            head, tail = first_ref[z - reach, :reach], last_ref[z - reach, 8 - reach :]
        else:
            y = z - depth - reach
            head, tail = high_ref[y, :reach], high_ref[y, rows - reach :]
        head_ref[to], tail_ref[to] = head, tail


def edges(below, density, above):
    depth, rows, width = density.shape
    count = -(-(depth + 2 * reach) * reach // 8) * 8
    slab = whole((reach, rows, width))
    side = lambda at: pl.BlockSpec((depth, 8, width), lambda i: (0, at, 0))
    return call(
        edges_body,
        [jax.ShapeDtypeStruct((count, width), f32)] * 2,
        16,
        grid=(1,),
        in_specs=[slab, side(0), side(rows // 8 - 1), slab],
        out_specs=[whole((count, width))] * 2,
        name="edges",
    )(below, density, density, above)


def roll_x(value, by):
    return pltpu.roll(value, by % value.shape[-1], value.ndim - 1)


def energy_slopes(rho, sigma):
    two_a = 2.0 * correlation_scale
    b1, b2, b3, b4 = correlation_terms
    sixth = jnp.exp(jnp.log(rho) * (-1.0 / 6.0))
    inv = sixth * sixth
    inv2 = inv * inv
    inv4 = inv2 * inv2
    cube = rho * inv2
    exchange = -0.75 * (3.0 / math.pi) ** (1.0 / 3.0)
    s_scale = 0.25 / (3.0 * math.pi**2) ** (2.0 / 3.0)
    scaled_sigma = sigma * inv4
    s_square = s_scale * scaled_sigma * inv4
    weight = 1.0 / (1.0 + (mu_value / kappa_value) * s_square)
    enhance = (1.0 + kappa_value) - kappa_value * weight
    steep = mu_value * weight * weight
    x_rho = (exchange * cube) * ((4.0 / 3.0) * enhance - (8.0 / 3.0) * steep * s_square)
    radius_scale = (3.0 / (4.0 * math.pi)) ** (1.0 / 3.0)
    root = math.sqrt(radius_scale) * sixth
    radius = radius_scale * inv
    denom = two_a * root * (b1 + root * (b2 + root * (b3 + root * b4)))
    root_slope = two_a * (0.5 * b1 + root * (b2 + root * (1.5 * b3 + root * (2.0 * b4))))
    recip = 1.0 / (denom * (denom + 1.0))
    log_term = jnp.log(1.0 + recip * (denom + 1.0))
    linear = two_a * (1.0 + correlation_alpha * radius)
    uniform = -linear * log_term
    rho_uniform = (1.0 / 3.0) * (
        (two_a * correlation_alpha) * radius * log_term - linear * recip * (root * root_slope)
    )
    ratio = beta_value / gamma_value
    t_scale = math.pi / (16.0 * (3.0 * math.pi**2) ** (1.0 / 3.0))
    t_square = t_scale * scaled_sigma * (inv2 * inv)
    coefficient = ratio / (jnp.exp(uniform * (-1.0 / gamma_value)) - 1.0)
    u = coefficient * t_square
    inv_d = 1.0 / (1.0 + u + u * u)
    inside = 1.0 + ratio * t_square * (1.0 + u) * inv_d
    gradient = gamma_value * jnp.log(inside)
    common = beta_value * inv_d * (inv_d / inside)
    h_t = common * (1.0 + 2.0 * u)
    h_uniform = -common * (u * u) * (2.0 + u) * t_square * (
        1.0 / gamma_value + coefficient * (1.0 / beta_value)
    )
    d_rho = (
        x_rho
        + uniform
        + gradient
        + rho_uniform * (1.0 + h_uniform)
        - (7.0 / 3.0) * h_t * t_square
    )
    two_d_sigma = inv4 * ((2.0 * exchange * s_scale) * steep + (2.0 * t_scale) * h_t)
    return d_rho, two_d_sigma


def potential_body(
    flag_ref, below_ref, rho_ref, above_ref, head_ref, tail_ref, out_ref,
    ext_ref, part_ref, smooth_ref, flat_ref, fx_ref, fy_ref, fz_ref,
):
    depth, rows, width = out_ref.shape
    total = depth + 2 * reach
    first, last = flag_ref[0] == 1, flag_ref[1] == 1
    slope = 1.0 / (2.0 * grid_step)
    tiles = rows // 8 + 1

    for z in range(total):
        if z < reach:
            plane = below_ref[z]
        elif z < depth + reach:
            plane = rho_ref[z - reach]
        else:
            plane = above_ref[z - depth - reach]
        side = slice(reach * z, reach * (z + 1))
        ext_ref[z, lead : lead + rows] = plane
        ext_ref[z, lead - reach : lead] = head_ref[side]
        ext_ref[z, lead + rows : lead + rows + reach] = tail_ref[side]

    @pl.when(first)
    def _():
        ext_ref[reach - 1] = ext_ref[reach]

    @pl.when(last)
    def _():
        ext_ref[depth + reach] = ext_ref[depth + reach - 1]

    def filter_plane(z, carry):
        for t in range(tiles):
            r = lead - 2 + 8 * t
            along_y = 0.25 * (ext_ref[z, r - 1 : r + 7] + ext_ref[z, r + 1 : r + 9]) + 0.5 * (
                ext_ref[z, r : r + 8]
            )
            part_ref[z, r : r + 8] = (
                0.25 * (roll_x(along_y, 1) + roll_x(along_y, -1)) + 0.5 * along_y
            )
        return carry

    lax.fori_loop(0, total, filter_plane, 0)

    def filter_depth(z, carry):
        r = slice(lead - 2, lead - 2 + 8 * tiles)
        smooth_ref[z, r] = 0.25 * (part_ref[z, r] + part_ref[z + 2, r]) + 0.5 * part_ref[z + 1, r]
        return carry

    lax.fori_loop(0, total - 2, filter_depth, 0)

    @pl.when(first)
    def _():
        smooth_ref[1] = smooth_ref[2]

    @pl.when(last)
    def _():
        smooth_ref[depth + 2] = smooth_ref[depth + 1]

    def local_terms(z, carry):
        for t in range(tiles):
            r = lead - 1 + 8 * t
            center = smooth_ref[z + 1, r : r + 8]
            gx = (roll_x(center, -1) - roll_x(center, 1)) * slope
            gy = (smooth_ref[z + 1, r + 1 : r + 9] - smooth_ref[z + 1, r - 1 : r + 7]) * slope
            gz = (smooth_ref[z + 2, r : r + 8] - smooth_ref[z, r : r + 8]) * slope
            d_rho, two_d_sigma = energy_slopes(center, gx * gx + gy * gy + gz * gz)
            flat_ref[z, r : r + 8] = d_rho
            fx_ref[z, r : r + 8] = two_d_sigma * gx
            fy_ref[z, r : r + 8] = two_d_sigma * gy
            fz_ref[z, r : r + 8] = two_d_sigma * gz
        return carry

    lax.fori_loop(0, depth + 2, local_terms, 0)

    @pl.when(first)
    def _():
        fz_ref[0] = fz_ref[1]

    @pl.when(last)
    def _():
        fz_ref[depth + 1] = fz_ref[depth]

    def collect(z, carry):
        for t in range(rows // 8):
            r = lead + 8 * t
            here = slice(r, r + 8)
            fx = fx_ref[z + 1, here]
            along_x = (roll_x(fx, -1) - roll_x(fx, 1)) * slope
            along_y = (fy_ref[z + 1, r + 1 : r + 9] - fy_ref[z + 1, r - 1 : r + 7]) * slope
            along_z = (fz_ref[z + 2, here] - fz_ref[z, here]) * slope
            out_ref[z, 8 * t : 8 * t + 8] = flat_ref[z + 1, here] - (along_x + along_y + along_z)
        return carry

    lax.fori_loop(0, depth, collect, 0)


def potential_of(flags, below, density, above, head, tail):
    depth, rows, width = density.shape
    tall = -(-(rows + lead + 8) // 8) * 8
    planes = lambda count: pltpu.VMEM((count, tall, width), f32)
    vmem = pl.BlockSpec(memory_space=pltpu.VMEM)
    return call(
        potential_body,
        jax.ShapeDtypeStruct((depth, rows, width), f32),
        56,
        in_specs=[pl.BlockSpec(memory_space=pltpu.SMEM)] + [vmem] * 5,
        out_specs=vmem,
        scratch_shapes=[
            planes(depth + 6), planes(depth + 6), planes(depth + 4),
            planes(depth + 2), planes(depth + 2), planes(depth + 2), planes(depth + 2),
        ],
        name="potential",
    )(flags, below, density, above, head, tail)


def forward_columns_body(x_ref, ch_ref, cl_ref, sh_ref, sl_ref, out_ref, high_ref, low_ref):
    rows = high_ref.shape[0]
    high_ref[...], low_ref[...] = split(x_ref[...].reshape(rows, x_ref.shape[2]))
    group = 4
    block = out_ref.shape[2]

    def step(m, carry):
        at = pl.ds(pl.multiple_of(m * group * block, group * block), group * block)
        to = pl.ds(m * group, group)
        high, low = high_ref[...], low_ref[...]
        out_re = triple(dot_nt, ch_ref[at], cl_ref[at], high, low)
        out_im = -triple(dot_nt, sh_ref[at], sl_ref[at], high, low)
        out_ref[to, 0] = out_re.reshape(group, block, rows)
        out_ref[to, 1] = out_im.reshape(group, block, rows)
        return carry

    lax.fori_loop(0, out_ref.shape[0] // group, step, 0)


def forward_columns(potential, tables, parts, steps):
    depth, local, width = potential.shape
    planes = depth // steps
    block = width // parts
    rows = planes * local
    return call(
        forward_columns_body,
        jax.ShapeDtypeStruct((parts, 2, block, depth * local), f32),
        48,
        grid=(steps,),
        in_specs=[pl.BlockSpec((planes, local, width), lambda i: (i, 0, 0))]
        + [whole((width, width))] * 4,
        out_specs=pl.BlockSpec((parts, 2, block, rows), lambda i: (0, 0, 0, i)),
        scratch_shapes=[pltpu.VMEM((rows, width), bf16), pltpu.VMEM((rows, width), bf16)],
        name="forward_columns",
    )(potential, *tables)


def forward_rows_body(flag_ref, in_ref, ch_ref, cl_ref, sh_ref, sl_ref, out_ref, high_ref, low_ref):
    gather_blocks(in_ref, high_ref, low_ref)
    _, planes, rows, width = out_ref.shape
    group = planes // 2

    def step(m, carry):
        at = pl.ds(pl.multiple_of(m * group * rows, group * rows), group * rows)
        to = pl.ds(m * group, group)
        real = (high_ref[0, at], low_ref[0, at])
        imag = (high_ref[1, at], low_ref[1, at])
        cos = (ch_ref[...], cl_ref[...])
        sin = (sh_ref[...], sl_ref[...])
        out_re = triple(dot_nn, *real, *cos) + triple(dot_nn, *imag, *sin)
        out_ref[0, to] = out_re.reshape(group, rows, width)
        out_im = triple(dot_nn, *imag, *cos) - triple(dot_nn, *real, *sin)
        out_ref[1, to] = out_im.reshape(group, rows, width)
        return carry

    lax.fori_loop(0, 2, step, 0)

    @pl.when(flag_ref[2] == 1)
    def _():
        tile = (8, 128)
        at_zero = (lax.broadcasted_iota(jnp.int32, tile, 0) == 0) & (
            lax.broadcasted_iota(jnp.int32, tile, 1) == 0
        )
        for c in range(2):
            for z in range(planes):
                out_ref[c, z, :8, :128] = jnp.where(at_zero, 0.0, out_ref[c, z, :8, :128])


def forward_rows(flags, blocks, tables, steps):
    parts, _, rows, lanes = blocks.shape
    width = tables[0].shape[0]
    depth = lanes * parts // width
    planes = depth // steps
    scratch = pltpu.VMEM((2, planes * rows, width), bf16)
    return call(
        forward_rows_body,
        jax.ShapeDtypeStruct((2, depth, rows, width), f32),
        48,
        grid=(steps,),
        in_specs=[
            pl.BlockSpec(memory_space=pltpu.SMEM),
            pl.BlockSpec((parts, 2, rows, lanes // steps), lambda i: (0, 0, 0, i)),
        ]
        + [whole((width, width))] * 4,
        out_specs=pl.BlockSpec((2, planes, rows, width), lambda i: (0, i, 0, 0)),
        scratch_shapes=[scratch, scratch],
        name="forward_rows",
    )(flags, blocks, *tables)


def on_device(rho_hat):
    parts = lax.axis_size("py")
    place_z, place_y = lax.axis_index("px"), lax.axis_index("py")
    flags = jnp.stack(
        [place_z == 0, place_z == lax.axis_size("px") - 1, place_y == 0]
    ).astype(jnp.int32)
    width = rho_hat.shape[3]
    tables = phase_tables(width, width // parts)
    columns = inverse_rows(rho_hat, tables, parts, 2)
    columns = lax.all_to_all(columns, "py", 0, 0, tiled=True)
    density = inverse_columns(columns, tables, 2)
    below = shift(density[-reach:], "px", True)
    above = shift(density[:reach], "px", False)
    head, tail = edges(below, density, above)
    head, tail = shift(tail, "py", True), shift(head, "py", False)
    potential = potential_of(flags, below, density, above, head, tail)
    spectral = forward_columns(potential, tables, parts, 2)
    spectral = lax.all_to_all(spectral, "py", 0, 0, tiled=True)
    return forward_rows(flags, spectral, tables, 2)


def solution(mesh):
    return jax.shard_map(
        on_device,
        mesh=mesh,
        in_specs=(P(None, "px", "py", None),),
        out_specs=P(None, "px", "py", None),
        check_vma=False,
    )
```

```python
import math

import jax
import jax.numpy as jnp
import numpy as np
from jax import lax
from jax.experimental import pallas as pl
from jax.experimental.pallas import tpu as pltpu
from jax.sharding import PartitionSpec as P

grid_step = 0.25
density_floor = 0.02
density_scale = 0.2
kappa_value = 0.804
mu_value = 0.2195149727645171
beta_value = 0.06672455060314922
gamma_value = (1.0 - math.log(2.0)) / (math.pi * math.pi)
correlation_scale = 0.031091
correlation_alpha = 0.2137
correlation_terms = (7.5957, 3.5876, 1.6382, 0.49294)

f32 = jnp.float32
bf16 = jnp.bfloat16
reach = 3
lead = 9


def params(mib):
    return pltpu.CompilerParams(vmem_limit_bytes=mib << 20)


def call(body, out, mib, cost, **options):
    estimate = pl.CostEstimate(flops=int(cost * 1e9), bytes_accessed=1 << 20, transcendentals=0)
    return pl.pallas_call(
        body, out_shape=out, compiler_params=params(mib), cost_estimate=estimate, **options
    )


def array(*shape):
    return jax.ShapeDtypeStruct(shape, f32)


def whole(shape):
    return pl.BlockSpec(shape, lambda *_: (0,) * len(shape))


def split(value):
    high = value.astype(bf16)
    return high, (value - high.astype(f32)).astype(bf16)


def dot_nt(left, right):
    return lax.dot_general(left, right, (((1,), (1,)), ((), ())), preferred_element_type=f32)


def dot_nn(left, right):
    return lax.dot_general(left, right, (((1,), (0,)), ((), ())), preferred_element_type=f32)


def triple(dot, left_high, left_low, right_high, right_low):
    return dot(left_high, right_high) + (dot(left_low, right_high) + dot(left_high, right_low))


def tables_body(stride, coarse_ref, fine_ref, ch_ref, cl_ref, sh_ref, sl_ref):
    fine_cos, fine_sin = fine_ref[0], fine_ref[1]
    for a in range(coarse_ref.shape[1]):
        cos_a, sin_a = coarse_ref[0, a : a + 1], coarse_ref[1, a : a + 1]
        rows = slice(stride * a, stride * (a + 1))
        ch_ref[rows], cl_ref[rows] = split(cos_a * fine_cos - sin_a * fine_sin)
        sh_ref[rows], sl_ref[rows] = split(sin_a * fine_cos + cos_a * fine_sin)


def phase_tables(length, stride):
    def waves(rows, scale):
        angle = (np.outer(rows, np.arange(length)) % length) * (2.0 * math.pi / length)
        return np.stack([np.cos(angle), np.sin(angle)]).astype(np.float32) * np.float32(scale)

    coarse = waves(np.arange(0, length, stride), 1.0)
    fine = waves(np.arange(stride), 1.0 / math.sqrt(length))
    out = [jax.ShapeDtypeStruct((length, length), bf16)] * 4
    body = lambda *refs: tables_body(stride, *refs)
    return call(body, out, 32, 2, name="tables")(jnp.asarray(coarse), jnp.asarray(fine))


def inverse_rows_body(count, *refs):
    planes, (ch_ref, cl_ref, sh_ref, sl_ref, out_ref, wide_ref) = refs[:count], refs[count:]
    width = ch_ref.shape[0]
    lanes = wide_ref.shape[1] // 2
    for c in range(2):
        joined = jnp.concatenate([ref[c].reshape(-1, width) for ref in planes], axis=0)
        high, low = split(joined.T)
        cos_at = slice(c * lanes, (c + 1) * lanes)
        sin_at = slice((1 - c) * lanes, (2 - c) * lanes)
        for k, value in enumerate((high, high, low)):
            wide_ref[k * width : (k + 1) * width, cos_at] = value
            wide_ref[(k + 3) * width : (k + 4) * width, sin_at] = value if c == 0 else -value
    _, block, out_lanes = out_ref.shape
    group = out_ref.shape[0] // 2

    def step(m, carry):
        at = pl.ds(pl.multiple_of(m * group * block, group * block), group * block)
        ch, sh = ch_ref[at], sh_ref[at]
        left = jnp.concatenate([ch, cl_ref[at], ch, sh, sl_ref[at], sh], axis=1)
        product = dot_nn(left, wide_ref[...])
        out_ref[pl.ds(m * group, group)] = product.reshape(group, block, out_lanes)
        return carry

    lax.fori_loop(0, 2, step, 0)


def inverse_rows(rho_hat, tables, parts, blocks):
    _, depth, local, width = rho_hat.shape
    unit = depth // 4
    lanes = len(blocks) * unit * local
    piece = lambda b: pl.BlockSpec((2, unit, local, width), lambda i: (0, b, 0, 0))
    out = (parts, width // parts, 2 * lanes)
    return call(
        lambda *refs: inverse_rows_body(len(blocks), *refs),
        array(*out),
        48,
        5.0 * len(blocks),
        grid=(1,),
        in_specs=[piece(b) for b in blocks] + [whole((width, width))] * 4,
        out_specs=whole(out),
        scratch_shapes=[pltpu.VMEM((6 * width, 2 * lanes), bf16)],
        name="inverse_rows",
    )(*[rho_hat] * len(blocks), *tables)


def gather_blocks(in_ref, high_ref, low_ref, total, start, count):
    parts, rows, _ = in_ref.shape
    local = high_ref.shape[2] // parts
    for z in range(count):
        to = slice(z * rows, (z + 1) * rows)
        for c in range(2):
            first = (c * total + start + z) * local
            pieces = [in_ref[s, :, first : first + local] for s in range(parts)]
            high_ref[c, to], low_ref[c, to] = split(jnp.concatenate(pieces, axis=-1))


def inverse_columns_body(
    in_ref, ch_ref, cl_ref, sh_ref, sl_ref, out_ref, head_ref, tail_ref, high_ref, low_ref
):
    planes, rows, width = out_ref.shape
    gather_blocks(in_ref, high_ref, low_ref, planes, 0, planes)
    field = triple(dot_nn, high_ref[0], low_ref[0], ch_ref[...], cl_ref[...])
    field = field - triple(dot_nn, high_ref[1], low_ref[1], sh_ref[...], sl_ref[...])
    soft = jnp.maximum(field, 0.0) + jnp.log1p(jnp.exp(-jnp.abs(field)))
    out_ref[...] = (density_floor + density_scale * soft).reshape(planes, rows, width)
    for z in range(planes):
        at = slice(reach * z, reach * (z + 1))
        head_ref[at] = out_ref[z, :reach]
        tail_ref[at] = out_ref[z, rows - reach :]


def inverse_columns(blocks, tables):
    parts, rows, lanes = blocks.shape
    width = tables[0].shape[0]
    planes = lanes * parts // (2 * width)
    scratch = pltpu.VMEM((2, planes * rows, width), bf16)
    side = (reach * planes, width)
    return call(
        inverse_columns_body,
        [array(planes, rows, width), array(*side), array(*side)],
        48,
        1.2 * planes,
        grid=(1,),
        in_specs=[whole(blocks.shape)] + [whole((width, width))] * 4,
        out_specs=[whole((planes, rows, width)), whole(side), whole(side)],
        scratch_shapes=[scratch, scratch],
        name="inverse_columns",
    )(blocks, *tables)


def shift(value, axis, up):
    count = lax.axis_size(axis)
    pairs = [(i, (i + 1) % count) for i in range(count)]
    return lax.ppermute(value, axis, pairs if up else [(b, a) for a, b in pairs])


def edges_body(below_ref, head_ref, tail_ref, above_ref, head_out, tail_out):
    rows = below_ref.shape[1]
    middle = head_ref.shape[0]
    for z in range(reach):
        for ref, first in ((below_ref, 0), (above_ref, reach * reach + middle)):
            to = slice(first + reach * z, first + reach * (z + 1))
            head_out[to], tail_out[to] = ref[z, :reach], ref[z, rows - reach :]
    to = slice(reach * reach, reach * reach + middle)
    head_out[to], tail_out[to] = head_ref[...], tail_ref[...]


def edges(below, head, tail, above):
    width = head.shape[1]
    count = -(-(head.shape[0] + 2 * reach * reach) // 8) * 8
    vmem = pl.BlockSpec(memory_space=pltpu.VMEM)
    return call(
        edges_body,
        [array(count, width)] * 2,
        16,
        1.0,
        in_specs=[vmem] * 4,
        out_specs=[vmem] * 2,
        name="edges",
    )(below, head, tail, above)


def roll_x(value, by):
    return pltpu.roll(value, by % value.shape[-1], value.ndim - 1)


def energy_slopes(rho, sigma):
    two_a = 2.0 * correlation_scale
    b1, b2, b3, b4 = correlation_terms
    sixth = jnp.exp(jnp.log(rho) * (-1.0 / 6.0))
    inv = sixth * sixth
    inv2 = inv * inv
    inv4 = inv2 * inv2
    cube = rho * inv2
    exchange = -0.75 * (3.0 / math.pi) ** (1.0 / 3.0)
    s_scale = 0.25 / (3.0 * math.pi**2) ** (2.0 / 3.0)
    scaled_sigma = sigma * inv4
    s_square = s_scale * scaled_sigma * inv4
    weight = 1.0 / (1.0 + (mu_value / kappa_value) * s_square)
    enhance = (1.0 + kappa_value) - kappa_value * weight
    steep = mu_value * weight * weight
    x_rho = (exchange * cube) * ((4.0 / 3.0) * enhance - (8.0 / 3.0) * steep * s_square)
    radius_scale = (3.0 / (4.0 * math.pi)) ** (1.0 / 3.0)
    root = math.sqrt(radius_scale) * sixth
    radius = radius_scale * inv
    denom = two_a * root * (b1 + root * (b2 + root * (b3 + root * b4)))
    root_slope = two_a * (0.5 * b1 + root * (b2 + root * (1.5 * b3 + root * (2.0 * b4))))
    recip = 1.0 / (denom * (denom + 1.0))
    log_term = jnp.log(1.0 + recip * (denom + 1.0))
    linear = two_a * (1.0 + correlation_alpha * radius)
    uniform = -linear * log_term
    rho_uniform = (1.0 / 3.0) * (
        (two_a * correlation_alpha) * radius * log_term - linear * recip * (root * root_slope)
    )
    ratio = beta_value / gamma_value
    t_scale = math.pi / (16.0 * (3.0 * math.pi**2) ** (1.0 / 3.0))
    t_square = t_scale * scaled_sigma * (inv2 * inv)
    coefficient = ratio / (jnp.exp(uniform * (-1.0 / gamma_value)) - 1.0)
    u = coefficient * t_square
    inv_d = 1.0 / (1.0 + u + u * u)
    inside = 1.0 + ratio * t_square * (1.0 + u) * inv_d
    gradient = gamma_value * jnp.log(inside)
    common = beta_value * inv_d * (inv_d / inside)
    h_t = common * (1.0 + 2.0 * u)
    h_uniform = -common * (u * u) * (2.0 + u) * t_square * (
        1.0 / gamma_value + coefficient * (1.0 / beta_value)
    )
    d_rho = (
        x_rho
        + uniform
        + gradient
        + rho_uniform * (1.0 + h_uniform)
        - (7.0 / 3.0) * h_t * t_square
    )
    two_d_sigma = inv4 * ((2.0 * exchange * s_scale) * steep + (2.0 * t_scale) * h_t)
    return d_rho, two_d_sigma


def potential_body(sources, bottom, top, flag_ref, *refs):
    out_ref, ext_ref, part_ref, smooth_ref, flat_ref, fx_ref, fy_ref, fz_ref = refs[-8:]
    depth, rows, width = out_ref.shape
    total = depth + 2 * reach
    slope = 1.0 / (2.0 * grid_step)
    tiles = rows // 8 + 1

    def at_end(is_end, flag):
        return pl.when(flag_ref[flag] == 1) if is_end else lambda body: None

    for z, (plane, at, side, row) in enumerate(sources):
        ext_ref[z, lead : lead + rows] = refs[plane][at]
        ext_ref[z, lead - reach : lead] = refs[side][row : row + reach]
        ext_ref[z, lead + rows : lead + rows + reach] = refs[side + 1][row : row + reach]

    @at_end(bottom, 0)
    def _():
        ext_ref[reach - 1] = ext_ref[reach]

    @at_end(top, 1)
    def _():
        ext_ref[depth + reach] = ext_ref[depth + reach - 1]

    def filter_plane(z, carry):
        for t in range(tiles):
            r = lead - 2 + 8 * t
            along_y = 0.25 * (ext_ref[z, r - 1 : r + 7] + ext_ref[z, r + 1 : r + 9]) + 0.5 * (
                ext_ref[z, r : r + 8]
            )
            part_ref[z, r : r + 8] = (
                0.25 * (roll_x(along_y, 1) + roll_x(along_y, -1)) + 0.5 * along_y
            )
        return carry

    lax.fori_loop(0, total, filter_plane, 0)

    def filter_depth(z, carry):
        r = slice(lead - 2, lead - 2 + 8 * tiles)
        smooth_ref[z, r] = 0.25 * (part_ref[z, r] + part_ref[z + 2, r]) + 0.5 * part_ref[z + 1, r]
        return carry

    lax.fori_loop(0, total - 2, filter_depth, 0)

    @at_end(bottom, 0)
    def _():
        smooth_ref[1] = smooth_ref[2]

    @at_end(top, 1)
    def _():
        smooth_ref[depth + 2] = smooth_ref[depth + 1]

    def local_terms(z, carry):
        for t in range(tiles):
            r = lead - 1 + 8 * t
            center = smooth_ref[z + 1, r : r + 8]
            gx = (roll_x(center, -1) - roll_x(center, 1)) * slope
            gy = (smooth_ref[z + 1, r + 1 : r + 9] - smooth_ref[z + 1, r - 1 : r + 7]) * slope
            gz = (smooth_ref[z + 2, r : r + 8] - smooth_ref[z, r : r + 8]) * slope
            d_rho, two_d_sigma = energy_slopes(center, gx * gx + gy * gy + gz * gz)
            flat_ref[z, r : r + 8] = d_rho
            fx_ref[z, r : r + 8] = two_d_sigma * gx
            fy_ref[z, r : r + 8] = two_d_sigma * gy
            fz_ref[z, r : r + 8] = two_d_sigma * gz
        return carry

    lax.fori_loop(0, depth + 2, local_terms, 0)

    @at_end(bottom, 0)
    def _():
        fz_ref[0] = fz_ref[1]

    @at_end(top, 1)
    def _():
        fz_ref[depth + 1] = fz_ref[depth]

    def collect(z, carry):
        for t in range(rows // 8):
            r = lead + 8 * t
            here = slice(r, r + 8)
            fx = fx_ref[z + 1, here]
            along_x = (roll_x(fx, -1) - roll_x(fx, 1)) * slope
            along_y = (fy_ref[z + 1, r + 1 : r + 9] - fy_ref[z + 1, r - 1 : r + 7]) * slope
            along_z = (fz_ref[z + 2, here] - fz_ref[z, here]) * slope
            out_ref[z, 8 * t : 8 * t + 8] = flat_ref[z + 1, here] - (along_x + along_y + along_z)
        return carry

    lax.fori_loop(0, depth, collect, 0)


def potential_of(flags, arrays, sources, start, count, depth):
    _, rows, width = arrays[0].shape
    tall = -(-(rows + lead + 8) // 8) * 8
    planes = lambda extra: pltpu.VMEM((count + extra, tall, width), f32)
    vmem = pl.BlockSpec(memory_space=pltpu.VMEM)
    used = sources[start : start + count + 2 * reach]
    body = lambda *refs: potential_body(used, start == 0, start + count == depth, *refs)
    return call(
        body,
        array(count, rows, width),
        56,
        2.0 * (count + 2),
        in_specs=[pl.BlockSpec(memory_space=pltpu.SMEM)] + [vmem] * len(arrays),
        out_specs=vmem,
        scratch_shapes=[planes(extra) for extra in (6, 6, 4, 2, 2, 2, 2)],
        name="potential",
    )(flags, *arrays)


def forward_columns_body(x_ref, ch_ref, cl_ref, sh_ref, sl_ref, out_ref, tall_ref):
    planes, rows, width = x_ref.shape
    high, low = split(x_ref[...].reshape(planes * rows, width).T)
    for k, value in enumerate((high, high, low)):
        tall_ref[k * width : (k + 1) * width] = value
    _, block, out_lanes = out_ref.shape
    group = out_ref.shape[0] // 2

    def step(m, carry):
        at = pl.ds(pl.multiple_of(m * group * block, group * block), group * block)
        ch, sh = ch_ref[at], sh_ref[at]
        real = dot_nn(jnp.concatenate([ch, cl_ref[at], ch], axis=1), tall_ref[...])
        imag = dot_nn(jnp.concatenate([sh, sl_ref[at], sh], axis=1), tall_ref[...])
        both = jnp.concatenate([real, -imag], axis=1)
        out_ref[pl.ds(m * group, group)] = both.reshape(group, block, out_lanes)
        return carry

    lax.fori_loop(0, 2, step, 0)


def forward_columns(potential, tables, parts):
    planes, rows, width = potential.shape
    lanes = planes * rows
    out = (parts, width // parts, 2 * lanes)
    return call(
        forward_columns_body,
        array(*out),
        48,
        1.2 * planes,
        grid=(1,),
        in_specs=[whole(potential.shape)] + [whole((width, width))] * 4,
        out_specs=whole(out),
        scratch_shapes=[pltpu.VMEM((3 * width, lanes), bf16)],
        name="forward_columns",
    )(potential, *tables)


def forward_rows_body(total, flag_ref, in_ref, *refs):
    ch_ref, cl_ref, sh_ref, sl_ref, out_ref, high_ref, low_ref = refs[-7:]
    _, planes, rows, width = out_ref.shape
    for i in range(total // planes):

        @pl.when(pl.program_id(0) == i)
        def _():
            gather_blocks(in_ref, high_ref, low_ref, total, i * planes, planes)

    real = (high_ref[0], low_ref[0])
    imag = (high_ref[1], low_ref[1])
    cos = (ch_ref[...], cl_ref[...])
    sin = (sh_ref[...], sl_ref[...])
    out_re = triple(dot_nn, *real, *cos) + triple(dot_nn, *imag, *sin)
    out_ref[0] = out_re.reshape(planes, rows, width)
    out_im = triple(dot_nn, *imag, *cos) - triple(dot_nn, *real, *sin)
    out_ref[1] = out_im.reshape(planes, rows, width)

    @pl.when(flag_ref[2] == 1)
    def _():
        tile = (8, 128)
        at_zero = (lax.broadcasted_iota(jnp.int32, tile, 0) == 0) & (
            lax.broadcasted_iota(jnp.int32, tile, 1) == 0
        )
        for c in range(2):
            for z in range(planes):
                out_ref[c, z, :8, :128] = jnp.where(at_zero, 0.0, out_ref[c, z, :8, :128])


def forward_rows(flags, blocks, tables, first, depth, before):
    parts, rows, lanes = blocks.shape
    width = tables[0].shape[0]
    total = lanes * parts // (2 * width)
    unit = depth // 4
    scratch = pltpu.VMEM((2, unit * rows, width), bf16)
    earlier = [] if before is None else [before]
    return call(
        lambda *refs: forward_rows_body(total, *refs),
        array(2, depth, rows, width),
        48,
        2.3 * total,
        grid=(total // unit,),
        in_specs=[pl.BlockSpec(memory_space=pltpu.SMEM), whole(blocks.shape)]
        + [pl.BlockSpec(memory_space=pl.ANY)] * len(earlier)
        + [whole((width, width))] * 4,
        out_specs=pl.BlockSpec((2, unit, rows, width), lambda i: (0, first + i, 0, 0)),
        scratch_shapes=[scratch, scratch],
        input_output_aliases={2: 0} if earlier else {},
        name="forward_rows",
    )(flags, blocks, *earlier, *tables)


def exchange(value):
    return lax.all_to_all(value, "py", 0, 0, tiled=True)


def on_device(rho_hat):
    parts = lax.axis_size("py")
    place_z, place_y = lax.axis_index("px"), lax.axis_index("py")
    flags = jnp.stack(
        [place_z == 0, place_z == lax.axis_size("px") - 1, place_y == 0]
    ).astype(jnp.int32)
    depth, width = rho_hat.shape[1], rho_hat.shape[3]
    unit = depth // 4
    tables = phase_tables(width, width // parts)

    outer = exchange(inverse_rows(rho_hat, tables, parts, (0, 3)))
    inner = exchange(inverse_rows(rho_hat, tables, parts, (1, 2)))
    outer, head, tail = inverse_columns(outer, tables)
    below = shift(outer[-reach:], "px", True)
    above = shift(outer[:reach], "px", False)
    head, tail = edges(below, head, tail, above)
    head, tail = shift(tail, "py", True), shift(head, "py", False)
    inner, inner_head, inner_tail = inverse_columns(inner, tables)
    inner_head, inner_tail = shift(inner_tail, "py", True), shift(inner_head, "py", False)

    arrays = [below, outer, inner, above, head, tail, inner_head, inner_tail]
    sources = []
    for z in range(-reach, depth + reach):
        if z < 0:
            sources.append((0, z + reach, 4, reach * (z + reach)))
        elif z < unit:
            sources.append((1, z, 4, reach * (z + reach)))
        elif z < depth - unit:
            sources.append((2, z - unit, 6, reach * (z - unit)))
        elif z < depth:
            at = z - depth + 2 * unit
            sources.append((1, at, 4, reach * (at + reach)))
        else:
            at = z - depth
            sources.append((3, at, 4, reach * (at + reach + 2 * unit)))

    result = None
    for first, count in ((0, 1), (1, 2), (3, 1)):
        planes = (first * unit, count * unit)
        potential = potential_of(flags, arrays, sources, *planes, depth)
        spectral = exchange(forward_columns(potential, tables, parts))
        result = forward_rows(flags, spectral, tables, first, depth, result)
    return result


def solution(mesh):
    return jax.shard_map(
        on_device,
        mesh=mesh,
        in_specs=(P(None, "px", "py", None),),
        out_specs=P(None, "px", "py", None),
        check_vma=False,
    )
```

```python
import math

import jax
import jax.numpy as jnp
import numpy as np
from jax import lax
from jax.experimental import pallas as pl
from jax.experimental.pallas import tpu as pltpu
from jax.sharding import PartitionSpec as P

grid_step = 0.25
density_floor = 0.02
density_scale = 0.2
kappa_value = 0.804
mu_value = 0.2195149727645171
beta_value = 0.06672455060314922
gamma_value = (1.0 - math.log(2.0)) / (math.pi * math.pi)
correlation_scale = 0.031091
correlation_alpha = 0.2137
correlation_terms = (7.5957, 3.5876, 1.6382, 0.49294)

f32 = jnp.float32
bf16 = jnp.bfloat16
reach = 3
lead = 9


in_hbm = pl.BlockSpec(memory_space=pltpu.HBM)


def call(body, out, cost, **options):
    estimate = pl.CostEstimate(flops=int(cost * 1e9), bytes_accessed=1 << 20, transcendentals=0)
    limit = pltpu.CompilerParams(vmem_limit_bytes=62 << 20)
    return pl.pallas_call(body, out_shape=out, compiler_params=limit, cost_estimate=estimate, **options)


def array(*shape):
    return jax.ShapeDtypeStruct(shape, f32)


def whole(shape):
    return pl.BlockSpec(shape, lambda *_: (0,) * len(shape))


def copy_all(pairs, sems):
    copies = [pltpu.make_async_copy(a, b, sems.at[i]) for i, (a, b) in enumerate(pairs)]
    for copy in copies:
        copy.start()
    return copies


def wait_all(copies):
    for copy in copies:
        copy.wait()


def load_tables(hbm_ref, tab_ref, sems):
    return copy_all([(hbm_ref.at[i], tab_ref.at[i]) for i in range(4)], sems)


def table_scratch(width):
    return [pltpu.VMEM((4, width, width), bf16), pltpu.SemaphoreType.DMA((4,))]


def split(value):
    high = value.astype(bf16)
    return high, (value - high.astype(f32)).astype(bf16)


def dot_nt(left, right):
    return lax.dot_general(left, right, (((1,), (1,)), ((), ())), preferred_element_type=f32)


def dot_nn(left, right):
    return lax.dot_general(left, right, (((1,), (0,)), ((), ())), preferred_element_type=f32)


def triple(dot, left_high, left_low, right_high, right_low):
    return dot(left_high, right_high) + (dot(left_low, right_high) + dot(left_high, right_low))


def fill_tables(coarse_ref, fine_ref, tab_ref):
    fine_cos, fine_sin = fine_ref[0], fine_ref[1]
    stride = fine_ref.shape[1]
    for a in range(coarse_ref.shape[1]):
        cos_a, sin_a = coarse_ref[0, a : a + 1], coarse_ref[1, a : a + 1]
        rows = slice(stride * a, stride * (a + 1))
        tab_ref[0, rows], tab_ref[1, rows] = split(cos_a * fine_cos - sin_a * fine_sin)
        tab_ref[2, rows], tab_ref[3, rows] = split(sin_a * fine_cos + cos_a * fine_sin)


def phase_factors(length, stride):
    def waves(rows, scale):
        angle = (np.outer(rows, np.arange(length)) % length) * (2.0 * math.pi / length)
        return np.stack([np.cos(angle), np.sin(angle)]).astype(np.float32) * np.float32(scale)

    coarse = waves(np.arange(0, length, stride), 1.0)
    fine = waves(np.arange(stride), 1.0 / math.sqrt(length))
    return jnp.asarray(coarse), jnp.asarray(fine)


def inverse_rows_body(blocks, fills, *refs):
    if fills:
        rho_ref, coarse_ref, fine_ref, out_ref, tab_out_ref = refs[:5]
    else:
        rho_ref, tab_hbm_ref, out_ref = refs[:3]
    tab_ref, tab_sems, x_ref, wide_ref, stage_ref, in_sems, out_sems = refs[-7:]
    width = tab_ref.shape[1]
    lanes = wide_ref.shape[1] // 2
    unit = x_ref.shape[1] // len(blocks)
    arriving = [
        copy_all(
            [
                (rho_ref.at[c, pl.ds(b * unit, unit)], x_ref.at[c, pl.ds(i * unit, unit)])
                for i, b in enumerate(blocks)
            ],
            in_sems.at[c],
        )
        for c in range(2)
    ]
    if fills:
        fill_tables(coarse_ref, fine_ref, tab_ref)
        tables = copy_all([(tab_ref.at[i], tab_out_ref.at[i]) for i in range(4)], tab_sems)
    else:
        tables = load_tables(tab_hbm_ref, tab_ref, tab_sems)
    for c in range(2):
        wait_all(arriving[c])
        high, low = split(x_ref[c].reshape(lanes, width).T)
        cos_at = slice(c * lanes, (c + 1) * lanes)
        sin_at = slice((1 - c) * lanes, (2 - c) * lanes)
        for k, value in enumerate((high, high, low)):
            wide_ref[k * width : (k + 1) * width, cos_at] = value
            wide_ref[(k + 3) * width : (k + 4) * width, sin_at] = value if c == 0 else -value
    if not fills:
        wait_all(tables)
    parts, block, out_lanes = stage_ref.shape
    group = parts // 2
    leaving = []
    for m in range(2):
        at = slice(m * group * block, (m + 1) * group * block)
        ch, sh = tab_ref[0, at], tab_ref[2, at]
        left = jnp.concatenate([ch, tab_ref[1, at], ch, sh, tab_ref[3, at], sh], axis=1)
        product = dot_nn(left, wide_ref[...])
        stage_ref[m * group : (m + 1) * group] = product.reshape(group, block, out_lanes)
        to = [pl.ds(m * group + g, 1) for g in range(group)]
        leaving += copy_all([(stage_ref.at[d], out_ref.at[d]) for d in to], out_sems.at[m])
    wait_all(leaving)
    if fills:
        wait_all(tables)


def inverse_rows(rho_hat, tables, parts, blocks):
    _, depth, local, width = rho_hat.shape
    unit = depth // 4
    planes = len(blocks) * unit
    lanes = planes * local
    block = width // parts
    out = (parts, block, 2 * lanes)
    scratch = table_scratch(width) + [
        pltpu.VMEM((2, planes, local, width), f32),
        pltpu.VMEM((6 * width, 2 * lanes), bf16),
        pltpu.VMEM(out, f32),
        pltpu.SemaphoreType.DMA((2, len(blocks))),
        pltpu.SemaphoreType.DMA((2, parts // 2)),
    ]
    body = lambda *refs: inverse_rows_body(blocks, tables is None, *refs)
    options = dict(scratch_shapes=scratch, name="inverse_rows", grid=(1,))
    if tables is None:
        factors = phase_factors(width, block)
        made = jax.ShapeDtypeStruct((4, width, width), bf16)
        return call(
            body,
            [array(*out), made],
            10.0,
            in_specs=[in_hbm] + [whole(factor.shape) for factor in factors],
            out_specs=[in_hbm, in_hbm],
            **options,
        )(rho_hat, *factors)
    return call(
        body, array(*out), 10.0, in_specs=[in_hbm] * 2, out_specs=in_hbm, **options
    )(rho_hat, tables)


def gather_blocks(in_ref, high_ref, low_ref, total, start, count):
    parts, rows, _ = in_ref.shape
    local = high_ref.shape[2] // parts
    for z in range(start, start + count):
        to = slice(z * rows, (z + 1) * rows)
        for c in range(2):
            first = (c * total + z) * local
            pieces = [in_ref[s, :, first : first + local] for s in range(parts)]
            high_ref[c, to], low_ref[c, to] = split(jnp.concatenate(pieces, axis=-1))


def fetch_blocks(hbm_ref, in_ref, sems):
    parts = in_ref.shape[0]
    return copy_all([(hbm_ref.at[pl.ds(d, 1)], in_ref.at[pl.ds(d, 1)]) for d in range(parts)], sems)


def inverse_columns_body(sends, blocks_ref, tab_hbm_ref, *refs):
    out_ref, head_ref, tail_ref = refs[:3]
    (tab_ref, tab_sems, in_ref, stage_ref, high_ref, low_ref, in_sems, out_sems, send_sems) = refs[-9:]
    planes, rows, width = stage_ref.shape
    arriving = fetch_blocks(blocks_ref, in_ref, in_sems)
    tables = load_tables(tab_hbm_ref, tab_ref, tab_sems)
    wait_all(arriving)
    half = planes // 2
    leaving = []
    for m in range(2):
        gather_blocks(in_ref, high_ref, low_ref, planes, m * half, half)
        if m == 0:
            wait_all(tables)
        at = slice(m * half * rows, (m + 1) * half * rows)
        field = triple(dot_nn, high_ref[0, at], low_ref[0, at], tab_ref[0], tab_ref[1])
        field = field - triple(dot_nn, high_ref[1, at], low_ref[1, at], tab_ref[2], tab_ref[3])
        soft = jnp.maximum(field, 0.0) + jnp.log1p(jnp.exp(-jnp.abs(field)))
        density = density_floor + density_scale * soft
        stage_ref[m * half : (m + 1) * half] = density.reshape(half, rows, width)
        to = [pl.ds(z, 1) for z in range(m * half, (m + 1) * half)]
        leaving += copy_all([(stage_ref.at[z], out_ref.at[z]) for z in to], out_sems.at[m])
        if sends:
            first = 0 if m == 0 else planes - reach
            slab = (stage_ref.at[pl.ds(first, reach)], refs[3 + m])
            leaving += copy_all([slab], send_sems.at[m])
    for z in range(planes):
        at = slice(reach * z, reach * (z + 1))
        head_ref[at] = stage_ref[z, :reach]
        tail_ref[at] = stage_ref[z, rows - reach :]
    wait_all(leaving)


def inverse_columns(blocks, tables, sends):
    parts, rows, lanes = blocks.shape
    width = tables.shape[1]
    planes = lanes * parts // (2 * width)
    side = (reach * planes, width)
    slabs = 2 if sends else 0
    scratch = table_scratch(width) + [
        pltpu.VMEM(blocks.shape, f32),
        pltpu.VMEM((planes, rows, width), f32),
        pltpu.VMEM((2, planes * rows, width), bf16),
        pltpu.VMEM((2, planes * rows, width), bf16),
        pltpu.SemaphoreType.DMA((parts,)),
        pltpu.SemaphoreType.DMA((2, planes // 2)),
        pltpu.SemaphoreType.DMA((2, 1)),
    ]
    return call(
        lambda *refs: inverse_columns_body(sends, *refs),
        [array(planes, rows, width), array(*side), array(*side)]
        + [array(reach, rows, width)] * slabs,
        7.0,
        grid=(1,),
        in_specs=[in_hbm] * 2,
        out_specs=[in_hbm, whole(side), whole(side)] + [in_hbm] * slabs,
        scratch_shapes=scratch,
        name="inverse_columns",
    )(blocks, tables)


def shift(value, axis, up, ring):
    count = lax.axis_size(axis)
    pairs = [(i, (i + 1) % count) for i in range(count if ring else count - 1)]
    return lax.ppermute(value, axis, pairs if up else [(b, a) for a, b in pairs])


def edges_body(below_ref, head_ref, tail_ref, above_ref, head_out, tail_out):
    rows = below_ref.shape[1]
    middle = head_ref.shape[0]
    for z in range(reach):
        for ref, first in ((below_ref, 0), (above_ref, reach * reach + middle)):
            to = slice(first + reach * z, first + reach * (z + 1))
            head_out[to], tail_out[to] = ref[z, :reach], ref[z, rows - reach :]
    to = slice(reach * reach, reach * reach + middle)
    head_out[to], tail_out[to] = head_ref[...], tail_ref[...]


def edges(below, head, tail, above):
    width = head.shape[1]
    count = -(-(head.shape[0] + 2 * reach * reach) // 8) * 8
    return call(
        edges_body,
        [array(count, width)] * 2,
        1.0,
        grid=(1,),
        in_specs=[whole(value.shape) for value in (below, head, tail, above)],
        out_specs=[whole((count, width))] * 2,
        name="edges",
    )(below, head, tail, above)


def roll_x(value, by):
    return pltpu.roll(value, by % value.shape[-1], value.ndim - 1)


def energy_slopes(rho, sigma):
    two_a = 2.0 * correlation_scale
    b1, b2, b3, b4 = [two_a * term for term in correlation_terms]
    ratio = beta_value / gamma_value
    exchange = -0.75 * (3.0 / math.pi) ** (1.0 / 3.0)
    s_scale = 0.25 / (3.0 * math.pi**2) ** (2.0 / 3.0)
    t_scale = math.pi / (16.0 * (3.0 * math.pi**2) ** (1.0 / 3.0))
    radius_scale = (3.0 / (4.0 * math.pi)) ** (1.0 / 3.0)
    sixth = jnp.exp(jnp.log(rho) * (-1.0 / 6.0))
    inv = sixth * sixth
    inv2 = inv * inv
    inv4 = inv2 * inv2
    scaled_sigma = sigma * inv4
    stretch = 1.0 + (mu_value / kappa_value * s_scale) * scaled_sigma * inv4
    v = (ratio * t_scale) * scaled_sigma * (inv2 * inv)
    root = math.sqrt(radius_scale) * sixth
    denom = root * (b1 + root * (b2 + root * (b3 + root * b4)))
    denom_slope = root * (0.5 * b1 + root * (b2 + root * (1.5 * b3 + root * (2.0 * b4))))
    pair = denom * denom + denom
    recip = 1.0 / (stretch * pair)
    weight = recip * pair
    recip = recip * stretch
    x_rho = (rho * inv2) * (
        exchange * (4.0 / 3.0) * (1.0 + kappa_value)
        + weight
        * ((-4.0 * exchange * kappa_value) + (8.0 / 3.0 * exchange * kappa_value) * weight)
    )
    radius_part = (two_a * correlation_alpha * radius_scale) * inv
    linear = two_a + radius_part
    log_term = jnp.log(1.0 + (recip * denom + recip))
    uniform = -linear * log_term
    rho_uniform = (1.0 / 3.0) * (radius_part * log_term - linear * (recip * denom_slope))
    grown = jnp.exp(uniform * (-1.0 / gamma_value))
    x = grown - 1.0
    vx = v * x
    v2 = v * v
    lower = x * x + (vx + v2)
    upper = lower + vx * (x + v)
    both = 1.0 / (lower * upper)
    gradient = gamma_value * jnp.log(upper * (upper * both))
    h_part = (x + 2.0 * v) * (x * x) * (x * both)
    h_uniform = (v2 * both) * (v * (2.0 * x + v)) * grown
    d_rho = (
        (x_rho + uniform)
        + (gradient + rho_uniform * (1.0 - h_uniform))
        - (7.0 / 3.0 * gamma_value) * (v * h_part)
    )
    two_d_sigma = inv4 * (
        (2.0 * exchange * s_scale * mu_value) * (weight * weight)
        + (2.0 * t_scale * beta_value) * h_part
    )
    return d_rho, two_d_sigma


def potential_body(sources, bottom, top, flag_ref, *refs):
    tab_hbm_ref, out_ref, tab_ref, tab_sems, pot_ref, tall_ref, stage_ref = refs[-16:-9]
    in_sems, out_sems = refs[-9:-7]
    ext_ref, part_ref, smooth_ref, flat_ref, fx_ref, fy_ref, fz_ref = refs[-7:]
    depth, rows, width = pot_ref.shape
    total = depth + 2 * reach
    arriving = copy_all(
        [
            (refs[plane].at[pl.ds(at, 1)], ext_ref.at[pl.ds(z, 1), pl.ds(lead - 1, rows)])
            for z, (plane, at, _, _) in enumerate(sources)
        ],
        in_sems,
    )
    tables = load_tables(tab_hbm_ref, tab_ref, tab_sems)
    slope = 1.0 / (2.0 * grid_step)
    tiles = rows // 8 + 1

    def at_end(is_end, flag):
        return pl.when(flag_ref[flag] == 1) if is_end else lambda body: None

    for z, (_, _, side, row) in enumerate(sources):
        ext_ref[z, lead - 1 - reach : lead - 1] = refs[side][row : row + reach]
        ext_ref[z, lead - 1 + rows : lead - 1 + rows + reach] = refs[side + 1][row : row + reach]
    wait_all(arriving)

    @at_end(bottom, 0)
    def _():
        ext_ref[reach - 1] = ext_ref[reach]

    @at_end(top, 1)
    def _():
        ext_ref[depth + reach] = ext_ref[depth + reach - 1]

    def filter_plane(z, carry):
        for t in range(tiles):
            r = lead - 2 + 8 * t
            along_y = 0.25 * (ext_ref[z, r - 2 : r + 6] + ext_ref[z, r : r + 8]) + 0.5 * (
                ext_ref[z, r - 1 : r + 7]
            )
            part_ref[z, r : r + 8] = (
                0.25 * (roll_x(along_y, 1) + roll_x(along_y, -1)) + 0.5 * along_y
            )
        return carry

    lax.fori_loop(0, total, filter_plane, 0)

    def filter_depth(z, carry):
        r = slice(lead - 2, lead - 2 + 8 * tiles)
        smooth_ref[z, r] = 0.25 * (part_ref[z, r] + part_ref[z + 2, r]) + 0.5 * part_ref[z + 1, r]
        return carry

    lax.fori_loop(0, total - 2, filter_depth, 0)

    @at_end(bottom, 0)
    def _():
        smooth_ref[1] = smooth_ref[2]

    @at_end(top, 1)
    def _():
        smooth_ref[depth + 2] = smooth_ref[depth + 1]

    def local_terms(z, carry):
        for t in range(tiles):
            r = lead - 1 + 8 * t
            center = smooth_ref[z + 1, r : r + 8]
            gx = (roll_x(center, -1) - roll_x(center, 1)) * slope
            gy = (smooth_ref[z + 1, r + 1 : r + 9] - smooth_ref[z + 1, r - 1 : r + 7]) * slope
            gz = (smooth_ref[z + 2, r : r + 8] - smooth_ref[z, r : r + 8]) * slope
            d_rho, two_d_sigma = energy_slopes(center, gx * gx + gy * gy + gz * gz)
            flat_ref[z, r : r + 8] = d_rho
            fx_ref[z, r : r + 8] = two_d_sigma * gx
            fy_ref[z, r : r + 8] = two_d_sigma * gy
            fz_ref[z, r : r + 8] = two_d_sigma * gz
        return carry

    lax.fori_loop(0, depth + 2, local_terms, 0)

    @at_end(bottom, 0)
    def _():
        fz_ref[0] = fz_ref[1]

    @at_end(top, 1)
    def _():
        fz_ref[depth + 1] = fz_ref[depth]

    def collect(z, carry):
        for t in range(rows // 8):
            r = lead + 8 * t
            here = slice(r, r + 8)
            fx = fx_ref[z + 1, here]
            along_x = (roll_x(fx, -1) - roll_x(fx, 1)) * slope
            along_y = (fy_ref[z + 1, r + 1 : r + 9] - fy_ref[z + 1, r - 1 : r + 7]) * slope
            along_z = (fz_ref[z + 2, here] - fz_ref[z, here]) * slope
            pot_ref[z, 8 * t : 8 * t + 8] = flat_ref[z + 1, here] - (along_x + along_y + along_z)
        return carry

    lax.fori_loop(0, depth, collect, 0)
    wait_all(tables)
    forward_columns(pot_ref, tab_ref, tall_ref, stage_ref, out_ref, out_sems)


def forward_columns(x_ref, tab_ref, tall_ref, stage_ref, out_ref, out_sems):
    planes, rows, width = x_ref.shape
    high, low = split(x_ref[...].reshape(planes * rows, width).T)
    for k, value in enumerate((high, high, low)):
        tall_ref[k * width : (k + 1) * width] = value
    parts, block, out_lanes = stage_ref.shape
    group = parts // 2
    leaving = []
    for m in range(2):
        at = slice(m * group * block, (m + 1) * group * block)
        ch, sh = tab_ref[0, at], tab_ref[2, at]
        real = dot_nn(jnp.concatenate([ch, tab_ref[1, at], ch], axis=1), tall_ref[...])
        imag = dot_nn(jnp.concatenate([sh, tab_ref[3, at], sh], axis=1), tall_ref[...])
        both = jnp.concatenate([real, -imag], axis=1)
        stage_ref[m * group : (m + 1) * group] = both.reshape(group, block, out_lanes)
        to = [pl.ds(m * group + g, 1) for g in range(group)]
        leaving += copy_all([(stage_ref.at[d], out_ref.at[d]) for d in to], out_sems.at[m])
    wait_all(leaving)


def potential_of(flags, arrays, sources, start, count, depth, tables, parts):
    rows, width = arrays[0].shape[1:]
    tall = -(-(rows + lead + 8) // 8) * 8
    planes = lambda extra: pltpu.VMEM((count + extra, tall, width), f32)
    used = sources[start : start + count + 2 * reach]
    lanes = count * rows
    out = (parts, width // parts, 2 * lanes)
    scratch = table_scratch(width) + [
        pltpu.VMEM((count, rows, width), f32),
        pltpu.VMEM((3 * width, lanes), bf16),
        pltpu.VMEM(out, f32),
        pltpu.SemaphoreType.DMA((len(used),)),
        pltpu.SemaphoreType.DMA((2, parts // 2)),
    ]
    body = lambda *refs: potential_body(used, start == 0, start + count == depth, *refs)
    sides = [whole(side.shape) for side in arrays[4:]]
    return call(
        body,
        array(*out),
        20.0,
        grid=(1,),
        in_specs=[pl.BlockSpec(memory_space=pltpu.SMEM)] + [in_hbm] * 4 + sides + [in_hbm],
        out_specs=in_hbm,
        scratch_shapes=scratch + [planes(extra) for extra in (6, 6, 4, 2, 2, 2, 2)],
        name="potential",
    )(flags, *arrays, tables)


def forward_rows_body(first, flag_ref, blocks_ref, tab_hbm_ref, *refs):
    out_ref, tab_ref, tab_sems, in_ref, stage_ref, high_ref, low_ref, in_sems, out_sems = refs[-9:]
    _, planes, rows, width = stage_ref.shape
    arriving = fetch_blocks(blocks_ref, in_ref, in_sems)
    tables = load_tables(tab_hbm_ref, tab_ref, tab_sems)
    wait_all(arriving)
    half = planes // 2
    leaving = []
    for m in range(2):
        gather_blocks(in_ref, high_ref, low_ref, planes, m * half, half)
        if m == 0:
            wait_all(tables)
        at = slice(m * half * rows, (m + 1) * half * rows)
        here = slice(m * half, (m + 1) * half)
        real = (high_ref[0, at], low_ref[0, at])
        imag = (high_ref[1, at], low_ref[1, at])
        cos = (tab_ref[0], tab_ref[1])
        sin = (tab_ref[2], tab_ref[3])
        for c in range(2):
            if c == 0:
                value = triple(dot_nn, *real, *cos) + triple(dot_nn, *imag, *sin)
            else:
                value = triple(dot_nn, *imag, *cos) - triple(dot_nn, *real, *sin)
            stage_ref[c, here] = value.reshape(half, rows, width)

            @pl.when(flag_ref[2] == 1)
            def _():
                tile = (8, 128)
                at_zero = (lax.broadcasted_iota(jnp.int32, tile, 0) == 0) & (
                    lax.broadcasted_iota(jnp.int32, tile, 1) == 0
                )
                for z in range(m * half, (m + 1) * half):
                    corner = stage_ref[c, z, :8, :128]
                    stage_ref[c, z, :8, :128] = jnp.where(at_zero, 0.0, corner)

            pairs = [
                (stage_ref.at[c, pl.ds(z, 1)], out_ref.at[c, pl.ds(first + z, 1)])
                for z in range(m * half, (m + 1) * half)
            ]
            leaving += copy_all(pairs, out_sems.at[m, c])
    wait_all(leaving)


def forward_rows(flags, blocks, tables, first, depth, before):
    parts, rows, lanes = blocks.shape
    width = tables.shape[1]
    planes = lanes * parts // (2 * width)
    earlier = [] if before is None else [before]
    scratch = table_scratch(width) + [
        pltpu.VMEM(blocks.shape, f32),
        pltpu.VMEM((2, planes, rows, width), f32),
        pltpu.VMEM((2, planes * rows, width), bf16),
        pltpu.VMEM((2, planes * rows, width), bf16),
        pltpu.SemaphoreType.DMA((parts,)),
        pltpu.SemaphoreType.DMA((2, 2, planes // 2)),
    ]
    return call(
        lambda *refs: forward_rows_body(first, *refs),
        array(2, depth, rows, width),
        10.0,
        grid=(1,),
        in_specs=[pl.BlockSpec(memory_space=pltpu.SMEM)] + [in_hbm] * (2 + len(earlier)),
        out_specs=in_hbm,
        scratch_shapes=scratch,
        input_output_aliases={3: 0} if earlier else {},
        name="forward_rows",
    )(flags, blocks, tables, *earlier)


def exchange(value):
    return lax.all_to_all(value, "py", 0, 0, tiled=True)


def on_device(rho_hat):
    parts = lax.axis_size("py")
    place_z, place_y = lax.axis_index("px"), lax.axis_index("py")
    flags = jnp.stack(
        [place_z == 0, place_z == lax.axis_size("px") - 1, place_y == 0]
    ).astype(jnp.int32)
    depth, width = rho_hat.shape[1], rho_hat.shape[3]
    unit = depth // 4
    outer, tables = inverse_rows(rho_hat, None, parts, (0, 3))
    outer = exchange(outer)
    inner = exchange(inverse_rows(rho_hat, tables, parts, (1, 2)))
    outer, head, tail, low_planes, high_planes = inverse_columns(outer, tables, True)
    below = shift(high_planes, "px", True, False)
    above = shift(low_planes, "px", False, False)
    head, tail = edges(below, head, tail, above)
    head, tail = shift(tail, "py", True, True), shift(head, "py", False, True)
    inner, inner_head, inner_tail = inverse_columns(inner, tables, False)
    inner_head, inner_tail = shift(inner_tail, "py", True, True), shift(inner_head, "py", False, True)

    arrays = [below, outer, inner, above, head, tail, inner_head, inner_tail]
    sources = []
    for z in range(-reach, depth + reach):
        if z < 0:
            sources.append((0, z + reach, 4, reach * (z + reach)))
        elif z < unit:
            sources.append((1, z, 4, reach * (z + reach)))
        elif z < depth - unit:
            sources.append((2, z - unit, 6, reach * (z - unit)))
        elif z < depth:
            at = z - depth + 2 * unit
            sources.append((1, at, 4, reach * (at + reach)))
        else:
            at = z - depth
            sources.append((3, at, 4, reach * (at + reach + 2 * unit)))

    result = None
    for first, count in ((0, 2), (2, 2)):
        planes = (first * unit, count * unit)
        spectral = potential_of(flags, arrays, sources, *planes, depth, tables, parts)
        result = forward_rows(flags, exchange(spectral), tables, planes[0], depth, result)
    return result


def solution(mesh):
    return jax.shard_map(
        on_device,
        mesh=mesh,
        in_specs=(P(None, "px", "py", None),),
        out_specs=P(None, "px", "py", None),
        check_vma=False,
    )
```

```python
import math

import jax
import jax.numpy as jnp
import numpy as np
from jax import lax
from jax.experimental import pallas as pl
from jax.experimental.pallas import tpu as pltpu
from jax.sharding import PartitionSpec as P

grid_step = 0.25
density_floor = 0.02
density_scale = 0.2
kappa_value = 0.804
mu_value = 0.2195149727645171
beta_value = 0.06672455060314922
gamma_value = (1.0 - math.log(2.0)) / (math.pi * math.pi)
correlation_scale = 0.031091
correlation_alpha = 0.2137
correlation_terms = (7.5957, 3.5876, 1.6382, 0.49294)

f32 = jnp.float32
bf16 = jnp.bfloat16
reach = 3
lead = 9


in_hbm = pl.BlockSpec(memory_space=pltpu.HBM)


def call(body, out, cost, **options):
    estimate = pl.CostEstimate(flops=int(cost * 1e9), bytes_accessed=1 << 20, transcendentals=0)
    limit = pltpu.CompilerParams(vmem_limit_bytes=62 << 20)
    return pl.pallas_call(body, out_shape=out, compiler_params=limit, cost_estimate=estimate, **options)


def array(*shape):
    return jax.ShapeDtypeStruct(shape, f32)


def whole(shape):
    return pl.BlockSpec(shape, lambda *_: (0,) * len(shape))


def copy_all(pairs, sems):
    copies = [pltpu.make_async_copy(a, b, sems.at[i]) for i, (a, b) in enumerate(pairs)]
    for copy in copies:
        copy.start()
    return copies


def wait_all(copies):
    for copy in copies:
        copy.wait()


def group_copies(stage_ref, out_ref, sems, m, group):
    to = [m * group + g for g in range(group)]
    return [
        pltpu.make_async_copy(stage_ref.at[d], out_ref.at[d], sems.at[m, g])
        for g, d in enumerate(to)
    ]


def send_group(*args):
    for copy in group_copies(*args):
        copy.start()


def load_tables(hbm_ref, tab_ref, sems):
    return copy_all([(hbm_ref.at[i], tab_ref.at[i]) for i in range(4)], sems)


def table_scratch(width):
    return [pltpu.VMEM((4, width, width), bf16), pltpu.SemaphoreType.DMA((4,))]


def split(value):
    high = value.astype(bf16)
    return high, (value - high.astype(f32)).astype(bf16)


def dot_nt(left, right):
    return lax.dot_general(left, right, (((1,), (1,)), ((), ())), preferred_element_type=f32)


def dot_nn(left, right):
    return lax.dot_general(left, right, (((1,), (0,)), ((), ())), preferred_element_type=f32)


def triple(dot, left_high, left_low, right_high, right_low):
    return dot(left_high, right_high) + (dot(left_low, right_high) + dot(left_high, right_low))


def fill_tables(coarse_ref, fine_ref, tab_ref):
    fine_cos, fine_sin = fine_ref[0], fine_ref[1]
    stride = fine_ref.shape[1]
    for a in range(coarse_ref.shape[1]):
        cos_a, sin_a = coarse_ref[0, a : a + 1], coarse_ref[1, a : a + 1]
        rows = slice(stride * a, stride * (a + 1))
        tab_ref[0, rows], tab_ref[1, rows] = split(cos_a * fine_cos - sin_a * fine_sin)
        tab_ref[2, rows], tab_ref[3, rows] = split(sin_a * fine_cos + cos_a * fine_sin)


def phase_factors(length, stride):
    def waves(rows, scale):
        angle = (np.outer(rows, np.arange(length)) % length) * (2.0 * math.pi / length)
        return np.stack([np.cos(angle), np.sin(angle)]).astype(np.float32) * np.float32(scale)

    coarse = waves(np.arange(0, length, stride), 1.0)
    fine = waves(np.arange(stride), 1.0 / math.sqrt(length))
    return jnp.asarray(coarse), jnp.asarray(fine)


def inverse_rows_body(blocks, fills, *refs):
    if fills:
        rho_ref, coarse_ref, fine_ref, out_ref, tab_out_ref = refs[:5]
    else:
        rho_ref, tab_hbm_ref, out_ref = refs[:3]
    tab_ref, tab_sems, x_ref, wide_ref, stage_ref, in_sems, out_sems = refs[-7:]
    width = tab_ref.shape[1]
    lanes = wide_ref.shape[1] // 2
    unit = x_ref.shape[1] // len(blocks)
    arriving = [
        copy_all(
            [
                (rho_ref.at[c, pl.ds(b * unit, unit)], x_ref.at[c, pl.ds(i * unit, unit)])
                for i, b in enumerate(blocks)
            ],
            in_sems.at[c],
        )
        for c in range(2)
    ]
    if fills:
        fill_tables(coarse_ref, fine_ref, tab_ref)
        tables = copy_all([(tab_ref.at[i], tab_out_ref.at[i]) for i in range(4)], tab_sems)
    else:
        tables = load_tables(tab_hbm_ref, tab_ref, tab_sems)
    for c in range(2):
        wait_all(arriving[c])
        high, low = split(x_ref[c].reshape(lanes, width).T)
        cos_at = slice(c * lanes, (c + 1) * lanes)
        sin_at = slice((1 - c) * lanes, (2 - c) * lanes)
        for k, value in enumerate((high, high, low)):
            wide_ref[k * width : (k + 1) * width, cos_at] = value
            wide_ref[(k + 3) * width : (k + 4) * width, sin_at] = value if c == 0 else -value
    if not fills:
        wait_all(tables)
    parts, block, out_lanes = stage_ref.shape
    group = parts // 2

    def step(m, carry):
        at = pl.ds(pl.multiple_of(m * group * block, group * block), group * block)
        ch, sh = tab_ref[0, at], tab_ref[2, at]
        left = jnp.concatenate([ch, tab_ref[1, at], ch, sh, tab_ref[3, at], sh], axis=1)
        product = dot_nn(left, wide_ref[...])
        stage_ref[pl.ds(m * group, group)] = product.reshape(group, block, out_lanes)
        send_group(stage_ref, out_ref, out_sems, m, group)
        return carry

    lax.fori_loop(0, 2, step, 0)
    for m in range(2):
        wait_all(group_copies(stage_ref, out_ref, out_sems, m, group))
    if fills:
        wait_all(tables)


def inverse_rows(rho_hat, tables, parts, blocks):
    _, depth, local, width = rho_hat.shape
    unit = depth // 4
    planes = len(blocks) * unit
    lanes = planes * local
    block = width // parts
    out = (parts, block, 2 * lanes)
    scratch = table_scratch(width) + [
        pltpu.VMEM((2, planes, local, width), f32),
        pltpu.VMEM((6 * width, 2 * lanes), bf16),
        pltpu.VMEM(out, f32),
        pltpu.SemaphoreType.DMA((2, len(blocks))),
        pltpu.SemaphoreType.DMA((2, parts // 2)),
    ]
    body = lambda *refs: inverse_rows_body(blocks, tables is None, *refs)
    options = dict(scratch_shapes=scratch, name="inverse_rows", grid=(1,))
    if tables is None:
        factors = phase_factors(width, block)
        made = jax.ShapeDtypeStruct((4, width, width), bf16)
        return call(
            body,
            [array(*out), made],
            10.0,
            in_specs=[in_hbm] + [whole(factor.shape) for factor in factors],
            out_specs=[in_hbm, in_hbm],
            **options,
        )(rho_hat, *factors)
    return call(
        body, array(*out), 10.0, in_specs=[in_hbm] * 2, out_specs=in_hbm, **options
    )(rho_hat, tables)


def gather_blocks(in_ref, high_ref, low_ref):
    parts, rows, lanes = in_ref.shape
    width = high_ref.shape[2]
    local = width // parts
    planes = lanes // (2 * local)
    tile = 16

    def gather_rows(t, carry):
        at = pl.ds(pl.multiple_of(t * tile, tile), tile)
        lane = lax.broadcasted_iota(jnp.int32, (tile, 128), 1)
        for piece in range(2 * planes):
            c, z = piece // planes, piece % planes
            first = piece * local
            block, offset = first // 128, first % 128
            turned = []
            for p in range(parts):
                value = in_ref[p, at, block * 128 : (block + 1) * 128]
                if offset + local > 128:
                    after = in_ref[p, at, (block + 1) * 128 : (block + 2) * 128]
                    value = jnp.where(lane < offset, after, value)
                turned.append(pltpu.roll(value, (p * local - offset) % 128, 1))
            to = pl.ds(pl.multiple_of(z * rows + t * tile, tile), tile)
            for out in range(width // 128):
                start = out * 128 // local
                value = turned[start]
                for p in range(start + 1, parts):
                    edge = p * local - out * 128
                    if edge < 128:
                        value = jnp.where(lane < edge, value, turned[p])
                high, low = split(value)
                high_ref[c, to, out * 128 : (out + 1) * 128] = high
                low_ref[c, to, out * 128 : (out + 1) * 128] = low
        return carry

    lax.fori_loop(0, rows // tile, gather_rows, 0)


def fetch_blocks(hbm_ref, in_ref, sems):
    parts = in_ref.shape[0]
    return copy_all([(hbm_ref.at[pl.ds(d, 1)], in_ref.at[pl.ds(d, 1)]) for d in range(parts)], sems)


def inverse_columns_body(sends, blocks_ref, tab_hbm_ref, *refs):
    out_ref, head_ref, tail_ref = refs[:3]
    (tab_ref, tab_sems, in_ref, stage_ref, high_ref, low_ref, in_sems, out_sems, send_sems) = refs[-9:]
    planes, rows, width = stage_ref.shape
    arriving = fetch_blocks(blocks_ref, in_ref, in_sems)
    tables = load_tables(tab_hbm_ref, tab_ref, tab_sems)
    wait_all(arriving)
    gather_blocks(in_ref, high_ref, low_ref)
    wait_all(tables)
    field = triple(dot_nn, high_ref[0], low_ref[0], tab_ref[0], tab_ref[1])
    field = field - triple(dot_nn, high_ref[1], low_ref[1], tab_ref[2], tab_ref[3])
    stage_ref[...] = field.reshape(planes, rows, width)

    def finish(z, carry):
        value = stage_ref[z]
        soft = jnp.maximum(value, 0.0) + jnp.log1p(jnp.exp(-jnp.abs(value)))
        stage_ref[z] = density_floor + density_scale * soft
        pltpu.make_async_copy(stage_ref.at[z], out_ref.at[z], out_sems.at[z]).start()
        return carry

    lax.fori_loop(0, planes, finish, 0)
    leaving = [
        pltpu.make_async_copy(stage_ref.at[z], out_ref.at[z], out_sems.at[z]) for z in range(planes)
    ]
    for m in range(2 if sends else 0):
        slab = (stage_ref.at[pl.ds(m * (planes - reach), reach)], refs[3 + m])
        leaving += copy_all([slab], send_sems.at[m])
    for z in range(planes):
        at = slice(reach * z, reach * (z + 1))
        head_ref[at] = stage_ref[z, :reach]
        tail_ref[at] = stage_ref[z, rows - reach :]
    wait_all(leaving)


def inverse_columns(blocks, tables, sends):
    parts, rows, lanes = blocks.shape
    width = tables.shape[1]
    planes = lanes * parts // (2 * width)
    side = (reach * planes, width)
    slabs = 2 if sends else 0
    scratch = table_scratch(width) + [
        pltpu.VMEM(blocks.shape, f32),
        pltpu.VMEM((planes, rows, width), f32),
        pltpu.VMEM((2, planes * rows, width), bf16),
        pltpu.VMEM((2, planes * rows, width), bf16),
        pltpu.SemaphoreType.DMA((parts,)),
        pltpu.SemaphoreType.DMA((planes,)),
        pltpu.SemaphoreType.DMA((2, 1)),
    ]
    return call(
        lambda *refs: inverse_columns_body(sends, *refs),
        [array(planes, rows, width), array(*side), array(*side)]
        + [array(reach, rows, width)] * slabs,
        7.0,
        grid=(1,),
        in_specs=[in_hbm] * 2,
        out_specs=[in_hbm, whole(side), whole(side)] + [in_hbm] * slabs,
        scratch_shapes=scratch,
        name="inverse_columns",
    )(blocks, tables)


def shift(value, axis, up, ring):
    count = lax.axis_size(axis)
    pairs = [(i, (i + 1) % count) for i in range(count if ring else count - 1)]
    return lax.ppermute(value, axis, pairs if up else [(b, a) for a, b in pairs])


def edges_body(below_ref, head_ref, tail_ref, above_ref, head_out, tail_out):
    rows = below_ref.shape[1]
    middle = head_ref.shape[0]
    for z in range(reach):
        for ref, first in ((below_ref, 0), (above_ref, reach * reach + middle)):
            to = slice(first + reach * z, first + reach * (z + 1))
            head_out[to], tail_out[to] = ref[z, :reach], ref[z, rows - reach :]
    to = slice(reach * reach, reach * reach + middle)
    head_out[to], tail_out[to] = head_ref[...], tail_ref[...]


def edges(below, head, tail, above):
    width = head.shape[1]
    count = -(-(head.shape[0] + 2 * reach * reach) // 8) * 8
    return call(
        edges_body,
        [array(count, width)] * 2,
        1.0,
        grid=(1,),
        in_specs=[whole(value.shape) for value in (below, head, tail, above)],
        out_specs=[whole((count, width))] * 2,
        name="edges",
    )(below, head, tail, above)


def roll_x(value, by):
    return pltpu.roll(value, by % value.shape[-1], value.ndim - 1)


def energy_slopes(rho, sigma):
    two_a = 2.0 * correlation_scale
    b1, b2, b3, b4 = [two_a * term for term in correlation_terms]
    ratio = beta_value / gamma_value
    exchange = -0.75 * (3.0 / math.pi) ** (1.0 / 3.0)
    s_scale = 0.25 / (3.0 * math.pi**2) ** (2.0 / 3.0)
    t_scale = math.pi / (16.0 * (3.0 * math.pi**2) ** (1.0 / 3.0))
    radius_scale = (3.0 / (4.0 * math.pi)) ** (1.0 / 3.0)
    sixth = jnp.exp(jnp.log(rho) * (-1.0 / 6.0))
    inv = sixth * sixth
    inv2 = inv * inv
    inv4 = inv2 * inv2
    scaled_sigma = sigma * inv4
    stretch = 1.0 + (mu_value / kappa_value * s_scale) * scaled_sigma * inv4
    v = (ratio * t_scale) * scaled_sigma * (inv2 * inv)
    root = math.sqrt(radius_scale) * sixth
    denom = root * (b1 + root * (b2 + root * (b3 + root * b4)))
    denom_slope = root * (0.5 * b1 + root * (b2 + root * (1.5 * b3 + root * (2.0 * b4))))
    pair = denom * denom + denom
    recip = 1.0 / (stretch * pair)
    weight = recip * pair
    recip = recip * stretch
    x_rho = (rho * inv2) * (
        exchange * (4.0 / 3.0) * (1.0 + kappa_value)
        + weight
        * ((-4.0 * exchange * kappa_value) + (8.0 / 3.0 * exchange * kappa_value) * weight)
    )
    radius_part = (two_a * correlation_alpha * radius_scale) * inv
    linear = two_a + radius_part
    log_term = jnp.log(1.0 + (recip * denom + recip))
    uniform = -linear * log_term
    rho_uniform = (1.0 / 3.0) * (radius_part * log_term - linear * (recip * denom_slope))
    grown = jnp.exp(uniform * (-1.0 / gamma_value))
    x = grown - 1.0
    vx = v * x
    v2 = v * v
    lower = x * x + (vx + v2)
    upper = lower + vx * (x + v)
    both = 1.0 / (lower * upper)
    gradient = gamma_value * jnp.log(upper * (upper * both))
    h_part = (x + 2.0 * v) * (x * x) * (x * both)
    h_uniform = (v2 * both) * (v * (2.0 * x + v)) * grown
    d_rho = (
        (x_rho + uniform)
        + (gradient + rho_uniform * (1.0 - h_uniform))
        - (7.0 / 3.0 * gamma_value) * (v * h_part)
    )
    two_d_sigma = inv4 * (
        (2.0 * exchange * s_scale * mu_value) * (weight * weight)
        + (2.0 * t_scale * beta_value) * h_part
    )
    return d_rho, two_d_sigma


def potential_body(sources, bottom, top, flag_ref, *refs):
    tab_hbm_ref, out_ref, tab_ref, tab_sems, pot_ref, tall_ref, stage_ref = refs[-16:-9]
    in_sems, out_sems = refs[-9:-7]
    ext_ref, part_ref, smooth_ref, flat_ref, fx_ref, fy_ref, fz_ref = refs[-7:]
    depth, rows, width = pot_ref.shape
    total = depth + 2 * reach
    arriving = copy_all(
        [
            (refs[plane].at[pl.ds(at, 1)], ext_ref.at[pl.ds(z, 1), pl.ds(lead - 1, rows)])
            for z, (plane, at, _, _) in enumerate(sources)
        ],
        in_sems,
    )
    slope = 1.0 / (2.0 * grid_step)
    tiles = rows // 8 + 1

    def at_end(is_end, flag):
        return pl.when(flag_ref[flag] == 1) if is_end else lambda body: None

    for z, (_, _, side, row) in enumerate(sources):
        ext_ref[z, lead - 1 - reach : lead - 1] = refs[side][row : row + reach]
        ext_ref[z, lead - 1 + rows : lead - 1 + rows + reach] = refs[side + 1][row : row + reach]
    wait_all(arriving)
    tables = load_tables(tab_hbm_ref, tab_ref, tab_sems)

    @at_end(bottom, 0)
    def _():
        ext_ref[reach - 1] = ext_ref[reach]

    @at_end(top, 1)
    def _():
        ext_ref[depth + reach] = ext_ref[depth + reach - 1]

    def filter_plane(z, carry):
        for t in range(tiles):
            r = lead - 2 + 8 * t
            along_y = 0.25 * (ext_ref[z, r - 2 : r + 6] + ext_ref[z, r : r + 8]) + 0.5 * (
                ext_ref[z, r - 1 : r + 7]
            )
            part_ref[z, r : r + 8] = (
                0.25 * (roll_x(along_y, 1) + roll_x(along_y, -1)) + 0.5 * along_y
            )
        return carry

    lax.fori_loop(0, total, filter_plane, 0)

    def filter_depth(z, carry):
        r = slice(lead - 2, lead - 2 + 8 * tiles)
        smooth_ref[z, r] = 0.25 * (part_ref[z, r] + part_ref[z + 2, r]) + 0.5 * part_ref[z + 1, r]
        return carry

    lax.fori_loop(0, total - 2, filter_depth, 0)

    @at_end(bottom, 0)
    def _():
        smooth_ref[1] = smooth_ref[2]

    @at_end(top, 1)
    def _():
        smooth_ref[depth + 2] = smooth_ref[depth + 1]

    def local_terms(z, carry):
        for t in range(tiles):
            r = lead - 1 + 8 * t
            center = smooth_ref[z + 1, r : r + 8]
            gx = (roll_x(center, -1) - roll_x(center, 1)) * slope
            gy = (smooth_ref[z + 1, r + 1 : r + 9] - smooth_ref[z + 1, r - 1 : r + 7]) * slope
            gz = (smooth_ref[z + 2, r : r + 8] - smooth_ref[z, r : r + 8]) * slope
            d_rho, two_d_sigma = energy_slopes(center, gx * gx + gy * gy + gz * gz)
            flat_ref[z, r : r + 8] = d_rho
            fx_ref[z, r : r + 8] = two_d_sigma * gx
            fy_ref[z, r : r + 8] = two_d_sigma * gy
            fz_ref[z, r : r + 8] = two_d_sigma * gz
        return carry

    lax.fori_loop(0, depth + 2, local_terms, 0)

    @at_end(bottom, 0)
    def _():
        fz_ref[0] = fz_ref[1]

    @at_end(top, 1)
    def _():
        fz_ref[depth + 1] = fz_ref[depth]

    def collect(z, carry):
        for t in range(rows // 8):
            r = lead + 8 * t
            here = slice(r, r + 8)
            fx = fx_ref[z + 1, here]
            along_x = (roll_x(fx, -1) - roll_x(fx, 1)) * slope
            along_y = (fy_ref[z + 1, r + 1 : r + 9] - fy_ref[z + 1, r - 1 : r + 7]) * slope
            along_z = (fz_ref[z + 2, here] - fz_ref[z, here]) * slope
            pot_ref[z, 8 * t : 8 * t + 8] = flat_ref[z + 1, here] - (along_x + along_y + along_z)
        return carry

    lax.fori_loop(0, depth, collect, 0)
    wait_all(tables)
    forward_columns(pot_ref, tab_ref, tall_ref, stage_ref, out_ref, out_sems)


def forward_columns(x_ref, tab_ref, tall_ref, stage_ref, out_ref, out_sems):
    planes, rows, width = x_ref.shape
    high, low = split(x_ref[...].reshape(planes * rows, width).T)
    for k, value in enumerate((high, high, low)):
        tall_ref[k * width : (k + 1) * width] = value
    parts, block, out_lanes = stage_ref.shape
    group = parts // 2

    def step(m, carry):
        at = pl.ds(pl.multiple_of(m * group * block, group * block), group * block)
        ch, sh = tab_ref[0, at], tab_ref[2, at]
        real = dot_nn(jnp.concatenate([ch, tab_ref[1, at], ch], axis=1), tall_ref[...])
        imag = dot_nn(jnp.concatenate([sh, tab_ref[3, at], sh], axis=1), tall_ref[...])
        both = jnp.concatenate([real, -imag], axis=1)
        stage_ref[pl.ds(m * group, group)] = both.reshape(group, block, out_lanes)
        send_group(stage_ref, out_ref, out_sems, m, group)
        return carry

    lax.fori_loop(0, 2, step, 0)
    for m in range(2):
        wait_all(group_copies(stage_ref, out_ref, out_sems, m, group))


def potential_of(flags, arrays, sources, start, count, depth, tables, parts):
    rows, width = arrays[0].shape[1:]
    tall = -(-(rows + lead + 8) // 8) * 8
    planes = lambda extra: pltpu.VMEM((count + extra, tall, width), f32)
    used = sources[start : start + count + 2 * reach]
    lanes = count * rows
    out = (parts, width // parts, 2 * lanes)
    scratch = table_scratch(width) + [
        pltpu.VMEM((count, rows, width), f32),
        pltpu.VMEM((3 * width, lanes), bf16),
        pltpu.VMEM(out, f32),
        pltpu.SemaphoreType.DMA((len(used),)),
        pltpu.SemaphoreType.DMA((2, parts // 2)),
    ]
    body = lambda *refs: potential_body(used, start == 0, start + count == depth, *refs)
    sides = [whole(side.shape) for side in arrays[4:]]
    return call(
        body,
        array(*out),
        20.0,
        grid=(1,),
        in_specs=[pl.BlockSpec(memory_space=pltpu.SMEM)] + [in_hbm] * 4 + sides + [in_hbm],
        out_specs=in_hbm,
        scratch_shapes=scratch + [planes(extra) for extra in (6, 6, 4, 2, 2, 2, 2)],
        name="potential",
    )(flags, *arrays, tables)


def forward_rows_body(first, flag_ref, blocks_ref, tab_hbm_ref, *refs):
    out_ref, tab_ref, tab_sems, in_ref, stage_ref, high_ref, low_ref, in_sems, out_sems = refs[-9:]
    _, planes, rows, width = stage_ref.shape
    arriving = fetch_blocks(blocks_ref, in_ref, in_sems)
    tables = load_tables(tab_hbm_ref, tab_ref, tab_sems)
    wait_all(arriving)
    gather_blocks(in_ref, high_ref, low_ref)
    high_ref[2], low_ref[2] = -high_ref[0], -low_ref[0]
    wait_all(tables)

    def copies(c):
        return [
            pltpu.make_async_copy(stage_ref.at[c, z], out_ref.at[c, first + z], out_sems.at[c, z])
            for z in range(planes)
        ]

    def step(c, carry):
        value = triple(dot_nn, high_ref[c], low_ref[c], tab_ref[0], tab_ref[1])
        value = value + triple(dot_nn, high_ref[c + 1], low_ref[c + 1], tab_ref[2], tab_ref[3])
        stage_ref[c] = value.reshape(planes, rows, width)

        @pl.when(flag_ref[2] == 1)
        def _():
            tile = (8, 128)
            at_zero = (lax.broadcasted_iota(jnp.int32, tile, 0) == 0) & (
                lax.broadcasted_iota(jnp.int32, tile, 1) == 0
            )
            for z in range(planes):
                stage_ref[c, z, :8, :128] = jnp.where(at_zero, 0.0, stage_ref[c, z, :8, :128])

        for copy in copies(c):
            copy.start()
        return carry

    lax.fori_loop(0, 2, step, 0)
    wait_all(copies(0) + copies(1))


def forward_rows(flags, blocks, tables, first, depth, before):
    parts, rows, lanes = blocks.shape
    width = tables.shape[1]
    planes = lanes * parts // (2 * width)
    earlier = [] if before is None else [before]
    scratch = table_scratch(width) + [
        pltpu.VMEM(blocks.shape, f32),
        pltpu.VMEM((2, planes, rows, width), f32),
        pltpu.VMEM((3, planes * rows, width), bf16),
        pltpu.VMEM((3, planes * rows, width), bf16),
        pltpu.SemaphoreType.DMA((parts,)),
        pltpu.SemaphoreType.DMA((2, planes)),
    ]
    return call(
        lambda *refs: forward_rows_body(first, *refs),
        array(2, depth, rows, width),
        10.0,
        grid=(1,),
        in_specs=[pl.BlockSpec(memory_space=pltpu.SMEM)] + [in_hbm] * (2 + len(earlier)),
        out_specs=in_hbm,
        scratch_shapes=scratch,
        input_output_aliases={3: 0} if earlier else {},
        name="forward_rows",
    )(flags, blocks, tables, *earlier)


def exchange(value):
    return lax.all_to_all(value, "py", 0, 0, tiled=True)


def on_device(rho_hat):
    parts = lax.axis_size("py")
    place_z, place_y = lax.axis_index("px"), lax.axis_index("py")
    flags = jnp.stack(
        [place_z == 0, place_z == lax.axis_size("px") - 1, place_y == 0]
    ).astype(jnp.int32)
    depth, width = rho_hat.shape[1], rho_hat.shape[3]
    unit = depth // 4
    outer, tables = inverse_rows(rho_hat, None, parts, (0, 3))
    outer = exchange(outer)
    inner = exchange(inverse_rows(rho_hat, tables, parts, (1, 2)))
    outer, head, tail, low_planes, high_planes = inverse_columns(outer, tables, True)
    below = shift(high_planes, "px", True, False)
    above = shift(low_planes, "px", False, False)
    head, tail = edges(below, head, tail, above)
    head, tail = shift(tail, "py", True, True), shift(head, "py", False, True)
    inner, inner_head, inner_tail = inverse_columns(inner, tables, False)
    inner_head, inner_tail = shift(inner_tail, "py", True, True), shift(inner_head, "py", False, True)

    arrays = [below, outer, inner, above, head, tail, inner_head, inner_tail]
    sources = []
    for z in range(-reach, depth + reach):
        if z < 0:
            sources.append((0, z + reach, 4, reach * (z + reach)))
        elif z < unit:
            sources.append((1, z, 4, reach * (z + reach)))
        elif z < depth - unit:
            sources.append((2, z - unit, 6, reach * (z - unit)))
        elif z < depth:
            at = z - depth + 2 * unit
            sources.append((1, at, 4, reach * (at + reach)))
        else:
            at = z - depth
            sources.append((3, at, 4, reach * (at + reach + 2 * unit)))

    result = None
    for first, count in ((0, 2), (2, 2)):
        planes = (first * unit, count * unit)
        spectral = potential_of(flags, arrays, sources, *planes, depth, tables, parts)
        result = forward_rows(flags, exchange(spectral), tables, planes[0], depth, result)
    return result


def solution(mesh):
    return jax.shard_map(
        on_device,
        mesh=mesh,
        in_specs=(P(None, "px", "py", None),),
        out_specs=P(None, "px", "py", None),
        check_vma=False,
    )
```

```python
import math

import jax
import jax.numpy as jnp
import numpy as np
from jax import lax
from jax.experimental import pallas as pl
from jax.experimental.pallas import tpu as pltpu
from jax.sharding import PartitionSpec as P

grid_step = 0.25
density_floor = 0.02
density_scale = 0.2
kappa_value = 0.804
mu_value = 0.2195149727645171
beta_value = 0.06672455060314922
gamma_value = (1.0 - math.log(2.0)) / (math.pi * math.pi)
correlation_scale = 0.031091
correlation_alpha = 0.2137
correlation_terms = (7.5957, 3.5876, 1.6382, 0.49294)

f32 = jnp.float32
bf16 = jnp.bfloat16
reach = 3
lead = 9


in_hbm = pl.BlockSpec(memory_space=pltpu.HBM)


def call(body, out, cost, **options):
    estimate = pl.CostEstimate(flops=int(cost * 1e9), bytes_accessed=1 << 20, transcendentals=0)
    limit = pltpu.CompilerParams(vmem_limit_bytes=62 << 20)
    return pl.pallas_call(body, out_shape=out, compiler_params=limit, cost_estimate=estimate, **options)


def array(*shape):
    return jax.ShapeDtypeStruct(shape, f32)


def whole(shape):
    return pl.BlockSpec(shape, lambda *_: (0,) * len(shape))


def copy_all(pairs, sems):
    copies = [pltpu.make_async_copy(a, b, sems.at[i]) for i, (a, b) in enumerate(pairs)]
    for copy in copies:
        copy.start()
    return copies


def wait_all(copies):
    for copy in copies:
        copy.wait()


def group_copies(stage_ref, out_ref, sems, m, group):
    to = [m * group + g for g in range(group)]
    return [
        pltpu.make_async_copy(stage_ref.at[d], out_ref.at[d], sems.at[m, g])
        for g, d in enumerate(to)
    ]


def send_group(*args):
    for copy in group_copies(*args):
        copy.start()


def load_tables(hbm_ref, tab_ref, sems):
    return copy_all([(hbm_ref.at[i], tab_ref.at[i]) for i in range(4)], sems)


def table_scratch(width):
    return [pltpu.VMEM((4, width, width), bf16), pltpu.SemaphoreType.DMA((4,))]


def split(value):
    high = value.astype(bf16)
    return high, (value - high.astype(f32)).astype(bf16)


def dot_nt(left, right):
    return lax.dot_general(left, right, (((1,), (1,)), ((), ())), preferred_element_type=f32)


def dot_nn(left, right):
    return lax.dot_general(left, right, (((1,), (0,)), ((), ())), preferred_element_type=f32)


def triple(dot, left_high, left_low, right_high, right_low):
    return dot(left_high, right_high) + (dot(left_low, right_high) + dot(left_high, right_low))


def fill_tables(hbm_refs, coarse_ref, fine_ref, tab_ref, sems):
    arriving = copy_all(list(zip(hbm_refs, (coarse_ref, fine_ref))), sems)
    wait_all(arriving)
    stride = fine_ref.shape[1]

    def step(a, carry):
        cos_a, sin_a = coarse_ref[0, pl.ds(a, 1)], coarse_ref[1, pl.ds(a, 1)]
        fine_cos, fine_sin = fine_ref[0], fine_ref[1]
        rows = pl.ds(pl.multiple_of(a * stride, stride), stride)
        tab_ref[0, rows], tab_ref[1, rows] = split(cos_a * fine_cos - sin_a * fine_sin)
        tab_ref[2, rows], tab_ref[3, rows] = split(sin_a * fine_cos + cos_a * fine_sin)
        return carry

    lax.fori_loop(0, coarse_ref.shape[1], step, 0)


def factor_scratch(factors):
    return [pltpu.VMEM(factor.shape, f32) for factor in factors] + [pltpu.SemaphoreType.DMA((2,))]


def phase_factors(length, stride):
    def waves(rows, scale):
        angle = (np.outer(rows, np.arange(length)) % length) * (2.0 * math.pi / length)
        return np.stack([np.cos(angle), np.sin(angle)]).astype(np.float32) * np.float32(scale)

    coarse = waves(np.arange(0, length, stride), 1.0)
    fine = waves(np.arange(stride), 1.0 / math.sqrt(length))
    return jnp.asarray(coarse), jnp.asarray(fine)


def inverse_rows_body(blocks, fills, *refs):
    if fills:
        rho_ref, coarse_hbm_ref, fine_hbm_ref, out_ref, tab_out_ref = refs[:5]
        coarse_ref, fine_ref, factor_sems = refs[-3:]
        refs = refs[:-3]
    else:
        rho_ref, tab_hbm_ref, _, out_ref = refs[:4]
    tab_ref, tab_sems, x_ref, wide_ref, stage_ref, in_sems, out_sems = refs[-7:]
    width = tab_ref.shape[1]
    lanes = wide_ref.shape[1] // 2
    unit = x_ref.shape[1] // len(blocks)
    arriving = [
        copy_all(
            [
                (rho_ref.at[c, pl.ds(b * unit, unit)], x_ref.at[c, pl.ds(i * unit, unit)])
                for i, b in enumerate(blocks)
            ],
            in_sems.at[c],
        )
        for c in range(2)
    ]
    if fills:
        fill_tables((coarse_hbm_ref, fine_hbm_ref), coarse_ref, fine_ref, tab_ref, factor_sems)
        tables = copy_all([(tab_ref.at[i], tab_out_ref.at[i]) for i in range(4)], tab_sems)
    else:
        tables = load_tables(tab_hbm_ref, tab_ref, tab_sems)
    for c in range(2):
        wait_all(arriving[c])
        high, low = split(x_ref[c].reshape(lanes, width).T)
        cos_at = slice(c * lanes, (c + 1) * lanes)
        sin_at = slice((1 - c) * lanes, (2 - c) * lanes)
        for k, value in enumerate((high, high, low)):
            wide_ref[k * width : (k + 1) * width, cos_at] = value
            wide_ref[(k + 3) * width : (k + 4) * width, sin_at] = value if c == 0 else -value
    if not fills:
        wait_all(tables)
    parts, block, out_lanes = stage_ref.shape
    group = parts // 2

    def step(m, carry):
        at = pl.ds(pl.multiple_of(m * group * block, group * block), group * block)
        ch, sh = tab_ref[0, at], tab_ref[2, at]
        left = jnp.concatenate([ch, tab_ref[1, at], ch, sh, tab_ref[3, at], sh], axis=1)
        product = dot_nn(left, wide_ref[...])
        stage_ref[pl.ds(m * group, group)] = product.reshape(group, block, out_lanes)
        send_group(stage_ref, out_ref, out_sems, m, group)
        return carry

    lax.fori_loop(0, 2, step, 0)
    for m in range(2):
        wait_all(group_copies(stage_ref, out_ref, out_sems, m, group))
    if fills:
        wait_all(tables)


def inverse_rows(rho_hat, factors, tables, flags, blocks):
    _, depth, local, width = rho_hat.shape
    parts = width // factors[1].shape[1]
    unit = depth // 4
    planes = len(blocks) * unit
    lanes = planes * local
    block = width // parts
    out = (parts, block, 2 * lanes)
    scratch = table_scratch(width) + [
        pltpu.VMEM((2, planes, local, width), f32),
        pltpu.VMEM((6 * width, 2 * lanes), bf16),
        pltpu.VMEM(out, f32),
        pltpu.SemaphoreType.DMA((2, len(blocks))),
        pltpu.SemaphoreType.DMA((2, parts // 2)),
    ]
    fills = tables is None
    body = lambda *refs: inverse_rows_body(blocks, fills, *refs)
    if fills:
        made = jax.ShapeDtypeStruct((4, width, width), bf16)
        return call(
            body,
            [array(*out), made],
            10.0,
            grid=(1,),
            in_specs=[in_hbm] * 3,
            out_specs=[in_hbm, in_hbm],
            scratch_shapes=scratch + factor_scratch(factors),
            name="inverse_rows",
        )(rho_hat, *factors)
    return call(
        body,
        array(*out),
        10.0,
        grid=(1,),
        in_specs=[in_hbm] * 2 + [pl.BlockSpec(memory_space=pltpu.SMEM)],
        out_specs=in_hbm,
        scratch_shapes=scratch,
        name="inverse_rows",
    )(rho_hat, tables, flags)


def gather_blocks(in_ref, high_ref, low_ref):
    parts, rows, lanes = in_ref.shape
    width = high_ref.shape[2]
    local = width // parts
    planes = lanes // (2 * local)
    tile = 16

    def gather_rows(t, carry):
        at = pl.ds(pl.multiple_of(t * tile, tile), tile)
        lane = lax.broadcasted_iota(jnp.int32, (tile, 128), 1)
        for piece in range(2 * planes):
            c, z = piece // planes, piece % planes
            first = piece * local
            block, offset = first // 128, first % 128
            turned = []
            for p in range(parts):
                value = in_ref[p, at, block * 128 : (block + 1) * 128]
                if offset + local > 128:
                    after = in_ref[p, at, (block + 1) * 128 : (block + 2) * 128]
                    value = jnp.where(lane < offset, after, value)
                turned.append(pltpu.roll(value, (p * local - offset) % 128, 1))
            to = pl.ds(pl.multiple_of(z * rows + t * tile, tile), tile)
            for out in range(width // 128):
                start = out * 128 // local
                value = turned[start]
                for p in range(start + 1, parts):
                    edge = p * local - out * 128
                    if edge < 128:
                        value = jnp.where(lane < edge, value, turned[p])
                high, low = split(value)
                high_ref[c, to, out * 128 : (out + 1) * 128] = high
                low_ref[c, to, out * 128 : (out + 1) * 128] = low
        return carry

    lax.fori_loop(0, rows // tile, gather_rows, 0)


def fetch_blocks(hbm_ref, in_ref, sems):
    parts = in_ref.shape[0]
    return copy_all([(hbm_ref.at[pl.ds(d, 1)], in_ref.at[pl.ds(d, 1)]) for d in range(parts)], sems)


def inverse_columns_body(sends, blocks_ref, coarse_hbm_ref, fine_hbm_ref, *refs):
    coarse_ref, fine_ref, factor_sems = refs[-3:]
    refs = refs[:-3]
    out_ref, head_ref, tail_ref = refs[:3]
    tab_ref, in_ref, stage_ref, high_ref, low_ref, in_sems, out_sems, send_sems = refs[-8:]
    planes, rows, width = stage_ref.shape
    arriving = fetch_blocks(blocks_ref, in_ref, in_sems)
    fill_tables((coarse_hbm_ref, fine_hbm_ref), coarse_ref, fine_ref, tab_ref, factor_sems)
    wait_all(arriving)
    gather_blocks(in_ref, high_ref, low_ref)
    field = triple(dot_nn, high_ref[0], low_ref[0], tab_ref[0], tab_ref[1])
    field = field - triple(dot_nn, high_ref[1], low_ref[1], tab_ref[2], tab_ref[3])
    stage_ref[...] = field.reshape(planes, rows, width)

    def finish(z, carry):
        value = stage_ref[z]
        soft = jnp.maximum(value, 0.0) + jnp.log1p(jnp.exp(-jnp.abs(value)))
        stage_ref[z] = density_floor + density_scale * soft
        pltpu.make_async_copy(stage_ref.at[z], out_ref.at[z], out_sems.at[z]).start()
        return carry

    lax.fori_loop(0, planes, finish, 0)
    leaving = [
        pltpu.make_async_copy(stage_ref.at[z], out_ref.at[z], out_sems.at[z]) for z in range(planes)
    ]
    for m in range(2 if sends else 0):
        slab = (stage_ref.at[pl.ds(m * (planes - reach), reach)], refs[3 + m])
        leaving += copy_all([slab], send_sems.at[m])
    for z in range(planes):
        at = slice(reach * z, reach * (z + 1))
        head_ref[at] = stage_ref[z, :reach]
        tail_ref[at] = stage_ref[z, rows - reach :]
    wait_all(leaving)


def inverse_columns(blocks, factors, sends):
    parts, rows, lanes = blocks.shape
    width = factors[0].shape[2]
    planes = lanes * parts // (2 * width)
    side = (reach * planes, width)
    slabs = 2 if sends else 0
    scratch = [
        pltpu.VMEM((4, width, width), bf16),
        pltpu.VMEM(blocks.shape, f32),
        pltpu.VMEM((planes, rows, width), f32),
        pltpu.VMEM((2, planes * rows, width), bf16),
        pltpu.VMEM((2, planes * rows, width), bf16),
        pltpu.SemaphoreType.DMA((parts,)),
        pltpu.SemaphoreType.DMA((planes,)),
        pltpu.SemaphoreType.DMA((2, 1)),
    ]
    return call(
        lambda *refs: inverse_columns_body(sends, *refs),
        [array(planes, rows, width), array(*side), array(*side)]
        + [array(reach, rows, width)] * slabs,
        7.0,
        grid=(1,),
        in_specs=[in_hbm] * 3,
        out_specs=[in_hbm, whole(side), whole(side)] + [in_hbm] * slabs,
        scratch_shapes=scratch + factor_scratch(factors),
        name="inverse_columns",
    )(blocks, *factors)


def shift(value, axis, up, ring):
    count = lax.axis_size(axis)
    pairs = [(i, (i + 1) % count) for i in range(count if ring else count - 1)]
    return lax.ppermute(value, axis, pairs if up else [(b, a) for a, b in pairs])


def edges_body(below_ref, head_ref, tail_ref, above_ref, head_out, tail_out):
    rows = below_ref.shape[1]
    middle = head_ref.shape[0]
    for z in range(reach):
        for ref, first in ((below_ref, 0), (above_ref, reach * reach + middle)):
            to = slice(first + reach * z, first + reach * (z + 1))
            head_out[to], tail_out[to] = ref[z, :reach], ref[z, rows - reach :]
    to = slice(reach * reach, reach * reach + middle)
    head_out[to], tail_out[to] = head_ref[...], tail_ref[...]


def edges(below, head, tail, above):
    width = head.shape[1]
    count = -(-(head.shape[0] + 2 * reach * reach) // 8) * 8
    return call(
        edges_body,
        [array(count, width)] * 2,
        1.0,
        grid=(1,),
        in_specs=[whole(value.shape) for value in (below, head, tail, above)],
        out_specs=[whole((count, width))] * 2,
        name="edges",
    )(below, head, tail, above)


def roll_x(value, by):
    return pltpu.roll(value, by % value.shape[-1], value.ndim - 1)


def energy_slopes(rho, sigma):
    two_a = 2.0 * correlation_scale
    b1, b2, b3, b4 = [two_a * term for term in correlation_terms]
    ratio = beta_value / gamma_value
    exchange = -0.75 * (3.0 / math.pi) ** (1.0 / 3.0)
    s_scale = 0.25 / (3.0 * math.pi**2) ** (2.0 / 3.0)
    t_scale = math.pi / (16.0 * (3.0 * math.pi**2) ** (1.0 / 3.0))
    radius_scale = (3.0 / (4.0 * math.pi)) ** (1.0 / 3.0)
    sixth = jnp.exp(jnp.log(rho) * (-1.0 / 6.0))
    inv = sixth * sixth
    inv2 = inv * inv
    inv4 = inv2 * inv2
    scaled_sigma = sigma * inv4
    stretch = 1.0 + (mu_value / kappa_value * s_scale) * scaled_sigma * inv4
    v = (ratio * t_scale) * scaled_sigma * (inv2 * inv)
    root = math.sqrt(radius_scale) * sixth
    denom = root * (b1 + root * (b2 + root * (b3 + root * b4)))
    denom_slope = root * (0.5 * b1 + root * (b2 + root * (1.5 * b3 + root * (2.0 * b4))))
    pair = denom * denom + denom
    recip = 1.0 / (stretch * pair)
    weight = recip * pair
    recip = recip * stretch
    x_rho = (rho * inv2) * (
        exchange * (4.0 / 3.0) * (1.0 + kappa_value)
        + weight
        * ((-4.0 * exchange * kappa_value) + (8.0 / 3.0 * exchange * kappa_value) * weight)
    )
    radius_part = (two_a * correlation_alpha * radius_scale) * inv
    linear = two_a + radius_part
    log_term = jnp.log(1.0 + (recip * denom + recip))
    uniform = -linear * log_term
    rho_uniform = (1.0 / 3.0) * (radius_part * log_term - linear * (recip * denom_slope))
    grown = jnp.exp(uniform * (-1.0 / gamma_value))
    x = grown - 1.0
    vx = v * x
    v2 = v * v
    lower = x * x + (vx + v2)
    upper = lower + vx * (x + v)
    both = 1.0 / (lower * upper)
    gradient = gamma_value * jnp.log(upper * (upper * both))
    h_part = (x + 2.0 * v) * (x * x) * (x * both)
    h_uniform = (v2 * both) * (v * (2.0 * x + v)) * grown
    d_rho = (
        (x_rho + uniform)
        + (gradient + rho_uniform * (1.0 - h_uniform))
        - (7.0 / 3.0 * gamma_value) * (v * h_part)
    )
    two_d_sigma = inv4 * (
        (2.0 * exchange * s_scale * mu_value) * (weight * weight)
        + (2.0 * t_scale * beta_value) * h_part
    )
    return d_rho, two_d_sigma


def potential_body(sources, bottom, top, flag_ref, *refs):
    tab_hbm_ref, out_ref, tab_ref, tab_sems, pot_ref, tall_ref, stage_ref = refs[-21:-14]
    in_sems, out_sems, side_sems = refs[-14:-11]
    side_refs = refs[-11:-7]
    ext_ref, part_ref, smooth_ref, flat_ref, fx_ref, fy_ref, fz_ref = refs[-7:]
    depth, rows, width = pot_ref.shape
    total = depth + 2 * reach
    sides = copy_all(list(zip(refs[4:8], side_refs)), side_sems)
    arriving = copy_all(
        [
            (refs[plane].at[pl.ds(at, 1)], ext_ref.at[pl.ds(z, 1), pl.ds(lead - 1, rows)])
            for z, (plane, at, _, _) in enumerate(sources)
        ],
        in_sems,
    )
    slope = 1.0 / (2.0 * grid_step)
    tiles = rows // 8 + 1

    def at_end(is_end, flag):
        return pl.when(flag_ref[flag] == 1) if is_end else lambda body: None

    wait_all(sides)
    for z, (_, _, side, row) in enumerate(sources):
        at = slice(row, row + reach)
        ext_ref[z, lead - 1 - reach : lead - 1] = side_refs[side - 4][at]
        ext_ref[z, lead - 1 + rows : lead - 1 + rows + reach] = side_refs[side - 3][at]
    wait_all(arriving)
    tables = load_tables(tab_hbm_ref, tab_ref, tab_sems)

    @at_end(bottom, 0)
    def _():
        ext_ref[reach - 1] = ext_ref[reach]

    @at_end(top, 1)
    def _():
        ext_ref[depth + reach] = ext_ref[depth + reach - 1]

    def filter_depth(z, carry):
        part_ref[z] = 0.25 * (ext_ref[z] + ext_ref[z + 2]) + 0.5 * ext_ref[z + 1]
        return carry

    lax.fori_loop(0, total - 2, filter_depth, 0)

    def filter_plane(z, carry):
        for t in range(tiles):
            r = lead - 2 + 8 * t
            along_y = 0.25 * (part_ref[z, r - 2 : r + 6] + part_ref[z, r : r + 8]) + 0.5 * (
                part_ref[z, r - 1 : r + 7]
            )
            smooth_ref[z, r : r + 8] = (
                0.25 * (roll_x(along_y, 1) + roll_x(along_y, -1)) + 0.5 * along_y
            )
        return carry

    lax.fori_loop(0, total - 2, filter_plane, 0)

    @at_end(bottom, 0)
    def _():
        smooth_ref[1] = smooth_ref[2]

    @at_end(top, 1)
    def _():
        smooth_ref[depth + 2] = smooth_ref[depth + 1]

    def local_terms(z, carry):
        for t in range(tiles):
            r = lead - 1 + 8 * t
            center = smooth_ref[z + 1, r : r + 8]
            gx = (roll_x(center, -1) - roll_x(center, 1)) * slope
            gy = (smooth_ref[z + 1, r + 1 : r + 9] - smooth_ref[z + 1, r - 1 : r + 7]) * slope
            gz = (smooth_ref[z + 2, r : r + 8] - smooth_ref[z, r : r + 8]) * slope
            d_rho, two_d_sigma = energy_slopes(center, gx * gx + gy * gy + gz * gz)
            flat_ref[z, r : r + 8] = d_rho
            fx_ref[z, r : r + 8] = two_d_sigma * gx
            fy_ref[z, r : r + 8] = two_d_sigma * gy
            fz_ref[z, r : r + 8] = two_d_sigma * gz
        return carry

    lax.fori_loop(0, depth + 2, local_terms, 0)

    @at_end(bottom, 0)
    def _():
        fz_ref[0] = fz_ref[1]

    @at_end(top, 1)
    def _():
        fz_ref[depth + 1] = fz_ref[depth]

    def collect(z, carry):
        for t in range(rows // 8):
            r = lead + 8 * t
            here = slice(r, r + 8)
            fx = fx_ref[z + 1, here]
            along_x = (roll_x(fx, -1) - roll_x(fx, 1)) * slope
            along_y = (fy_ref[z + 1, r + 1 : r + 9] - fy_ref[z + 1, r - 1 : r + 7]) * slope
            along_z = (fz_ref[z + 2, here] - fz_ref[z, here]) * slope
            pot_ref[z, 8 * t : 8 * t + 8] = flat_ref[z + 1, here] - (along_x + along_y + along_z)
        return carry

    lax.fori_loop(0, depth, collect, 0)
    wait_all(tables)
    forward_columns(pot_ref, tab_ref, tall_ref, stage_ref, out_ref, out_sems)


def forward_columns(x_ref, tab_ref, tall_ref, stage_ref, out_ref, out_sems):
    planes, rows, width = x_ref.shape
    high, low = split(x_ref[...].reshape(planes * rows, width).T)
    for k, value in enumerate((high, high, low)):
        tall_ref[k * width : (k + 1) * width] = value
    parts, block, out_lanes = stage_ref.shape
    group = parts // 2

    def step(m, carry):
        at = pl.ds(pl.multiple_of(m * group * block, group * block), group * block)
        ch, sh = tab_ref[0, at], tab_ref[2, at]
        real = dot_nn(jnp.concatenate([ch, tab_ref[1, at], ch], axis=1), tall_ref[...])
        imag = dot_nn(jnp.concatenate([sh, tab_ref[3, at], sh], axis=1), tall_ref[...])
        both = jnp.concatenate([real, -imag], axis=1)
        stage_ref[pl.ds(m * group, group)] = both.reshape(group, block, out_lanes)
        send_group(stage_ref, out_ref, out_sems, m, group)
        return carry

    lax.fori_loop(0, 2, step, 0)
    for m in range(2):
        wait_all(group_copies(stage_ref, out_ref, out_sems, m, group))


def potential_of(flags, arrays, sources, start, count, depth, tables, parts):
    rows, width = arrays[0].shape[1:]
    tall = -(-(rows + lead + 8) // 8) * 8
    planes = lambda extra: pltpu.VMEM((count + extra, tall, width), f32)
    used = sources[start : start + count + 2 * reach]
    lanes = count * rows
    out = (parts, width // parts, 2 * lanes)
    scratch = table_scratch(width) + [
        pltpu.VMEM((count, rows, width), f32),
        pltpu.VMEM((3 * width, lanes), bf16),
        pltpu.VMEM(out, f32),
        pltpu.SemaphoreType.DMA((len(used),)),
        pltpu.SemaphoreType.DMA((2, parts // 2)),
        pltpu.SemaphoreType.DMA((4,)),
    ]
    body = lambda *refs: potential_body(used, start == 0, start + count == depth, *refs)
    sides = [pltpu.VMEM(side.shape, f32) for side in arrays[4:]]
    return call(
        body,
        array(*out),
        20.0,
        grid=(1,),
        in_specs=[pl.BlockSpec(memory_space=pltpu.SMEM)] + [in_hbm] * 9,
        out_specs=in_hbm,
        scratch_shapes=scratch + sides + [planes(extra) for extra in (6, 4, 4, 2, 2, 2, 2)],
        name="potential",
    )(flags, *arrays, tables)


def forward_rows_body(first, flag_ref, blocks_ref, coarse_hbm_ref, fine_hbm_ref, *refs):
    coarse_ref, fine_ref, factor_sems = refs[-3:]
    out_ref, tab_ref, in_ref, stage_ref, high_ref, low_ref, in_sems, out_sems = refs[-11:-3]
    _, planes, rows, width = stage_ref.shape
    arriving = fetch_blocks(blocks_ref, in_ref, in_sems)
    fill_tables((coarse_hbm_ref, fine_hbm_ref), coarse_ref, fine_ref, tab_ref, factor_sems)
    wait_all(arriving)
    gather_blocks(in_ref, high_ref, low_ref)
    high_ref[2], low_ref[2] = -high_ref[0], -low_ref[0]

    def copies(c):
        return [
            pltpu.make_async_copy(stage_ref.at[c, z], out_ref.at[c, first + z], out_sems.at[c, z])
            for z in range(planes)
        ]

    def step(c, carry):
        value = triple(dot_nn, high_ref[c], low_ref[c], tab_ref[0], tab_ref[1])
        value = value + triple(dot_nn, high_ref[c + 1], low_ref[c + 1], tab_ref[2], tab_ref[3])
        stage_ref[c] = value.reshape(planes, rows, width)

        @pl.when(flag_ref[2] == 1)
        def _():
            tile = (8, 128)
            at_zero = (lax.broadcasted_iota(jnp.int32, tile, 0) == 0) & (
                lax.broadcasted_iota(jnp.int32, tile, 1) == 0
            )
            for z in range(planes):
                stage_ref[c, z, :8, :128] = jnp.where(at_zero, 0.0, stage_ref[c, z, :8, :128])

        for copy in copies(c):
            copy.start()
        return carry

    lax.fori_loop(0, 2, step, 0)
    wait_all(copies(0) + copies(1))


def forward_rows(flags, blocks, factors, first, depth, before):
    parts, rows, lanes = blocks.shape
    width = factors[0].shape[2]
    planes = lanes * parts // (2 * width)
    earlier = [] if before is None else [before]
    scratch = [
        pltpu.VMEM((4, width, width), bf16),
        pltpu.VMEM(blocks.shape, f32),
        pltpu.VMEM((2, planes, rows, width), f32),
        pltpu.VMEM((3, planes * rows, width), bf16),
        pltpu.VMEM((3, planes * rows, width), bf16),
        pltpu.SemaphoreType.DMA((parts,)),
        pltpu.SemaphoreType.DMA((2, planes)),
    ]
    return call(
        lambda *refs: forward_rows_body(first, *refs),
        array(2, depth, rows, width),
        10.0,
        grid=(1,),
        in_specs=[pl.BlockSpec(memory_space=pltpu.SMEM)] + [in_hbm] * (3 + len(earlier)),
        out_specs=in_hbm,
        scratch_shapes=scratch + factor_scratch(factors),
        input_output_aliases={4: 0} if earlier else {},
        name="forward_rows",
    )(flags, blocks, *factors, *earlier)


def exchange(value):
    return lax.all_to_all(value, "py", 0, 0, tiled=True)


def on_device(rho_hat):
    parts = lax.axis_size("py")
    place_z, place_y = lax.axis_index("px"), lax.axis_index("py")
    flags = jnp.stack(
        [place_z == 0, place_z == lax.axis_size("px") - 1, place_y == 0]
    ).astype(jnp.int32)
    depth, width = rho_hat.shape[1], rho_hat.shape[3]
    unit = depth // 4
    factors = phase_factors(width, width // parts)

    outer, tables = inverse_rows(rho_hat, factors, None, None, (0, 3))
    outer = exchange(outer)
    inner = exchange(inverse_rows(rho_hat, factors, tables, flags, (1, 2)))
    outer, head, tail, low_planes, high_planes = inverse_columns(outer, factors, True)
    below = shift(high_planes, "px", True, False)
    above = shift(low_planes, "px", False, False)
    head, tail = edges(below, head, tail, above)
    head, tail = shift(tail, "py", True, True), shift(head, "py", False, True)
    inner, inner_head, inner_tail = inverse_columns(inner, factors, False)
    inner_head, inner_tail = shift(inner_tail, "py", True, True), shift(inner_head, "py", False, True)

    arrays = [below, outer, inner, above, head, tail, inner_head, inner_tail]
    sources = []
    for z in range(-reach, depth + reach):
        if z < 0:
            sources.append((0, z + reach, 4, reach * (z + reach)))
        elif z < unit:
            sources.append((1, z, 4, reach * (z + reach)))
        elif z < depth - unit:
            sources.append((2, z - unit, 6, reach * (z - unit)))
        elif z < depth:
            at = z - depth + 2 * unit
            sources.append((1, at, 4, reach * (at + reach)))
        else:
            at = z - depth
            sources.append((3, at, 4, reach * (at + reach + 2 * unit)))

    result = None
    for first, count in ((0, 2), (2, 2)):
        planes = (first * unit, count * unit)
        spectral = potential_of(flags, arrays, sources, *planes, depth, tables, parts)
        result = forward_rows(flags, exchange(spectral), factors, planes[0], depth, result)
    return result


def solution(mesh):
    return jax.shard_map(
        on_device,
        mesh=mesh,
        in_specs=(P(None, "px", "py", None),),
        out_specs=P(None, "px", "py", None),
        check_vma=False,
    )
```

```python
import math

import jax
import jax.numpy as jnp
import numpy as np
from jax import lax
from jax.experimental import pallas as pl
from jax.experimental.pallas import tpu as pltpu
from jax.sharding import PartitionSpec as P

grid_step = 0.25
density_floor = 0.02
density_scale = 0.2
kappa_value = 0.804
mu_value = 0.2195149727645171
beta_value = 0.06672455060314922
gamma_value = (1.0 - math.log(2.0)) / (math.pi * math.pi)
correlation_scale = 0.031091
correlation_alpha = 0.2137
correlation_terms = (7.5957, 3.5876, 1.6382, 0.49294)

f32 = jnp.float32
bf16 = jnp.bfloat16
reach = 3
gather_tile = 16
lead = 9


in_hbm = pl.BlockSpec(memory_space=pltpu.HBM)


def call(body, out, cost, **options):
    estimate = pl.CostEstimate(flops=int(cost * 1e9), bytes_accessed=1 << 20, transcendentals=0)
    limit = pltpu.CompilerParams(vmem_limit_bytes=62 << 20)
    return pl.pallas_call(body, out_shape=out, compiler_params=limit, cost_estimate=estimate, **options)


def array(*shape):
    return jax.ShapeDtypeStruct(shape, f32)


def whole(shape):
    return pl.BlockSpec(shape, lambda *_: (0,) * len(shape))


def copy_all(pairs, sems):
    copies = [pltpu.make_async_copy(a, b, sems.at[i]) for i, (a, b) in enumerate(pairs)]
    for copy in copies:
        copy.start()
    return copies


def wait_all(copies):
    for copy in copies:
        copy.wait()


def group_copies(stage_ref, out_ref, sems, m, group):
    to = [m * group + g for g in range(group)]
    return [
        pltpu.make_async_copy(stage_ref.at[d], out_ref.at[d], sems.at[m, g])
        for g, d in enumerate(to)
    ]


def send_group(*args):
    for copy in group_copies(*args):
        copy.start()


def load_tables(hbm_ref, tab_ref, sems):
    return copy_all([(hbm_ref.at[i], tab_ref.at[i]) for i in range(4)], sems)


def table_scratch(width):
    return [pltpu.VMEM((4, width, width), bf16), pltpu.SemaphoreType.DMA((4,))]


def split(value):
    high = value.astype(bf16)
    return high, (value - high.astype(f32)).astype(bf16)


def dot_nt(left, right):
    return lax.dot_general(left, right, (((1,), (1,)), ((), ())), preferred_element_type=f32)


def dot_nn(left, right):
    return lax.dot_general(left, right, (((1,), (0,)), ((), ())), preferred_element_type=f32)


def triple(dot, left_high, left_low, right_high, right_low):
    return dot(left_high, right_high) + (dot(left_low, right_high) + dot(left_high, right_low))


def fill_tables(hbm_refs, coarse_ref, fine_ref, tab_ref, sems):
    arriving = copy_all(list(zip(hbm_refs, (coarse_ref, fine_ref))), sems)
    wait_all(arriving)
    stride = fine_ref.shape[1]

    def step(a, carry):
        cos_a, sin_a = coarse_ref[0, pl.ds(a, 1)], coarse_ref[1, pl.ds(a, 1)]
        fine_cos, fine_sin = fine_ref[0], fine_ref[1]
        rows = pl.ds(pl.multiple_of(a * stride, stride), stride)
        tab_ref[0, rows], tab_ref[1, rows] = split(cos_a * fine_cos - sin_a * fine_sin)
        tab_ref[2, rows], tab_ref[3, rows] = split(sin_a * fine_cos + cos_a * fine_sin)
        return carry

    lax.fori_loop(0, coarse_ref.shape[1], step, 0)

    tile = 16
    width = tab_ref.shape[2]
    quarter = width // 4
    turn = lax.broadcasted_iota(jnp.int32, (tile, width), 1) % 4
    turn_cos = jnp.where(turn == 0, 1.0, jnp.where(turn == 2, -1.0, 0.0)).astype(bf16)
    turn_sin = jnp.where(turn == 1, 1.0, jnp.where(turn == 3, -1.0, 0.0)).astype(bf16)
    flip = jnp.where(turn % 2 == 0, 1.0, -1.0).astype(bf16)

    def spread(t, carry):
        for part in range(2):
            rows = [pl.ds(pl.multiple_of(q * quarter + t * tile, tile), tile) for q in range(4)]
            cos, sin = tab_ref[part, rows[0]], tab_ref[2 + part, rows[0]]
            next_cos = cos * turn_cos - sin * turn_sin
            next_sin = sin * turn_cos + cos * turn_sin
            tab_ref[part, rows[1]], tab_ref[2 + part, rows[1]] = next_cos, next_sin
            tab_ref[part, rows[2]], tab_ref[2 + part, rows[2]] = cos * flip, sin * flip
            tab_ref[part, rows[3]], tab_ref[2 + part, rows[3]] = next_cos * flip, next_sin * flip
        return carry

    lax.fori_loop(0, quarter // tile, spread, 0)


def factor_scratch(factors):
    return [pltpu.VMEM(factor.shape, f32) for factor in factors] + [pltpu.SemaphoreType.DMA((2,))]


def phase_factors(length, stride):
    def waves(rows, scale):
        angle = (np.outer(rows, np.arange(length)) % length) * (2.0 * math.pi / length)
        return np.stack([np.cos(angle), np.sin(angle)]).astype(np.float32) * np.float32(scale)

    coarse = waves(np.arange(0, length // 4, stride), 1.0)
    fine = waves(np.arange(stride), 1.0 / math.sqrt(length))
    return jnp.asarray(coarse), jnp.asarray(fine)


def inverse_rows_body(blocks, fills, *refs):
    if fills:
        rho_ref, coarse_hbm_ref, fine_hbm_ref, out_ref, tab_out_ref = refs[:5]
        coarse_ref, fine_ref, factor_sems = refs[-3:]
        refs = refs[:-3]
    else:
        rho_ref, tab_hbm_ref, _, out_ref = refs[:4]
    tab_ref, tab_sems, x_ref, wide_ref, stage_ref, in_sems, out_sems = refs[-7:]
    width = tab_ref.shape[1]
    lanes = wide_ref.shape[1] // 2
    unit = x_ref.shape[1] // len(blocks)
    arriving = [
        copy_all(
            [
                (rho_ref.at[c, pl.ds(b * unit, unit)], x_ref.at[c, pl.ds(i * unit, unit)])
                for i, b in enumerate(blocks)
            ],
            in_sems.at[c],
        )
        for c in range(2)
    ]
    if fills:
        fill_tables((coarse_hbm_ref, fine_hbm_ref), coarse_ref, fine_ref, tab_ref, factor_sems)
        tables = copy_all([(tab_ref.at[i], tab_out_ref.at[i]) for i in range(4)], tab_sems)
    else:
        tables = load_tables(tab_hbm_ref, tab_ref, tab_sems)
    for c in range(2):
        wait_all(arriving[c])
        high, low = split(x_ref[c].reshape(lanes, width).T)
        cos_at = slice(c * lanes, (c + 1) * lanes)
        sin_at = slice((1 - c) * lanes, (2 - c) * lanes)
        for k, value in enumerate((high, high, low)):
            wide_ref[k * width : (k + 1) * width, cos_at] = value
            wide_ref[(k + 3) * width : (k + 4) * width, sin_at] = value if c == 0 else -value
    if not fills:
        wait_all(tables)
    parts, block, out_lanes = stage_ref.shape
    group = parts // 2

    def step(m, carry):
        at = pl.ds(pl.multiple_of(m * group * block, group * block), group * block)
        ch, sh = tab_ref[0, at], tab_ref[2, at]
        left = jnp.concatenate([ch, tab_ref[1, at], ch, sh, tab_ref[3, at], sh], axis=1)
        product = dot_nn(left, wide_ref[...])
        stage_ref[pl.ds(m * group, group)] = product.reshape(group, block, out_lanes)
        send_group(stage_ref, out_ref, out_sems, m, group)
        return carry

    lax.fori_loop(0, 2, step, 0)
    for m in range(2):
        wait_all(group_copies(stage_ref, out_ref, out_sems, m, group))
    if fills:
        wait_all(tables)


def inverse_rows(rho_hat, factors, tables, flags, blocks):
    _, depth, local, width = rho_hat.shape
    parts = width // factors[1].shape[1]
    unit = depth // 4
    planes = len(blocks) * unit
    lanes = planes * local
    block = width // parts
    out = (parts, block, 2 * lanes)
    scratch = table_scratch(width) + [
        pltpu.VMEM((2, planes, local, width), f32),
        pltpu.VMEM((6 * width, 2 * lanes), bf16),
        pltpu.VMEM(out, f32),
        pltpu.SemaphoreType.DMA((2, len(blocks))),
        pltpu.SemaphoreType.DMA((2, parts // 2)),
    ]
    fills = tables is None
    body = lambda *refs: inverse_rows_body(blocks, fills, *refs)
    if fills:
        made = jax.ShapeDtypeStruct((4, width, width), bf16)
        return call(
            body,
            [array(*out), made],
            10.0,
            grid=(1,),
            in_specs=[in_hbm] * 3,
            out_specs=[in_hbm, in_hbm],
            scratch_shapes=scratch + factor_scratch(factors),
            name="inverse_rows",
        )(rho_hat, *factors)
    return call(
        body,
        array(*out),
        10.0,
        grid=(1,),
        in_specs=[in_hbm] * 2 + [pl.BlockSpec(memory_space=pltpu.SMEM)],
        out_specs=in_hbm,
        scratch_shapes=scratch,
        name="inverse_rows",
    )(rho_hat, tables, flags)


def tile_copies(hbm_ref, in_ref, sems, t):
    group = in_ref.shape[0] // 4
    at = pl.ds(t * gather_tile, gather_tile)
    if not isinstance(t, int):
        at = pl.ds(pl.multiple_of(t * gather_tile, gather_tile), gather_tile)
    blocks = [pl.ds(g * group, group) for g in range(4)]
    return [
        pltpu.make_async_copy(hbm_ref.at[d, at], in_ref.at[d, at], sems.at[t, g])
        for g, d in enumerate(blocks)
    ]


def fetch_blocks(hbm_ref, in_ref, sems):
    for t in range(in_ref.shape[1] // gather_tile):
        for copy in tile_copies(hbm_ref, in_ref, sems, t):
            copy.start()


def gather_blocks(hbm_ref, in_ref, sems, high_ref, low_ref):
    parts, rows, lanes = in_ref.shape
    width = high_ref.shape[2]
    local = width // parts
    planes = lanes // (2 * local)
    tile = gather_tile

    def gather_rows(t, carry):
        wait_all(tile_copies(hbm_ref, in_ref, sems, t))
        at = pl.ds(pl.multiple_of(t * tile, tile), tile)
        lane = lax.broadcasted_iota(jnp.int32, (tile, 128), 1)
        for piece in range(2 * planes):
            c, z = piece // planes, piece % planes
            first = piece * local
            block, offset = first // 128, first % 128
            turned = []
            for p in range(parts):
                value = in_ref[p, at, block * 128 : (block + 1) * 128]
                if offset + local > 128:
                    after = in_ref[p, at, (block + 1) * 128 : (block + 2) * 128]
                    value = jnp.where(lane < offset, after, value)
                turned.append(pltpu.roll(value, (p * local - offset) % 128, 1))
            to = pl.ds(pl.multiple_of(z * rows + t * tile, tile), tile)
            for out in range(width // 128):
                start = out * 128 // local
                value = turned[start]
                for p in range(start + 1, parts):
                    edge = p * local - out * 128
                    if edge < 128:
                        value = jnp.where(lane < edge, value, turned[p])
                high, low = split(value)
                high_ref[c, to, out * 128 : (out + 1) * 128] = high
                low_ref[c, to, out * 128 : (out + 1) * 128] = low
        return carry

    lax.fori_loop(0, rows // tile, gather_rows, 0)


def inverse_columns_body(sends, blocks_ref, coarse_hbm_ref, fine_hbm_ref, *refs):
    coarse_ref, fine_ref, factor_sems = refs[-3:]
    refs = refs[:-3]
    out_ref, head_ref, tail_ref = refs[:3]
    tab_ref, in_ref, stage_ref, high_ref, low_ref, in_sems, out_sems, send_sems = refs[-8:]
    planes, rows, width = stage_ref.shape
    fetch_blocks(blocks_ref, in_ref, in_sems)
    fill_tables((coarse_hbm_ref, fine_hbm_ref), coarse_ref, fine_ref, tab_ref, factor_sems)
    gather_blocks(blocks_ref, in_ref, in_sems, high_ref, low_ref)
    half = planes // 2

    def finish(z, carry):
        value = stage_ref[z]
        soft = jnp.maximum(value, 0.0) + jnp.log1p(jnp.exp(-jnp.abs(value)))
        stage_ref[z] = density_floor + density_scale * soft
        pltpu.make_async_copy(stage_ref.at[z], out_ref.at[z], out_sems.at[z]).start()
        return carry

    def step(m, carry):
        at = pl.ds(pl.multiple_of(m * half * rows, half * rows), half * rows)
        field = triple(dot_nn, high_ref[0, at], low_ref[0, at], tab_ref[0], tab_ref[1])
        field = field - triple(dot_nn, high_ref[1, at], low_ref[1, at], tab_ref[2], tab_ref[3])
        stage_ref[pl.ds(m * half, half)] = field.reshape(half, rows, width)
        lax.fori_loop(m * half, (m + 1) * half, finish, 0)
        return carry

    lax.fori_loop(0, 2, step, 0)
    leaving = [
        pltpu.make_async_copy(stage_ref.at[z], out_ref.at[z], out_sems.at[z]) for z in range(planes)
    ]
    for m in range(2 if sends else 0):
        slab = (stage_ref.at[pl.ds(m * (planes - reach), reach)], refs[3 + m])
        leaving += copy_all([slab], send_sems.at[m])
    for z in range(planes):
        at = slice(reach * z, reach * (z + 1))
        head_ref[at] = stage_ref[z, :reach]
        tail_ref[at] = stage_ref[z, rows - reach :]
    wait_all(leaving)


def inverse_columns(blocks, factors, sends):
    parts, rows, lanes = blocks.shape
    width = factors[0].shape[2]
    planes = lanes * parts // (2 * width)
    side = (reach * planes, width)
    slabs = 2 if sends else 0
    scratch = [
        pltpu.VMEM((4, width, width), bf16),
        pltpu.VMEM(blocks.shape, f32),
        pltpu.VMEM((planes, rows, width), f32),
        pltpu.VMEM((2, planes * rows, width), bf16),
        pltpu.VMEM((2, planes * rows, width), bf16),
        pltpu.SemaphoreType.DMA((rows // gather_tile, 4)),
        pltpu.SemaphoreType.DMA((planes,)),
        pltpu.SemaphoreType.DMA((2, 1)),
    ]
    return call(
        lambda *refs: inverse_columns_body(sends, *refs),
        [array(planes, rows, width), array(*side), array(*side)]
        + [array(reach, rows, width)] * slabs,
        7.0,
        grid=(1,),
        in_specs=[in_hbm] * 3,
        out_specs=[in_hbm, whole(side), whole(side)] + [in_hbm] * slabs,
        scratch_shapes=scratch + factor_scratch(factors),
        name="inverse_columns",
    )(blocks, *factors)


def shift(value, axis, up, ring):
    count = lax.axis_size(axis)
    pairs = [(i, (i + 1) % count) for i in range(count if ring else count - 1)]
    return lax.ppermute(value, axis, pairs if up else [(b, a) for a, b in pairs])


def edges_body(below_ref, above_ref, head_out, tail_out):
    rows = below_ref.shape[1]
    for z in range(reach):
        for ref, first in ((below_ref, 0), (above_ref, reach * reach)):
            to = slice(first + reach * z, first + reach * (z + 1))
            head_out[to], tail_out[to] = ref[z, :reach], ref[z, rows - reach :]


def edges(below, above):
    width = below.shape[2]
    count = -(-2 * reach * reach // 8) * 8
    return call(
        edges_body,
        [array(count, width)] * 2,
        1.0,
        grid=(1,),
        in_specs=[whole(below.shape)] * 2,
        out_specs=[whole((count, width))] * 2,
        name="edges",
    )(below, above)


def roll_x(value, by):
    return pltpu.roll(value, by % value.shape[-1], value.ndim - 1)


def energy_slopes(rho, sigma):
    two_a = 2.0 * correlation_scale
    b1, b2, b3, b4 = [two_a * term for term in correlation_terms]
    ratio = beta_value / gamma_value
    exchange = -0.75 * (3.0 / math.pi) ** (1.0 / 3.0)
    s_scale = 0.25 / (3.0 * math.pi**2) ** (2.0 / 3.0)
    t_scale = math.pi / (16.0 * (3.0 * math.pi**2) ** (1.0 / 3.0))
    radius_scale = (3.0 / (4.0 * math.pi)) ** (1.0 / 3.0)
    sixth = jnp.exp(jnp.log(rho) * (-1.0 / 6.0))
    inv = sixth * sixth
    inv2 = inv * inv
    inv4 = inv2 * inv2
    scaled_sigma = sigma * inv4
    stretch = 1.0 + (mu_value / kappa_value * s_scale) * scaled_sigma * inv4
    v = (ratio * t_scale) * scaled_sigma * (inv2 * inv)
    root = math.sqrt(radius_scale) * sixth
    denom = root * (b1 + root * (b2 + root * (b3 + root * b4)))
    denom_slope = root * (0.5 * b1 + root * (b2 + root * (1.5 * b3 + root * (2.0 * b4))))
    pair = denom * denom + denom
    recip = 1.0 / (stretch * pair)
    weight = recip * pair
    recip = recip * stretch
    x_rho = (rho * inv2) * (
        exchange * (4.0 / 3.0) * (1.0 + kappa_value)
        + weight
        * ((-4.0 * exchange * kappa_value) + (8.0 / 3.0 * exchange * kappa_value) * weight)
    )
    radius_part = (two_a * correlation_alpha * radius_scale) * inv
    linear = two_a + radius_part
    log_term = jnp.log(1.0 + (recip * denom + recip))
    uniform = -linear * log_term
    rho_uniform = (1.0 / 3.0) * (radius_part * log_term - linear * (recip * denom_slope))
    grown = jnp.exp(uniform * (-1.0 / gamma_value))
    x = grown - 1.0
    vx = v * x
    v2 = v * v
    lower = x * x + (vx + v2)
    upper = lower + vx * (x + v)
    both = 1.0 / (lower * upper)
    gradient = gamma_value * jnp.log(upper * (upper * both))
    h_part = (x + 2.0 * v) * (x * x) * (x * both)
    h_uniform = (v2 * both) * (v * (2.0 * x + v)) * grown
    d_rho = (
        (x_rho + uniform)
        + (gradient + rho_uniform * (1.0 - h_uniform))
        - (7.0 / 3.0 * gamma_value) * (v * h_part)
    )
    two_d_sigma = inv4 * (
        (2.0 * exchange * s_scale * mu_value) * (weight * weight)
        + (2.0 * t_scale * beta_value) * h_part
    )
    return d_rho, two_d_sigma


def potential_body(sources, groups, flag_ref, *refs):
    ext_ref, part_ref, smooth_ref, flat_ref, fx_ref, fy_ref, fz_ref = refs[-7:]
    count = max(source[2] for source in sources) + 2
    plane_refs = refs[: -count - 17]
    sides_hbm = plane_refs[-count:]
    tab_hbm_ref, out_ref, tab_ref, tab_sems, pot_ref, tall_ref, stage_ref = refs[-count - 17 : -count - 10]
    in_sems, out_sems, side_sems = refs[-count - 10 : -count - 7]
    side_refs = refs[-count - 7 : -7]
    planes, rows, width = pot_ref.shape
    each = planes // groups
    sides = copy_all(list(zip(sides_hbm, side_refs)), side_sems)
    arriving = copy_all(
        [
            (plane_refs[plane].at[pl.ds(at, 1)], ext_ref.at[pl.ds(z, 1), pl.ds(lead - 1, rows)])
            for z, (plane, at, _, _) in enumerate(sources)
        ],
        in_sems,
    )
    slope = 1.0 / (2.0 * grid_step)
    tiles = rows // 8 + 1

    def at_end(flag):
        return pl.when(flag_ref[flag] == 1) if groups == 2 else lambda body: None

    wait_all(sides)
    for z, (_, _, side, row) in enumerate(sources):
        at = slice(row, row + reach)
        ext_ref[z, lead - 1 - reach : lead - 1] = side_refs[side][at]
        ext_ref[z, lead - 1 + rows : lead - 1 + rows + reach] = side_refs[side + 1][at]
    wait_all(arriving)
    tables = load_tables(tab_hbm_ref, tab_ref, tab_sems)

    def widened(z, size, margin):
        return z + margin * (z // size) if groups > 1 else z

    @at_end(0)
    def _():
        ext_ref[reach - 1] = ext_ref[reach]

    @at_end(1)
    def _():
        ext_ref[ext_ref.shape[0] - reach] = ext_ref[ext_ref.shape[0] - reach - 1]

    def filter_depth(z, carry):
        w = widened(z, each + 4, 2)
        part_ref[z] = 0.25 * (ext_ref[w] + ext_ref[w + 2]) + 0.5 * ext_ref[w + 1]
        return carry

    lax.fori_loop(0, part_ref.shape[0], filter_depth, 0)

    def filter_plane(z, carry):
        for t in range(tiles):
            r = lead - 2 + 8 * t
            along_y = 0.25 * (part_ref[z, r - 2 : r + 6] + part_ref[z, r : r + 8]) + 0.5 * (
                part_ref[z, r - 1 : r + 7]
            )
            smooth_ref[z, r : r + 8] = (
                0.25 * (roll_x(along_y, 1) + roll_x(along_y, -1)) + 0.5 * along_y
            )
        return carry

    lax.fori_loop(0, part_ref.shape[0], filter_plane, 0)

    @at_end(0)
    def _():
        smooth_ref[1] = smooth_ref[2]

    @at_end(1)
    def _():
        smooth_ref[smooth_ref.shape[0] - 2] = smooth_ref[smooth_ref.shape[0] - 3]

    def local_terms(z, carry):
        w = widened(z, each + 2, 2)
        for t in range(tiles):
            r = lead - 1 + 8 * t
            center = smooth_ref[w + 1, r : r + 8]
            gx = (roll_x(center, -1) - roll_x(center, 1)) * slope
            gy = (smooth_ref[w + 1, r + 1 : r + 9] - smooth_ref[w + 1, r - 1 : r + 7]) * slope
            gz = (smooth_ref[w + 2, r : r + 8] - smooth_ref[w, r : r + 8]) * slope
            d_rho, two_d_sigma = energy_slopes(center, gx * gx + gy * gy + gz * gz)
            flat_ref[z, r : r + 8] = d_rho
            fx_ref[z, r : r + 8] = two_d_sigma * gx
            fy_ref[z, r : r + 8] = two_d_sigma * gy
            fz_ref[z, r : r + 8] = two_d_sigma * gz
        return carry

    lax.fori_loop(0, flat_ref.shape[0], local_terms, 0)

    @at_end(0)
    def _():
        fz_ref[0] = fz_ref[1]

    @at_end(1)
    def _():
        fz_ref[fz_ref.shape[0] - 1] = fz_ref[fz_ref.shape[0] - 2]

    def collect(z, carry):
        w = widened(z, each, 2)
        for t in range(rows // 8):
            r = lead + 8 * t
            here = slice(r, r + 8)
            fx = fx_ref[w + 1, here]
            along_x = (roll_x(fx, -1) - roll_x(fx, 1)) * slope
            along_y = (fy_ref[w + 1, r + 1 : r + 9] - fy_ref[w + 1, r - 1 : r + 7]) * slope
            along_z = (fz_ref[w + 2, here] - fz_ref[w, here]) * slope
            pot_ref[z, 8 * t : 8 * t + 8] = flat_ref[w + 1, here] - (along_x + along_y + along_z)
        return carry

    lax.fori_loop(0, planes, collect, 0)
    wait_all(tables)
    forward_columns(pot_ref, tab_ref, tall_ref, stage_ref, out_ref, out_sems)


def forward_columns(x_ref, tab_ref, tall_ref, stage_ref, out_ref, out_sems):
    planes, rows, width = x_ref.shape
    high, low = split(x_ref[...].reshape(planes * rows, width).T)
    for k, value in enumerate((high, high, low)):
        tall_ref[k * width : (k + 1) * width] = value
    parts, block, out_lanes = stage_ref.shape
    group = parts // 2

    def step(m, carry):
        at = pl.ds(pl.multiple_of(m * group * block, group * block), group * block)
        ch, sh = tab_ref[0, at], tab_ref[2, at]
        real = dot_nn(jnp.concatenate([ch, tab_ref[1, at], ch], axis=1), tall_ref[...])
        imag = dot_nn(jnp.concatenate([sh, tab_ref[3, at], sh], axis=1), tall_ref[...])
        both = jnp.concatenate([real, -imag], axis=1)
        stage_ref[pl.ds(m * group, group)] = both.reshape(group, block, out_lanes)
        send_group(stage_ref, out_ref, out_sems, m, group)
        return carry

    lax.fori_loop(0, 2, step, 0)
    for m in range(2):
        wait_all(group_copies(stage_ref, out_ref, out_sems, m, group))


def potential_of(flags, planes, sides, sources, groups, tables, parts):
    rows, width = planes[0].shape[1:]
    tall = -(-(rows + lead + 8) // 8) * 8
    count = len(sources) - 2 * reach * groups
    lanes = count * rows
    out = (parts, width // parts, 2 * lanes)
    scratch = table_scratch(width) + [
        pltpu.VMEM((count, rows, width), f32),
        pltpu.VMEM((3 * width, lanes), bf16),
        pltpu.VMEM(out, f32),
        pltpu.SemaphoreType.DMA((len(sources),)),
        pltpu.SemaphoreType.DMA((2, parts // 2)),
        pltpu.SemaphoreType.DMA((len(sides),)),
    ]
    scratch += [pltpu.VMEM(side.shape, f32) for side in sides]
    for margin in (6, 4, 4, 2, 2, 2, 2):
        scratch.append(pltpu.VMEM((count + margin * groups, tall, width), f32))
    return call(
        lambda *refs: potential_body(sources, groups, *refs),
        array(*out),
        20.0,
        grid=(1,),
        in_specs=[pl.BlockSpec(memory_space=pltpu.SMEM)]
        + [in_hbm] * (len(planes) + len(sides) + 1),
        out_specs=in_hbm,
        scratch_shapes=scratch,
        name="potential",
    )(flags, *planes, *sides, tables)


def forward_rows_body(starts, flag_ref, blocks_ref, coarse_hbm_ref, fine_hbm_ref, *refs):
    coarse_ref, fine_ref, factor_sems = refs[-3:]
    out_ref, tab_ref, in_ref, stage_ref, high_ref, low_ref, in_sems, out_sems = refs[-11:-3]
    _, planes, rows, width = stage_ref.shape
    fetch_blocks(blocks_ref, in_ref, in_sems)
    fill_tables((coarse_hbm_ref, fine_hbm_ref), coarse_ref, fine_ref, tab_ref, factor_sems)
    gather_blocks(blocks_ref, in_ref, in_sems, high_ref, low_ref)
    high_ref[2], low_ref[2] = -high_ref[0], -low_ref[0]

    half = planes // 2

    def copies(c, m):
        to = starts[0] + m * (starts[1] - starts[0])
        return [
            pltpu.make_async_copy(stage_ref.at[c, z], out_ref.at[c, to + y], out_sems.at[c, z])
            for y, z in enumerate([m * half + y for y in range(half)])
        ]

    def step(i, carry):
        c, m = i // 2, i % 2
        at = pl.ds(pl.multiple_of(m * half * rows, half * rows), half * rows)
        value = triple(dot_nn, high_ref[c, at], low_ref[c, at], tab_ref[0], tab_ref[1])
        value = value + triple(dot_nn, high_ref[c + 1, at], low_ref[c + 1, at], tab_ref[2], tab_ref[3])
        stage_ref[c, pl.ds(m * half, half)] = value.reshape(half, rows, width)

        @pl.when(flag_ref[2] == 1)
        def _():
            tile = (8, 128)
            at_zero = (lax.broadcasted_iota(jnp.int32, tile, 0) == 0) & (
                lax.broadcasted_iota(jnp.int32, tile, 1) == 0
            )
            for y in range(half):
                z = m * half + y
                stage_ref[c, z, :8, :128] = jnp.where(at_zero, 0.0, stage_ref[c, z, :8, :128])

        for copy in copies(c, m):
            copy.start()
        return carry

    lax.fori_loop(0, 4, step, 0)
    for c in range(2):
        wait_all(copies(c, 0) + copies(c, 1))


def forward_rows(flags, blocks, factors, starts, depth, before):
    parts, rows, lanes = blocks.shape
    width = factors[0].shape[2]
    planes = lanes * parts // (2 * width)
    earlier = [] if before is None else [before]
    scratch = [
        pltpu.VMEM((4, width, width), bf16),
        pltpu.VMEM(blocks.shape, f32),
        pltpu.VMEM((2, planes, rows, width), f32),
        pltpu.VMEM((3, planes * rows, width), bf16),
        pltpu.VMEM((3, planes * rows, width), bf16),
        pltpu.SemaphoreType.DMA((rows // gather_tile, 4)),
        pltpu.SemaphoreType.DMA((2, planes)),
    ]
    return call(
        lambda *refs: forward_rows_body(starts, *refs),
        array(2, depth, rows, width),
        10.0,
        grid=(1,),
        in_specs=[pl.BlockSpec(memory_space=pltpu.SMEM)] + [in_hbm] * (3 + len(earlier)),
        out_specs=in_hbm,
        scratch_shapes=scratch + factor_scratch(factors),
        input_output_aliases={4: 0} if earlier else {},
        name="forward_rows",
    )(flags, blocks, *factors, *earlier)


def exchange(value):
    return lax.all_to_all(value, "py", 0, 0, tiled=True)


def on_device(rho_hat):
    parts = lax.axis_size("py")
    place_z, place_y = lax.axis_index("px"), lax.axis_index("py")
    flags = jnp.stack(
        [place_z == 0, place_z == lax.axis_size("px") - 1, place_y == 0]
    ).astype(jnp.int32)
    depth, width = rho_hat.shape[1], rho_hat.shape[3]
    unit = depth // 4
    factors = phase_factors(width, width // parts)

    outer, tables = inverse_rows(rho_hat, factors, None, None, (0, 3))
    outer = exchange(outer)
    inner = exchange(inverse_rows(rho_hat, factors, tables, flags, (1, 2)))
    outer, head, tail, low_planes, high_planes = inverse_columns(outer, factors, True)
    outer_sides = shift(tail, "py", True, True), shift(head, "py", False, True)
    inner, head, tail = inverse_columns(inner, factors, False)
    inner_sides = shift(tail, "py", True, True), shift(head, "py", False, True)

    low_planes, high_planes, _ = lax.optimization_barrier((low_planes, high_planes, head))
    below = shift(high_planes, "px", True, False)
    above = shift(low_planes, "px", False, False)

    def source(z):
        if unit <= z < depth - unit:
            return 1, z - unit, 2, reach * (z - unit)
        if 0 <= z < depth:
            at = z if z < unit else z - depth + 2 * unit
            return 0, at, 0, reach * at
        at = z + reach if z < 0 else z - depth
        return (2 if z < 0 else 3), at, 4, reach * (at + (0 if z < 0 else reach))

    inside = [source(z) for z in range(unit - reach, depth - unit + reach)]
    outside = [source(z) for z in range(-reach, unit + reach)]
    outside += [source(z) for z in range(depth - unit - reach, depth + reach)]
    planes, sides = [outer, inner], [*outer_sides, *inner_sides]
    spectral = potential_of(flags, planes, sides, inside, 1, tables, parts)
    inner_waves = exchange(spectral)

    head, tail = edges(below, above)
    planes += [below, above]
    sides += [shift(tail, "py", True, True), shift(head, "py", False, True)]
    spectral = potential_of(flags, planes, sides, outside, 2, tables, parts)
    outer_waves = exchange(spectral)
    result = forward_rows(flags, inner_waves, factors, (unit, 2 * unit), depth, None)
    result = forward_rows(flags, outer_waves, factors, (0, depth - unit), depth, result)
    return result


def solution(mesh):
    return jax.shard_map(
        on_device,
        mesh=mesh,
        in_specs=(P(None, "px", "py", None),),
        out_specs=P(None, "px", "py", None),
        check_vma=False,
    )
```

```python
import math

import jax
import jax.numpy as jnp
import numpy as np
from jax import lax
from jax.experimental import pallas as pl
from jax.experimental.pallas import tpu as pltpu
from jax.sharding import PartitionSpec as P

grid_step = 0.25
density_floor = 0.02
density_scale = 0.2
kappa_value = 0.804
mu_value = 0.2195149727645171
beta_value = 0.06672455060314922
gamma_value = (1.0 - math.log(2.0)) / (math.pi * math.pi)
correlation_scale = 0.031091
correlation_alpha = 0.2137
correlation_terms = (7.5957, 3.5876, 1.6382, 0.49294)

f32 = jnp.float32
bf16 = jnp.bfloat16
reach = 3
gather_tile = 16
lead = 9


in_hbm = pl.BlockSpec(memory_space=pltpu.HBM)


def call(body, out, cost, **options):
    estimate = pl.CostEstimate(flops=int(cost * 1e9), bytes_accessed=1 << 20, transcendentals=0)
    limit = pltpu.CompilerParams(vmem_limit_bytes=62 << 20)
    return pl.pallas_call(body, out_shape=out, compiler_params=limit, cost_estimate=estimate, **options)


def array(*shape):
    return jax.ShapeDtypeStruct(shape, f32)


def whole(shape):
    return pl.BlockSpec(shape, lambda *_: (0,) * len(shape))


def copy_all(pairs, sems):
    copies = [pltpu.make_async_copy(a, b, sems.at[i]) for i, (a, b) in enumerate(pairs)]
    for copy in copies:
        copy.start()
    return copies


def wait_all(copies):
    for copy in copies:
        copy.wait()


def group_copies(stage_ref, out_ref, sems, m, group):
    to = [m * group + g for g in range(group)]
    return [
        pltpu.make_async_copy(stage_ref.at[d], out_ref.at[d], sems.at[m, g])
        for g, d in enumerate(to)
    ]


def send_group(*args):
    for copy in group_copies(*args):
        copy.start()


def load_tables(hbm_ref, tab_ref, sems):
    return copy_all([(hbm_ref.at[i], tab_ref.at[i]) for i in range(4)], sems)


def table_scratch(width):
    return [pltpu.VMEM((4, width, width), bf16), pltpu.SemaphoreType.DMA((4,))]


def split(value):
    high = value.astype(bf16)
    return high, (value - high.astype(f32)).astype(bf16)


def dot_nt(left, right):
    return lax.dot_general(left, right, (((1,), (1,)), ((), ())), preferred_element_type=f32)


def dot_nn(left, right):
    return lax.dot_general(left, right, (((1,), (0,)), ((), ())), preferred_element_type=f32)


def triple(dot, left_high, left_low, right_high, right_low):
    return dot(left_high, right_high) + (dot(left_low, right_high) + dot(left_high, right_low))


def fill_tables(hbm_refs, coarse_ref, fine_ref, tab_ref, sems):
    arriving = copy_all(list(zip(hbm_refs, (coarse_ref, fine_ref))), sems)
    wait_all(arriving)
    stride = fine_ref.shape[1]

    def step(a, carry):
        cos_a, sin_a = coarse_ref[0, pl.ds(a, 1)], coarse_ref[1, pl.ds(a, 1)]
        fine_cos, fine_sin = fine_ref[0], fine_ref[1]
        rows = pl.ds(pl.multiple_of(a * stride, stride), stride)
        tab_ref[0, rows], tab_ref[1, rows] = split(cos_a * fine_cos - sin_a * fine_sin)
        tab_ref[2, rows], tab_ref[3, rows] = split(sin_a * fine_cos + cos_a * fine_sin)
        return carry

    lax.fori_loop(0, coarse_ref.shape[1], step, 0)

    tile = 16
    width = tab_ref.shape[2]
    quarter = width // 4
    turn = lax.broadcasted_iota(jnp.int32, (tile, width), 1) % 4
    turn_cos = jnp.where(turn == 0, 1.0, jnp.where(turn == 2, -1.0, 0.0)).astype(bf16)
    turn_sin = jnp.where(turn == 1, 1.0, jnp.where(turn == 3, -1.0, 0.0)).astype(bf16)
    flip = jnp.where(turn % 2 == 0, 1.0, -1.0).astype(bf16)

    def spread(t, carry):
        for part in range(2):
            rows = [pl.ds(pl.multiple_of(q * quarter + t * tile, tile), tile) for q in range(4)]
            cos, sin = tab_ref[part, rows[0]], tab_ref[2 + part, rows[0]]
            next_cos = cos * turn_cos - sin * turn_sin
            next_sin = sin * turn_cos + cos * turn_sin
            tab_ref[part, rows[1]], tab_ref[2 + part, rows[1]] = next_cos, next_sin
            tab_ref[part, rows[2]], tab_ref[2 + part, rows[2]] = cos * flip, sin * flip
            tab_ref[part, rows[3]], tab_ref[2 + part, rows[3]] = next_cos * flip, next_sin * flip
        return carry

    lax.fori_loop(0, quarter // tile, spread, 0)


def factor_scratch(factors):
    return [pltpu.VMEM(factor.shape, f32) for factor in factors] + [pltpu.SemaphoreType.DMA((2,))]


def phase_factors(length, stride):
    def waves(rows, scale):
        angle = (np.outer(rows, np.arange(length)) % length) * (2.0 * math.pi / length)
        return np.stack([np.cos(angle), np.sin(angle)]).astype(np.float32) * np.float32(scale)

    coarse = waves(np.arange(0, length // 4, stride), 1.0)
    fine = waves(np.arange(stride), 1.0 / math.sqrt(length))
    return jnp.asarray(coarse), jnp.asarray(fine)


def inverse_rows_body(blocks, fills, *refs):
    if fills:
        rho_ref, coarse_hbm_ref, fine_hbm_ref, out_ref, tab_out_ref = refs[:5]
        coarse_ref, fine_ref, factor_sems = refs[-3:]
        refs = refs[:-3]
    else:
        rho_ref, tab_hbm_ref, _, out_ref = refs[:4]
    tab_ref, tab_sems, x_ref, wide_ref, stage_ref, in_sems, out_sems = refs[-7:]
    width = tab_ref.shape[1]
    lanes = wide_ref.shape[1] // 2
    unit = x_ref.shape[1] // len(blocks)
    arriving = [
        copy_all(
            [
                (rho_ref.at[c, pl.ds(b * unit, unit)], x_ref.at[c, pl.ds(i * unit, unit)])
                for i, b in enumerate(blocks)
            ],
            in_sems.at[c],
        )
        for c in range(2)
    ]
    if fills:
        fill_tables((coarse_hbm_ref, fine_hbm_ref), coarse_ref, fine_ref, tab_ref, factor_sems)
        tables = copy_all([(tab_ref.at[i], tab_out_ref.at[i]) for i in range(4)], tab_sems)
    else:
        tables = load_tables(tab_hbm_ref, tab_ref, tab_sems)
    for c in range(2):
        wait_all(arriving[c])
        high, low = split(x_ref[c].reshape(lanes, width).T)
        cos_at = slice(c * lanes, (c + 1) * lanes)
        sin_at = slice((1 - c) * lanes, (2 - c) * lanes)
        for k, value in enumerate((high, high, low)):
            wide_ref[k * width : (k + 1) * width, cos_at] = value
            wide_ref[(k + 3) * width : (k + 4) * width, sin_at] = value if c == 0 else -value
    if not fills:
        wait_all(tables)
    parts, block, out_lanes = stage_ref.shape
    group = parts // 2

    def step(m, carry):
        at = pl.ds(pl.multiple_of(m * group * block, group * block), group * block)
        ch, sh = tab_ref[0, at], tab_ref[2, at]
        left = jnp.concatenate([ch, tab_ref[1, at], ch, sh, tab_ref[3, at], sh], axis=1)
        product = dot_nn(left, wide_ref[...])
        stage_ref[pl.ds(m * group, group)] = product.reshape(group, block, out_lanes)
        send_group(stage_ref, out_ref, out_sems, m, group)
        return carry

    lax.fori_loop(0, 2, step, 0)
    for m in range(2):
        wait_all(group_copies(stage_ref, out_ref, out_sems, m, group))
    if fills:
        wait_all(tables)


def inverse_rows(rho_hat, factors, tables, flags, blocks):
    _, depth, local, width = rho_hat.shape
    parts = width // factors[1].shape[1]
    unit = depth // 4
    planes = len(blocks) * unit
    lanes = planes * local
    block = width // parts
    out = (parts, block, 2 * lanes)
    scratch = table_scratch(width) + [
        pltpu.VMEM((2, planes, local, width), f32),
        pltpu.VMEM((6 * width, 2 * lanes), bf16),
        pltpu.VMEM(out, f32),
        pltpu.SemaphoreType.DMA((2, len(blocks))),
        pltpu.SemaphoreType.DMA((2, parts // 2)),
    ]
    fills = tables is None
    body = lambda *refs: inverse_rows_body(blocks, fills, *refs)
    if fills:
        made = jax.ShapeDtypeStruct((4, width, width), bf16)
        return call(
            body,
            [array(*out), made],
            10.0,
            grid=(1,),
            in_specs=[in_hbm] * 3,
            out_specs=[in_hbm, in_hbm],
            scratch_shapes=scratch + factor_scratch(factors),
            name="inverse_rows",
        )(rho_hat, *factors)
    return call(
        body,
        array(*out),
        10.0,
        grid=(1,),
        in_specs=[in_hbm] * 2 + [pl.BlockSpec(memory_space=pltpu.SMEM)],
        out_specs=in_hbm,
        scratch_shapes=scratch,
        name="inverse_rows",
    )(rho_hat, tables, flags)


def tile_copies(hbm_ref, in_ref, sems, t):
    group = in_ref.shape[0] // 4
    at = pl.ds(t * gather_tile, gather_tile)
    if not isinstance(t, int):
        at = pl.ds(pl.multiple_of(t * gather_tile, gather_tile), gather_tile)
    blocks = [pl.ds(g * group, group) for g in range(4)]
    return [
        pltpu.make_async_copy(hbm_ref.at[d, at], in_ref.at[d, at], sems.at[t, g])
        for g, d in enumerate(blocks)
    ]


def fetch_blocks(hbm_ref, in_ref, sems):
    for t in range(in_ref.shape[1] // gather_tile):
        for copy in tile_copies(hbm_ref, in_ref, sems, t):
            copy.start()


def gather_blocks(hbm_ref, in_ref, sems, high_ref, low_ref):
    parts, rows, lanes = in_ref.shape
    width = high_ref.shape[2]
    local = width // parts
    planes = lanes // (2 * local)
    tile = gather_tile

    def gather_rows(t, carry):
        wait_all(tile_copies(hbm_ref, in_ref, sems, t))
        at = pl.ds(pl.multiple_of(t * tile, tile), tile)
        lane = lax.broadcasted_iota(jnp.int32, (tile, 128), 1)
        for piece in range(2 * planes):
            c, z = piece // planes, piece % planes
            first = piece * local
            block, offset = first // 128, first % 128
            turned = []
            for p in range(parts):
                value = in_ref[p, at, block * 128 : (block + 1) * 128]
                if offset + local > 128:
                    after = in_ref[p, at, (block + 1) * 128 : (block + 2) * 128]
                    value = jnp.where(lane < offset, after, value)
                turned.append(pltpu.roll(value, (p * local - offset) % 128, 1))
            to = pl.ds(pl.multiple_of(z * rows + t * tile, tile), tile)
            for out in range(width // 128):
                start = out * 128 // local
                value = turned[start]
                for p in range(start + 1, parts):
                    edge = p * local - out * 128
                    if edge < 128:
                        value = jnp.where(lane < edge, value, turned[p])
                high, low = split(value)
                high_ref[c, to, out * 128 : (out + 1) * 128] = high
                low_ref[c, to, out * 128 : (out + 1) * 128] = low
        return carry

    lax.fori_loop(0, rows // tile, gather_rows, 0)


def inverse_columns_body(sends, blocks_ref, coarse_hbm_ref, fine_hbm_ref, *refs):
    coarse_ref, fine_ref, factor_sems = refs[-3:]
    refs = refs[:-3]
    out_ref, head_ref, tail_ref = refs[:3]
    tab_ref, in_ref, stage_ref, high_ref, low_ref, in_sems, out_sems, send_sems = refs[-8:]
    planes, rows, width = stage_ref.shape
    fetch_blocks(blocks_ref, in_ref, in_sems)
    fill_tables((coarse_hbm_ref, fine_hbm_ref), coarse_ref, fine_ref, tab_ref, factor_sems)
    gather_blocks(blocks_ref, in_ref, in_sems, high_ref, low_ref)
    half = planes // 2

    def finish(z, carry):
        value = stage_ref[z]
        soft = jnp.maximum(value, 0.0) + jnp.log1p(jnp.exp(-jnp.abs(value)))
        stage_ref[z] = density_floor + density_scale * soft
        pltpu.make_async_copy(stage_ref.at[z], out_ref.at[z], out_sems.at[z]).start()
        return carry

    def step(m, carry):
        at = pl.ds(pl.multiple_of(m * half * rows, half * rows), half * rows)
        field = triple(dot_nn, high_ref[0, at], low_ref[0, at], tab_ref[0], tab_ref[1])
        field = field - triple(dot_nn, high_ref[1, at], low_ref[1, at], tab_ref[2], tab_ref[3])
        stage_ref[pl.ds(m * half, half)] = field.reshape(half, rows, width)
        lax.fori_loop(m * half, (m + 1) * half, finish, 0)
        return carry

    lax.fori_loop(0, 2, step, 0)
    leaving = [
        pltpu.make_async_copy(stage_ref.at[z], out_ref.at[z], out_sems.at[z]) for z in range(planes)
    ]
    for m in range(2 if sends else 0):
        slab = (stage_ref.at[pl.ds(m * (planes - reach), reach)], refs[3 + m])
        leaving += copy_all([slab], send_sems.at[m])
    for z in range(planes):
        at = slice(reach * z, reach * (z + 1))
        head_ref[at] = stage_ref[z, :reach]
        tail_ref[at] = stage_ref[z, rows - reach :]
    wait_all(leaving)


def inverse_columns(blocks, factors, sends):
    parts, rows, lanes = blocks.shape
    width = factors[0].shape[2]
    planes = lanes * parts // (2 * width)
    side = (reach * planes, width)
    slabs = 2 if sends else 0
    scratch = [
        pltpu.VMEM((4, width, width), bf16),
        pltpu.VMEM(blocks.shape, f32),
        pltpu.VMEM((planes, rows, width), f32),
        pltpu.VMEM((2, planes * rows, width), bf16),
        pltpu.VMEM((2, planes * rows, width), bf16),
        pltpu.SemaphoreType.DMA((rows // gather_tile, 4)),
        pltpu.SemaphoreType.DMA((planes,)),
        pltpu.SemaphoreType.DMA((2, 1)),
    ]
    return call(
        lambda *refs: inverse_columns_body(sends, *refs),
        [array(planes, rows, width), array(*side), array(*side)]
        + [array(reach, rows, width)] * slabs,
        7.0,
        grid=(1,),
        in_specs=[in_hbm] * 3,
        out_specs=[in_hbm, whole(side), whole(side)] + [in_hbm] * slabs,
        scratch_shapes=scratch + factor_scratch(factors),
        name="inverse_columns",
    )(blocks, *factors)


def shift(value, axis, up, ring):
    count = lax.axis_size(axis)
    pairs = [(i, (i + 1) % count) for i in range(count if ring else count - 1)]
    return lax.ppermute(value, axis, pairs if up else [(b, a) for a, b in pairs])


def halo_body(low_ref, high_ref, head_ref, tail_ref, down_ref, up_ref):
    count, rows, width = low_ref.shape
    side = reach * count
    held = head_ref.shape[0]
    for planes_ref, first, out_ref in ((low_ref, 0, down_ref), (high_ref, held - side, up_ref)):
        out_ref[: count * rows] = planes_ref[...].reshape(count * rows, width)
        out_ref[count * rows : count * rows + side] = head_ref[first : first + side]
        out_ref[count * rows + side : count * rows + 2 * side] = tail_ref[first : first + side]


def halo_slabs(*inputs):
    count, rows, width = inputs[0].shape
    total = -(-count * (rows + 2 * reach) // 8) * 8
    return call(
        halo_body,
        [array(total, width)] * 2,
        1.0,
        grid=(1,),
        in_specs=[whole(value.shape) for value in inputs],
        out_specs=[whole((total, width))] * 2,
        name="halo_slabs",
    )(*inputs)


def roll_x(value, by):
    return pltpu.roll(value, by % value.shape[-1], value.ndim - 1)


def energy_slopes(rho, sigma):
    two_a = 2.0 * correlation_scale
    b1, b2, b3, b4 = [two_a * term for term in correlation_terms]
    ratio = beta_value / gamma_value
    exchange = -0.75 * (3.0 / math.pi) ** (1.0 / 3.0)
    s_scale = 0.25 / (3.0 * math.pi**2) ** (2.0 / 3.0)
    t_scale = math.pi / (16.0 * (3.0 * math.pi**2) ** (1.0 / 3.0))
    radius_scale = (3.0 / (4.0 * math.pi)) ** (1.0 / 3.0)
    sixth = jnp.exp(jnp.log(rho) * (-1.0 / 6.0))
    inv = sixth * sixth
    inv2 = inv * inv
    inv4 = inv2 * inv2
    scaled_sigma = sigma * inv4
    stretch = 1.0 + (mu_value / kappa_value * s_scale) * scaled_sigma * inv4
    v = (ratio * t_scale) * scaled_sigma * (inv2 * inv)
    root = math.sqrt(radius_scale) * sixth
    denom = root * (b1 + root * (b2 + root * (b3 + root * b4)))
    denom_slope = root * (0.5 * b1 + root * (b2 + root * (1.5 * b3 + root * (2.0 * b4))))
    pair = denom * denom + denom
    recip = 1.0 / (stretch * pair)
    weight = recip * pair
    recip = recip * stretch
    x_rho = (rho * inv2) * (
        exchange * (4.0 / 3.0) * (1.0 + kappa_value)
        + weight
        * ((-4.0 * exchange * kappa_value) + (8.0 / 3.0 * exchange * kappa_value) * weight)
    )
    radius_part = (two_a * correlation_alpha * radius_scale) * inv
    linear = two_a + radius_part
    log_term = jnp.log(1.0 + (recip * denom + recip))
    uniform = -linear * log_term
    rho_uniform = (1.0 / 3.0) * (radius_part * log_term - linear * (recip * denom_slope))
    grown = jnp.exp(uniform * (-1.0 / gamma_value))
    x = grown - 1.0
    vx = v * x
    v2 = v * v
    lower = x * x + (vx + v2)
    upper = lower + vx * (x + v)
    both = 1.0 / (lower * upper)
    gradient = gamma_value * jnp.log(upper * (upper * both))
    h_part = (x + 2.0 * v) * (x * x) * (x * both)
    h_uniform = (v2 * both) * (v * (2.0 * x + v)) * grown
    d_rho = (
        (x_rho + uniform)
        + (gradient + rho_uniform * (1.0 - h_uniform))
        - (7.0 / 3.0 * gamma_value) * (v * h_part)
    )
    two_d_sigma = inv4 * (
        (2.0 * exchange * s_scale * mu_value) * (weight * weight)
        + (2.0 * t_scale * beta_value) * h_part
    )
    return d_rho, two_d_sigma


def potential_body(sources, groups, flag_ref, *refs):
    ext_ref, part_ref, smooth_ref, flat_ref, fx_ref, fy_ref, fz_ref = refs[-7:]
    count = 6 if groups == 2 else 4
    plane_refs = refs[: -count - 17]
    sides_hbm = plane_refs[-count:]
    tab_hbm_ref, out_ref, tab_ref, tab_sems, pot_ref, tall_ref, stage_ref = refs[-count - 17 : -count - 10]
    in_sems, out_sems, side_sems = refs[-count - 10 : -count - 7]
    side_refs = refs[-count - 7 : -7]
    planes, rows, width = pot_ref.shape
    each = planes // groups
    sides = copy_all(
        [
            (hbm.at[pl.ds(hbm.shape[0] - ref.shape[0], ref.shape[0])], ref)
            for hbm, ref in zip(sides_hbm, side_refs)
        ],
        side_sems,
    )

    def plane_of(plane, at):
        ref = plane_refs[plane]
        return ref.at[at] if len(ref.shape) == 3 else ref.at[pl.ds(at * rows, rows)]

    arriving = copy_all(
        [
            (plane_of(plane, at), ext_ref.at[z, pl.ds(lead - 1, rows)])
            for z, (plane, at, *_) in enumerate(sources)
        ],
        in_sems,
    )
    slope = 1.0 / (2.0 * grid_step)
    tiles = rows // 8 + 1

    def at_end(flag):
        return pl.when(flag_ref[flag] == 1) if groups == 2 else lambda body: None

    wait_all(sides)
    for z, (_, _, head, head_row, tail, tail_row) in enumerate(sources):
        ext_ref[z, lead - 1 - reach : lead - 1] = side_refs[head][head_row : head_row + reach]
        after = side_refs[tail][tail_row : tail_row + reach]
        ext_ref[z, lead - 1 + rows : lead - 1 + rows + reach] = after
    wait_all(arriving)
    tables = load_tables(tab_hbm_ref, tab_ref, tab_sems)

    def widened(z, size, margin):
        return z + margin * (z // size) if groups > 1 else z

    @at_end(0)
    def _():
        ext_ref[reach - 1] = ext_ref[reach]

    @at_end(1)
    def _():
        ext_ref[ext_ref.shape[0] - reach] = ext_ref[ext_ref.shape[0] - reach - 1]

    def filter_depth(z, carry):
        w = widened(z, each + 4, 2)
        part_ref[z] = 0.25 * (ext_ref[w] + ext_ref[w + 2]) + 0.5 * ext_ref[w + 1]
        return carry

    lax.fori_loop(0, part_ref.shape[0], filter_depth, 0)

    def filter_plane(z, carry):
        for t in range(tiles):
            r = lead - 2 + 8 * t
            along_y = 0.25 * (part_ref[z, r - 2 : r + 6] + part_ref[z, r : r + 8]) + 0.5 * (
                part_ref[z, r - 1 : r + 7]
            )
            smooth_ref[z, r : r + 8] = (
                0.25 * (roll_x(along_y, 1) + roll_x(along_y, -1)) + 0.5 * along_y
            )
        return carry

    lax.fori_loop(0, part_ref.shape[0], filter_plane, 0)

    @at_end(0)
    def _():
        smooth_ref[1] = smooth_ref[2]

    @at_end(1)
    def _():
        smooth_ref[smooth_ref.shape[0] - 2] = smooth_ref[smooth_ref.shape[0] - 3]

    def local_terms(z, carry):
        w = widened(z, each + 2, 2)
        for t in range(tiles):
            r = lead - 1 + 8 * t
            center = smooth_ref[w + 1, r : r + 8]
            gx = (roll_x(center, -1) - roll_x(center, 1)) * slope
            gy = (smooth_ref[w + 1, r + 1 : r + 9] - smooth_ref[w + 1, r - 1 : r + 7]) * slope
            gz = (smooth_ref[w + 2, r : r + 8] - smooth_ref[w, r : r + 8]) * slope
            d_rho, two_d_sigma = energy_slopes(center, gx * gx + gy * gy + gz * gz)
            flat_ref[z, r : r + 8] = d_rho
            fx_ref[z, r : r + 8] = two_d_sigma * gx
            fy_ref[z, r : r + 8] = two_d_sigma * gy
            fz_ref[z, r : r + 8] = two_d_sigma * gz
        return carry

    lax.fori_loop(0, flat_ref.shape[0], local_terms, 0)

    @at_end(0)
    def _():
        fz_ref[0] = fz_ref[1]

    @at_end(1)
    def _():
        fz_ref[fz_ref.shape[0] - 1] = fz_ref[fz_ref.shape[0] - 2]

    def collect(z, carry):
        w = widened(z, each, 2)
        for t in range(rows // 8):
            r = lead + 8 * t
            here = slice(r, r + 8)
            fx = fx_ref[w + 1, here]
            along_x = (roll_x(fx, -1) - roll_x(fx, 1)) * slope
            along_y = (fy_ref[w + 1, r + 1 : r + 9] - fy_ref[w + 1, r - 1 : r + 7]) * slope
            along_z = (fz_ref[w + 2, here] - fz_ref[w, here]) * slope
            pot_ref[z, 8 * t : 8 * t + 8] = flat_ref[w + 1, here] - (along_x + along_y + along_z)
        return carry

    lax.fori_loop(0, planes, collect, 0)
    wait_all(tables)
    forward_columns(pot_ref, tab_ref, tall_ref, stage_ref, out_ref, out_sems)


def forward_columns(x_ref, tab_ref, tall_ref, stage_ref, out_ref, out_sems):
    planes, rows, width = x_ref.shape
    high, low = split(x_ref[...].reshape(planes * rows, width).T)
    for k, value in enumerate((high, high, low)):
        tall_ref[k * width : (k + 1) * width] = value
    parts, block, out_lanes = stage_ref.shape
    group = parts // 2

    def step(m, carry):
        at = pl.ds(pl.multiple_of(m * group * block, group * block), group * block)
        ch, sh = tab_ref[0, at], tab_ref[2, at]
        real = dot_nn(jnp.concatenate([ch, tab_ref[1, at], ch], axis=1), tall_ref[...])
        imag = dot_nn(jnp.concatenate([sh, tab_ref[3, at], sh], axis=1), tall_ref[...])
        both = jnp.concatenate([real, -imag], axis=1)
        stage_ref[pl.ds(m * group, group)] = both.reshape(group, block, out_lanes)
        send_group(stage_ref, out_ref, out_sems, m, group)
        return carry

    lax.fori_loop(0, 2, step, 0)
    for m in range(2):
        wait_all(group_copies(stage_ref, out_ref, out_sems, m, group))


def potential_of(flags, planes, sides, sources, groups, tables, parts):
    rows, width = planes[0].shape[1:]
    tall = -(-(rows + lead + 8) // 8) * 8
    count = len(sources) - 2 * reach * groups
    lanes = count * rows
    out = (parts, width // parts, 2 * lanes)
    scratch = table_scratch(width) + [
        pltpu.VMEM((count, rows, width), f32),
        pltpu.VMEM((3 * width, lanes), bf16),
        pltpu.VMEM(out, f32),
        pltpu.SemaphoreType.DMA((len(sources),)),
        pltpu.SemaphoreType.DMA((2, parts // 2)),
        pltpu.SemaphoreType.DMA((len(sides),)),
    ]
    scratch += [pltpu.VMEM((min(side.shape[0], sides[0].shape[0]), width), f32) for side in sides]
    for margin in (6, 4, 4, 2, 2, 2, 2):
        scratch.append(pltpu.VMEM((count + margin * groups, tall, width), f32))
    return call(
        lambda *refs: potential_body(sources, groups, *refs),
        array(*out),
        20.0,
        grid=(1,),
        in_specs=[pl.BlockSpec(memory_space=pltpu.SMEM)]
        + [in_hbm] * (len(planes) + len(sides) + 1),
        out_specs=in_hbm,
        scratch_shapes=scratch,
        name="potential",
    )(flags, *planes, *sides, tables)


def forward_rows_body(starts, flag_ref, blocks_ref, coarse_hbm_ref, fine_hbm_ref, *refs):
    coarse_ref, fine_ref, factor_sems = refs[-3:]
    out_ref, tab_ref, in_ref, stage_ref, high_ref, low_ref, in_sems, out_sems = refs[-11:-3]
    _, planes, rows, width = stage_ref.shape
    fetch_blocks(blocks_ref, in_ref, in_sems)
    fill_tables((coarse_hbm_ref, fine_hbm_ref), coarse_ref, fine_ref, tab_ref, factor_sems)
    gather_blocks(blocks_ref, in_ref, in_sems, high_ref, low_ref)
    high_ref[2], low_ref[2] = -high_ref[0], -low_ref[0]

    half = planes // 2

    def copies(c, m):
        to = starts[0] + m * (starts[1] - starts[0])
        return [
            pltpu.make_async_copy(stage_ref.at[c, z], out_ref.at[c, to + y], out_sems.at[c, z])
            for y, z in enumerate([m * half + y for y in range(half)])
        ]

    def step(i, carry):
        c, m = i // 2, i % 2
        at = pl.ds(pl.multiple_of(m * half * rows, half * rows), half * rows)
        value = triple(dot_nn, high_ref[c, at], low_ref[c, at], tab_ref[0], tab_ref[1])
        value = value + triple(dot_nn, high_ref[c + 1, at], low_ref[c + 1, at], tab_ref[2], tab_ref[3])
        stage_ref[c, pl.ds(m * half, half)] = value.reshape(half, rows, width)

        @pl.when(flag_ref[2] == 1)
        def _():
            tile = (8, 128)
            at_zero = (lax.broadcasted_iota(jnp.int32, tile, 0) == 0) & (
                lax.broadcasted_iota(jnp.int32, tile, 1) == 0
            )
            for y in range(half):
                z = m * half + y
                stage_ref[c, z, :8, :128] = jnp.where(at_zero, 0.0, stage_ref[c, z, :8, :128])

        for copy in copies(c, m):
            copy.start()
        return carry

    lax.fori_loop(0, 4, step, 0)
    for c in range(2):
        wait_all(copies(c, 0) + copies(c, 1))


def forward_rows(flags, blocks, factors, starts, depth, before):
    parts, rows, lanes = blocks.shape
    width = factors[0].shape[2]
    planes = lanes * parts // (2 * width)
    earlier = [] if before is None else [before]
    scratch = [
        pltpu.VMEM((4, width, width), bf16),
        pltpu.VMEM(blocks.shape, f32),
        pltpu.VMEM((2, planes, rows, width), f32),
        pltpu.VMEM((3, planes * rows, width), bf16),
        pltpu.VMEM((3, planes * rows, width), bf16),
        pltpu.SemaphoreType.DMA((rows // gather_tile, 4)),
        pltpu.SemaphoreType.DMA((2, planes)),
    ]
    return call(
        lambda *refs: forward_rows_body(starts, *refs),
        array(2, depth, rows, width),
        10.0,
        grid=(1,),
        in_specs=[pl.BlockSpec(memory_space=pltpu.SMEM)] + [in_hbm] * (3 + len(earlier)),
        out_specs=in_hbm,
        scratch_shapes=scratch + factor_scratch(factors),
        input_output_aliases={4: 0} if earlier else {},
        name="forward_rows",
    )(flags, blocks, *factors, *earlier)


def exchange(value):
    return lax.all_to_all(value, "py", 0, 0, tiled=True)


def on_device(rho_hat):
    parts = lax.axis_size("py")
    place_z, place_y = lax.axis_index("px"), lax.axis_index("py")
    flags = jnp.stack(
        [place_z == 0, place_z == lax.axis_size("px") - 1, place_y == 0]
    ).astype(jnp.int32)
    depth, width = rho_hat.shape[1], rho_hat.shape[3]
    unit = depth // 4
    factors = phase_factors(width, width // parts)

    outer, tables = inverse_rows(rho_hat, factors, None, None, (0, 3))
    outer = exchange(outer)
    inner = exchange(inverse_rows(rho_hat, factors, tables, flags, (1, 2)))
    outer, head, tail, low_planes, high_planes = inverse_columns(outer, factors, True)
    outer_sides = shift(tail, "py", True, True), shift(head, "py", False, True)
    inner, head, tail = inverse_columns(inner, factors, False)
    inner_sides = shift(tail, "py", True, True), shift(head, "py", False, True)

    down, up = halo_slabs(low_planes, high_planes, *outer_sides)
    down, up, _ = lax.optimization_barrier((down, up, head))
    below, above = shift(up, "px", True, False), shift(down, "px", False, False)

    def source(z):
        if unit <= z < depth - unit:
            row = reach * (z - unit)
            return 1, z - unit, 2, row, 3, row
        if 0 <= z < depth:
            at = z if z < unit else z - depth + 2 * unit
            return 0, at, 0, reach * at, 1, reach * at
        at = z + reach if z < 0 else z - depth
        side = 2 if z < 0 else 3
        return side, at, side + 2, reach * at, side + 2, reach * (reach + at)

    inside = [source(z) for z in range(unit - reach, depth - unit + reach)]
    outside = [source(z) for z in range(-reach, unit + reach)]
    outside += [source(z) for z in range(depth - unit - reach, depth + reach)]
    planes, sides = [outer, inner], [*outer_sides, *inner_sides]
    inner_waves = exchange(potential_of(flags, planes, sides, inside, 1, tables, parts))
    halo = [below, above]
    spectral = potential_of(flags, planes + halo, sides + halo, outside, 2, tables, parts)
    outer_waves = exchange(spectral)
    result = forward_rows(flags, inner_waves, factors, (unit, 2 * unit), depth, None)
    result = forward_rows(flags, outer_waves, factors, (0, depth - unit), depth, result)
    return result


def solution(mesh):
    return jax.shard_map(
        on_device,
        mesh=mesh,
        in_specs=(P(None, "px", "py", None),),
        out_specs=P(None, "px", "py", None),
        check_vma=False,
    )
```

```python
import math

import jax
import jax.numpy as jnp
import numpy as np
from jax import lax
from jax.experimental import pallas as pl
from jax.experimental.pallas import tpu as pltpu
from jax.sharding import PartitionSpec as P

grid_step = 0.25
density_floor = 0.02
density_scale = 0.2
kappa_value = 0.804
mu_value = 0.2195149727645171
beta_value = 0.06672455060314922
gamma_value = (1.0 - math.log(2.0)) / (math.pi * math.pi)
correlation_scale = 0.031091
correlation_alpha = 0.2137
correlation_terms = (7.5957, 3.5876, 1.6382, 0.49294)

f32 = jnp.float32
bf16 = jnp.bfloat16
reach = 3
gather_tile = 16
lead = 9


in_hbm = pl.BlockSpec(memory_space=pltpu.HBM)


def call(body, out, cost, **options):
    estimate = pl.CostEstimate(flops=int(cost * 1e9), bytes_accessed=1 << 20, transcendentals=0)
    limit = pltpu.CompilerParams(vmem_limit_bytes=62 << 20)
    return pl.pallas_call(body, out_shape=out, compiler_params=limit, cost_estimate=estimate, **options)


def array(*shape):
    return jax.ShapeDtypeStruct(shape, f32)


def whole(shape):
    return pl.BlockSpec(shape, lambda *_: (0,) * len(shape))


def copy_all(pairs, sems):
    copies = [pltpu.make_async_copy(a, b, sems.at[i]) for i, (a, b) in enumerate(pairs)]
    for copy in copies:
        copy.start()
    return copies


def wait_all(copies):
    for copy in copies:
        copy.wait()


def group_copies(stage_ref, out_ref, sems, m, group):
    to = [m * group + g for g in range(group)]
    return [
        pltpu.make_async_copy(stage_ref.at[d], out_ref.at[d], sems.at[m, g])
        for g, d in enumerate(to)
    ]


def send_group(*args):
    for copy in group_copies(*args):
        copy.start()


def load_tables(hbm_ref, tab_ref, sems):
    return copy_all([(hbm_ref.at[i], tab_ref.at[i]) for i in range(4)], sems)


def table_scratch(width):
    return [pltpu.VMEM((4, width, width), bf16), pltpu.SemaphoreType.DMA((4,))]


def split(value):
    high = value.astype(bf16)
    return high, (value - high.astype(f32)).astype(bf16)


def dot_nt(left, right):
    return lax.dot_general(left, right, (((1,), (1,)), ((), ())), preferred_element_type=f32)


def dot_nn(left, right):
    return lax.dot_general(left, right, (((1,), (0,)), ((), ())), preferred_element_type=f32)


def triple(dot, left_high, left_low, right_high, right_low):
    return dot(left_high, right_high) + (dot(left_low, right_high) + dot(left_high, right_low))


def fill_tables(hbm_refs, coarse_ref, fine_ref, tab_ref, sems):
    arriving = copy_all(list(zip(hbm_refs, (coarse_ref, fine_ref))), sems)
    wait_all(arriving)
    stride = fine_ref.shape[1]

    def step(a, carry):
        cos_a, sin_a = coarse_ref[0, pl.ds(a, 1)], coarse_ref[1, pl.ds(a, 1)]
        fine_cos, fine_sin = fine_ref[0], fine_ref[1]
        rows = pl.ds(pl.multiple_of(a * stride, stride), stride)
        tab_ref[0, rows], tab_ref[1, rows] = split(cos_a * fine_cos - sin_a * fine_sin)
        tab_ref[2, rows], tab_ref[3, rows] = split(sin_a * fine_cos + cos_a * fine_sin)
        return carry

    lax.fori_loop(0, tab_ref.shape[1] // 4 // stride, step, 0)

    tile = 16
    width = tab_ref.shape[2]
    quarter = width // 4
    turn = lax.broadcasted_iota(jnp.int32, (tile, width), 1) % 4
    turn_cos = jnp.where(turn == 0, 1.0, jnp.where(turn == 2, -1.0, 0.0)).astype(bf16)
    turn_sin = jnp.where(turn == 1, 1.0, jnp.where(turn == 3, -1.0, 0.0)).astype(bf16)
    flip = jnp.where(turn % 2 == 0, 1.0, -1.0).astype(bf16)

    def spread(t, carry):
        for part in range(2):
            rows = [pl.ds(pl.multiple_of(q * quarter + t * tile, tile), tile) for q in range(4)]
            cos, sin = tab_ref[part, rows[0]], tab_ref[2 + part, rows[0]]
            next_cos = cos * turn_cos - sin * turn_sin
            next_sin = sin * turn_cos + cos * turn_sin
            tab_ref[part, rows[1]], tab_ref[2 + part, rows[1]] = next_cos, next_sin
            tab_ref[part, rows[2]], tab_ref[2 + part, rows[2]] = cos * flip, sin * flip
            tab_ref[part, rows[3]], tab_ref[2 + part, rows[3]] = next_cos * flip, next_sin * flip
        return carry

    lax.fori_loop(0, quarter // tile, spread, 0)


def factor_scratch(factors):
    return [pltpu.VMEM(factor.shape, f32) for factor in factors] + [pltpu.SemaphoreType.DMA((2,))]


def phase_factors(length, stride, norm):
    def waves(rows, scale, period):
        angle = (np.outer(rows, np.arange(length)) % period) * (2.0 * math.pi / period)
        return np.stack([np.cos(angle), np.sin(angle)]).astype(np.float32) * np.float32(scale)

    coarse = waves(np.arange(0, length // 4, stride), 1.0, length)
    coarse = np.concatenate([coarse, waves(np.arange(1, 2), 1.0, 2 * length)], axis=1)
    fine = waves(np.arange(stride), 1.0 / math.sqrt(norm), length)
    return jnp.asarray(coarse), jnp.asarray(fine)


def inverse_rows_body(blocks, makes, *refs):
    rho_ref, coarse_hbm_ref, fine_hbm_ref = refs[:3]
    if makes:
        factors_hbm, out_ref, tab_out_ref = refs[3:5], refs[6], refs[7]
        full_ref, full_coarse_ref, full_fine_ref, full_factor_sems, full_sems = refs[-5:]
        refs = refs[:-5]
    else:
        out_ref = refs[3]
    tab_ref, x_ref, wide_ref, stage_ref, in_sems, out_sems, coarse_ref, fine_ref, factor_sems = refs[-9:]
    half = tab_ref.shape[1]
    lanes = wide_ref.shape[2] // 2
    unit = x_ref.shape[1] // len(blocks)
    arriving = [
        copy_all(
            [
                (rho_ref.at[c, pl.ds(b * unit, unit)], x_ref.at[c, pl.ds(i * unit, unit)])
                for i, b in enumerate(blocks)
            ],
            in_sems.at[c],
        )
        for c in range(2)
    ]
    fill_tables((coarse_hbm_ref, fine_hbm_ref), coarse_ref, fine_ref, tab_ref, factor_sems)
    for c in range(2):
        wait_all(arriving[c])
    real, imag = [x_ref[c].reshape(lanes, 2 * half) for c in range(2)]
    last = coarse_ref.shape[1] - 1
    wave_cos, wave_sin = coarse_ref[0, last:], coarse_ref[1, last:]
    for p in range(2):
        if p == 0:
            values = real[:, :half] + real[:, half:], imag[:, :half] + imag[:, half:]
        else:
            odd_re, odd_im = real[:, :half] - real[:, half:], imag[:, :half] - imag[:, half:]
            values = odd_re * wave_cos - odd_im * wave_sin, odd_re * wave_sin + odd_im * wave_cos
        for c in range(2):
            high, low = split(values[c].T)
            cos_at = slice(c * lanes, (c + 1) * lanes)
            sin_at = slice((1 - c) * lanes, (2 - c) * lanes)
            for k, value in enumerate((high, high, low)):
                wide_ref[p, k * half : (k + 1) * half, cos_at] = value
                turned = value if c == 0 else -value
                wide_ref[p, (k + 3) * half : (k + 4) * half, sin_at] = turned
    parts, _, block, _ = stage_ref.shape
    out_lanes = 2 * lanes
    group = parts // 2
    count = half // 2

    def step(m, carry):
        at = pl.ds(pl.multiple_of(m * count, count), count)
        ch, sh = tab_ref[0, at], tab_ref[2, at]
        left = jnp.concatenate([ch, tab_ref[1, at], ch, sh, tab_ref[3, at], sh], axis=1)
        for p in range(2):
            product = dot_nn(left, wide_ref[p]).reshape(group, block // 2, out_lanes)
            for g in range(group):
                for i in range(out_lanes // 128):
                    to = pl.ds(p, block // 2, stride=2)
                    stage_ref[m * group + g, i, to, :] = product[g, :, i * 128 : (i + 1) * 128]
        send_group(stage_ref, out_ref, out_sems, m, group)
        return carry

    lax.fori_loop(0, 2, step, 0)
    if makes:
        fill_tables(factors_hbm, full_coarse_ref, full_fine_ref, full_ref, full_factor_sems)
        wait_all(copy_all([(full_ref.at[i], tab_out_ref.at[i]) for i in range(4)], full_sems))
    for m in range(2):
        wait_all(group_copies(stage_ref, out_ref, out_sems, m, group))


def inverse_rows(rho_hat, factors, full, flags, blocks):
    _, depth, local, width = rho_hat.shape
    half = factors[1].shape[2]
    block = factors[1].shape[1]
    parts = width // block
    unit = depth // 4
    planes = len(blocks) * unit
    lanes = planes * local
    out = (parts, 2 * lanes // 128, block, 128)
    scratch = [
        pltpu.VMEM((4, half, half), bf16),
        pltpu.VMEM((2, planes, local, width), f32),
        pltpu.VMEM((2, 6 * half, 2 * lanes), bf16),
        pltpu.VMEM(out, f32),
        pltpu.SemaphoreType.DMA((2, len(blocks))),
        pltpu.SemaphoreType.DMA((2, parts // 2)),
    ] + factor_scratch(factors)
    makes = full is not None
    body = lambda *refs: inverse_rows_body(blocks, makes, *refs)
    if makes:
        scratch += [pltpu.VMEM((4, width, width), bf16)] + factor_scratch(full)
        return call(
            body,
            [array(*out), jax.ShapeDtypeStruct((4, width, width), bf16)],
            10.0,
            grid=(1,),
            in_specs=[in_hbm] * 5 + [pl.BlockSpec(memory_space=pltpu.SMEM)],
            out_specs=[in_hbm] * 2,
            scratch_shapes=scratch + [pltpu.SemaphoreType.DMA((4,))],
            name="inverse_rows",
        )(rho_hat, *factors, *full, flags)
    return call(
        body,
        array(*out),
        10.0,
        grid=(1,),
        in_specs=[in_hbm] * 3,
        out_specs=in_hbm,
        scratch_shapes=scratch,
        name="inverse_rows",
    )(rho_hat, *factors)


def tile_copies(hbm_ref, in_ref, sems, t):
    group = in_ref.shape[0] // 4
    at = pl.ds(t * gather_tile, gather_tile)
    if not isinstance(t, int):
        at = pl.ds(pl.multiple_of(t * gather_tile, gather_tile), gather_tile)
    blocks = [pl.ds(g * group, group) for g in range(4)]
    return [
        pltpu.make_async_copy(hbm_ref.at[d, :, at], in_ref.at[d, :, at], sems.at[t, g])
        if len(in_ref.shape) == 4
        else pltpu.make_async_copy(hbm_ref.at[d, at], in_ref.at[d, at], sems.at[t, g])
        for g, d in enumerate(blocks)
    ]


def fetch_blocks(hbm_ref, in_ref, sems):
    for t in range(in_ref.shape[-2] // gather_tile):
        for copy in tile_copies(hbm_ref, in_ref, sems, t):
            copy.start()


def gather_blocks(hbm_ref, in_ref, sems, high_ref, low_ref):
    parts, rows = in_ref.shape[0], in_ref.shape[-2]
    width = high_ref.shape[2]
    local = width // parts
    planes = high_ref.shape[1] // rows
    tile = gather_tile

    def load(p, at, block):
        if len(in_ref.shape) == 4:
            return in_ref[p, block, at]
        return in_ref[p, at, block * 128 : (block + 1) * 128]

    def gather_rows(t, carry):
        wait_all(tile_copies(hbm_ref, in_ref, sems, t))
        at = pl.ds(pl.multiple_of(t * tile, tile), tile)
        lane = lax.broadcasted_iota(jnp.int32, (tile, 128), 1)
        for piece in range(2 * planes):
            c, z = piece // planes, piece % planes
            first = piece * local
            block, offset = first // 128, first % 128
            turned = []
            for p in range(parts):
                value = load(p, at, block)
                if offset + local > 128:
                    after = load(p, at, block + 1)
                    value = jnp.where(lane < offset, after, value)
                turned.append(pltpu.roll(value, (p * local - offset) % 128, 1))
            to = pl.ds(pl.multiple_of(z * rows + t * tile, tile), tile)
            for out in range(width // 128):
                start = out * 128 // local
                value = turned[start]
                for p in range(start + 1, parts):
                    edge = p * local - out * 128
                    if edge < 128:
                        value = jnp.where(lane < edge, value, turned[p])
                high, low = split(value)
                high_ref[c, to, out * 128 : (out + 1) * 128] = high
                low_ref[c, to, out * 128 : (out + 1) * 128] = low
        return carry

    lax.fori_loop(0, rows // tile, gather_rows, 0)


def inverse_columns_body(sends, blocks_ref, coarse_hbm_ref, fine_hbm_ref, *refs):
    coarse_ref, fine_ref, factor_sems = refs[-3:]
    refs = refs[:-3]
    out_ref, head_ref, tail_ref = refs[:3]
    tab_ref, in_ref, stage_ref, high_ref, low_ref, in_sems, out_sems, send_sems = refs[-8:]
    planes, rows, width = stage_ref.shape
    fetch_blocks(blocks_ref, in_ref, in_sems)
    fill_tables((coarse_hbm_ref, fine_hbm_ref), coarse_ref, fine_ref, tab_ref, factor_sems)
    gather_blocks(blocks_ref, in_ref, in_sems, high_ref, low_ref)
    half = planes // 2

    def finish(z, carry):
        value = stage_ref[z]
        soft = jnp.maximum(value, 0.0) + jnp.log1p(jnp.exp(-jnp.abs(value)))
        stage_ref[z] = density_floor + density_scale * soft
        pltpu.make_async_copy(stage_ref.at[z], out_ref.at[z], out_sems.at[z]).start()
        return carry

    def step(m, carry):
        at = pl.ds(pl.multiple_of(m * half * rows, half * rows), half * rows)
        field = triple(dot_nn, high_ref[0, at], low_ref[0, at], tab_ref[0], tab_ref[1])
        field = field - triple(dot_nn, high_ref[1, at], low_ref[1, at], tab_ref[2], tab_ref[3])
        stage_ref[pl.ds(m * half, half)] = field.reshape(half, rows, width)
        lax.fori_loop(m * half, (m + 1) * half, finish, 0)
        return carry

    lax.fori_loop(0, 2, step, 0)
    leaving = [
        pltpu.make_async_copy(stage_ref.at[z], out_ref.at[z], out_sems.at[z]) for z in range(planes)
    ]
    for m in range(2 if sends else 0):
        first = m * (planes - reach)
        pairs = [(stage_ref.at[first + z], refs[3 + m].at[pl.ds(z * rows, rows)]) for z in range(reach)]
        leaving += copy_all(pairs, send_sems.at[m])
    for z in range(planes):
        at = slice(reach * z, reach * (z + 1))
        head_ref[at] = stage_ref[z, :reach]
        tail_ref[at] = stage_ref[z, rows - reach :]
    wait_all(leaving)


def inverse_columns(blocks, factors, sends):
    parts, _, rows, _ = blocks.shape
    lanes = blocks.shape[1] * blocks.shape[3]
    width = factors[0].shape[2]
    planes = lanes * parts // (2 * width)
    side = (reach * planes, width)
    slabs = 2 if sends else 0
    scratch = [
        pltpu.VMEM((4, width, width), bf16),
        pltpu.VMEM(blocks.shape, f32),
        pltpu.VMEM((planes, rows, width), f32),
        pltpu.VMEM((2, planes * rows, width), bf16),
        pltpu.VMEM((2, planes * rows, width), bf16),
        pltpu.SemaphoreType.DMA((rows // gather_tile, 4)),
        pltpu.SemaphoreType.DMA((planes,)),
        pltpu.SemaphoreType.DMA((2, reach)),
    ]
    return call(
        lambda *refs: inverse_columns_body(sends, *refs),
        [array(planes, rows, width), array(*side), array(*side)]
        + [array(slab_rows(rows), width)] * slabs,
        7.0,
        grid=(1,),
        in_specs=[in_hbm] * 3,
        out_specs=[in_hbm, whole(side), whole(side)] + [in_hbm] * slabs,
        scratch_shapes=scratch + factor_scratch(factors),
        name="inverse_columns",
    )(blocks, *factors)


def shift(value, axis, up, ring):
    count = lax.axis_size(axis)
    pairs = [(i, (i + 1) % count) for i in range(count if ring else count - 1)]
    return lax.ppermute(value, axis, pairs if up else [(b, a) for a, b in pairs])


def slab_rows(rows):
    return reach * rows + -(-2 * reach * reach // 8) * 8


def halo_body(head_ref, tail_ref, low_ref, high_ref, down_ref, up_ref, edge_ref, sems):
    side = reach * reach
    held = head_ref.shape[0]
    copies = []
    for i, (first, out_ref) in enumerate(((0, down_ref), (held - side, up_ref))):
        edge_ref[i, :side] = head_ref[first : first + side]
        edge_ref[i, side : 2 * side] = tail_ref[first : first + side]
        count = edge_ref.shape[1]
        to = out_ref.at[pl.ds(out_ref.shape[0] - count, count)]
        copies += copy_all([(edge_ref.at[i], to)], sems.at[i])
    wait_all(copies)


def halo_slabs(low, high, head, tail):
    total, width = low.shape
    count = -(-2 * reach * reach // 8) * 8
    return call(
        halo_body,
        [array(total, width)] * 2,
        1.0,
        grid=(1,),
        in_specs=[whole(head.shape), whole(tail.shape), in_hbm, in_hbm],
        out_specs=[in_hbm] * 2,
        scratch_shapes=[pltpu.VMEM((2, count, width), f32), pltpu.SemaphoreType.DMA((2, 1))],
        input_output_aliases={2: 0, 3: 1},
        name="halo_slabs",
    )(head, tail, low, high)


def roll_x(value, by):
    return pltpu.roll(value, by % value.shape[-1], value.ndim - 1)


def energy_slopes(rho, sigma):
    two_a = 2.0 * correlation_scale
    b1, b2, b3, b4 = [two_a * term for term in correlation_terms]
    ratio = beta_value / gamma_value
    exchange = -0.75 * (3.0 / math.pi) ** (1.0 / 3.0)
    s_scale = 0.25 / (3.0 * math.pi**2) ** (2.0 / 3.0)
    t_scale = math.pi / (16.0 * (3.0 * math.pi**2) ** (1.0 / 3.0))
    radius_scale = (3.0 / (4.0 * math.pi)) ** (1.0 / 3.0)
    sixth = jnp.exp(jnp.log(rho) * (-1.0 / 6.0))
    inv = sixth * sixth
    inv2 = inv * inv
    inv4 = inv2 * inv2
    scaled_sigma = sigma * inv4
    stretch = 1.0 + (mu_value / kappa_value * s_scale) * scaled_sigma * inv4
    v = (ratio * t_scale) * scaled_sigma * (inv2 * inv)
    root = math.sqrt(radius_scale) * sixth
    denom = root * (b1 + root * (b2 + root * (b3 + root * b4)))
    denom_slope = root * (0.5 * b1 + root * (b2 + root * (1.5 * b3 + root * (2.0 * b4))))
    pair = denom * denom + denom
    recip = 1.0 / (stretch * pair)
    weight = recip * pair
    recip = recip * stretch
    x_rho = (rho * inv2) * (
        exchange * (4.0 / 3.0) * (1.0 + kappa_value)
        + weight
        * ((-4.0 * exchange * kappa_value) + (8.0 / 3.0 * exchange * kappa_value) * weight)
    )
    radius_part = (two_a * correlation_alpha * radius_scale) * inv
    linear = two_a + radius_part
    log_term = jnp.log(1.0 + (recip * denom + recip))
    uniform = -linear * log_term
    rho_uniform = (1.0 / 3.0) * (radius_part * log_term - linear * (recip * denom_slope))
    grown = jnp.exp(uniform * (-1.0 / gamma_value))
    x = grown - 1.0
    vx = v * x
    v2 = v * v
    lower = x * x + (vx + v2)
    upper = lower + vx * (x + v)
    both = 1.0 / (lower * upper)
    gradient = gamma_value * jnp.log(upper * (upper * both))
    h_part = (x + 2.0 * v) * (x * x) * (x * both)
    h_uniform = (v2 * both) * (v * (2.0 * x + v)) * grown
    d_rho = (
        (x_rho + uniform)
        + (gradient + rho_uniform * (1.0 - h_uniform))
        - (7.0 / 3.0 * gamma_value) * (v * h_part)
    )
    two_d_sigma = inv4 * (
        (2.0 * exchange * s_scale * mu_value) * (weight * weight)
        + (2.0 * t_scale * beta_value) * h_part
    )
    return d_rho, two_d_sigma


def potential_body(sources, groups, flag_ref, *refs):
    ext_ref, part_ref, smooth_ref, flat_ref, fx_ref, fy_ref, fz_ref = refs[-7:]
    count = 6 if groups == 2 else 4
    plane_refs = refs[: -count - 17]
    sides_hbm = plane_refs[-count:]
    tab_hbm_ref, out_ref, tab_ref, tab_sems, pot_ref, tall_ref, stage_ref = refs[-count - 17 : -count - 10]
    in_sems, out_sems, side_sems = refs[-count - 10 : -count - 7]
    side_refs = refs[-count - 7 : -7]
    planes, rows, width = pot_ref.shape
    each = planes // groups
    sides = copy_all(
        [
            (hbm.at[pl.ds(hbm.shape[0] - ref.shape[0], ref.shape[0])], ref)
            for hbm, ref in zip(sides_hbm, side_refs)
        ],
        side_sems,
    )

    def plane_of(plane, at):
        ref = plane_refs[plane]
        return ref.at[at] if len(ref.shape) == 3 else ref.at[pl.ds(at * rows, rows)]

    arriving = copy_all(
        [
            (plane_of(plane, at), ext_ref.at[z, pl.ds(lead - 1, rows)])
            for z, (plane, at, *_) in enumerate(sources)
        ],
        in_sems,
    )
    slope = 1.0 / (2.0 * grid_step)
    tiles = rows // 8 + 1

    def at_end(flag):
        return pl.when(flag_ref[flag] == 1) if groups == 2 else lambda body: None

    wait_all(sides)
    for z, (_, _, head, head_row, tail, tail_row) in enumerate(sources):
        ext_ref[z, lead - 1 - reach : lead - 1] = side_refs[head][head_row : head_row + reach]
        after = side_refs[tail][tail_row : tail_row + reach]
        ext_ref[z, lead - 1 + rows : lead - 1 + rows + reach] = after
    wait_all(arriving)
    tables = load_tables(tab_hbm_ref, tab_ref, tab_sems)

    def widened(z, size, margin):
        return z + margin * (z // size) if groups > 1 else z

    @at_end(0)
    def _():
        ext_ref[reach - 1] = ext_ref[reach]

    @at_end(1)
    def _():
        ext_ref[ext_ref.shape[0] - reach] = ext_ref[ext_ref.shape[0] - reach - 1]

    def filter_depth(z, carry):
        w = widened(z, each + 4, 2)
        part_ref[z] = 0.25 * (ext_ref[w] + ext_ref[w + 2]) + 0.5 * ext_ref[w + 1]
        return carry

    lax.fori_loop(0, part_ref.shape[0], filter_depth, 0)

    def filter_plane(z, carry):
        for t in range(tiles):
            r = lead - 2 + 8 * t
            along_y = 0.25 * (part_ref[z, r - 2 : r + 6] + part_ref[z, r : r + 8]) + 0.5 * (
                part_ref[z, r - 1 : r + 7]
            )
            smooth_ref[z, r : r + 8] = (
                0.25 * (roll_x(along_y, 1) + roll_x(along_y, -1)) + 0.5 * along_y
            )
        return carry

    lax.fori_loop(0, part_ref.shape[0], filter_plane, 0)

    @at_end(0)
    def _():
        smooth_ref[1] = smooth_ref[2]

    @at_end(1)
    def _():
        smooth_ref[smooth_ref.shape[0] - 2] = smooth_ref[smooth_ref.shape[0] - 3]

    def local_terms(z, carry):
        w = widened(z, each + 2, 2)
        for t in range(tiles):
            r = lead - 1 + 8 * t
            center = smooth_ref[w + 1, r : r + 8]
            gx = (roll_x(center, -1) - roll_x(center, 1)) * slope
            gy = (smooth_ref[w + 1, r + 1 : r + 9] - smooth_ref[w + 1, r - 1 : r + 7]) * slope
            gz = (smooth_ref[w + 2, r : r + 8] - smooth_ref[w, r : r + 8]) * slope
            d_rho, two_d_sigma = energy_slopes(center, gx * gx + gy * gy + gz * gz)
            flat_ref[z, r : r + 8] = d_rho
            fx_ref[z, r : r + 8] = two_d_sigma * gx
            fy_ref[z, r : r + 8] = two_d_sigma * gy
            fz_ref[z, r : r + 8] = two_d_sigma * gz
        return carry

    lax.fori_loop(0, flat_ref.shape[0], local_terms, 0)

    @at_end(0)
    def _():
        fz_ref[0] = fz_ref[1]

    @at_end(1)
    def _():
        fz_ref[fz_ref.shape[0] - 1] = fz_ref[fz_ref.shape[0] - 2]

    def collect(z, carry):
        w = widened(z, each, 2)
        for t in range(rows // 8):
            r = lead + 8 * t
            here = slice(r, r + 8)
            fx = fx_ref[w + 1, here]
            along_x = (roll_x(fx, -1) - roll_x(fx, 1)) * slope
            along_y = (fy_ref[w + 1, r + 1 : r + 9] - fy_ref[w + 1, r - 1 : r + 7]) * slope
            along_z = (fz_ref[w + 2, here] - fz_ref[w, here]) * slope
            pot_ref[z, 8 * t : 8 * t + 8] = flat_ref[w + 1, here] - (along_x + along_y + along_z)
        return carry

    lax.fori_loop(0, planes, collect, 0)
    wait_all(tables)
    forward_columns(pot_ref, tab_ref, tall_ref, stage_ref, out_ref, out_sems)


def forward_columns(x_ref, tab_ref, tall_ref, stage_ref, out_ref, out_sems):
    planes, rows, width = x_ref.shape
    high, low = split(x_ref[...].reshape(planes * rows, width).T)
    for k, value in enumerate((high, high, low)):
        tall_ref[k * width : (k + 1) * width] = value
    parts, block, out_lanes = stage_ref.shape
    group = parts // 2

    def step(m, carry):
        at = pl.ds(pl.multiple_of(m * group * block, group * block), group * block)
        ch, sh = tab_ref[0, at], tab_ref[2, at]
        real = dot_nn(jnp.concatenate([ch, tab_ref[1, at], ch], axis=1), tall_ref[...])
        imag = dot_nn(jnp.concatenate([sh, tab_ref[3, at], sh], axis=1), tall_ref[...])
        both = jnp.concatenate([real, -imag], axis=1)
        stage_ref[pl.ds(m * group, group)] = both.reshape(group, block, out_lanes)
        send_group(stage_ref, out_ref, out_sems, m, group)
        return carry

    lax.fori_loop(0, 2, step, 0)
    for m in range(2):
        wait_all(group_copies(stage_ref, out_ref, out_sems, m, group))


def potential_of(flags, planes, sides, sources, groups, tables, parts):
    rows, width = planes[0].shape[1:]
    tall = -(-(rows + lead + 8) // 8) * 8
    count = len(sources) - 2 * reach * groups
    lanes = count * rows
    out = (parts, width // parts, 2 * lanes)
    scratch = table_scratch(width) + [
        pltpu.VMEM((count, rows, width), f32),
        pltpu.VMEM((3 * width, lanes), bf16),
        pltpu.VMEM(out, f32),
        pltpu.SemaphoreType.DMA((len(sources),)),
        pltpu.SemaphoreType.DMA((2, parts // 2)),
        pltpu.SemaphoreType.DMA((len(sides),)),
    ]
    scratch += [pltpu.VMEM((min(side.shape[0], sides[0].shape[0]), width), f32) for side in sides]
    for margin in (6, 4, 4, 2, 2, 2, 2):
        scratch.append(pltpu.VMEM((count + margin * groups, tall, width), f32))
    return call(
        lambda *refs: potential_body(sources, groups, *refs),
        array(*out),
        20.0,
        grid=(1,),
        in_specs=[pl.BlockSpec(memory_space=pltpu.SMEM)]
        + [in_hbm] * len(planes)
        + [pl.BlockSpec(memory_space=pl.ANY)] * len(sides)
        + [in_hbm],
        out_specs=in_hbm,
        scratch_shapes=scratch,
        name="potential",
    )(flags, *planes, *sides, tables)


def forward_rows_body(starts, flag_ref, blocks_ref, coarse_hbm_ref, fine_hbm_ref, *refs):
    coarse_ref, fine_ref, factor_sems = refs[-3:]
    out_ref, tab_ref, in_ref, stage_ref, high_ref, low_ref, in_sems, out_sems = refs[-11:-3]
    _, planes, rows, width = stage_ref.shape
    fetch_blocks(blocks_ref, in_ref, in_sems)
    fill_tables((coarse_hbm_ref, fine_hbm_ref), coarse_ref, fine_ref, tab_ref, factor_sems)
    gather_blocks(blocks_ref, in_ref, in_sems, high_ref, low_ref)
    high_ref[2], low_ref[2] = -high_ref[0], -low_ref[0]

    half = planes // 2

    def copies(c, m):
        to = starts[0] + m * (starts[1] - starts[0])
        return [
            pltpu.make_async_copy(stage_ref.at[c, z], out_ref.at[c, to + y], out_sems.at[c, z])
            for y, z in enumerate([m * half + y for y in range(half)])
        ]

    def step(i, carry):
        c, m = i // 2, i % 2
        at = pl.ds(pl.multiple_of(m * half * rows, half * rows), half * rows)
        value = triple(dot_nn, high_ref[c, at], low_ref[c, at], tab_ref[0], tab_ref[1])
        value = value + triple(dot_nn, high_ref[c + 1, at], low_ref[c + 1, at], tab_ref[2], tab_ref[3])
        stage_ref[c, pl.ds(m * half, half)] = value.reshape(half, rows, width)

        @pl.when(flag_ref[2] == 1)
        def _():
            tile = (8, 128)
            at_zero = (lax.broadcasted_iota(jnp.int32, tile, 0) == 0) & (
                lax.broadcasted_iota(jnp.int32, tile, 1) == 0
            )
            for y in range(half):
                z = m * half + y
                stage_ref[c, z, :8, :128] = jnp.where(at_zero, 0.0, stage_ref[c, z, :8, :128])

        for copy in copies(c, m):
            copy.start()
        return carry

    lax.fori_loop(0, 4, step, 0)
    for c in range(2):
        wait_all(copies(c, 0) + copies(c, 1))


def forward_rows(flags, blocks, factors, starts, depth, before):
    parts, rows, lanes = blocks.shape
    width = factors[0].shape[2]
    planes = lanes * parts // (2 * width)
    earlier = [] if before is None else [before]
    scratch = [
        pltpu.VMEM((4, width, width), bf16),
        pltpu.VMEM(blocks.shape, f32),
        pltpu.VMEM((2, planes, rows, width), f32),
        pltpu.VMEM((3, planes * rows, width), bf16),
        pltpu.VMEM((3, planes * rows, width), bf16),
        pltpu.SemaphoreType.DMA((rows // gather_tile, 4)),
        pltpu.SemaphoreType.DMA((2, planes)),
    ]
    return call(
        lambda *refs: forward_rows_body(starts, *refs),
        array(2, depth, rows, width),
        10.0,
        grid=(1,),
        in_specs=[pl.BlockSpec(memory_space=pltpu.SMEM)] + [in_hbm] * (3 + len(earlier)),
        out_specs=in_hbm,
        scratch_shapes=scratch + factor_scratch(factors),
        input_output_aliases={4: 0} if earlier else {},
        name="forward_rows",
    )(flags, blocks, *factors, *earlier)


def exchange(value):
    return lax.all_to_all(value, "py", 0, 0, tiled=True)


def on_device(rho_hat):
    parts = lax.axis_size("py")
    place_z, place_y = lax.axis_index("px"), lax.axis_index("py")
    flags = jnp.stack(
        [place_z == 0, place_z == lax.axis_size("px") - 1, place_y == 0]
    ).astype(jnp.int32)
    depth, width = rho_hat.shape[1], rho_hat.shape[3]
    unit = depth // 4
    block = width // parts
    factors = phase_factors(width, block, width)
    half_factors = phase_factors(width // 2, block, width)

    outer = exchange(inverse_rows(rho_hat, half_factors, None, None, (0, 3)))
    inner, tables = inverse_rows(rho_hat, half_factors, factors, flags, (1, 2))
    inner = exchange(inner)
    outer, head, tail, low_planes, high_planes = inverse_columns(outer, factors, True)
    outer_sides = shift(tail, "py", True, True), shift(head, "py", False, True)
    inner, head, tail = inverse_columns(inner, factors, False)
    inner_sides = shift(tail, "py", True, True), shift(head, "py", False, True)

    down, up = halo_slabs(low_planes, high_planes, *outer_sides)
    down, up, _ = lax.optimization_barrier((down, up, head))
    below, above = shift(up, "px", True, False), shift(down, "px", False, False)

    def source(z):
        if unit <= z < depth - unit:
            row = reach * (z - unit)
            return 1, z - unit, 2, row, 3, row
        if 0 <= z < depth:
            at = z if z < unit else z - depth + 2 * unit
            return 0, at, 0, reach * at, 1, reach * at
        at = z + reach if z < 0 else z - depth
        side = 2 if z < 0 else 3
        return side, at, side + 2, reach * at, side + 2, reach * (reach + at)

    inside = [source(z) for z in range(unit - reach, depth - unit + reach)]
    outside = [source(z) for z in range(-reach, unit + reach)]
    outside += [source(z) for z in range(depth - unit - reach, depth + reach)]
    planes, sides = [outer, inner], [*outer_sides, *inner_sides]
    inner_waves = exchange(potential_of(flags, planes, sides, inside, 1, tables, parts))
    halo = [below, above]
    spectral = potential_of(flags, planes + halo, sides + halo, outside, 2, tables, parts)
    outer_waves = exchange(spectral)
    result = forward_rows(flags, inner_waves, factors, (unit, 2 * unit), depth, None)
    result = forward_rows(flags, outer_waves, factors, (0, depth - unit), depth, result)
    return result


def solution(mesh):
    return jax.shard_map(
        on_device,
        mesh=mesh,
        in_specs=(P(None, "px", "py", None),),
        out_specs=P(None, "px", "py", None),
        check_vma=False,
    )
```

```python
import math

import jax
import jax.numpy as jnp
import numpy as np
from jax import lax
from jax.experimental import pallas as pl
from jax.experimental.pallas import tpu as pltpu
from jax.sharding import PartitionSpec as P

grid_step = 0.25
density_floor = 0.02
density_scale = 0.2
kappa_value = 0.804
mu_value = 0.2195149727645171
beta_value = 0.06672455060314922
gamma_value = (1.0 - math.log(2.0)) / (math.pi * math.pi)
correlation_scale = 0.031091
correlation_alpha = 0.2137
correlation_terms = (7.5957, 3.5876, 1.6382, 0.49294)

f32 = jnp.float32
bf16 = jnp.bfloat16
reach = 3
gather_tile = 16
edge_rows = -(-2 * reach * reach // 8) * 8
lead = 9


in_hbm = pl.BlockSpec(memory_space=pltpu.HBM)


def call(body, out, cost, **options):
    estimate = pl.CostEstimate(flops=int(cost * 1e9), bytes_accessed=1 << 20, transcendentals=0)
    limit = pltpu.CompilerParams(vmem_limit_bytes=63 << 20)
    return pl.pallas_call(body, out_shape=out, compiler_params=limit, cost_estimate=estimate, **options)


def array(*shape):
    return jax.ShapeDtypeStruct(shape, f32)


def whole(shape):
    return pl.BlockSpec(shape, lambda *_: (0,) * len(shape))


def copy_all(pairs, sems):
    copies = [pltpu.make_async_copy(a, b, sems.at[i]) for i, (a, b) in enumerate(pairs)]
    for copy in copies:
        copy.start()
    return copies


def wait_all(copies):
    for copy in copies:
        copy.wait()


def group_copies(stage_ref, out_ref, sems, m, group):
    to = [m * group + g for g in range(group)]
    return [
        pltpu.make_async_copy(stage_ref.at[d], out_ref.at[d], sems.at[m, g])
        for g, d in enumerate(to)
    ]


def send_group(*args):
    for copy in group_copies(*args):
        copy.start()


def load_tables(hbm_ref, tab_ref, sems):
    return copy_all([(hbm_ref.at[i], tab_ref.at[i]) for i in range(4)], sems)


def table_scratch(width):
    return [pltpu.VMEM((4, width, width), bf16), pltpu.SemaphoreType.DMA((4,))]


def split(value):
    high = value.astype(bf16)
    return high, (value - high.astype(f32)).astype(bf16)


def dot_nt(left, right):
    return lax.dot_general(left, right, (((1,), (1,)), ((), ())), preferred_element_type=f32)


def dot_nn(left, right):
    return lax.dot_general(left, right, (((1,), (0,)), ((), ())), preferred_element_type=f32)


def triple(dot, left_high, left_low, right_high, right_low):
    return dot(left_high, right_high) + (dot(left_low, right_high) + dot(left_high, right_low))


def fill_tables(hbm_refs, coarse_ref, fine_ref, tab_ref, sems):
    arriving = copy_all(list(zip(hbm_refs, (coarse_ref, fine_ref))), sems)
    wait_all(arriving)
    stride = fine_ref.shape[1]

    def step(a, carry):
        cos_a, sin_a = coarse_ref[0, pl.ds(a, 1)], coarse_ref[1, pl.ds(a, 1)]
        fine_cos, fine_sin = fine_ref[0], fine_ref[1]
        rows = pl.ds(pl.multiple_of(a * stride, stride), stride)
        tab_ref[0, rows], tab_ref[1, rows] = split(cos_a * fine_cos - sin_a * fine_sin)
        tab_ref[2, rows], tab_ref[3, rows] = split(sin_a * fine_cos + cos_a * fine_sin)
        return carry

    lax.fori_loop(0, tab_ref.shape[1] // 4 // stride, step, 0)

    tile = 16
    width = tab_ref.shape[2]
    quarter = width // 4
    turn = lax.broadcasted_iota(jnp.int32, (tile, width), 1) % 4
    turn_cos = jnp.where(turn == 0, 1.0, jnp.where(turn == 2, -1.0, 0.0)).astype(bf16)
    turn_sin = jnp.where(turn == 1, 1.0, jnp.where(turn == 3, -1.0, 0.0)).astype(bf16)
    flip = jnp.where(turn % 2 == 0, 1.0, -1.0).astype(bf16)

    def spread(t, carry):
        for part in range(2):
            rows = [pl.ds(pl.multiple_of(q * quarter + t * tile, tile), tile) for q in range(4)]
            cos, sin = tab_ref[part, rows[0]], tab_ref[2 + part, rows[0]]
            next_cos = cos * turn_cos - sin * turn_sin
            next_sin = sin * turn_cos + cos * turn_sin
            tab_ref[part, rows[1]], tab_ref[2 + part, rows[1]] = next_cos, next_sin
            tab_ref[part, rows[2]], tab_ref[2 + part, rows[2]] = cos * flip, sin * flip
            tab_ref[part, rows[3]], tab_ref[2 + part, rows[3]] = next_cos * flip, next_sin * flip
        return carry

    lax.fori_loop(0, quarter // tile, spread, 0)


def factor_scratch(factors):
    return [pltpu.VMEM(factor.shape, f32) for factor in factors] + [pltpu.SemaphoreType.DMA((2,))]


def phase_factors(length, stride, norm):
    def waves(rows, scale, period):
        angle = (np.outer(rows, np.arange(length)) % period) * (2.0 * math.pi / period)
        return np.stack([np.cos(angle), np.sin(angle)]).astype(np.float32) * np.float32(scale)

    coarse = waves(np.arange(0, length // 4, stride), 1.0, length)
    coarse = np.concatenate([coarse, waves(np.arange(1, 2), 1.0, 2 * length)], axis=1)
    fine = waves(np.arange(stride), 1.0 / math.sqrt(norm), length)
    return jnp.asarray(coarse), jnp.asarray(fine)


def inverse_rows_body(blocks, makes, *refs):
    rho_ref, coarse_hbm_ref, fine_hbm_ref = refs[:3]
    if makes:
        factors_hbm, out_ref, tab_out_ref = refs[3:5], refs[6], refs[7]
        full_ref, full_coarse_ref, full_fine_ref, full_factor_sems, full_sems = refs[-5:]
        refs = refs[:-5]
    else:
        out_ref = refs[3]
    tab_ref, x_ref, wide_ref, stage_ref, in_sems, out_sems, coarse_ref, fine_ref, factor_sems = refs[-9:]
    half = tab_ref.shape[1]
    lanes = wide_ref.shape[2] // 2
    unit = x_ref.shape[1] // len(blocks)
    arriving = [
        copy_all(
            [
                (rho_ref.at[c, pl.ds(b * unit, unit)], x_ref.at[c, pl.ds(i * unit, unit)])
                for i, b in enumerate(blocks)
            ],
            in_sems.at[c],
        )
        for c in range(2)
    ]
    fill_tables((coarse_hbm_ref, fine_hbm_ref), coarse_ref, fine_ref, tab_ref, factor_sems)
    for c in range(2):
        wait_all(arriving[c])
    real, imag = [x_ref[c].reshape(lanes, 2 * half) for c in range(2)]
    last = coarse_ref.shape[1] - 1
    wave_cos, wave_sin = coarse_ref[0, last:], coarse_ref[1, last:]
    for p in range(2):
        if p == 0:
            values = real[:, :half] + real[:, half:], imag[:, :half] + imag[:, half:]
        else:
            odd_re, odd_im = real[:, :half] - real[:, half:], imag[:, :half] - imag[:, half:]
            values = odd_re * wave_cos - odd_im * wave_sin, odd_re * wave_sin + odd_im * wave_cos
        (high, low), (high_im, low_im) = [split(value.T) for value in values]
        cos_high, cos_low = [jnp.concatenate(pair, axis=1) for pair in ((high, high_im), (low, low_im))]
        sin_high, sin_low = [
            jnp.concatenate(pair, axis=1) for pair in ((-high_im, high), (-low_im, low))
        ]
        stacked = (cos_high, cos_high, cos_low, sin_high, sin_high, sin_low)
        for k, value in enumerate(stacked):
            wide_ref[p, k * half : (k + 1) * half] = value
    parts, _, block, _ = stage_ref.shape
    out_lanes = 2 * lanes
    group = parts // 2
    count = half // 2

    def step(m, carry):
        at = pl.ds(pl.multiple_of(m * count, count), count)
        ch, sh = tab_ref[0, at], tab_ref[2, at]
        left = jnp.concatenate([ch, tab_ref[1, at], ch, sh, tab_ref[3, at], sh], axis=1)
        for p in range(2):
            product = dot_nn(left, wide_ref[p]).reshape(group, block // 2, out_lanes)
            for g in range(group):
                for i in range(out_lanes // 128):
                    to = pl.ds(p, block // 2, stride=2)
                    stage_ref[m * group + g, i, to, :] = product[g, :, i * 128 : (i + 1) * 128]
        send_group(stage_ref, out_ref, out_sems, m, group)
        return carry

    lax.fori_loop(0, 2, step, 0)
    if makes:
        fill_tables(factors_hbm, full_coarse_ref, full_fine_ref, full_ref, full_factor_sems)
        wait_all(copy_all([(full_ref.at[i], tab_out_ref.at[i]) for i in range(4)], full_sems))
    for m in range(2):
        wait_all(group_copies(stage_ref, out_ref, out_sems, m, group))


def inverse_rows(rho_hat, factors, full, flags, blocks):
    _, depth, local, width = rho_hat.shape
    half = factors[1].shape[2]
    block = factors[1].shape[1]
    parts = width // block
    unit = depth // 4
    planes = len(blocks) * unit
    lanes = planes * local
    out = (parts, 2 * lanes // 128, block, 128)
    scratch = [
        pltpu.VMEM((4, half, half), bf16),
        pltpu.VMEM((2, planes, local, width), f32),
        pltpu.VMEM((2, 6 * half, 2 * lanes), bf16),
        pltpu.VMEM(out, f32),
        pltpu.SemaphoreType.DMA((2, len(blocks))),
        pltpu.SemaphoreType.DMA((2, parts // 2)),
    ] + factor_scratch(factors)
    makes = full is not None
    body = lambda *refs: inverse_rows_body(blocks, makes, *refs)
    if makes:
        scratch += [pltpu.VMEM((4, width, width), bf16)] + factor_scratch(full)
        return call(
            body,
            [array(*out), jax.ShapeDtypeStruct((4, width, width), bf16)],
            10.0,
            grid=(1,),
            in_specs=[in_hbm] * 5 + [pl.BlockSpec(memory_space=pltpu.SMEM)],
            out_specs=[in_hbm] * 2,
            scratch_shapes=scratch + [pltpu.SemaphoreType.DMA((4,))],
            name="inverse_rows",
        )(rho_hat, *factors, *full, flags)
    return call(
        body,
        array(*out),
        10.0,
        grid=(1,),
        in_specs=[in_hbm] * 3,
        out_specs=in_hbm,
        scratch_shapes=scratch,
        name="inverse_rows",
    )(rho_hat, *factors)


def tile_copies(hbm_ref, in_ref, sems, t):
    group = in_ref.shape[0] // 4
    at = pl.ds(t * gather_tile, gather_tile)
    if not isinstance(t, int):
        at = pl.ds(pl.multiple_of(t * gather_tile, gather_tile), gather_tile)
    blocks = [pl.ds(g * group, group) for g in range(4)]
    return [
        pltpu.make_async_copy(hbm_ref.at[d, :, at], in_ref.at[d, :, at], sems.at[t, g])
        if len(in_ref.shape) == 4
        else pltpu.make_async_copy(hbm_ref.at[d, at], in_ref.at[d, at], sems.at[t, g])
        for g, d in enumerate(blocks)
    ]


def fetch_blocks(hbm_ref, in_ref, sems):
    for t in range(in_ref.shape[-2] // gather_tile):
        for copy in tile_copies(hbm_ref, in_ref, sems, t):
            copy.start()


def gather_blocks(hbm_ref, in_ref, sems, high_ref, low_ref):
    parts, rows = in_ref.shape[0], in_ref.shape[-2]
    width = high_ref.shape[2]
    local = width // parts
    planes = high_ref.shape[1] // rows
    tile = gather_tile

    def load(p, at, block):
        if len(in_ref.shape) == 4:
            return in_ref[p, block, at]
        return in_ref[p, at, block * 128 : (block + 1) * 128]

    def gather_rows(t, carry):
        wait_all(tile_copies(hbm_ref, in_ref, sems, t))
        at = pl.ds(pl.multiple_of(t * tile, tile), tile)
        lane = lax.broadcasted_iota(jnp.int32, (tile, 128), 1)
        for piece in range(2 * planes):
            c, z = piece // planes, piece % planes
            first = piece * local
            block, offset = first // 128, first % 128
            turned = []
            for p in range(parts):
                value = load(p, at, block)
                if offset + local > 128:
                    after = load(p, at, block + 1)
                    value = jnp.where(lane < offset, after, value)
                turned.append(pltpu.roll(value, (p * local - offset) % 128, 1))
            to = pl.ds(pl.multiple_of(z * rows + t * tile, tile), tile)
            for out in range(width // 128):
                start = out * 128 // local
                value = turned[start]
                for p in range(start + 1, parts):
                    edge = p * local - out * 128
                    if edge < 128:
                        value = jnp.where(lane < edge, value, turned[p])
                high, low = split(value)
                high_ref[c, to, out * 128 : (out + 1) * 128] = high
                low_ref[c, to, out * 128 : (out + 1) * 128] = low
        return carry

    lax.fori_loop(0, rows // tile, gather_rows, 0)


def inverse_columns_body(sends, blocks_ref, coarse_hbm_ref, fine_hbm_ref, *refs):
    coarse_ref, fine_ref, factor_sems = refs[-3:]
    refs = refs[:-3]
    out_ref, head_ref, tail_ref = refs[:3]
    tab_ref, in_ref, stage_ref, high_ref, low_ref, in_sems, out_sems, send_sems = refs[-8:]
    planes, rows, width = stage_ref.shape
    fetch_blocks(blocks_ref, in_ref, in_sems)
    fill_tables((coarse_hbm_ref, fine_hbm_ref), coarse_ref, fine_ref, tab_ref, factor_sems)
    gather_blocks(blocks_ref, in_ref, in_sems, high_ref, low_ref)
    half = planes // 2

    def finish(z, carry):
        value = stage_ref[z]
        soft = jnp.maximum(value, 0.0) + jnp.log1p(jnp.exp(-jnp.abs(value)))
        stage_ref[z] = density_floor + density_scale * soft
        pltpu.make_async_copy(stage_ref.at[z], out_ref.at[z], out_sems.at[z]).start()
        return carry

    def step(m, carry):
        at = pl.ds(pl.multiple_of(m * half * rows, half * rows), half * rows)
        field = triple(dot_nn, high_ref[0, at], low_ref[0, at], tab_ref[0], tab_ref[1])
        field = field - triple(dot_nn, high_ref[1, at], low_ref[1, at], tab_ref[2], tab_ref[3])
        stage_ref[pl.ds(m * half, half)] = field.reshape(half, rows, width)
        lax.fori_loop(m * half, (m + 1) * half, finish, 0)
        return carry

    lax.fori_loop(0, 2, step, 0)
    leaving = [
        pltpu.make_async_copy(stage_ref.at[z], out_ref.at[z], out_sems.at[z]) for z in range(planes)
    ]
    for m in range(2 if sends else 0):
        first = m * (planes - reach)
        pairs = [(stage_ref.at[first + z], refs[3 + m].at[pl.ds(z * rows, rows)]) for z in range(reach)]
        leaving += copy_all(pairs, send_sems.at[m])
    for z in range(planes):
        at = slice(reach * z, reach * (z + 1))
        head_ref[at] = stage_ref[z, :reach]
        tail_ref[at] = stage_ref[z, rows - reach :]
    wait_all(leaving)


def inverse_columns(blocks, factors, sends):
    parts, _, rows, _ = blocks.shape
    lanes = blocks.shape[1] * blocks.shape[3]
    width = factors[0].shape[2]
    planes = lanes * parts // (2 * width)
    side = (reach * planes, width)
    slabs = 2 if sends else 0
    scratch = [
        pltpu.VMEM((4, width, width), bf16),
        pltpu.VMEM(blocks.shape, f32),
        pltpu.VMEM((planes, rows, width), f32),
        pltpu.VMEM((2, planes * rows, width), bf16),
        pltpu.VMEM((2, planes * rows, width), bf16),
        pltpu.SemaphoreType.DMA((rows // gather_tile, 4)),
        pltpu.SemaphoreType.DMA((planes,)),
        pltpu.SemaphoreType.DMA((2, reach)),
    ]
    return call(
        lambda *refs: inverse_columns_body(sends, *refs),
        [array(planes, rows, width), array(*side), array(*side)]
        + [array(slab_rows(rows), width)] * slabs,
        7.0,
        grid=(1,),
        in_specs=[in_hbm] * 3,
        out_specs=[in_hbm, whole(side), whole(side)] + [in_hbm] * slabs,
        scratch_shapes=scratch + factor_scratch(factors),
        name="inverse_columns",
    )(blocks, *factors)


def shift(value, axis, up, ring):
    count = lax.axis_size(axis)
    pairs = [(i, (i + 1) % count) for i in range(count if ring else count - 1)]
    return lax.ppermute(value, axis, pairs if up else [(b, a) for a, b in pairs])


def slab_rows(rows):
    return reach * rows + edge_rows


def halo_body(head_ref, tail_ref, low_ref, high_ref, down_ref, up_ref, edge_ref, sems):
    side = reach * reach
    held = head_ref.shape[0]
    copies = []
    for i, (first, out_ref) in enumerate(((0, down_ref), (held - side, up_ref))):
        edge_ref[i, :side] = head_ref[first : first + side]
        edge_ref[i, side : 2 * side] = tail_ref[first : first + side]
        count = edge_ref.shape[1]
        to = out_ref.at[pl.ds(out_ref.shape[0] - count, count)]
        copies += copy_all([(edge_ref.at[i], to)], sems.at[i])
    wait_all(copies)


def halo_slabs(low, high, head, tail):
    total, width = low.shape
    return call(
        halo_body,
        [array(total, width)] * 2,
        1.0,
        grid=(1,),
        in_specs=[whole(head.shape), whole(tail.shape), in_hbm, in_hbm],
        out_specs=[in_hbm] * 2,
        scratch_shapes=[pltpu.VMEM((2, edge_rows, width), f32), pltpu.SemaphoreType.DMA((2, 1))],
        input_output_aliases={2: 0, 3: 1},
        name="halo_slabs",
    )(head, tail, low, high)


def roll_x(value, by):
    return pltpu.roll(value, by % value.shape[-1], value.ndim - 1)


def energy_slopes(rho, sigma):
    two_a = 2.0 * correlation_scale
    b1, b2, b3, b4 = [two_a * term for term in correlation_terms]
    ratio = beta_value / gamma_value
    exchange = -0.75 * (3.0 / math.pi) ** (1.0 / 3.0)
    s_scale = 0.25 / (3.0 * math.pi**2) ** (2.0 / 3.0)
    t_scale = math.pi / (16.0 * (3.0 * math.pi**2) ** (1.0 / 3.0))
    radius_scale = (3.0 / (4.0 * math.pi)) ** (1.0 / 3.0)
    sixth = jnp.exp(jnp.log(rho) * (-1.0 / 6.0))
    inv = sixth * sixth
    inv2 = inv * inv
    inv4 = inv2 * inv2
    scaled_sigma = sigma * inv4
    stretch = 1.0 + (mu_value / kappa_value * s_scale) * scaled_sigma * inv4
    v = (ratio * t_scale) * scaled_sigma * (inv2 * inv)
    root = math.sqrt(radius_scale) * sixth
    denom = root * (b1 + root * (b2 + root * (b3 + root * b4)))
    denom_slope = root * (0.5 * b1 + root * (b2 + root * (1.5 * b3 + root * (2.0 * b4))))
    pair = denom * denom + denom
    recip = 1.0 / (stretch * pair)
    weight = recip * pair
    recip = recip * stretch
    x_rho = (rho * inv2) * (
        exchange * (4.0 / 3.0) * (1.0 + kappa_value)
        + weight
        * ((-4.0 * exchange * kappa_value) + (8.0 / 3.0 * exchange * kappa_value) * weight)
    )
    radius_part = (two_a * correlation_alpha * radius_scale) * inv
    linear = two_a + radius_part
    log_term = jnp.log(1.0 + (recip * denom + recip))
    uniform = -linear * log_term
    rho_uniform = (1.0 / 3.0) * (radius_part * log_term - linear * (recip * denom_slope))
    grown = jnp.exp(uniform * (-1.0 / gamma_value))
    x = grown - 1.0
    vx = v * x
    v2 = v * v
    lower = x * x + (vx + v2)
    upper = lower + vx * (x + v)
    both = 1.0 / (lower * upper)
    gradient = gamma_value * jnp.log(upper * (upper * both))
    h_part = (x + 2.0 * v) * (x * x) * (x * both)
    h_uniform = (v2 * both) * (v * (2.0 * x + v)) * grown
    d_rho = (
        (x_rho + uniform)
        + (gradient + rho_uniform * (1.0 - h_uniform))
        - (7.0 / 3.0 * gamma_value) * (v * h_part)
    )
    two_d_sigma = inv4 * (
        (2.0 * exchange * s_scale * mu_value) * (weight * weight)
        + (2.0 * t_scale * beta_value) * h_part
    )
    return d_rho, two_d_sigma


def potential_body(sources, groups, flag_ref, *refs):
    ext_ref, part_ref, smooth_ref, flat_ref, fx_ref, fy_ref, fz_ref = refs[-7:]
    count = 6 if groups == 2 else 4
    plane_refs = refs[: -count - 17]
    sides_hbm = plane_refs[-count:]
    tab_hbm_ref, out_ref, tab_ref, tab_sems, pot_ref, tall_ref, stage_ref = refs[-count - 17 : -count - 10]
    in_sems, out_sems, side_sems = refs[-count - 10 : -count - 7]
    side_refs = refs[-count - 7 : -7]
    planes, rows, width = pot_ref.shape
    each = planes // groups
    sides = copy_all(
        [
            (hbm.at[pl.ds(hbm.shape[0] - ref.shape[0], ref.shape[0])], ref)
            for hbm, ref in zip(sides_hbm, side_refs)
        ],
        side_sems,
    )

    def plane_of(plane, at):
        ref = plane_refs[plane]
        return ref.at[at] if len(ref.shape) == 3 else ref.at[pl.ds(at * rows, rows)]

    arriving = copy_all(
        [
            (plane_of(plane, at), ext_ref.at[z, pl.ds(lead - 1, rows)])
            for z, (plane, at, *_) in enumerate(sources)
        ],
        in_sems,
    )
    slope = 1.0 / (2.0 * grid_step)
    tiles = rows // 8 + 1

    def at_end(flag):
        return pl.when(flag_ref[flag] == 1) if groups == 2 else lambda body: None

    wait_all(sides)
    for z, (_, _, head, head_row, tail, tail_row) in enumerate(sources):
        ext_ref[z, lead - 1 - reach : lead - 1] = side_refs[head][head_row : head_row + reach]
        after = side_refs[tail][tail_row : tail_row + reach]
        ext_ref[z, lead - 1 + rows : lead - 1 + rows + reach] = after
    wait_all(arriving)
    tables = load_tables(tab_hbm_ref, tab_ref, tab_sems)

    def widened(z, size, margin):
        return z + margin * (z // size) if groups > 1 else z

    @at_end(0)
    def _():
        ext_ref[reach - 1] = ext_ref[reach]

    @at_end(1)
    def _():
        ext_ref[ext_ref.shape[0] - reach] = ext_ref[ext_ref.shape[0] - reach - 1]

    def filter_depth(z, carry):
        w = widened(z, each + 4, 2)
        part_ref[z] = 0.25 * (ext_ref[w] + ext_ref[w + 2]) + 0.5 * ext_ref[w + 1]
        return carry

    lax.fori_loop(0, part_ref.shape[0], filter_depth, 0)

    def filter_plane(z, carry):
        for t in range(tiles):
            r = lead - 2 + 8 * t
            along_y = 0.25 * (part_ref[z, r - 2 : r + 6] + part_ref[z, r : r + 8]) + 0.5 * (
                part_ref[z, r - 1 : r + 7]
            )
            smooth_ref[z, r : r + 8] = (
                0.25 * (roll_x(along_y, 1) + roll_x(along_y, -1)) + 0.5 * along_y
            )
        return carry

    lax.fori_loop(0, part_ref.shape[0], filter_plane, 0)

    @at_end(0)
    def _():
        smooth_ref[1] = smooth_ref[2]

    @at_end(1)
    def _():
        smooth_ref[smooth_ref.shape[0] - 2] = smooth_ref[smooth_ref.shape[0] - 3]

    def local_terms(z, carry):
        w = widened(z, each + 2, 2)
        for t in range(tiles):
            r = lead - 1 + 8 * t
            center = smooth_ref[w + 1, r : r + 8]
            gx = (roll_x(center, -1) - roll_x(center, 1)) * slope
            gy = (smooth_ref[w + 1, r + 1 : r + 9] - smooth_ref[w + 1, r - 1 : r + 7]) * slope
            gz = (smooth_ref[w + 2, r : r + 8] - smooth_ref[w, r : r + 8]) * slope
            d_rho, two_d_sigma = energy_slopes(center, gx * gx + gy * gy + gz * gz)
            flat_ref[z, r : r + 8] = d_rho
            fx_ref[z, r : r + 8] = two_d_sigma * gx
            fy_ref[z, r : r + 8] = two_d_sigma * gy
            fz_ref[z, r : r + 8] = two_d_sigma * gz
        return carry

    lax.fori_loop(0, flat_ref.shape[0], local_terms, 0)

    @at_end(0)
    def _():
        fz_ref[0] = fz_ref[1]

    @at_end(1)
    def _():
        fz_ref[fz_ref.shape[0] - 1] = fz_ref[fz_ref.shape[0] - 2]

    def collect(z, carry):
        w = widened(z, each, 2)
        for t in range(rows // 8):
            r = lead + 8 * t
            here = slice(r, r + 8)
            fx = fx_ref[w + 1, here]
            along_x = (roll_x(fx, -1) - roll_x(fx, 1)) * slope
            along_y = (fy_ref[w + 1, r + 1 : r + 9] - fy_ref[w + 1, r - 1 : r + 7]) * slope
            along_z = (fz_ref[w + 2, here] - fz_ref[w, here]) * slope
            pot_ref[z, 8 * t : 8 * t + 8] = flat_ref[w + 1, here] - (along_x + along_y + along_z)
        return carry

    lax.fori_loop(0, planes, collect, 0)
    wait_all(tables)
    forward_columns(pot_ref, tab_ref, tall_ref, stage_ref, out_ref, out_sems)


def forward_columns(x_ref, tab_ref, tall_ref, stage_ref, out_ref, out_sems):
    planes, rows, width = x_ref.shape
    high, low = split(x_ref[...].reshape(planes * rows, width).T)
    for k, value in enumerate((high, high, low)):
        tall_ref[k * width : (k + 1) * width] = value
    parts, block, out_lanes = stage_ref.shape
    group = parts // 2

    def step(m, carry):
        at = pl.ds(pl.multiple_of(m * group * block, group * block), group * block)
        ch, sh = tab_ref[0, at], tab_ref[2, at]
        real = dot_nn(jnp.concatenate([ch, tab_ref[1, at], ch], axis=1), tall_ref[...])
        imag = dot_nn(jnp.concatenate([sh, tab_ref[3, at], sh], axis=1), tall_ref[...])
        both = jnp.concatenate([real, -imag], axis=1)
        stage_ref[pl.ds(m * group, group)] = both.reshape(group, block, out_lanes)
        send_group(stage_ref, out_ref, out_sems, m, group)
        return carry

    lax.fori_loop(0, 2, step, 0)
    for m in range(2):
        wait_all(group_copies(stage_ref, out_ref, out_sems, m, group))


def potential_of(flags, planes, sides, sources, groups, tables, parts):
    rows, width = planes[0].shape[1:]
    tall = -(-(rows + lead + 8) // 8) * 8
    count = len(sources) - 2 * reach * groups
    lanes = count * rows
    out = (parts, width // parts, 2 * lanes)
    scratch = table_scratch(width) + [
        pltpu.VMEM((count, rows, width), f32),
        pltpu.VMEM((3 * width, lanes), bf16),
        pltpu.VMEM(out, f32),
        pltpu.SemaphoreType.DMA((len(sources),)),
        pltpu.SemaphoreType.DMA((2, parts // 2)),
        pltpu.SemaphoreType.DMA((len(sides),)),
    ]
    scratch += [
        pltpu.VMEM((min(side.shape[0], edge_rows if i >= 4 else 1 << 20), width), f32)
        for i, side in enumerate(sides)
    ]
    for margin in (6, 4, 4, 2, 2, 2, 2):
        scratch.append(pltpu.VMEM((count + margin * groups, tall, width), f32))
    return call(
        lambda *refs: potential_body(sources, groups, *refs),
        array(*out),
        20.0,
        grid=(1,),
        in_specs=[pl.BlockSpec(memory_space=pltpu.SMEM)]
        + [in_hbm] * len(planes)
        + [pl.BlockSpec(memory_space=pl.ANY)] * len(sides)
        + [in_hbm],
        out_specs=in_hbm,
        scratch_shapes=scratch,
        name="potential",
    )(flags, *planes, *sides, tables)


def forward_rows_body(starts, flag_ref, blocks_ref, coarse_hbm_ref, fine_hbm_ref, *refs):
    coarse_ref, fine_ref, factor_sems = refs[-3:]
    out_ref, tab_ref, in_ref, stage_ref, high_ref, low_ref, in_sems, out_sems = refs[-11:-3]
    _, planes, rows, width = stage_ref.shape
    fetch_blocks(blocks_ref, in_ref, in_sems)
    fill_tables((coarse_hbm_ref, fine_hbm_ref), coarse_ref, fine_ref, tab_ref, factor_sems)
    gather_blocks(blocks_ref, in_ref, in_sems, high_ref, low_ref)
    high_ref[2], low_ref[2] = -high_ref[0], -low_ref[0]

    half = planes // 2

    def copies(c, m):
        to = starts[0] + m * (starts[1] - starts[0])
        return [
            pltpu.make_async_copy(stage_ref.at[c, z], out_ref.at[c, to + y], out_sems.at[c, z])
            for y, z in enumerate([m * half + y for y in range(half)])
        ]

    def step(i, carry):
        c, m = i // 2, i % 2
        at = pl.ds(pl.multiple_of(m * half * rows, half * rows), half * rows)
        value = triple(dot_nn, high_ref[c, at], low_ref[c, at], tab_ref[0], tab_ref[1])
        value = value + triple(dot_nn, high_ref[c + 1, at], low_ref[c + 1, at], tab_ref[2], tab_ref[3])
        stage_ref[c, pl.ds(m * half, half)] = value.reshape(half, rows, width)

        @pl.when(flag_ref[2] == 1)
        def _():
            tile = (8, 128)
            at_zero = (lax.broadcasted_iota(jnp.int32, tile, 0) == 0) & (
                lax.broadcasted_iota(jnp.int32, tile, 1) == 0
            )
            for y in range(half):
                z = m * half + y
                stage_ref[c, z, :8, :128] = jnp.where(at_zero, 0.0, stage_ref[c, z, :8, :128])

        for copy in copies(c, m):
            copy.start()
        return carry

    lax.fori_loop(0, 4, step, 0)
    for c in range(2):
        wait_all(copies(c, 0) + copies(c, 1))


def forward_rows(flags, blocks, factors, starts, depth, before):
    parts, rows, lanes = blocks.shape
    width = factors[0].shape[2]
    planes = lanes * parts // (2 * width)
    earlier = [] if before is None else [before]
    scratch = [
        pltpu.VMEM((4, width, width), bf16),
        pltpu.VMEM(blocks.shape, f32),
        pltpu.VMEM((2, planes, rows, width), f32),
        pltpu.VMEM((3, planes * rows, width), bf16),
        pltpu.VMEM((3, planes * rows, width), bf16),
        pltpu.SemaphoreType.DMA((rows // gather_tile, 4)),
        pltpu.SemaphoreType.DMA((2, planes)),
    ]
    return call(
        lambda *refs: forward_rows_body(starts, *refs),
        array(2, depth, rows, width),
        10.0,
        grid=(1,),
        in_specs=[pl.BlockSpec(memory_space=pltpu.SMEM)] + [in_hbm] * (3 + len(earlier)),
        out_specs=in_hbm,
        scratch_shapes=scratch + factor_scratch(factors),
        input_output_aliases={4: 0} if earlier else {},
        name="forward_rows",
    )(flags, blocks, *factors, *earlier)


def exchange(value):
    return lax.all_to_all(value, "py", 0, 0, tiled=True)


def on_device(rho_hat):
    parts = lax.axis_size("py")
    place_z, place_y = lax.axis_index("px"), lax.axis_index("py")
    flags = jnp.stack(
        [place_z == 0, place_z == lax.axis_size("px") - 1, place_y == 0]
    ).astype(jnp.int32)
    depth, width = rho_hat.shape[1], rho_hat.shape[3]
    unit = depth // 4
    block = width // parts
    factors = phase_factors(width, block, width)
    half_factors = phase_factors(width // 2, block, width)

    outer = exchange(inverse_rows(rho_hat, half_factors, None, None, (0, 2, 3)))
    inner, tables = inverse_rows(rho_hat, half_factors, factors, flags, (1,))
    inner = exchange(inner)
    outer, head, tail, low_planes, high_planes = inverse_columns(outer, factors, True)
    outer_sides = shift(tail, "py", True, True), shift(head, "py", False, True)
    inner, head, tail = inverse_columns(inner, factors, False)
    inner_sides = shift(tail, "py", True, True), shift(head, "py", False, True)

    down, up = halo_slabs(low_planes, high_planes, *outer_sides)
    down, up, _ = lax.optimization_barrier((down, up, head))
    below, above = shift(up, "px", True, False), shift(down, "px", False, False)

    def source(z):
        if unit <= z < 2 * unit:
            row = reach * (z - unit)
            return 1, z - unit, 2, row, 3, row
        if 0 <= z < depth:
            at = z if z < unit else z - unit
            return 0, at, 0, reach * at, 1, reach * at
        at = z + reach if z < 0 else z - depth
        side = 2 if z < 0 else 3
        return side, at, side + 2, reach * at, side + 2, reach * (reach + at)

    inside = [source(z) for z in range(unit - reach, depth - unit + reach)]
    outside = [source(z) for z in range(-reach, unit + reach)]
    outside += [source(z) for z in range(depth - unit - reach, depth + reach)]
    planes, sides = [outer, inner], [*outer_sides, *inner_sides]
    inner_waves = exchange(potential_of(flags, planes, sides, inside, 1, tables, parts))
    halo = [below, above]
    spectral = potential_of(flags, planes + halo, sides + halo, outside, 2, tables, parts)
    outer_waves = exchange(spectral)
    result = forward_rows(flags, inner_waves, factors, (unit, 2 * unit), depth, None)
    result = forward_rows(flags, outer_waves, factors, (0, depth - unit), depth, result)
    return result


def solution(mesh):
    return jax.shard_map(
        on_device,
        mesh=mesh,
        in_specs=(P(None, "px", "py", None),),
        out_specs=P(None, "px", "py", None),
        check_vma=False,
    )
```

```python
import math

import jax
import jax.numpy as jnp
import numpy as np
from jax import lax
from jax.experimental import pallas as pl
from jax.experimental.pallas import tpu as pltpu
from jax.sharding import PartitionSpec as P

grid_step = 0.25
density_floor = 0.02
density_scale = 0.2
kappa_value = 0.804
mu_value = 0.2195149727645171
beta_value = 0.06672455060314922
gamma_value = (1.0 - math.log(2.0)) / (math.pi * math.pi)
correlation_scale = 0.031091
correlation_alpha = 0.2137
correlation_terms = (7.5957, 3.5876, 1.6382, 0.49294)

f32 = jnp.float32
bf16 = jnp.bfloat16
reach = 3
gather_tile = 16
lead = 9


in_hbm = pl.BlockSpec(memory_space=pltpu.HBM)


def call(body, out, cost, **options):
    estimate = pl.CostEstimate(flops=int(cost * 1e9), bytes_accessed=1 << 20, transcendentals=0)
    limit = pltpu.CompilerParams(vmem_limit_bytes=62 << 20)
    return pl.pallas_call(body, out_shape=out, compiler_params=limit, cost_estimate=estimate, **options)


def array(*shape):
    return jax.ShapeDtypeStruct(shape, f32)


def whole(shape):
    return pl.BlockSpec(shape, lambda *_: (0,) * len(shape))


def copy_all(pairs, sems):
    copies = [pltpu.make_async_copy(a, b, sems.at[i]) for i, (a, b) in enumerate(pairs)]
    for copy in copies:
        copy.start()
    return copies


def wait_all(copies):
    for copy in copies:
        copy.wait()


def group_copies(stage_ref, out_ref, sems, m, group):
    to = [m * group + g for g in range(group)]
    return [
        pltpu.make_async_copy(stage_ref.at[d], out_ref.at[d], sems.at[m, g])
        for g, d in enumerate(to)
    ]


def send_group(*args):
    for copy in group_copies(*args):
        copy.start()


def load_tables(hbm_ref, tab_ref, sems):
    return copy_all([(hbm_ref.at[i], tab_ref.at[i]) for i in range(4)], sems)


def table_scratch(width):
    return [pltpu.VMEM((4, width, width), bf16), pltpu.SemaphoreType.DMA((4,))]


def split(value):
    high = value.astype(bf16)
    return high, (value - high.astype(f32)).astype(bf16)


def dot_nt(left, right):
    return lax.dot_general(left, right, (((1,), (1,)), ((), ())), preferred_element_type=f32)


def dot_nn(left, right):
    return lax.dot_general(left, right, (((1,), (0,)), ((), ())), preferred_element_type=f32)


def triple(dot, left_high, left_low, right_high, right_low):
    return dot(left_high, right_high) + (dot(left_low, right_high) + dot(left_high, right_low))


def fill_tables(arriving, coarse_ref, fine_ref, tab_ref):
    wait_all(arriving)
    stride = fine_ref.shape[1]

    def step(a, carry):
        cos_a, sin_a = coarse_ref[0, pl.ds(a, 1)], coarse_ref[1, pl.ds(a, 1)]
        fine_cos, fine_sin = fine_ref[0], fine_ref[1]
        rows = pl.ds(pl.multiple_of(a * stride, stride), stride)
        tab_ref[0, rows], tab_ref[1, rows] = split(cos_a * fine_cos - sin_a * fine_sin)
        tab_ref[2, rows], tab_ref[3, rows] = split(sin_a * fine_cos + cos_a * fine_sin)
        return carry

    lax.fori_loop(0, tab_ref.shape[1] // 4 // stride, step, 0)

    tile = 16
    width = tab_ref.shape[2]
    quarter = width // 4
    turn = lax.broadcasted_iota(jnp.int32, (tile, width), 1) % 4
    turn_cos = jnp.where(turn == 0, 1.0, jnp.where(turn == 2, -1.0, 0.0)).astype(bf16)
    turn_sin = jnp.where(turn == 1, 1.0, jnp.where(turn == 3, -1.0, 0.0)).astype(bf16)
    flip = jnp.where(turn % 2 == 0, 1.0, -1.0).astype(bf16)

    def spread(t, carry):
        for part in range(2):
            rows = [pl.ds(pl.multiple_of(q * quarter + t * tile, tile), tile) for q in range(4)]
            cos, sin = tab_ref[part, rows[0]], tab_ref[2 + part, rows[0]]
            next_cos = cos * turn_cos - sin * turn_sin
            next_sin = sin * turn_cos + cos * turn_sin
            tab_ref[part, rows[1]], tab_ref[2 + part, rows[1]] = next_cos, next_sin
            tab_ref[part, rows[2]], tab_ref[2 + part, rows[2]] = cos * flip, sin * flip
            tab_ref[part, rows[3]], tab_ref[2 + part, rows[3]] = next_cos * flip, next_sin * flip
        return carry

    lax.fori_loop(0, quarter // tile, spread, 0)


def factor_scratch(factors):
    return [pltpu.VMEM(factor.shape, f32) for factor in factors] + [pltpu.SemaphoreType.DMA((2,))]


def phase_factors(length, stride, norm):
    def waves(rows, scale, period):
        angle = (np.outer(rows, np.arange(length)) % period) * (2.0 * math.pi / period)
        return np.stack([np.cos(angle), np.sin(angle)]).astype(np.float32) * np.float32(scale)

    coarse = waves(np.arange(0, length // 4, stride), 1.0, length)
    coarse = np.concatenate([coarse, waves(np.arange(1, 2), 1.0, 2 * length)], axis=1)
    fine = waves(np.arange(stride), 1.0 / math.sqrt(norm), length)
    return jnp.asarray(coarse), jnp.asarray(fine)


def inverse_rows_body(blocks, makes, *refs):
    rho_ref, coarse_hbm_ref, fine_hbm_ref = refs[:3]
    if makes:
        factors_hbm, out_ref, tab_out_ref = refs[3:5], refs[6], refs[7]
        full_ref, full_coarse_ref, full_fine_ref, full_factor_sems, full_sems = refs[-5:]
        refs = refs[:-5]
    else:
        out_ref = refs[3]
    tab_ref, x_ref, wide_ref, stage_ref, in_sems, out_sems, coarse_ref, fine_ref, factor_sems = refs[-9:]
    half = tab_ref.shape[1]
    lanes = wide_ref.shape[2] // 2
    unit = x_ref.shape[1] // len(blocks)
    small = copy_all([(coarse_hbm_ref, coarse_ref), (fine_hbm_ref, fine_ref)], factor_sems)
    arriving = [
        copy_all(
            [
                (rho_ref.at[c, pl.ds(b * unit, unit)], x_ref.at[c, pl.ds(i * unit, unit)])
                for i, b in enumerate(blocks)
            ],
            in_sems.at[c],
        )
        for c in range(2)
    ]
    fill_tables(small, coarse_ref, fine_ref, tab_ref)
    for c in range(2):
        wait_all(arriving[c])
    real, imag = [x_ref[c].reshape(lanes, 2 * half) for c in range(2)]
    last = coarse_ref.shape[1] - 1
    wave_cos, wave_sin = coarse_ref[0, last:], coarse_ref[1, last:]
    for p in range(2):
        if p == 0:
            values = real[:, :half] + real[:, half:], imag[:, :half] + imag[:, half:]
        else:
            odd_re, odd_im = real[:, :half] - real[:, half:], imag[:, :half] - imag[:, half:]
            values = odd_re * wave_cos - odd_im * wave_sin, odd_re * wave_sin + odd_im * wave_cos
        for c in range(2):
            high, low = split(values[c].T)
            cos_at = slice(c * lanes, (c + 1) * lanes)
            sin_at = slice((1 - c) * lanes, (2 - c) * lanes)
            for k, value in enumerate((high, high, low)):
                wide_ref[p, k * half : (k + 1) * half, cos_at] = value
                turned = value if c == 0 else -value
                wide_ref[p, (k + 3) * half : (k + 4) * half, sin_at] = turned
    parts, _, block, _ = stage_ref.shape
    out_lanes = 2 * lanes
    group = parts // 2
    count = half // 2

    def step(m, carry):
        at = pl.ds(pl.multiple_of(m * count, count), count)
        ch, sh = tab_ref[0, at], tab_ref[2, at]
        left = jnp.concatenate([ch, tab_ref[1, at], ch, sh, tab_ref[3, at], sh], axis=1)
        for p in range(2):
            product = dot_nn(left, wide_ref[p]).reshape(group, block // 2, out_lanes)
            for g in range(group):
                for i in range(out_lanes // 128):
                    to = pl.ds(p, block // 2, stride=2)
                    stage_ref[m * group + g, i, to, :] = product[g, :, i * 128 : (i + 1) * 128]
        send_group(stage_ref, out_ref, out_sems, m, group)
        return carry

    lax.fori_loop(0, 2, step, 0)
    if makes:
        pairs = zip(factors_hbm, (full_coarse_ref, full_fine_ref))
        small = copy_all(list(pairs), full_factor_sems)
        fill_tables(small, full_coarse_ref, full_fine_ref, full_ref)
        wait_all(copy_all([(full_ref.at[i], tab_out_ref.at[i]) for i in range(4)], full_sems))
    for m in range(2):
        wait_all(group_copies(stage_ref, out_ref, out_sems, m, group))


def inverse_rows(rho_hat, factors, full, flags, blocks):
    _, depth, local, width = rho_hat.shape
    half = factors[1].shape[2]
    block = factors[1].shape[1]
    parts = width // block
    unit = depth // 4
    planes = len(blocks) * unit
    lanes = planes * local
    out = (parts, 2 * lanes // 128, block, 128)
    scratch = [
        pltpu.VMEM((4, half, half), bf16),
        pltpu.VMEM((2, planes, local, width), f32),
        pltpu.VMEM((2, 6 * half, 2 * lanes), bf16),
        pltpu.VMEM(out, f32),
        pltpu.SemaphoreType.DMA((2, len(blocks))),
        pltpu.SemaphoreType.DMA((2, parts // 2)),
    ] + factor_scratch(factors)
    makes = full is not None
    body = lambda *refs: inverse_rows_body(blocks, makes, *refs)
    if makes:
        scratch += [pltpu.VMEM((4, width, width), bf16)] + factor_scratch(full)
        return call(
            body,
            [array(*out), jax.ShapeDtypeStruct((4, width, width), bf16)],
            10.0,
            grid=(1,),
            in_specs=[in_hbm] * 5 + [pl.BlockSpec(memory_space=pltpu.SMEM)],
            out_specs=[in_hbm] * 2,
            scratch_shapes=scratch + [pltpu.SemaphoreType.DMA((4,))],
            name="inverse_rows",
        )(rho_hat, *factors, *full, flags)
    return call(
        body,
        array(*out),
        10.0,
        grid=(1,),
        in_specs=[in_hbm] * 3,
        out_specs=in_hbm,
        scratch_shapes=scratch,
        name="inverse_rows",
    )(rho_hat, *factors)


def tile_copies(hbm_ref, in_ref, sems, t):
    group = in_ref.shape[0] // 4
    at = pl.ds(t * gather_tile, gather_tile)
    if not isinstance(t, int):
        at = pl.ds(pl.multiple_of(t * gather_tile, gather_tile), gather_tile)
    blocks = [pl.ds(g * group, group) for g in range(4)]
    return [
        pltpu.make_async_copy(hbm_ref.at[d, :, at], in_ref.at[d, :, at], sems.at[t, g])
        if len(in_ref.shape) == 4
        else pltpu.make_async_copy(hbm_ref.at[d, at], in_ref.at[d, at], sems.at[t, g])
        for g, d in enumerate(blocks)
    ]


def fetch_blocks(hbm_ref, in_ref, sems):
    for t in range(in_ref.shape[-2] // gather_tile):
        for copy in tile_copies(hbm_ref, in_ref, sems, t):
            copy.start()


def gather_blocks(hbm_ref, in_ref, sems, high_ref, low_ref):
    parts, rows = in_ref.shape[0], in_ref.shape[-2]
    width = high_ref.shape[2]
    local = width // parts
    planes = high_ref.shape[1] // rows
    tile = gather_tile

    def load(p, at, block):
        if len(in_ref.shape) == 4:
            return in_ref[p, block, at]
        return in_ref[p, at, block * 128 : (block + 1) * 128]

    def gather_rows(t, carry):
        wait_all(tile_copies(hbm_ref, in_ref, sems, t))
        at = pl.ds(pl.multiple_of(t * tile, tile), tile)
        lane = lax.broadcasted_iota(jnp.int32, (tile, 128), 1)
        for piece in range(2 * planes):
            c, z = piece // planes, piece % planes
            first = piece * local
            block, offset = first // 128, first % 128
            turned = []
            for p in range(parts):
                value = load(p, at, block)
                if offset + local > 128:
                    after = load(p, at, block + 1)
                    value = jnp.where(lane < offset, after, value)
                turned.append(pltpu.roll(value, (p * local - offset) % 128, 1))
            to = pl.ds(pl.multiple_of(z * rows + t * tile, tile), tile)
            for out in range(width // 128):
                start = out * 128 // local
                value = turned[start]
                for p in range(start + 1, parts):
                    edge = p * local - out * 128
                    if edge < 128:
                        value = jnp.where(lane < edge, value, turned[p])
                high, low = split(value)
                high_ref[c, to, out * 128 : (out + 1) * 128] = high
                low_ref[c, to, out * 128 : (out + 1) * 128] = low
        return carry

    lax.fori_loop(0, rows // tile, gather_rows, 0)


def inverse_columns_body(sends, blocks_ref, coarse_hbm_ref, fine_hbm_ref, *refs):
    edge_ref, edge_sems, coarse_ref, fine_ref, factor_sems = refs[-5:]
    refs = refs[:-5]
    out_ref, head_ref, tail_ref = refs[:3]
    tab_ref, in_ref, stage_ref, high_ref, low_ref, in_sems, out_sems, send_sems = refs[-8:]
    planes, rows, width = stage_ref.shape
    small = copy_all([(coarse_hbm_ref, coarse_ref), (fine_hbm_ref, fine_ref)], factor_sems)
    fetch_blocks(blocks_ref, in_ref, in_sems)
    fill_tables(small, coarse_ref, fine_ref, tab_ref)
    gather_blocks(blocks_ref, in_ref, in_sems, high_ref, low_ref)
    half = planes // 2

    def finish(z, carry):
        value = stage_ref[z]
        soft = jnp.maximum(value, 0.0) + jnp.log1p(jnp.exp(-jnp.abs(value)))
        stage_ref[z] = density_floor + density_scale * soft
        pltpu.make_async_copy(stage_ref.at[z], out_ref.at[z], out_sems.at[z]).start()
        return carry

    def step(m, carry):
        at = pl.ds(pl.multiple_of(m * half * rows, half * rows), half * rows)
        field = triple(dot_nn, high_ref[0, at], low_ref[0, at], tab_ref[0], tab_ref[1])
        field = field - triple(dot_nn, high_ref[1, at], low_ref[1, at], tab_ref[2], tab_ref[3])
        stage_ref[pl.ds(m * half, half)] = field.reshape(half, rows, width)
        lax.fori_loop(m * half, (m + 1) * half, finish, 0)
        return carry

    lax.fori_loop(0, 2, step, 0)
    leaving = [
        pltpu.make_async_copy(stage_ref.at[z], out_ref.at[z], out_sems.at[z]) for z in range(planes)
    ]
    for m in range(2 if sends else 0):
        first = m * (planes - reach)
        pairs = [(stage_ref.at[first + z], refs[3 + m].at[pl.ds(z * rows, rows)]) for z in range(reach)]
        leaving += copy_all(pairs, send_sems.at[m])
    for z in range(planes):
        at = slice(reach * z, reach * (z + 1))
        edge_ref[0, at] = stage_ref[z, :reach]
        edge_ref[1, at] = stage_ref[z, rows - reach :]
    leaving += copy_all([(edge_ref.at[0], head_ref), (edge_ref.at[1], tail_ref)], edge_sems)
    wait_all(leaving)


def inverse_columns(blocks, factors, sends):
    parts, _, rows, _ = blocks.shape
    lanes = blocks.shape[1] * blocks.shape[3]
    width = factors[0].shape[2]
    planes = lanes * parts // (2 * width)
    side = (reach * planes, width)
    slabs = 2 if sends else 0
    scratch = [
        pltpu.VMEM((4, width, width), bf16),
        pltpu.VMEM(blocks.shape, f32),
        pltpu.VMEM((planes, rows, width), f32),
        pltpu.VMEM((2, planes * rows, width), bf16),
        pltpu.VMEM((2, planes * rows, width), bf16),
        pltpu.SemaphoreType.DMA((rows // gather_tile, 4)),
        pltpu.SemaphoreType.DMA((planes,)),
        pltpu.SemaphoreType.DMA((2, reach)),
    ]
    edges = [pltpu.VMEM((2, *side), f32), pltpu.SemaphoreType.DMA((2,))]
    return call(
        lambda *refs: inverse_columns_body(sends, *refs),
        [array(planes, rows, width), array(*side), array(*side)]
        + [array(slab_rows(rows), width)] * slabs,
        7.0,
        grid=(1,),
        in_specs=[in_hbm] * 3,
        out_specs=[in_hbm] * (3 + slabs),
        scratch_shapes=scratch + edges + factor_scratch(factors),
        name="inverse_columns",
    )(blocks, *factors)


def shift(value, axis, up, ring):
    count = lax.axis_size(axis)
    pairs = [(i, (i + 1) % count) for i in range(count if ring else count - 1)]
    return lax.ppermute(value, axis, pairs if up else [(b, a) for a, b in pairs])


def slab_rows(rows):
    return reach * rows + -(-2 * reach * reach // 8) * 8


def halo_body(head_ref, tail_ref, low_ref, high_ref, down_ref, up_ref, edge_ref, sems):
    side = reach * reach
    held = head_ref.shape[0]
    copies = []
    for i, (first, out_ref) in enumerate(((0, down_ref), (held - side, up_ref))):
        edge_ref[i, :side] = head_ref[first : first + side]
        edge_ref[i, side : 2 * side] = tail_ref[first : first + side]
        count = edge_ref.shape[1]
        to = out_ref.at[pl.ds(out_ref.shape[0] - count, count)]
        copies += copy_all([(edge_ref.at[i], to)], sems.at[i])
    wait_all(copies)


def halo_slabs(low, high, head, tail):
    total, width = low.shape
    count = -(-2 * reach * reach // 8) * 8
    return call(
        halo_body,
        [array(total, width)] * 2,
        1.0,
        grid=(1,),
        in_specs=[whole(head.shape), whole(tail.shape), in_hbm, in_hbm],
        out_specs=[in_hbm] * 2,
        scratch_shapes=[pltpu.VMEM((2, count, width), f32), pltpu.SemaphoreType.DMA((2, 1))],
        input_output_aliases={2: 0, 3: 1},
        name="halo_slabs",
    )(head, tail, low, high)


def roll_x(value, by):
    return pltpu.roll(value, by % value.shape[-1], value.ndim - 1)


def energy_slopes(rho, sigma):
    two_a = 2.0 * correlation_scale
    b1, b2, b3, b4 = [two_a * term for term in correlation_terms]
    ratio = beta_value / gamma_value
    exchange = -0.75 * (3.0 / math.pi) ** (1.0 / 3.0)
    s_scale = 0.25 / (3.0 * math.pi**2) ** (2.0 / 3.0)
    t_scale = math.pi / (16.0 * (3.0 * math.pi**2) ** (1.0 / 3.0))
    radius_scale = (3.0 / (4.0 * math.pi)) ** (1.0 / 3.0)
    sixth = jnp.exp(jnp.log(rho) * (-1.0 / 6.0))
    inv = sixth * sixth
    inv2 = inv * inv
    inv4 = inv2 * inv2
    scaled_sigma = sigma * inv4
    stretch = 1.0 + (mu_value / kappa_value * s_scale) * scaled_sigma * inv4
    v = (ratio * t_scale) * scaled_sigma * (inv2 * inv)
    root = math.sqrt(radius_scale) * sixth
    denom = root * (b1 + root * (b2 + root * (b3 + root * b4)))
    denom_slope = root * (0.5 * b1 + root * (b2 + root * (1.5 * b3 + root * (2.0 * b4))))
    pair = denom * denom + denom
    recip = 1.0 / (stretch * pair)
    weight = recip * pair
    recip = recip * stretch
    x_rho = (rho * inv2) * (
        exchange * (4.0 / 3.0) * (1.0 + kappa_value)
        + weight
        * ((-4.0 * exchange * kappa_value) + (8.0 / 3.0 * exchange * kappa_value) * weight)
    )
    radius_part = (two_a * correlation_alpha * radius_scale) * inv
    linear = two_a + radius_part
    log_term = jnp.log(1.0 + (recip * denom + recip))
    uniform = -linear * log_term
    rho_uniform = (1.0 / 3.0) * (radius_part * log_term - linear * (recip * denom_slope))
    grown = jnp.exp(uniform * (-1.0 / gamma_value))
    x = grown - 1.0
    vx = v * x
    v2 = v * v
    lower = x * x + (vx + v2)
    upper = lower + vx * (x + v)
    both = 1.0 / (lower * upper)
    gradient = gamma_value * jnp.log(upper * (upper * both))
    h_part = (x + 2.0 * v) * (x * x) * (x * both)
    h_uniform = (v2 * both) * (v * (2.0 * x + v)) * grown
    d_rho = (
        (x_rho + uniform)
        + (gradient + rho_uniform * (1.0 - h_uniform))
        - (7.0 / 3.0 * gamma_value) * (v * h_part)
    )
    two_d_sigma = inv4 * (
        (2.0 * exchange * s_scale * mu_value) * (weight * weight)
        + (2.0 * t_scale * beta_value) * h_part
    )
    return d_rho, two_d_sigma


def potential_body(sources, groups, flag_ref, *refs):
    ext_ref, part_ref, smooth_ref, flat_ref, fx_ref, fy_ref, fz_ref = refs[-7:]
    count = 6 if groups == 2 else 4
    plane_refs = refs[: -count - 17]
    sides_hbm = plane_refs[-count:]
    tab_hbm_ref, out_ref, tab_ref, tab_sems, pot_ref, tall_ref, stage_ref = refs[-count - 17 : -count - 10]
    in_sems, out_sems, side_sems = refs[-count - 10 : -count - 7]
    side_refs = refs[-count - 7 : -7]
    planes, rows, width = pot_ref.shape
    each = planes // groups
    sides = copy_all(
        [
            (hbm.at[pl.ds(hbm.shape[0] - ref.shape[0], ref.shape[0])], ref)
            for hbm, ref in zip(sides_hbm, side_refs)
        ],
        side_sems,
    )

    def plane_of(plane, at):
        ref = plane_refs[plane]
        return ref.at[at] if len(ref.shape) == 3 else ref.at[pl.ds(at * rows, rows)]

    arriving = copy_all(
        [
            (plane_of(plane, at), ext_ref.at[z, pl.ds(lead - 1, rows)])
            for z, (plane, at, *_) in enumerate(sources)
        ],
        in_sems,
    )
    slope = 1.0 / (2.0 * grid_step)
    tiles = rows // 8 + 1

    def at_end(flag):
        return pl.when(flag_ref[flag] == 1) if groups == 2 else lambda body: None

    wait_all(sides)
    for z, (_, _, head, head_row, tail, tail_row) in enumerate(sources):
        ext_ref[z, lead - 1 - reach : lead - 1] = side_refs[head][head_row : head_row + reach]
        after = side_refs[tail][tail_row : tail_row + reach]
        ext_ref[z, lead - 1 + rows : lead - 1 + rows + reach] = after
    wait_all(arriving)
    tables = load_tables(tab_hbm_ref, tab_ref, tab_sems)

    def widened(z, size, margin):
        return z + margin * (z // size) if groups > 1 else z

    @at_end(0)
    def _():
        ext_ref[reach - 1] = ext_ref[reach]

    @at_end(1)
    def _():
        ext_ref[ext_ref.shape[0] - reach] = ext_ref[ext_ref.shape[0] - reach - 1]

    def filter_depth(z, carry):
        w = widened(z, each + 4, 2)
        part_ref[z] = 0.25 * (ext_ref[w] + ext_ref[w + 2]) + 0.5 * ext_ref[w + 1]
        return carry

    lax.fori_loop(0, part_ref.shape[0], filter_depth, 0)

    def filter_plane(z, carry):
        for t in range(tiles):
            r = lead - 2 + 8 * t
            along_y = 0.25 * (part_ref[z, r - 2 : r + 6] + part_ref[z, r : r + 8]) + 0.5 * (
                part_ref[z, r - 1 : r + 7]
            )
            smooth_ref[z, r : r + 8] = (
                0.25 * (roll_x(along_y, 1) + roll_x(along_y, -1)) + 0.5 * along_y
            )
        return carry

    lax.fori_loop(0, part_ref.shape[0], filter_plane, 0)

    @at_end(0)
    def _():
        smooth_ref[1] = smooth_ref[2]

    @at_end(1)
    def _():
        smooth_ref[smooth_ref.shape[0] - 2] = smooth_ref[smooth_ref.shape[0] - 3]

    def local_terms(z, carry):
        w = widened(z, each + 2, 2)
        for t in range(tiles):
            r = lead - 1 + 8 * t
            center = smooth_ref[w + 1, r : r + 8]
            gx = (roll_x(center, -1) - roll_x(center, 1)) * slope
            gy = (smooth_ref[w + 1, r + 1 : r + 9] - smooth_ref[w + 1, r - 1 : r + 7]) * slope
            gz = (smooth_ref[w + 2, r : r + 8] - smooth_ref[w, r : r + 8]) * slope
            d_rho, two_d_sigma = energy_slopes(center, gx * gx + gy * gy + gz * gz)
            flat_ref[z, r : r + 8] = d_rho
            fx_ref[z, r : r + 8] = two_d_sigma * gx
            fy_ref[z, r : r + 8] = two_d_sigma * gy
            fz_ref[z, r : r + 8] = two_d_sigma * gz
        return carry

    lax.fori_loop(0, flat_ref.shape[0], local_terms, 0)

    @at_end(0)
    def _():
        fz_ref[0] = fz_ref[1]

    @at_end(1)
    def _():
        fz_ref[fz_ref.shape[0] - 1] = fz_ref[fz_ref.shape[0] - 2]

    def collect(z, carry):
        w = widened(z, each, 2)
        for t in range(rows // 8):
            r = lead + 8 * t
            here = slice(r, r + 8)
            fx = fx_ref[w + 1, here]
            along_x = (roll_x(fx, -1) - roll_x(fx, 1)) * slope
            along_y = (fy_ref[w + 1, r + 1 : r + 9] - fy_ref[w + 1, r - 1 : r + 7]) * slope
            along_z = (fz_ref[w + 2, here] - fz_ref[w, here]) * slope
            pot_ref[z, 8 * t : 8 * t + 8] = flat_ref[w + 1, here] - (along_x + along_y + along_z)
        return carry

    lax.fori_loop(0, planes, collect, 0)
    wait_all(tables)
    forward_columns(pot_ref, tab_ref, tall_ref, stage_ref, out_ref, out_sems)


def forward_columns(x_ref, tab_ref, tall_ref, stage_ref, out_ref, out_sems):
    planes, rows, width = x_ref.shape
    high, low = split(x_ref[...].reshape(planes * rows, width).T)
    for k, value in enumerate((high, high, low)):
        tall_ref[k * width : (k + 1) * width] = value
    parts, block, out_lanes = stage_ref.shape
    group = parts // 2

    def step(m, carry):
        at = pl.ds(pl.multiple_of(m * group * block, group * block), group * block)
        ch, sh = tab_ref[0, at], tab_ref[2, at]
        real = dot_nn(jnp.concatenate([ch, tab_ref[1, at], ch], axis=1), tall_ref[...])
        imag = dot_nn(jnp.concatenate([sh, tab_ref[3, at], sh], axis=1), tall_ref[...])
        both = jnp.concatenate([real, -imag], axis=1)
        stage_ref[pl.ds(m * group, group)] = both.reshape(group, block, out_lanes)
        send_group(stage_ref, out_ref, out_sems, m, group)
        return carry

    lax.fori_loop(0, 2, step, 0)
    for m in range(2):
        wait_all(group_copies(stage_ref, out_ref, out_sems, m, group))


def potential_of(flags, planes, sides, sources, groups, tables, parts):
    rows, width = planes[0].shape[1:]
    tall = -(-(rows + lead + 8) // 8) * 8
    count = len(sources) - 2 * reach * groups
    lanes = count * rows
    out = (parts, width // parts, 2 * lanes)
    scratch = table_scratch(width) + [
        pltpu.VMEM((count, rows, width), f32),
        pltpu.VMEM((3 * width, lanes), bf16),
        pltpu.VMEM(out, f32),
        pltpu.SemaphoreType.DMA((len(sources),)),
        pltpu.SemaphoreType.DMA((2, parts // 2)),
        pltpu.SemaphoreType.DMA((len(sides),)),
    ]
    scratch += [pltpu.VMEM((min(side.shape[0], sides[0].shape[0]), width), f32) for side in sides]
    for margin in (6, 4, 4, 2, 2, 2, 2):
        scratch.append(pltpu.VMEM((count + margin * groups, tall, width), f32))
    return call(
        lambda *refs: potential_body(sources, groups, *refs),
        array(*out),
        20.0,
        grid=(1,),
        in_specs=[pl.BlockSpec(memory_space=pltpu.SMEM)]
        + [in_hbm] * len(planes)
        + [pl.BlockSpec(memory_space=pl.ANY)] * len(sides)
        + [in_hbm],
        out_specs=in_hbm,
        scratch_shapes=scratch,
        name="potential",
    )(flags, *planes, *sides, tables)


def forward_rows_body(starts, flag_ref, blocks_ref, coarse_hbm_ref, fine_hbm_ref, *refs):
    coarse_ref, fine_ref, factor_sems = refs[-3:]
    out_ref, tab_ref, in_ref, stage_ref, high_ref, low_ref, in_sems, out_sems = refs[-11:-3]
    _, planes, rows, width = stage_ref.shape
    small = copy_all([(coarse_hbm_ref, coarse_ref), (fine_hbm_ref, fine_ref)], factor_sems)
    fetch_blocks(blocks_ref, in_ref, in_sems)
    fill_tables(small, coarse_ref, fine_ref, tab_ref)
    gather_blocks(blocks_ref, in_ref, in_sems, high_ref, low_ref)
    high_ref[2], low_ref[2] = -high_ref[0], -low_ref[0]

    half = planes // 2

    def copies(c, m):
        to = starts[0] + m * (starts[1] - starts[0])
        return [
            pltpu.make_async_copy(stage_ref.at[c, z], out_ref.at[c, to + y], out_sems.at[c, z])
            for y, z in enumerate([m * half + y for y in range(half)])
        ]

    def step(i, carry):
        c, m = i // 2, i % 2
        at = pl.ds(pl.multiple_of(m * half * rows, half * rows), half * rows)
        value = triple(dot_nn, high_ref[c, at], low_ref[c, at], tab_ref[0], tab_ref[1])
        value = value + triple(dot_nn, high_ref[c + 1, at], low_ref[c + 1, at], tab_ref[2], tab_ref[3])
        stage_ref[c, pl.ds(m * half, half)] = value.reshape(half, rows, width)

        @pl.when(flag_ref[2] == 1)
        def _():
            tile = (8, 128)
            at_zero = (lax.broadcasted_iota(jnp.int32, tile, 0) == 0) & (
                lax.broadcasted_iota(jnp.int32, tile, 1) == 0
            )
            for y in range(half):
                z = m * half + y
                stage_ref[c, z, :8, :128] = jnp.where(at_zero, 0.0, stage_ref[c, z, :8, :128])

        for copy in copies(c, m):
            copy.start()
        return carry

    lax.fori_loop(0, 4, step, 0)
    for c in range(2):
        wait_all(copies(c, 0) + copies(c, 1))


def forward_rows(flags, blocks, factors, starts, depth, before):
    parts, rows, lanes = blocks.shape
    width = factors[0].shape[2]
    planes = lanes * parts // (2 * width)
    earlier = [] if before is None else [before]
    scratch = [
        pltpu.VMEM((4, width, width), bf16),
        pltpu.VMEM(blocks.shape, f32),
        pltpu.VMEM((2, planes, rows, width), f32),
        pltpu.VMEM((3, planes * rows, width), bf16),
        pltpu.VMEM((3, planes * rows, width), bf16),
        pltpu.SemaphoreType.DMA((rows // gather_tile, 4)),
        pltpu.SemaphoreType.DMA((2, planes)),
    ]
    return call(
        lambda *refs: forward_rows_body(starts, *refs),
        array(2, depth, rows, width),
        10.0,
        grid=(1,),
        in_specs=[pl.BlockSpec(memory_space=pltpu.SMEM)] + [in_hbm] * (3 + len(earlier)),
        out_specs=in_hbm,
        scratch_shapes=scratch + factor_scratch(factors),
        input_output_aliases={4: 0} if earlier else {},
        name="forward_rows",
    )(flags, blocks, *factors, *earlier)


def exchange(value):
    return lax.all_to_all(value, "py", 0, 0, tiled=True)


def on_device(rho_hat):
    parts = lax.axis_size("py")
    place_z, place_y = lax.axis_index("px"), lax.axis_index("py")
    flags = jnp.stack(
        [place_z == 0, place_z == lax.axis_size("px") - 1, place_y == 0]
    ).astype(jnp.int32)
    depth, width = rho_hat.shape[1], rho_hat.shape[3]
    unit = depth // 4
    block = width // parts
    factors = phase_factors(width, block, width)
    half_factors = phase_factors(width // 2, block, width)

    outer = exchange(inverse_rows(rho_hat, half_factors, None, None, (0, 3)))
    inner, tables = inverse_rows(rho_hat, half_factors, factors, flags, (1, 2))
    inner = exchange(inner)
    outer, head, tail, low_planes, high_planes = inverse_columns(outer, factors, True)
    outer_sides = shift(tail, "py", True, True), shift(head, "py", False, True)
    inner, head, tail = inverse_columns(inner, factors, False)
    inner_sides = shift(tail, "py", True, True), shift(head, "py", False, True)

    down, up = halo_slabs(low_planes, high_planes, *outer_sides)
    down, up, _ = lax.optimization_barrier((down, up, head))
    below, above = shift(up, "px", True, False), shift(down, "px", False, False)

    def source(z):
        if unit <= z < depth - unit:
            row = reach * (z - unit)
            return 1, z - unit, 2, row, 3, row
        if 0 <= z < depth:
            at = z if z < unit else z - depth + 2 * unit
            return 0, at, 0, reach * at, 1, reach * at
        at = z + reach if z < 0 else z - depth
        side = 2 if z < 0 else 3
        return side, at, side + 2, reach * at, side + 2, reach * (reach + at)

    inside = [source(z) for z in range(unit - reach, depth - unit + reach)]
    outside = [source(z) for z in range(-reach, unit + reach)]
    outside += [source(z) for z in range(depth - unit - reach, depth + reach)]
    planes, sides = [outer, inner], [*outer_sides, *inner_sides]
    inner_waves = exchange(potential_of(flags, planes, sides, inside, 1, tables, parts))
    halo = [below, above]
    spectral = potential_of(flags, planes + halo, sides + halo, outside, 2, tables, parts)
    outer_waves = exchange(spectral)
    result = forward_rows(flags, inner_waves, factors, (unit, 2 * unit), depth, None)
    result = forward_rows(flags, outer_waves, factors, (0, depth - unit), depth, result)
    return result


def solution(mesh):
    return jax.shard_map(
        on_device,
        mesh=mesh,
        in_specs=(P(None, "px", "py", None),),
        out_specs=P(None, "px", "py", None),
        check_vma=False,
    )
```

```python
import math

import jax
import jax.numpy as jnp
import numpy as np
from jax import lax
from jax.experimental import pallas as pl
from jax.experimental.pallas import tpu as pltpu
from jax.sharding import PartitionSpec as P

grid_step = 0.25
density_floor = 0.02
density_scale = 0.2
kappa_value = 0.804
mu_value = 0.2195149727645171
beta_value = 0.06672455060314922
gamma_value = (1.0 - math.log(2.0)) / (math.pi * math.pi)
correlation_scale = 0.031091
correlation_alpha = 0.2137
correlation_terms = (7.5957, 3.5876, 1.6382, 0.49294)

f32 = jnp.float32
bf16 = jnp.bfloat16
reach = 3
gather_tile = 16
lead = 9


in_hbm = pl.BlockSpec(memory_space=pltpu.HBM)


def call(body, out, cost, **options):
    estimate = pl.CostEstimate(flops=int(cost * 1e9), bytes_accessed=1 << 20, transcendentals=0)
    limit = pltpu.CompilerParams(vmem_limit_bytes=62 << 20)
    return pl.pallas_call(body, out_shape=out, compiler_params=limit, cost_estimate=estimate, **options)


def array(*shape):
    return jax.ShapeDtypeStruct(shape, f32)


def whole(shape):
    return pl.BlockSpec(shape, lambda *_: (0,) * len(shape))


def copy_all(pairs, sems):
    copies = [pltpu.make_async_copy(a, b, sems.at[i]) for i, (a, b) in enumerate(pairs)]
    for copy in copies:
        copy.start()
    return copies


def wait_all(copies):
    for copy in copies:
        copy.wait()


def group_copies(stage_ref, out_ref, sems, m, group):
    to = [m * group + g for g in range(group)]
    return [
        pltpu.make_async_copy(stage_ref.at[d], out_ref.at[d], sems.at[m, g])
        for g, d in enumerate(to)
    ]


def send_group(*args):
    for copy in group_copies(*args):
        copy.start()


def load_tables(hbm_ref, tab_ref, sems):
    return copy_all([(hbm_ref.at[i], tab_ref.at[i]) for i in range(4)], sems)


def table_scratch(width):
    return [pltpu.VMEM((4, width, width), bf16), pltpu.SemaphoreType.DMA((4,))]


def split(value):
    high = value.astype(bf16)
    return high, (value - high.astype(f32)).astype(bf16)


def dot_nt(left, right):
    return lax.dot_general(left, right, (((1,), (1,)), ((), ())), preferred_element_type=f32)


def dot_nn(left, right):
    return lax.dot_general(left, right, (((1,), (0,)), ((), ())), preferred_element_type=f32)


def triple(dot, left_high, left_low, right_high, right_low):
    return dot(left_high, right_high) + (dot(left_low, right_high) + dot(left_high, right_low))


def fill_tables(arriving, coarse_ref, fine_ref, tab_ref):
    wait_all(arriving)
    stride = fine_ref.shape[1]

    def step(a, carry):
        cos_a, sin_a = coarse_ref[0, pl.ds(a, 1)], coarse_ref[1, pl.ds(a, 1)]
        fine_cos, fine_sin = fine_ref[0], fine_ref[1]
        rows = pl.ds(pl.multiple_of(a * stride, stride), stride)
        tab_ref[0, rows], tab_ref[1, rows] = split(cos_a * fine_cos - sin_a * fine_sin)
        tab_ref[2, rows], tab_ref[3, rows] = split(sin_a * fine_cos + cos_a * fine_sin)
        return carry

    lax.fori_loop(0, tab_ref.shape[1] // 4 // stride, step, 0)

    tile = 16
    width = tab_ref.shape[2]
    quarter = width // 4
    turn = lax.broadcasted_iota(jnp.int32, (tile, width), 1) % 4
    turn_cos = jnp.where(turn == 0, 1.0, jnp.where(turn == 2, -1.0, 0.0)).astype(bf16)
    turn_sin = jnp.where(turn == 1, 1.0, jnp.where(turn == 3, -1.0, 0.0)).astype(bf16)
    flip = jnp.where(turn % 2 == 0, 1.0, -1.0).astype(bf16)

    def spread(t, carry):
        for part in range(2):
            rows = [pl.ds(pl.multiple_of(q * quarter + t * tile, tile), tile) for q in range(4)]
            cos, sin = tab_ref[part, rows[0]], tab_ref[2 + part, rows[0]]
            next_cos = cos * turn_cos - sin * turn_sin
            next_sin = sin * turn_cos + cos * turn_sin
            tab_ref[part, rows[1]], tab_ref[2 + part, rows[1]] = next_cos, next_sin
            tab_ref[part, rows[2]], tab_ref[2 + part, rows[2]] = cos * flip, sin * flip
            tab_ref[part, rows[3]], tab_ref[2 + part, rows[3]] = next_cos * flip, next_sin * flip
        return carry

    lax.fori_loop(0, quarter // tile, spread, 0)


def factor_scratch(factors):
    return [pltpu.VMEM(factor.shape, f32) for factor in factors] + [pltpu.SemaphoreType.DMA((2,))]


def phase_factors(length, stride, norm):
    def waves(rows, scale, period):
        angle = (np.outer(rows, np.arange(length)) % period) * (2.0 * math.pi / period)
        return np.stack([np.cos(angle), np.sin(angle)]).astype(np.float32) * np.float32(scale)

    coarse = waves(np.arange(0, length // 4, stride), 1.0, length)
    coarse = np.concatenate([coarse, waves(np.array([1, stride - 1]), 1.0, 2 * length)], axis=1)
    fine = waves(np.arange(stride), 1.0 / math.sqrt(norm), length)
    return jnp.asarray(coarse), jnp.asarray(fine)


def inverse_rows_body(blocks, makes, *refs):
    rho_ref, coarse_hbm_ref, fine_hbm_ref = refs[:3]
    if makes:
        factors_hbm, out_ref, tab_out_ref = refs[3:5], refs[6], refs[7]
        full_ref, full_coarse_ref, full_fine_ref, full_factor_sems, full_sems = refs[-5:]
        refs = refs[:-5]
    else:
        out_ref = refs[3]
    tab_ref, x_ref, wide_ref, stage_ref, in_sems, out_sems, coarse_ref, fine_ref, factor_sems = refs[-9:]
    half = tab_ref.shape[1]
    lanes = wide_ref.shape[2] // 2
    unit = x_ref.shape[1] // len(blocks)
    small = copy_all([(coarse_hbm_ref, coarse_ref), (fine_hbm_ref, fine_ref)], factor_sems)
    arriving = [
        copy_all(
            [
                (rho_ref.at[c, pl.ds(b * unit, unit)], x_ref.at[c, pl.ds(i * unit, unit)])
                for i, b in enumerate(blocks)
            ],
            in_sems.at[c],
        )
        for c in range(2)
    ]
    fill_tables(small, coarse_ref, fine_ref, tab_ref)
    for c in range(2):
        wait_all(arriving[c])
    real, imag = [x_ref[c].reshape(lanes, 2 * half) for c in range(2)]
    first = coarse_ref.shape[1] - 2
    wave_cos, wave_sin = [coarse_ref[i, first : first + 1] for i in range(2)]
    for p in range(2):
        if p == 0:
            values = real[:, :half] + real[:, half:], imag[:, :half] + imag[:, half:]
        else:
            odd_re, odd_im = real[:, :half] - real[:, half:], imag[:, :half] - imag[:, half:]
            values = odd_re * wave_cos - odd_im * wave_sin, odd_re * wave_sin + odd_im * wave_cos
        for c in range(2):
            high, low = split(values[c].T)
            cos_at = slice(c * lanes, (c + 1) * lanes)
            sin_at = slice((1 - c) * lanes, (2 - c) * lanes)
            for k, value in enumerate((high, high, low)):
                wide_ref[p, k * half : (k + 1) * half, cos_at] = value
                turned = value if c == 0 else -value
                wide_ref[p, (k + 3) * half : (k + 4) * half, sin_at] = turned
    parts, _, block, _ = stage_ref.shape
    out_lanes = 2 * lanes
    group = parts // 2
    count = half // 2

    def step(m, carry):
        at = pl.ds(pl.multiple_of(m * count, count), count)
        ch, sh = tab_ref[0, at], tab_ref[2, at]
        left = jnp.concatenate([ch, tab_ref[1, at], ch, sh, tab_ref[3, at], sh], axis=1)
        for p in range(2):
            product = dot_nn(left, wide_ref[p]).reshape(group, block // 2, out_lanes)
            for g in range(group):
                for i in range(out_lanes // 128):
                    to = pl.ds(p, block // 2, stride=2)
                    stage_ref[m * group + g, i, to, :] = product[g, :, i * 128 : (i + 1) * 128]
        send_group(stage_ref, out_ref, out_sems, m, group)
        return carry

    lax.fori_loop(0, 2, step, 0)
    if makes:
        pairs = zip(factors_hbm, (full_coarse_ref, full_fine_ref))
        small = copy_all(list(pairs), full_factor_sems)
        fill_tables(small, full_coarse_ref, full_fine_ref, full_ref)
        wait_all(copy_all([(full_ref.at[i], tab_out_ref.at[i]) for i in range(4)], full_sems))
    for m in range(2):
        wait_all(group_copies(stage_ref, out_ref, out_sems, m, group))


def inverse_rows(rho_hat, factors, full, flags, blocks):
    _, depth, local, width = rho_hat.shape
    half = factors[1].shape[2]
    block = factors[1].shape[1]
    parts = width // block
    unit = depth // 4
    planes = len(blocks) * unit
    lanes = planes * local
    out = (parts, 2 * lanes // 128, block, 128)
    scratch = [
        pltpu.VMEM((4, half, half), bf16),
        pltpu.VMEM((2, planes, local, width), f32),
        pltpu.VMEM((2, 6 * half, 2 * lanes), bf16),
        pltpu.VMEM(out, f32),
        pltpu.SemaphoreType.DMA((2, len(blocks))),
        pltpu.SemaphoreType.DMA((2, parts // 2)),
    ] + factor_scratch(factors)
    makes = full is not None
    body = lambda *refs: inverse_rows_body(blocks, makes, *refs)
    if makes:
        scratch += [pltpu.VMEM((4, width, width), bf16)] + factor_scratch(full)
        return call(
            body,
            [array(*out), jax.ShapeDtypeStruct((4, width, width), bf16)],
            10.0,
            grid=(1,),
            in_specs=[in_hbm] * 5 + [pl.BlockSpec(memory_space=pltpu.SMEM)],
            out_specs=[in_hbm] * 2,
            scratch_shapes=scratch + [pltpu.SemaphoreType.DMA((4,))],
            name="inverse_rows",
        )(rho_hat, *factors, *full, flags)
    return call(
        body,
        array(*out),
        10.0,
        grid=(1,),
        in_specs=[in_hbm] * 3,
        out_specs=in_hbm,
        scratch_shapes=scratch,
        name="inverse_rows",
    )(rho_hat, *factors)


def tile_copies(hbm_ref, in_ref, sems, t):
    group = in_ref.shape[0] // 4
    at = pl.ds(t * gather_tile, gather_tile)
    if not isinstance(t, int):
        at = pl.ds(pl.multiple_of(t * gather_tile, gather_tile), gather_tile)
    blocks = [pl.ds(g * group, group) for g in range(4)]
    return [
        pltpu.make_async_copy(hbm_ref.at[d, :, at], in_ref.at[d, :, at], sems.at[t, g])
        if len(in_ref.shape) == 4
        else pltpu.make_async_copy(hbm_ref.at[d, at], in_ref.at[d, at], sems.at[t, g])
        for g, d in enumerate(blocks)
    ]


def fetch_blocks(hbm_ref, in_ref, sems):
    for t in range(in_ref.shape[-2] // gather_tile):
        for copy in tile_copies(hbm_ref, in_ref, sems, t):
            copy.start()


def gather_blocks(hbm_ref, in_ref, sems, high_ref, low_ref, ways):
    parts, rows = in_ref.shape[0], in_ref.shape[-2]
    width = high_ref.shape[2]
    local = width // parts
    planes = high_ref.shape[1] // rows
    tile = gather_tile

    def load(p, at, block):
        if len(in_ref.shape) == 4:
            return in_ref[p, block, at]
        return in_ref[p, at, block * 128 : (block + 1) * 128]

    def gather_rows(t, carry):
        wait_all(tile_copies(hbm_ref, in_ref, sems, t))
        at = pl.ds(pl.multiple_of(t * tile, tile), tile)
        lane = lax.broadcasted_iota(jnp.int32, (tile, 128), 1)
        for piece in range(2 * planes):
            c, z = piece // planes, piece % planes
            first = piece * local
            block, offset = first // 128, first % 128
            turned = []
            for p in range(parts):
                value = load(p, at, block)
                if offset + local > 128:
                    after = load(p, at, block + 1)
                    value = jnp.where(lane < offset, after, value)
                turned.append(pltpu.roll(value, (p * (local // ways) - offset) % 128, 1))
            to = pl.ds(pl.multiple_of(z * rows + t * tile, tile), tile)
            for out in range(width // 128):
                way, within = out * ways // (width // 128), out % (width // 128 // ways)
                short = local // ways
                start = within * 128 // short
                value = turned[(start - way) % parts]
                for p in range(start + 1, parts):
                    edge = p * short - within * 128
                    if edge < 128:
                        value = jnp.where(lane < edge, value, turned[(p - way) % parts])
                high, low = split(value)
                high_ref[c, to, out * 128 : (out + 1) * 128] = high
                low_ref[c, to, out * 128 : (out + 1) * 128] = low
        return carry

    lax.fori_loop(0, rows // tile, gather_rows, 0)


def inverse_columns_body(sends, blocks_ref, coarse_hbm_ref, fine_hbm_ref, *refs):
    edge_ref, edge_sems, coarse_ref, fine_ref, factor_sems = refs[-5:]
    refs = refs[:-5]
    out_ref, head_ref, tail_ref = refs[:3]
    tab_ref, in_ref, stage_ref, high_ref, low_ref, in_sems, out_sems, send_sems = refs[-8:]
    planes, rows, width = stage_ref.shape
    small = copy_all([(coarse_hbm_ref, coarse_ref), (fine_hbm_ref, fine_ref)], factor_sems)
    fetch_blocks(blocks_ref, in_ref, in_sems)
    fill_tables(small, coarse_ref, fine_ref, tab_ref)
    gather_blocks(blocks_ref, in_ref, in_sems, high_ref, low_ref, 1)
    half = planes // 2

    def finish(z, carry):
        value = stage_ref[z]
        soft = jnp.maximum(value, 0.0) + jnp.log1p(jnp.exp(-jnp.abs(value)))
        stage_ref[z] = density_floor + density_scale * soft
        pltpu.make_async_copy(stage_ref.at[z], out_ref.at[z], out_sems.at[z]).start()
        return carry

    def step(m, carry):
        at = pl.ds(pl.multiple_of(m * half * rows, half * rows), half * rows)
        field = triple(dot_nn, high_ref[0, at], low_ref[0, at], tab_ref[0], tab_ref[1])
        field = field - triple(dot_nn, high_ref[1, at], low_ref[1, at], tab_ref[2], tab_ref[3])
        stage_ref[pl.ds(m * half, half)] = field.reshape(half, rows, width)
        lax.fori_loop(m * half, (m + 1) * half, finish, 0)
        return carry

    lax.fori_loop(0, 2, step, 0)
    leaving = [
        pltpu.make_async_copy(stage_ref.at[z], out_ref.at[z], out_sems.at[z]) for z in range(planes)
    ]
    for m in range(2 if sends else 0):
        first = m * (planes - reach)
        pairs = [(stage_ref.at[first + z], refs[3 + m].at[pl.ds(z * rows, rows)]) for z in range(reach)]
        leaving += copy_all(pairs, send_sems.at[m])
    for z in range(planes):
        at = slice(reach * z, reach * (z + 1))
        edge_ref[0, at] = stage_ref[z, :reach]
        edge_ref[1, at] = stage_ref[z, rows - reach :]
    leaving += copy_all([(edge_ref.at[0], head_ref), (edge_ref.at[1], tail_ref)], edge_sems)
    wait_all(leaving)


def inverse_columns(blocks, factors, sends):
    parts, _, rows, _ = blocks.shape
    lanes = blocks.shape[1] * blocks.shape[3]
    width = factors[0].shape[2]
    planes = lanes * parts // (2 * width)
    side = (reach * planes, width)
    slabs = 2 if sends else 0
    scratch = [
        pltpu.VMEM((4, width, width), bf16),
        pltpu.VMEM(blocks.shape, f32),
        pltpu.VMEM((planes, rows, width), f32),
        pltpu.VMEM((2, planes * rows, width), bf16),
        pltpu.VMEM((2, planes * rows, width), bf16),
        pltpu.SemaphoreType.DMA((rows // gather_tile, 4)),
        pltpu.SemaphoreType.DMA((planes,)),
        pltpu.SemaphoreType.DMA((2, reach)),
    ]
    edges = [pltpu.VMEM((2, *side), f32), pltpu.SemaphoreType.DMA((2,))]
    return call(
        lambda *refs: inverse_columns_body(sends, *refs),
        [array(planes, rows, width), array(*side), array(*side)]
        + [array(slab_rows(rows), width)] * slabs,
        7.0,
        grid=(1,),
        in_specs=[in_hbm] * 3,
        out_specs=[in_hbm] * (3 + slabs),
        scratch_shapes=scratch + edges + factor_scratch(factors),
        name="inverse_columns",
    )(blocks, *factors)


def shift(value, axis, up, ring):
    count = lax.axis_size(axis)
    pairs = [(i, (i + 1) % count) for i in range(count if ring else count - 1)]
    return lax.ppermute(value, axis, pairs if up else [(b, a) for a, b in pairs])


def slab_rows(rows):
    return reach * rows + -(-2 * reach * reach // 8) * 8


def halo_body(head_ref, tail_ref, low_ref, high_ref, down_ref, up_ref, edge_ref, sems):
    side = reach * reach
    held = head_ref.shape[0]
    copies = []
    for i, (first, out_ref) in enumerate(((0, down_ref), (held - side, up_ref))):
        edge_ref[i, :side] = head_ref[first : first + side]
        edge_ref[i, side : 2 * side] = tail_ref[first : first + side]
        count = edge_ref.shape[1]
        to = out_ref.at[pl.ds(out_ref.shape[0] - count, count)]
        copies += copy_all([(edge_ref.at[i], to)], sems.at[i])
    wait_all(copies)


def halo_slabs(low, high, head, tail):
    total, width = low.shape
    count = -(-2 * reach * reach // 8) * 8
    return call(
        halo_body,
        [array(total, width)] * 2,
        1.0,
        grid=(1,),
        in_specs=[whole(head.shape), whole(tail.shape), in_hbm, in_hbm],
        out_specs=[in_hbm] * 2,
        scratch_shapes=[pltpu.VMEM((2, count, width), f32), pltpu.SemaphoreType.DMA((2, 1))],
        input_output_aliases={2: 0, 3: 1},
        name="halo_slabs",
    )(head, tail, low, high)


def roll_x(value, by):
    return pltpu.roll(value, by % value.shape[-1], value.ndim - 1)


def energy_slopes(rho, sigma):
    two_a = 2.0 * correlation_scale
    b1, b2, b3, b4 = [two_a * term for term in correlation_terms]
    ratio = beta_value / gamma_value
    exchange = -0.75 * (3.0 / math.pi) ** (1.0 / 3.0)
    s_scale = 0.25 / (3.0 * math.pi**2) ** (2.0 / 3.0)
    t_scale = math.pi / (16.0 * (3.0 * math.pi**2) ** (1.0 / 3.0))
    radius_scale = (3.0 / (4.0 * math.pi)) ** (1.0 / 3.0)
    sixth = jnp.exp(jnp.log(rho) * (-1.0 / 6.0))
    inv = sixth * sixth
    inv2 = inv * inv
    inv4 = inv2 * inv2
    scaled_sigma = sigma * inv4
    stretch = 1.0 + (mu_value / kappa_value * s_scale) * scaled_sigma * inv4
    v = (ratio * t_scale) * scaled_sigma * (inv2 * inv)
    root = math.sqrt(radius_scale) * sixth
    denom = root * (b1 + root * (b2 + root * (b3 + root * b4)))
    denom_slope = root * (0.5 * b1 + root * (b2 + root * (1.5 * b3 + root * (2.0 * b4))))
    pair = denom * denom + denom
    recip = 1.0 / (stretch * pair)
    weight = recip * pair
    recip = recip * stretch
    x_rho = (rho * inv2) * (
        exchange * (4.0 / 3.0) * (1.0 + kappa_value)
        + weight
        * ((-4.0 * exchange * kappa_value) + (8.0 / 3.0 * exchange * kappa_value) * weight)
    )
    radius_part = (two_a * correlation_alpha * radius_scale) * inv
    linear = two_a + radius_part
    log_term = jnp.log(1.0 + (recip * denom + recip))
    uniform = -linear * log_term
    rho_uniform = (1.0 / 3.0) * (radius_part * log_term - linear * (recip * denom_slope))
    grown = jnp.exp(uniform * (-1.0 / gamma_value))
    x = grown - 1.0
    vx = v * x
    v2 = v * v
    lower = x * x + (vx + v2)
    upper = lower + vx * (x + v)
    both = 1.0 / (lower * upper)
    gradient = gamma_value * jnp.log(upper * (upper * both))
    h_part = (x + 2.0 * v) * (x * x) * (x * both)
    h_uniform = (v2 * both) * (v * (2.0 * x + v)) * grown
    d_rho = (
        (x_rho + uniform)
        + (gradient + rho_uniform * (1.0 - h_uniform))
        - (7.0 / 3.0 * gamma_value) * (v * h_part)
    )
    two_d_sigma = inv4 * (
        (2.0 * exchange * s_scale * mu_value) * (weight * weight)
        + (2.0 * t_scale * beta_value) * h_part
    )
    return d_rho, two_d_sigma


def potential_body(sources, groups, flag_ref, *refs):
    ext_ref, part_ref, smooth_ref, flat_ref, fx_ref, fy_ref, fz_ref = refs[-7:]
    count = 6 if groups == 2 else 4
    plane_refs = refs[: -count - 17]
    sides_hbm = plane_refs[-count:]
    tab_hbm_ref, out_ref, tab_ref, tab_sems, pot_ref, tall_ref, stage_ref = refs[-count - 17 : -count - 10]
    in_sems, out_sems, side_sems = refs[-count - 10 : -count - 7]
    side_refs = refs[-count - 7 : -7]
    planes, blocks, rows, _ = pot_ref.shape
    each = planes // groups
    sides = copy_all(
        [
            (hbm.at[pl.ds(hbm.shape[0] - ref.shape[0], ref.shape[0])], ref)
            for hbm, ref in zip(sides_hbm, side_refs)
        ],
        side_sems,
    )

    def plane_of(plane, at):
        ref = plane_refs[plane]
        return ref.at[at] if len(ref.shape) == 3 else ref.at[pl.ds(at * rows, rows)]

    arriving = copy_all(
        [
            (plane_of(plane, at), ext_ref.at[z, pl.ds(lead - 1, rows)])
            for z, (plane, at, *_) in enumerate(sources)
        ],
        in_sems,
    )
    slope = 1.0 / (2.0 * grid_step)
    tiles = rows // 8 + 1

    def at_end(flag):
        return pl.when(flag_ref[flag] == 1) if groups == 2 else lambda body: None

    wait_all(sides)
    for z, (_, _, head, head_row, tail, tail_row) in enumerate(sources):
        ext_ref[z, lead - 1 - reach : lead - 1] = side_refs[head][head_row : head_row + reach]
        after = side_refs[tail][tail_row : tail_row + reach]
        ext_ref[z, lead - 1 + rows : lead - 1 + rows + reach] = after
    wait_all(arriving)
    tables = load_tables(tab_hbm_ref, tab_ref, tab_sems)

    def widened(z, size, margin):
        return z + margin * (z // size) if groups > 1 else z

    @at_end(0)
    def _():
        ext_ref[reach - 1] = ext_ref[reach]

    @at_end(1)
    def _():
        ext_ref[ext_ref.shape[0] - reach] = ext_ref[ext_ref.shape[0] - reach - 1]

    def filter_depth(z, carry):
        w = widened(z, each + 4, 2)
        part_ref[z] = 0.25 * (ext_ref[w] + ext_ref[w + 2]) + 0.5 * ext_ref[w + 1]
        return carry

    lax.fori_loop(0, part_ref.shape[0], filter_depth, 0)

    def filter_plane(z, carry):
        for t in range(tiles):
            r = lead - 2 + 8 * t
            along_y = 0.25 * (part_ref[z, r - 2 : r + 6] + part_ref[z, r : r + 8]) + 0.5 * (
                part_ref[z, r - 1 : r + 7]
            )
            smooth_ref[z, r : r + 8] = (
                0.25 * (roll_x(along_y, 1) + roll_x(along_y, -1)) + 0.5 * along_y
            )
        return carry

    lax.fori_loop(0, part_ref.shape[0], filter_plane, 0)

    @at_end(0)
    def _():
        smooth_ref[1] = smooth_ref[2]

    @at_end(1)
    def _():
        smooth_ref[smooth_ref.shape[0] - 2] = smooth_ref[smooth_ref.shape[0] - 3]

    def local_terms(z, carry):
        w = widened(z, each + 2, 2)
        for t in range(tiles):
            r = lead - 1 + 8 * t
            center = smooth_ref[w + 1, r : r + 8]
            gx = (roll_x(center, -1) - roll_x(center, 1)) * slope
            gy = (smooth_ref[w + 1, r + 1 : r + 9] - smooth_ref[w + 1, r - 1 : r + 7]) * slope
            gz = (smooth_ref[w + 2, r : r + 8] - smooth_ref[w, r : r + 8]) * slope
            d_rho, two_d_sigma = energy_slopes(center, gx * gx + gy * gy + gz * gz)
            flat_ref[z, r : r + 8] = d_rho
            fx_ref[z, r : r + 8] = two_d_sigma * gx
            fy_ref[z, r : r + 8] = two_d_sigma * gy
            fz_ref[z, r : r + 8] = two_d_sigma * gz
        return carry

    lax.fori_loop(0, flat_ref.shape[0], local_terms, 0)

    @at_end(0)
    def _():
        fz_ref[0] = fz_ref[1]

    @at_end(1)
    def _():
        fz_ref[fz_ref.shape[0] - 1] = fz_ref[fz_ref.shape[0] - 2]

    def collect(z, carry):
        w = widened(z, each, 2)
        for t in range(rows // 8):
            r = lead + 8 * t
            here = slice(r, r + 8)
            fx = fx_ref[w + 1, here]
            along_x = (roll_x(fx, -1) - roll_x(fx, 1)) * slope
            along_y = (fy_ref[w + 1, r + 1 : r + 9] - fy_ref[w + 1, r - 1 : r + 7]) * slope
            along_z = (fz_ref[w + 2, here] - fz_ref[w, here]) * slope
            value = flat_ref[w + 1, here] - (along_x + along_y + along_z)
            for i in range(blocks):
                pot_ref[z, i, 8 * t : 8 * t + 8, :] = value[:, i * 128 : (i + 1) * 128]
        return carry

    lax.fori_loop(0, planes, collect, 0)
    wait_all(tables)
    forward_columns(pot_ref, tab_ref, tall_ref, stage_ref, out_ref, out_sems)


def forward_columns(x_ref, tab_ref, tall_ref, stage_ref, out_ref, out_sems):
    planes, blocks, rows, _ = x_ref.shape
    width = blocks * 128
    for i in range(blocks):
        pieces = [
            x_ref[z, i, pl.ds(p, rows // 2, stride=2), :] for z in range(planes) for p in range(2)
        ]
        high, low = split(jnp.concatenate(pieces, axis=0).T)
        for k, value in enumerate((high, high, low)):
            tall_ref[k * width + i * 128 : k * width + (i + 1) * 128] = value
    parts, block, out_lanes = stage_ref.shape
    group = parts // 2

    def step(m, carry):
        at = pl.ds(pl.multiple_of(m * group * block, group * block), group * block)
        ch, sh = tab_ref[0, at], tab_ref[2, at]
        real = dot_nn(jnp.concatenate([ch, tab_ref[1, at], ch], axis=1), tall_ref[...])
        imag = dot_nn(jnp.concatenate([sh, tab_ref[3, at], sh], axis=1), tall_ref[...])
        both = jnp.concatenate([real, -imag], axis=1)
        stage_ref[pl.ds(m * group, group)] = both.reshape(group, block, out_lanes)
        send_group(stage_ref, out_ref, out_sems, m, group)
        return carry

    lax.fori_loop(0, 2, step, 0)
    for m in range(2):
        wait_all(group_copies(stage_ref, out_ref, out_sems, m, group))


def potential_of(flags, planes, sides, sources, groups, tables, parts):
    rows, width = planes[0].shape[1:]
    tall = -(-(rows + lead + 8) // 8) * 8
    count = len(sources) - 2 * reach * groups
    lanes = count * rows
    out = (parts, width // parts, 2 * lanes)
    scratch = table_scratch(width) + [
        pltpu.VMEM((count, width // 128, rows, 128), f32),
        pltpu.VMEM((3 * width, lanes), bf16),
        pltpu.VMEM(out, f32),
        pltpu.SemaphoreType.DMA((len(sources),)),
        pltpu.SemaphoreType.DMA((2, parts // 2)),
        pltpu.SemaphoreType.DMA((len(sides),)),
    ]
    scratch += [pltpu.VMEM((min(side.shape[0], sides[0].shape[0]), width), f32) for side in sides]
    for margin in (6, 4, 4, 2, 2, 2, 2):
        scratch.append(pltpu.VMEM((count + margin * groups, tall, width), f32))
    return call(
        lambda *refs: potential_body(sources, groups, *refs),
        array(*out),
        20.0,
        grid=(1,),
        in_specs=[pl.BlockSpec(memory_space=pltpu.SMEM)]
        + [in_hbm] * len(planes)
        + [pl.BlockSpec(memory_space=pl.ANY)] * len(sides)
        + [in_hbm],
        out_specs=in_hbm,
        scratch_shapes=scratch,
        name="potential",
    )(flags, *planes, *sides, tables)


def forward_rows_body(starts, flag_ref, blocks_ref, coarse_hbm_ref, fine_hbm_ref, *refs):
    coarse_ref, fine_ref, factor_sems = refs[-3:]
    out_ref, tab_ref, wide_ref, in_ref, stage_ref, high_ref, low_ref, in_sems, out_sems = refs[-12:-3]
    _, planes, rows, width = stage_ref.shape
    small = copy_all([(coarse_hbm_ref, coarse_ref), (fine_hbm_ref, fine_ref)], factor_sems)
    fetch_blocks(blocks_ref, in_ref, in_sems)
    fill_tables(small, coarse_ref, fine_ref, tab_ref)
    length = tab_ref.shape[1]
    for k, part in enumerate((0, 0, 1)):
        re_at = slice(k * length, (k + 1) * length)
        im_at = slice((k + 3) * length, (k + 4) * length)
        wide_ref[re_at, :length], wide_ref[re_at, length:] = tab_ref[part], -tab_ref[2 + part]
        wide_ref[im_at, :length], wide_ref[im_at, length:] = tab_ref[2 + part], tab_ref[part]
    gather_blocks(blocks_ref, in_ref, in_sems, high_ref, low_ref, 2)
    last = coarse_ref.shape[1] - 1
    wave_cos, wave_sin = coarse_ref[0, last:], coarse_ref[1, last:]
    half = planes // 2

    def copies(c, m):
        to = starts[0] + m * (starts[1] - starts[0])
        return [
            pltpu.make_async_copy(stage_ref.at[c, z], out_ref.at[c, to + y], out_sems.at[c, z])
            for y, z in enumerate([m * half + y for y in range(half)])
        ]

    def step(m, carry):
        at = pl.ds(pl.multiple_of(m * half * rows, half * rows), half * rows)
        to = pl.ds(m * half, half)

        def product(way):
            lanes = slice(way * length, (way + 1) * length)
            pairs = [(high_ref[c, at, lanes], low_ref[c, at, lanes]) for c in range(2)]
            left = [value for high, low in pairs for value in (high, low, high)]
            both = dot_nn(jnp.concatenate(left, axis=1), wide_ref[...])
            return both[:, :length], both[:, length:]

        even = product(0)
        odd_re, odd_im = product(1)
        odd = odd_re * wave_cos - odd_im * wave_sin, odd_re * wave_sin + odd_im * wave_cos
        for c in range(2):
            shape = (half, rows, length)
            stage_ref[c, to, :, :length] = (even[c] + odd[c]).reshape(shape)
            stage_ref[c, to, :, length:] = (even[c] - odd[c]).reshape(shape)

        @pl.when(flag_ref[2] == 1)
        def _():
            tile = (8, 128)
            at_zero = (lax.broadcasted_iota(jnp.int32, tile, 0) == 0) & (
                lax.broadcasted_iota(jnp.int32, tile, 1) == 0
            )
            for c in range(2):
                for y in range(half):
                    z = m * half + y
                    corner = stage_ref[c, z, :8, :128]
                    stage_ref[c, z, :8, :128] = jnp.where(at_zero, 0.0, corner)

        for copy in copies(0, m) + copies(1, m):
            copy.start()
        return carry

    lax.fori_loop(0, 2, step, 0)
    for c in range(2):
        wait_all(copies(c, 0) + copies(c, 1))


def forward_rows(flags, blocks, factors, starts, depth, before):
    parts, rows, lanes = blocks.shape
    length = factors[0].shape[2]
    width = 2 * length
    planes = lanes * parts // (2 * width)
    earlier = [] if before is None else [before]
    scratch = [
        pltpu.VMEM((4, length, length), bf16),
        pltpu.VMEM((6 * length, width), bf16),
        pltpu.VMEM(blocks.shape, f32),
        pltpu.VMEM((2, planes, rows, width), f32),
        pltpu.VMEM((2, planes * rows, width), bf16),
        pltpu.VMEM((2, planes * rows, width), bf16),
        pltpu.SemaphoreType.DMA((rows // gather_tile, 4)),
        pltpu.SemaphoreType.DMA((2, planes)),
    ]
    return call(
        lambda *refs: forward_rows_body(starts, *refs),
        array(2, depth, rows, width),
        10.0,
        grid=(1,),
        in_specs=[pl.BlockSpec(memory_space=pltpu.SMEM)] + [in_hbm] * (3 + len(earlier)),
        out_specs=in_hbm,
        scratch_shapes=scratch + factor_scratch(factors),
        input_output_aliases={4: 0} if earlier else {},
        name="forward_rows",
    )(flags, blocks, *factors, *earlier)


def exchange(value):
    return lax.all_to_all(value, "py", 0, 0, tiled=True)


def on_device(rho_hat):
    parts = lax.axis_size("py")
    place_z, place_y = lax.axis_index("px"), lax.axis_index("py")
    flags = jnp.stack(
        [place_z == 0, place_z == lax.axis_size("px") - 1, place_y == 0]
    ).astype(jnp.int32)
    depth, width = rho_hat.shape[1], rho_hat.shape[3]
    unit = depth // 4
    block = width // parts
    factors = phase_factors(width, block, width)
    half_factors = phase_factors(width // 2, block, width)

    outer = exchange(inverse_rows(rho_hat, half_factors, None, None, (0, 3)))
    inner, tables = inverse_rows(rho_hat, half_factors, factors, flags, (1, 2))
    inner = exchange(inner)
    outer, head, tail, low_planes, high_planes = inverse_columns(outer, factors, True)
    outer_sides = shift(tail, "py", True, True), shift(head, "py", False, True)
    inner, head, tail = inverse_columns(inner, factors, False)
    inner_sides = shift(tail, "py", True, True), shift(head, "py", False, True)

    down, up = halo_slabs(low_planes, high_planes, *outer_sides)
    down, up, _ = lax.optimization_barrier((down, up, head))
    below, above = shift(up, "px", True, False), shift(down, "px", False, False)

    def source(z):
        if unit <= z < depth - unit:
            row = reach * (z - unit)
            return 1, z - unit, 2, row, 3, row
        if 0 <= z < depth:
            at = z if z < unit else z - depth + 2 * unit
            return 0, at, 0, reach * at, 1, reach * at
        at = z + reach if z < 0 else z - depth
        side = 2 if z < 0 else 3
        return side, at, side + 2, reach * at, side + 2, reach * (reach + at)

    inside = [source(z) for z in range(unit - reach, depth - unit + reach)]
    outside = [source(z) for z in range(-reach, unit + reach)]
    outside += [source(z) for z in range(depth - unit - reach, depth + reach)]
    planes, sides = [outer, inner], [*outer_sides, *inner_sides]
    inner_waves = exchange(potential_of(flags, planes, sides, inside, 1, tables, parts))
    halo = [below, above]
    spectral = potential_of(flags, planes + halo, sides + halo, outside, 2, tables, parts)
    outer_waves = exchange(spectral)
    result = forward_rows(flags, inner_waves, half_factors, (unit, 2 * unit), depth, None)
    result = forward_rows(flags, outer_waves, half_factors, (0, depth - unit), depth, result)
    return result


def solution(mesh):
    return jax.shard_map(
        on_device,
        mesh=mesh,
        in_specs=(P(None, "px", "py", None),),
        out_specs=P(None, "px", "py", None),
        check_vma=False,
    )
```

```python
import math

import jax
import jax.numpy as jnp
import numpy as np
from jax import lax
from jax.experimental import pallas as pl
from jax.experimental.pallas import tpu as pltpu
from jax.sharding import PartitionSpec as P

grid_step = 0.25
density_floor = 0.02
density_scale = 0.2
kappa_value = 0.804
mu_value = 0.2195149727645171
beta_value = 0.06672455060314922
gamma_value = (1.0 - math.log(2.0)) / (math.pi * math.pi)
correlation_scale = 0.031091
correlation_alpha = 0.2137
correlation_terms = (7.5957, 3.5876, 1.6382, 0.49294)

f32 = jnp.float32
bf16 = jnp.bfloat16
reach = 3
gather_tile = 16
lead = 9


in_hbm = pl.BlockSpec(memory_space=pltpu.HBM)


def call(body, out, cost, **options):
    estimate = pl.CostEstimate(flops=int(cost * 1e9), bytes_accessed=1 << 20, transcendentals=0)
    limit = pltpu.CompilerParams(vmem_limit_bytes=62 << 20)
    return pl.pallas_call(body, out_shape=out, compiler_params=limit, cost_estimate=estimate, **options)


def array(*shape):
    return jax.ShapeDtypeStruct(shape, f32)


def whole(shape):
    return pl.BlockSpec(shape, lambda *_: (0,) * len(shape))


def copy_all(pairs, sems):
    copies = [pltpu.make_async_copy(a, b, sems.at[i]) for i, (a, b) in enumerate(pairs)]
    for copy in copies:
        copy.start()
    return copies


def wait_all(copies):
    for copy in copies:
        copy.wait()


def group_copies(stage_ref, out_ref, sems, m, group):
    to = [m * group + g for g in range(group)]
    return [
        pltpu.make_async_copy(stage_ref.at[d], out_ref.at[d], sems.at[m, g])
        for g, d in enumerate(to)
    ]


def send_group(*args):
    for copy in group_copies(*args):
        copy.start()


def load_tables(hbm_ref, tab_ref, sems):
    return copy_all([(hbm_ref.at[i], tab_ref.at[i]) for i in range(4)], sems)


def table_scratch(width):
    return [pltpu.VMEM((4, width, width), bf16), pltpu.SemaphoreType.DMA((4,))]


def split(value):
    high = value.astype(bf16)
    return high, (value - high.astype(f32)).astype(bf16)


def dot_nt(left, right):
    return lax.dot_general(left, right, (((1,), (1,)), ((), ())), preferred_element_type=f32)


def dot_nn(left, right):
    return lax.dot_general(left, right, (((1,), (0,)), ((), ())), preferred_element_type=f32)


def triple(dot, left_high, left_low, right_high, right_low):
    return dot(left_high, right_high) + (dot(left_low, right_high) + dot(left_high, right_low))


def fill_tables(arriving, coarse_ref, fine_ref, tab_ref):
    wait_all(arriving)
    stride = fine_ref.shape[1]

    def step(a, carry):
        cos_a, sin_a = coarse_ref[0, pl.ds(a, 1)], coarse_ref[1, pl.ds(a, 1)]
        fine_cos, fine_sin = fine_ref[0], fine_ref[1]
        rows = pl.ds(pl.multiple_of(a * stride, stride), stride)
        tab_ref[0, rows], tab_ref[1, rows] = split(cos_a * fine_cos - sin_a * fine_sin)
        tab_ref[2, rows], tab_ref[3, rows] = split(sin_a * fine_cos + cos_a * fine_sin)
        return carry

    lax.fori_loop(0, tab_ref.shape[1] // 4 // stride, step, 0)

    tile = 16
    width = tab_ref.shape[2]
    quarter = width // 4
    turn = lax.broadcasted_iota(jnp.int32, (tile, width), 1) % 4
    turn_cos = jnp.where(turn == 0, 1.0, jnp.where(turn == 2, -1.0, 0.0)).astype(bf16)
    turn_sin = jnp.where(turn == 1, 1.0, jnp.where(turn == 3, -1.0, 0.0)).astype(bf16)
    flip = jnp.where(turn % 2 == 0, 1.0, -1.0).astype(bf16)

    def spread(t, carry):
        for part in range(2):
            rows = [pl.ds(pl.multiple_of(q * quarter + t * tile, tile), tile) for q in range(4)]
            cos, sin = tab_ref[part, rows[0]], tab_ref[2 + part, rows[0]]
            next_cos = cos * turn_cos - sin * turn_sin
            next_sin = sin * turn_cos + cos * turn_sin
            tab_ref[part, rows[1]], tab_ref[2 + part, rows[1]] = next_cos, next_sin
            tab_ref[part, rows[2]], tab_ref[2 + part, rows[2]] = cos * flip, sin * flip
            tab_ref[part, rows[3]], tab_ref[2 + part, rows[3]] = next_cos * flip, next_sin * flip
        return carry

    lax.fori_loop(0, quarter // tile, spread, 0)


def factor_scratch(factors):
    return [pltpu.VMEM(factor.shape, f32) for factor in factors] + [pltpu.SemaphoreType.DMA((2,))]


def phase_factors(length, stride, norm):
    def waves(rows, scale, period):
        angle = (np.outer(rows, np.arange(length)) % period) * (2.0 * math.pi / period)
        return np.stack([np.cos(angle), np.sin(angle)]).astype(np.float32) * np.float32(scale)

    coarse = waves(np.arange(0, length // 4, stride), 1.0, length)
    coarse = np.concatenate([coarse, waves(np.array([1, stride - 1]), 1.0, 2 * length)], axis=1)
    fine = waves(np.arange(stride), 1.0 / math.sqrt(norm), length)
    return jnp.asarray(coarse), jnp.asarray(fine)


def inverse_rows_body(blocks, makes, *refs):
    rho_ref, coarse_hbm_ref, fine_hbm_ref = refs[:3]
    if makes:
        factors_hbm, out_ref, tab_out_ref = refs[3:5], refs[6], refs[7]
        full_ref, full_coarse_ref, full_fine_ref, full_factor_sems, full_sems = refs[-5:]
        refs = refs[:-5]
    else:
        out_ref = refs[3]
    tab_ref, x_ref, wide_ref, stage_ref, in_sems, out_sems, coarse_ref, fine_ref, factor_sems = refs[-9:]
    half = tab_ref.shape[1]
    lanes = wide_ref.shape[2] // 2
    unit = x_ref.shape[1] // len(blocks)
    small = copy_all([(coarse_hbm_ref, coarse_ref), (fine_hbm_ref, fine_ref)], factor_sems)
    arriving = [
        copy_all(
            [
                (rho_ref.at[c, pl.ds(b * unit, unit)], x_ref.at[c, pl.ds(i * unit, unit)])
                for i, b in enumerate(blocks)
            ],
            in_sems.at[c],
        )
        for c in range(2)
    ]
    fill_tables(small, coarse_ref, fine_ref, tab_ref)
    for c in range(2):
        wait_all(arriving[c])
    real, imag = [x_ref[c].reshape(lanes, 2 * half) for c in range(2)]
    first = coarse_ref.shape[1] - 2
    wave_cos, wave_sin = [coarse_ref[i, first : first + 1] for i in range(2)]
    for p in range(2):
        if p == 0:
            values = real[:, :half] + real[:, half:], imag[:, :half] + imag[:, half:]
        else:
            odd_re, odd_im = real[:, :half] - real[:, half:], imag[:, :half] - imag[:, half:]
            values = odd_re * wave_cos - odd_im * wave_sin, odd_re * wave_sin + odd_im * wave_cos
        for c in range(2):
            high, low = split(values[c].T)
            cos_at = slice(c * lanes, (c + 1) * lanes)
            sin_at = slice((1 - c) * lanes, (2 - c) * lanes)
            for k, value in enumerate((high, high, low)):
                wide_ref[p, k * half : (k + 1) * half, cos_at] = value
                turned = value if c == 0 else -value
                wide_ref[p, (k + 3) * half : (k + 4) * half, sin_at] = turned
    parts, _, block, _ = stage_ref.shape
    out_lanes = 2 * lanes
    group = parts // 2
    count = half // 2

    def step(m, carry):
        at = pl.ds(pl.multiple_of(m * count, count), count)
        ch, sh = tab_ref[0, at], tab_ref[2, at]
        left = jnp.concatenate([ch, tab_ref[1, at], ch, sh, tab_ref[3, at], sh], axis=1)
        for p in range(2):
            product = dot_nn(left, wide_ref[p]).reshape(group, block // 2, out_lanes)
            for g in range(group):
                for i in range(out_lanes // 128):
                    to = pl.ds(p, block // 2, stride=2)
                    stage_ref[m * group + g, i, to, :] = product[g, :, i * 128 : (i + 1) * 128]
        send_group(stage_ref, out_ref, out_sems, m, group)
        return carry

    lax.fori_loop(0, 2, step, 0)
    if makes:
        pairs = zip(factors_hbm, (full_coarse_ref, full_fine_ref))
        small = copy_all(list(pairs), full_factor_sems)
        fill_tables(small, full_coarse_ref, full_fine_ref, full_ref)
        wait_all(copy_all([(full_ref.at[i], tab_out_ref.at[i]) for i in range(4)], full_sems))
    for m in range(2):
        wait_all(group_copies(stage_ref, out_ref, out_sems, m, group))


def inverse_rows(rho_hat, factors, full, flags, blocks):
    _, depth, local, width = rho_hat.shape
    half = factors[1].shape[2]
    block = factors[1].shape[1]
    parts = width // block
    unit = depth // 4
    planes = len(blocks) * unit
    lanes = planes * local
    out = (parts, 2 * lanes // 128, block, 128)
    scratch = [
        pltpu.VMEM((4, half, half), bf16),
        pltpu.VMEM((2, planes, local, width), f32),
        pltpu.VMEM((2, 6 * half, 2 * lanes), bf16),
        pltpu.VMEM(out, f32),
        pltpu.SemaphoreType.DMA((2, len(blocks))),
        pltpu.SemaphoreType.DMA((2, parts // 2)),
    ] + factor_scratch(factors)
    makes = full is not None
    body = lambda *refs: inverse_rows_body(blocks, makes, *refs)
    if makes:
        scratch += [pltpu.VMEM((4, width, width), bf16)] + factor_scratch(full)
        return call(
            body,
            [array(*out), jax.ShapeDtypeStruct((4, width, width), bf16)],
            10.0,
            grid=(1,),
            in_specs=[in_hbm] * 5 + [pl.BlockSpec(memory_space=pltpu.SMEM)],
            out_specs=[in_hbm] * 2,
            scratch_shapes=scratch + [pltpu.SemaphoreType.DMA((4,))],
            name="inverse_rows",
        )(rho_hat, *factors, *full, flags)
    return call(
        body,
        array(*out),
        10.0,
        grid=(1,),
        in_specs=[in_hbm] * 3,
        out_specs=in_hbm,
        scratch_shapes=scratch,
        name="inverse_rows",
    )(rho_hat, *factors)


def tile_copies(hbm_ref, in_ref, sems, t):
    group = in_ref.shape[0] // 4
    at = pl.ds(t * gather_tile, gather_tile)
    if not isinstance(t, int):
        at = pl.ds(pl.multiple_of(t * gather_tile, gather_tile), gather_tile)
    blocks = [pl.ds(g * group, group) for g in range(4)]
    return [
        pltpu.make_async_copy(hbm_ref.at[d, :, at], in_ref.at[d, :, at], sems.at[t, g])
        if len(in_ref.shape) == 4
        else pltpu.make_async_copy(hbm_ref.at[d, at], in_ref.at[d, at], sems.at[t, g])
        for g, d in enumerate(blocks)
    ]


def fetch_blocks(hbm_ref, in_ref, sems):
    for t in range(in_ref.shape[-2] // gather_tile):
        for copy in tile_copies(hbm_ref, in_ref, sems, t):
            copy.start()


def gather_blocks(hbm_ref, in_ref, sems, high_ref, low_ref, ways):
    parts, rows = in_ref.shape[0], in_ref.shape[-2]
    width = high_ref.shape[2]
    local = width // parts
    planes = high_ref.shape[1] // rows
    tile = gather_tile

    def load(p, at, block):
        if len(in_ref.shape) == 4:
            return in_ref[p, block, at]
        return in_ref[p, at, block * 128 : (block + 1) * 128]

    def gather_rows(t, carry):
        wait_all(tile_copies(hbm_ref, in_ref, sems, t))
        at = pl.ds(pl.multiple_of(t * tile, tile), tile)
        lane = lax.broadcasted_iota(jnp.int32, (tile, 128), 1)
        for piece in range(2 * planes):
            c, z = piece // planes, piece % planes
            first = piece * local
            block, offset = first // 128, first % 128
            turned = []
            for p in range(parts):
                value = load(p, at, block)
                if offset + local > 128:
                    after = load(p, at, block + 1)
                    value = jnp.where(lane < offset, after, value)
                turned.append(pltpu.roll(value, (p * (local // ways) - offset) % 128, 1))
            to = pl.ds(pl.multiple_of(z * rows + t * tile, tile), tile)
            for out in range(width // 128):
                way, within = out * ways // (width // 128), out % (width // 128 // ways)
                short = local // ways
                start = within * 128 // short
                value = turned[(start - way) % parts]
                for p in range(start + 1, parts):
                    edge = p * short - within * 128
                    if edge < 128:
                        value = jnp.where(lane < edge, value, turned[(p - way) % parts])
                high, low = split(value)
                high_ref[c, to, out * 128 : (out + 1) * 128] = high
                low_ref[c, to, out * 128 : (out + 1) * 128] = low
        return carry

    lax.fori_loop(0, rows // tile, gather_rows, 0)


def inverse_columns_body(sends, blocks_ref, coarse_hbm_ref, fine_hbm_ref, *refs):
    edge_ref, edge_sems, coarse_ref, fine_ref, factor_sems = refs[-5:]
    refs = refs[:-5]
    out_ref, head_ref, tail_ref = refs[:3]
    tab_ref, in_ref, stage_ref, high_ref, low_ref, in_sems, out_sems, send_sems = refs[-8:]
    planes, rows, width = stage_ref.shape
    small = copy_all([(coarse_hbm_ref, coarse_ref), (fine_hbm_ref, fine_ref)], factor_sems)
    fetch_blocks(blocks_ref, in_ref, in_sems)
    fill_tables(small, coarse_ref, fine_ref, tab_ref)
    gather_blocks(blocks_ref, in_ref, in_sems, high_ref, low_ref, 1)
    half = planes // 2

    def finish(z, carry):
        value = stage_ref[z]
        soft = jnp.maximum(value, 0.0) + jnp.log1p(jnp.exp(-jnp.abs(value)))
        stage_ref[z] = density_floor + density_scale * soft
        pltpu.make_async_copy(stage_ref.at[z], out_ref.at[z], out_sems.at[z]).start()
        return carry

    def step(m, carry):
        at = pl.ds(pl.multiple_of(m * half * rows, half * rows), half * rows)
        field = triple(dot_nn, high_ref[0, at], low_ref[0, at], tab_ref[0], tab_ref[1])
        field = field - triple(dot_nn, high_ref[1, at], low_ref[1, at], tab_ref[2], tab_ref[3])
        stage_ref[pl.ds(m * half, half)] = field.reshape(half, rows, width)
        lax.fori_loop(m * half, (m + 1) * half, finish, 0)
        return carry

    lax.fori_loop(0, 2, step, 0)
    leaving = [
        pltpu.make_async_copy(stage_ref.at[z], out_ref.at[z], out_sems.at[z]) for z in range(planes)
    ]
    for m in range(2 if sends else 0):
        first = m * (planes - reach)
        pairs = [(stage_ref.at[first + z], refs[3 + m].at[pl.ds(z * rows, rows)]) for z in range(reach)]
        leaving += copy_all(pairs, send_sems.at[m])
    for z in range(planes):
        at = slice(reach * z, reach * (z + 1))
        edge_ref[0, at] = stage_ref[z, :reach]
        edge_ref[1, at] = stage_ref[z, rows - reach :]
    leaving += copy_all([(edge_ref.at[0], head_ref), (edge_ref.at[1], tail_ref)], edge_sems)
    wait_all(leaving)


def inverse_columns(blocks, factors, sends):
    parts, _, rows, _ = blocks.shape
    lanes = blocks.shape[1] * blocks.shape[3]
    width = factors[0].shape[2]
    planes = lanes * parts // (2 * width)
    side = (reach * planes, width)
    slabs = 2 if sends else 0
    scratch = [
        pltpu.VMEM((4, width, width), bf16),
        pltpu.VMEM(blocks.shape, f32),
        pltpu.VMEM((planes, rows, width), f32),
        pltpu.VMEM((2, planes * rows, width), bf16),
        pltpu.VMEM((2, planes * rows, width), bf16),
        pltpu.SemaphoreType.DMA((rows // gather_tile, 4)),
        pltpu.SemaphoreType.DMA((planes,)),
        pltpu.SemaphoreType.DMA((2, reach)),
    ]
    edges = [pltpu.VMEM((2, *side), f32), pltpu.SemaphoreType.DMA((2,))]
    return call(
        lambda *refs: inverse_columns_body(sends, *refs),
        [array(planes, rows, width), array(*side), array(*side)]
        + [array(slab_rows(rows), width)] * slabs,
        7.0,
        grid=(1,),
        in_specs=[in_hbm] * 3,
        out_specs=[in_hbm] * (3 + slabs),
        scratch_shapes=scratch + edges + factor_scratch(factors),
        name="inverse_columns",
    )(blocks, *factors)


def shift(value, axis, up, ring):
    count = lax.axis_size(axis)
    pairs = [(i, (i + 1) % count) for i in range(count if ring else count - 1)]
    return lax.ppermute(value, axis, pairs if up else [(b, a) for a, b in pairs])


def slab_rows(rows):
    return reach * rows + -(-2 * reach * reach // 8) * 8


def halo_body(head_ref, tail_ref, low_ref, high_ref, down_ref, up_ref, edge_ref, sems):
    side = reach * reach
    held = head_ref.shape[0]
    copies = []
    for i, (first, out_ref) in enumerate(((0, down_ref), (held - side, up_ref))):
        edge_ref[i, :side] = head_ref[first : first + side]
        edge_ref[i, side : 2 * side] = tail_ref[first : first + side]
        count = edge_ref.shape[1]
        to = out_ref.at[pl.ds(out_ref.shape[0] - count, count)]
        copies += copy_all([(edge_ref.at[i], to)], sems.at[i])
    wait_all(copies)


def halo_slabs(low, high, head, tail):
    total, width = low.shape
    count = -(-2 * reach * reach // 8) * 8
    return call(
        halo_body,
        [array(total, width)] * 2,
        1.0,
        grid=(1,),
        in_specs=[whole(head.shape), whole(tail.shape), in_hbm, in_hbm],
        out_specs=[in_hbm] * 2,
        scratch_shapes=[pltpu.VMEM((2, count, width), f32), pltpu.SemaphoreType.DMA((2, 1))],
        input_output_aliases={2: 0, 3: 1},
        name="halo_slabs",
    )(head, tail, low, high)


def roll_x(value, by):
    return pltpu.roll(value, by % value.shape[-1], value.ndim - 1)


def energy_slopes(rho, sigma):
    two_a = 2.0 * correlation_scale
    b1, b2, b3, b4 = [two_a * term for term in correlation_terms]
    ratio = beta_value / gamma_value
    exchange = -0.75 * (3.0 / math.pi) ** (1.0 / 3.0)
    s_scale = 0.25 / (3.0 * math.pi**2) ** (2.0 / 3.0)
    t_scale = math.pi / (16.0 * (3.0 * math.pi**2) ** (1.0 / 3.0))
    radius_scale = (3.0 / (4.0 * math.pi)) ** (1.0 / 3.0)
    sixth = jnp.exp(jnp.log(rho) * (-1.0 / 6.0))
    inv = sixth * sixth
    inv2 = inv * inv
    inv4 = inv2 * inv2
    scaled_sigma = sigma * inv4
    stretch = 1.0 + (mu_value / kappa_value * s_scale) * scaled_sigma * inv4
    v = (ratio * t_scale) * scaled_sigma * (inv2 * inv)
    root = math.sqrt(radius_scale) * sixth
    denom = root * (b1 + root * (b2 + root * (b3 + root * b4)))
    denom_slope = root * (0.5 * b1 + root * (b2 + root * (1.5 * b3 + root * (2.0 * b4))))
    pair = denom * denom + denom
    recip = 1.0 / (stretch * pair)
    weight = recip * pair
    recip = recip * stretch
    x_rho = (rho * inv2) * (
        exchange * (4.0 / 3.0) * (1.0 + kappa_value)
        + weight
        * ((-4.0 * exchange * kappa_value) + (8.0 / 3.0 * exchange * kappa_value) * weight)
    )
    radius_part = (two_a * correlation_alpha * radius_scale) * inv
    linear = two_a + radius_part
    log_term = jnp.log(1.0 + (recip * denom + recip))
    uniform = -linear * log_term
    rho_uniform = (1.0 / 3.0) * (radius_part * log_term - linear * (recip * denom_slope))
    grown = jnp.exp(uniform * (-1.0 / gamma_value))
    x = grown - 1.0
    vx = v * x
    v2 = v * v
    lower = x * x + (vx + v2)
    upper = lower + vx * (x + v)
    both = 1.0 / (lower * upper)
    gradient = gamma_value * jnp.log(upper * (upper * both))
    h_part = (x + 2.0 * v) * (x * x) * (x * both)
    h_uniform = (v2 * both) * (v * (2.0 * x + v)) * grown
    d_rho = (
        (x_rho + uniform)
        + (gradient + rho_uniform * (1.0 - h_uniform))
        - (7.0 / 3.0 * gamma_value) * (v * h_part)
    )
    two_d_sigma = inv4 * (
        (2.0 * exchange * s_scale * mu_value) * (weight * weight)
        + (2.0 * t_scale * beta_value) * h_part
    )
    return d_rho, two_d_sigma


def potential_body(sources, groups, flag_ref, *refs):
    ext_ref, part_ref, smooth_ref, flat_ref, fx_ref, fy_ref, fz_ref = refs[-7:]
    count = 6 if groups == 2 else 4
    plane_refs = refs[: -count - 17]
    sides_hbm = plane_refs[-count:]
    tab_hbm_ref, out_ref, tab_ref, tab_sems, pot_ref, tall_ref, stage_ref = refs[-count - 17 : -count - 10]
    in_sems, out_sems, side_sems = refs[-count - 10 : -count - 7]
    side_refs = refs[-count - 7 : -7]
    planes, blocks, rows, _ = pot_ref.shape
    each = planes // groups
    sides = copy_all(
        [
            (hbm.at[pl.ds(hbm.shape[0] - ref.shape[0], ref.shape[0])], ref)
            for hbm, ref in zip(sides_hbm, side_refs)
        ],
        side_sems,
    )

    def plane_of(plane, at):
        ref = plane_refs[plane]
        return ref.at[at] if len(ref.shape) == 3 else ref.at[pl.ds(at * rows, rows)]

    arriving = copy_all(
        [
            (plane_of(plane, at), ext_ref.at[z, pl.ds(lead - 1, rows)])
            for z, (plane, at, *_) in enumerate(sources)
        ],
        in_sems,
    )
    slope = 1.0 / (2.0 * grid_step)
    tiles = rows // 8 + 1

    def at_end(flag):
        return pl.when(flag_ref[flag] == 1) if groups == 2 else lambda body: None

    wait_all(sides)
    for z, (_, _, head, head_row, tail, tail_row) in enumerate(sources):
        ext_ref[z, lead - 1 - reach : lead - 1] = side_refs[head][head_row : head_row + reach]
        after = side_refs[tail][tail_row : tail_row + reach]
        ext_ref[z, lead - 1 + rows : lead - 1 + rows + reach] = after
    wait_all(arriving)
    tables = load_tables(tab_hbm_ref, tab_ref, tab_sems)

    def widened(z, size, margin):
        return z + margin * (z // size) if groups > 1 else z

    @at_end(0)
    def _():
        ext_ref[reach - 1] = ext_ref[reach]

    @at_end(1)
    def _():
        ext_ref[ext_ref.shape[0] - reach] = ext_ref[ext_ref.shape[0] - reach - 1]

    def filter_depth(z, carry):
        w = widened(z, each + 4, 2)
        part_ref[z] = 0.25 * (ext_ref[w] + ext_ref[w + 2]) + 0.5 * ext_ref[w + 1]
        return carry

    lax.fori_loop(0, part_ref.shape[0], filter_depth, 0)

    def filter_plane(z, carry):
        for t in range(tiles):
            r = lead - 2 + 8 * t
            along_y = 0.25 * (part_ref[z, r - 2 : r + 6] + part_ref[z, r : r + 8]) + 0.5 * (
                part_ref[z, r - 1 : r + 7]
            )
            smooth_ref[z, r : r + 8] = (
                0.25 * (roll_x(along_y, 1) + roll_x(along_y, -1)) + 0.5 * along_y
            )
        return carry

    lax.fori_loop(0, part_ref.shape[0], filter_plane, 0)

    @at_end(0)
    def _():
        smooth_ref[1] = smooth_ref[2]

    @at_end(1)
    def _():
        smooth_ref[smooth_ref.shape[0] - 2] = smooth_ref[smooth_ref.shape[0] - 3]

    def local_terms(z, carry):
        w = widened(z, each + 2, 2)
        for t in range(tiles):
            r = lead - 1 + 8 * t
            center = smooth_ref[w + 1, r : r + 8]
            gx = (roll_x(center, -1) - roll_x(center, 1)) * slope
            gy = (smooth_ref[w + 1, r + 1 : r + 9] - smooth_ref[w + 1, r - 1 : r + 7]) * slope
            gz = (smooth_ref[w + 2, r : r + 8] - smooth_ref[w, r : r + 8]) * slope
            d_rho, two_d_sigma = energy_slopes(center, gx * gx + gy * gy + gz * gz)
            flat_ref[z, r : r + 8] = d_rho
            fx_ref[z, r : r + 8] = two_d_sigma * gx
            fy_ref[z, r : r + 8] = two_d_sigma * gy
            fz_ref[z, r : r + 8] = two_d_sigma * gz
        return carry

    lax.fori_loop(0, flat_ref.shape[0], local_terms, 0)

    @at_end(0)
    def _():
        fz_ref[0] = fz_ref[1]

    @at_end(1)
    def _():
        fz_ref[fz_ref.shape[0] - 1] = fz_ref[fz_ref.shape[0] - 2]

    def collect(z, carry):
        w = widened(z, each, 2)
        for t in range(rows // 8):
            r = lead + 8 * t
            here = slice(r, r + 8)
            fx = fx_ref[w + 1, here]
            along_x = (roll_x(fx, -1) - roll_x(fx, 1)) * slope
            along_y = (fy_ref[w + 1, r + 1 : r + 9] - fy_ref[w + 1, r - 1 : r + 7]) * slope
            along_z = (fz_ref[w + 2, here] - fz_ref[w, here]) * slope
            value = flat_ref[w + 1, here] - (along_x + along_y + along_z)
            for i in range(blocks):
                pot_ref[z, i, 8 * t : 8 * t + 8, :] = value[:, i * 128 : (i + 1) * 128]
        return carry

    lax.fori_loop(0, planes, collect, 0)
    wait_all(tables)
    forward_columns(pot_ref, tab_ref, tall_ref, stage_ref, out_ref, out_sems)


def forward_columns(x_ref, tab_ref, tall_ref, stage_ref, out_ref, out_sems):
    planes, blocks, rows, _ = x_ref.shape
    width = blocks * 128
    for i in range(blocks):
        pieces = [
            x_ref[z, i, pl.ds(p, rows // 2, stride=2), :] for z in range(planes) for p in range(2)
        ]
        high, low = split(jnp.concatenate(pieces, axis=0).T)
        for k, value in enumerate((high, high, low)):
            tall_ref[k * width + i * 128 : k * width + (i + 1) * 128] = value
    parts, block, out_lanes = stage_ref.shape
    group = parts // 2

    def step(m, carry):
        at = pl.ds(pl.multiple_of(m * group * block, group * block), group * block)
        ch, sh = tab_ref[0, at], tab_ref[2, at]
        real = dot_nn(jnp.concatenate([ch, tab_ref[1, at], ch], axis=1), tall_ref[...])
        imag = dot_nn(jnp.concatenate([sh, tab_ref[3, at], sh], axis=1), tall_ref[...])
        both = jnp.concatenate([real, -imag], axis=1)
        stage_ref[pl.ds(m * group, group)] = both.reshape(group, block, out_lanes)
        send_group(stage_ref, out_ref, out_sems, m, group)
        return carry

    lax.fori_loop(0, 2, step, 0)
    for m in range(2):
        wait_all(group_copies(stage_ref, out_ref, out_sems, m, group))


def potential_of(flags, planes, sides, sources, groups, tables, parts):
    rows, width = planes[0].shape[1:]
    tall = -(-(rows + lead + 8) // 8) * 8
    count = len(sources) - 2 * reach * groups
    lanes = count * rows
    out = (parts, width // parts, 2 * lanes)
    scratch = table_scratch(width) + [
        pltpu.VMEM((count, width // 128, rows, 128), f32),
        pltpu.VMEM((3 * width, lanes), bf16),
        pltpu.VMEM(out, f32),
        pltpu.SemaphoreType.DMA((len(sources),)),
        pltpu.SemaphoreType.DMA((2, parts // 2)),
        pltpu.SemaphoreType.DMA((len(sides),)),
    ]
    scratch += [pltpu.VMEM((min(side.shape[0], sides[0].shape[0]), width), f32) for side in sides]
    for margin in (6, 4, 4, 2, 2, 2, 2):
        scratch.append(pltpu.VMEM((count + margin * groups, tall, width), f32))
    return call(
        lambda *refs: potential_body(sources, groups, *refs),
        array(*out),
        20.0,
        grid=(1,),
        in_specs=[pl.BlockSpec(memory_space=pltpu.SMEM)]
        + [in_hbm] * len(planes)
        + [pl.BlockSpec(memory_space=pl.ANY)] * len(sides)
        + [in_hbm],
        out_specs=in_hbm,
        scratch_shapes=scratch,
        name="potential",
    )(flags, *planes, *sides, tables)


def forward_rows_body(starts, flag_ref, blocks_ref, coarse_hbm_ref, fine_hbm_ref, *refs):
    coarse_ref, fine_ref, factor_sems = refs[-3:]
    out_ref, tab_ref, wide_ref, in_ref, stage_ref, high_ref, low_ref, in_sems, out_sems = refs[-12:-3]
    _, planes, rows, width = stage_ref.shape
    small = copy_all([(coarse_hbm_ref, coarse_ref), (fine_hbm_ref, fine_ref)], factor_sems)
    fetch_blocks(blocks_ref, in_ref, in_sems)
    fill_tables(small, coarse_ref, fine_ref, tab_ref)
    length = tab_ref.shape[1]
    for k, part in enumerate((0, 0, 1)):
        re_at = slice(k * length, (k + 1) * length)
        im_at = slice((k + 3) * length, (k + 4) * length)
        wide_ref[re_at, :length], wide_ref[re_at, length:] = tab_ref[part], -tab_ref[2 + part]
        wide_ref[im_at, :length], wide_ref[im_at, length:] = tab_ref[2 + part], tab_ref[part]
    gather_blocks(blocks_ref, in_ref, in_sems, high_ref, low_ref, 2)
    last = coarse_ref.shape[1] - 1
    wave_cos, wave_sin = coarse_ref[0, last:], coarse_ref[1, last:]
    half = planes // 2

    def copies(c, m):
        to = starts[0] + m * (starts[1] - starts[0])
        return [
            pltpu.make_async_copy(stage_ref.at[c, z], out_ref.at[c, to + y], out_sems.at[c, z])
            for y, z in enumerate([m * half + y for y in range(half)])
        ]

    def step(m, carry):
        at = pl.ds(pl.multiple_of(m * half * rows, half * rows), half * rows)
        to = pl.ds(m * half, half)

        def product(way):
            lanes = slice(way * length, (way + 1) * length)
            pairs = [(high_ref[c, at, lanes], low_ref[c, at, lanes]) for c in range(2)]
            left = [value for high, low in pairs for value in (high, low, high)]
            both = dot_nn(jnp.concatenate(left, axis=1), wide_ref[...])
            return both[:, :length], both[:, length:]

        even = product(0)
        odd_re, odd_im = product(1)
        odd = odd_re * wave_cos - odd_im * wave_sin, odd_re * wave_sin + odd_im * wave_cos
        for c in range(2):
            shape = (half, rows, length)
            stage_ref[c, to, :, :length] = (even[c] + odd[c]).reshape(shape)
            stage_ref[c, to, :, length:] = (even[c] - odd[c]).reshape(shape)

        @pl.when(flag_ref[2] == 1)
        def _():
            tile = (8, 128)
            at_zero = (lax.broadcasted_iota(jnp.int32, tile, 0) == 0) & (
                lax.broadcasted_iota(jnp.int32, tile, 1) == 0
            )
            for c in range(2):
                for y in range(half):
                    z = m * half + y
                    corner = stage_ref[c, z, :8, :128]
                    stage_ref[c, z, :8, :128] = jnp.where(at_zero, 0.0, corner)

        for copy in copies(0, m) + copies(1, m):
            copy.start()
        return carry

    lax.fori_loop(0, 2, step, 0)
    for c in range(2):
        wait_all(copies(c, 0) + copies(c, 1))


def forward_rows(flags, blocks, factors, starts, depth, before):
    parts, rows, lanes = blocks.shape
    length = factors[0].shape[2]
    width = 2 * length
    planes = lanes * parts // (2 * width)
    earlier = [] if before is None else [before]
    scratch = [
        pltpu.VMEM((4, length, length), bf16),
        pltpu.VMEM((6 * length, width), bf16),
        pltpu.VMEM(blocks.shape, f32),
        pltpu.VMEM((2, planes, rows, width), f32),
        pltpu.VMEM((2, planes * rows, width), bf16),
        pltpu.VMEM((2, planes * rows, width), bf16),
        pltpu.SemaphoreType.DMA((rows // gather_tile, 4)),
        pltpu.SemaphoreType.DMA((2, planes)),
    ]
    return call(
        lambda *refs: forward_rows_body(starts, *refs),
        array(2, depth, rows, width),
        10.0,
        grid=(1,),
        in_specs=[pl.BlockSpec(memory_space=pltpu.SMEM)] + [in_hbm] * (3 + len(earlier)),
        out_specs=in_hbm,
        scratch_shapes=scratch + factor_scratch(factors),
        input_output_aliases={4: 0} if earlier else {},
        name="forward_rows",
    )(flags, blocks, *factors, *earlier)


def exchange(value):
    return lax.all_to_all(value, "py", 0, 0, tiled=True)


def on_device(rho_hat):
    parts = lax.axis_size("py")
    place_z, place_y = lax.axis_index("px"), lax.axis_index("py")
    flags = jnp.stack(
        [place_z == 0, place_z == lax.axis_size("px") - 1, place_y == 0]
    ).astype(jnp.int32)
    depth, width = rho_hat.shape[1], rho_hat.shape[3]
    unit = depth // 4
    block = width // parts
    factors = phase_factors(width, block, width)
    half_factors = phase_factors(width // 2, block, width)

    outer = exchange(inverse_rows(rho_hat, half_factors, None, None, (0, 3)))
    inner, tables = inverse_rows(rho_hat, half_factors, factors, flags, (1, 2))
    inner = exchange(inner)
    outer, head, tail, low_planes, high_planes = inverse_columns(outer, factors, True)
    outer_sides = shift(tail, "py", True, True), shift(head, "py", False, True)
    down, up = halo_slabs(low_planes, high_planes, *outer_sides)
    inner, down, up = lax.optimization_barrier((inner, down, up))
    inner, head, tail = inverse_columns(inner, factors, False)
    inner_sides = shift(tail, "py", True, True), shift(head, "py", False, True)

    down, up, _ = lax.optimization_barrier((down, up, head))
    below, above = shift(up, "px", True, False), shift(down, "px", False, False)

    def source(z):
        if unit <= z < depth - unit:
            row = reach * (z - unit)
            return 1, z - unit, 2, row, 3, row
        if 0 <= z < depth:
            at = z if z < unit else z - depth + 2 * unit
            return 0, at, 0, reach * at, 1, reach * at
        at = z + reach if z < 0 else z - depth
        side = 2 if z < 0 else 3
        return side, at, side + 2, reach * at, side + 2, reach * (reach + at)

    inside = [source(z) for z in range(unit - reach, depth - unit + reach)]
    outside = [source(z) for z in range(-reach, unit + reach)]
    outside += [source(z) for z in range(depth - unit - reach, depth + reach)]
    planes, sides = [outer, inner], [*outer_sides, *inner_sides]
    inner_waves = exchange(potential_of(flags, planes, sides, inside, 1, tables, parts))
    halo = [below, above]
    spectral = potential_of(flags, planes + halo, sides + halo, outside, 2, tables, parts)
    outer_waves = exchange(spectral)
    result = forward_rows(flags, inner_waves, half_factors, (unit, 2 * unit), depth, None)
    result = forward_rows(flags, outer_waves, half_factors, (0, depth - unit), depth, result)
    return result


def solution(mesh):
    return jax.shard_map(
        on_device,
        mesh=mesh,
        in_specs=(P(None, "px", "py", None),),
        out_specs=P(None, "px", "py", None),
        check_vma=False,
    )
```

```python
import math

import jax
import jax.numpy as jnp
import numpy as np
from jax import lax
from jax.experimental import pallas as pl
from jax.experimental.pallas import tpu as pltpu
from jax.sharding import PartitionSpec as P

grid_step = 0.25
density_floor = 0.02
density_scale = 0.2
kappa_value = 0.804
mu_value = 0.2195149727645171
beta_value = 0.06672455060314922
gamma_value = (1.0 - math.log(2.0)) / (math.pi * math.pi)
correlation_scale = 0.031091
correlation_alpha = 0.2137
correlation_terms = (7.5957, 3.5876, 1.6382, 0.49294)

f32 = jnp.float32
bf16 = jnp.bfloat16
reach = 3
gather_tile = 16
lead = 9


in_hbm = pl.BlockSpec(memory_space=pltpu.HBM)


def call(body, out, cost, mib=62, **options):
    estimate = pl.CostEstimate(flops=int(cost * 1e9), bytes_accessed=1 << 20, transcendentals=0)
    limit = pltpu.CompilerParams(vmem_limit_bytes=mib << 20)
    return pl.pallas_call(body, out_shape=out, compiler_params=limit, cost_estimate=estimate, **options)


def array(*shape):
    return jax.ShapeDtypeStruct(shape, f32)


def whole(shape):
    return pl.BlockSpec(shape, lambda *_: (0,) * len(shape))


def copy_all(pairs, sems):
    copies = [pltpu.make_async_copy(a, b, sems.at[i]) for i, (a, b) in enumerate(pairs)]
    for copy in copies:
        copy.start()
    return copies


def wait_all(copies):
    for copy in copies:
        copy.wait()


def group_copies(stage_ref, out_ref, sems, m, group):
    to = [m * group + g for g in range(group)]
    return [
        pltpu.make_async_copy(stage_ref.at[d], out_ref.at[d], sems.at[m, g])
        for g, d in enumerate(to)
    ]


def send_group(*args):
    for copy in group_copies(*args):
        copy.start()


def load_tables(hbm_ref, tab_ref, sems):
    return copy_all([(hbm_ref.at[i], tab_ref.at[i]) for i in range(4)], sems)


def table_scratch(width):
    return [pltpu.VMEM((4, width, width), bf16), pltpu.SemaphoreType.DMA((4,))]


def split(value):
    high = value.astype(bf16)
    return high, (value - high.astype(f32)).astype(bf16)


def dot_nt(left, right):
    return lax.dot_general(left, right, (((1,), (1,)), ((), ())), preferred_element_type=f32)


def dot_nn(left, right):
    return lax.dot_general(left, right, (((1,), (0,)), ((), ())), preferred_element_type=f32)


def triple(dot, left_high, left_low, right_high, right_low):
    return dot(left_high, right_high) + (dot(left_low, right_high) + dot(left_high, right_low))


def fill_tables(arriving, coarse_ref, fine_ref, tab_ref):
    wait_all(arriving)
    stride = fine_ref.shape[1]

    def step(a, carry):
        cos_a, sin_a = coarse_ref[0, pl.ds(a, 1)], coarse_ref[1, pl.ds(a, 1)]
        fine_cos, fine_sin = fine_ref[0], fine_ref[1]
        rows = pl.ds(pl.multiple_of(a * stride, stride), stride)
        tab_ref[0, rows], tab_ref[1, rows] = split(cos_a * fine_cos - sin_a * fine_sin)
        tab_ref[2, rows], tab_ref[3, rows] = split(sin_a * fine_cos + cos_a * fine_sin)
        return carry

    lax.fori_loop(0, tab_ref.shape[1] // 4 // stride, step, 0)

    tile = 16
    width = tab_ref.shape[2]
    quarter = width // 4
    turn = lax.broadcasted_iota(jnp.int32, (tile, width), 1) % 4
    turn_cos = jnp.where(turn == 0, 1.0, jnp.where(turn == 2, -1.0, 0.0)).astype(bf16)
    turn_sin = jnp.where(turn == 1, 1.0, jnp.where(turn == 3, -1.0, 0.0)).astype(bf16)
    flip = jnp.where(turn % 2 == 0, 1.0, -1.0).astype(bf16)

    def spread(t, carry):
        for part in range(2):
            rows = [pl.ds(pl.multiple_of(q * quarter + t * tile, tile), tile) for q in range(4)]
            cos, sin = tab_ref[part, rows[0]], tab_ref[2 + part, rows[0]]
            next_cos = cos * turn_cos - sin * turn_sin
            next_sin = sin * turn_cos + cos * turn_sin
            tab_ref[part, rows[1]], tab_ref[2 + part, rows[1]] = next_cos, next_sin
            tab_ref[part, rows[2]], tab_ref[2 + part, rows[2]] = cos * flip, sin * flip
            tab_ref[part, rows[3]], tab_ref[2 + part, rows[3]] = next_cos * flip, next_sin * flip
        return carry

    lax.fori_loop(0, quarter // tile, spread, 0)


def factor_scratch(factors):
    return [pltpu.VMEM(factor.shape, f32) for factor in factors] + [pltpu.SemaphoreType.DMA((2,))]


def phase_factors(length, stride, norm):
    def waves(rows, scale, period):
        angle = (np.outer(rows, np.arange(length)) % period) * (2.0 * math.pi / period)
        return np.stack([np.cos(angle), np.sin(angle)]).astype(np.float32) * np.float32(scale)

    coarse = waves(np.arange(0, length // 4, stride), 1.0, length)
    coarse = np.concatenate([coarse, waves(np.array([1, stride - 1]), 1.0, 2 * length)], axis=1)
    fine = waves(np.arange(stride), 1.0 / math.sqrt(norm), length)
    return jnp.asarray(coarse), jnp.asarray(fine)


def inverse_rows_body(blocks, makes, *refs):
    rho_ref, coarse_hbm_ref, fine_hbm_ref = refs[:3]
    if makes:
        factors_hbm, out_ref, tab_out_ref = refs[3:5], refs[6], refs[7]
        full_ref, full_coarse_ref, full_fine_ref, full_factor_sems, full_sems = refs[-5:]
        refs = refs[:-5]
    else:
        out_ref = refs[3]
    tab_ref, x_ref, wide_ref, stage_ref, in_sems, out_sems, coarse_ref, fine_ref, factor_sems = refs[-9:]
    half = tab_ref.shape[1]
    lanes = wide_ref.shape[2] // 2
    unit = x_ref.shape[1] // len(blocks)
    small = copy_all([(coarse_hbm_ref, coarse_ref), (fine_hbm_ref, fine_ref)], factor_sems)
    arriving = [
        copy_all(
            [
                (rho_ref.at[c, pl.ds(b * unit, unit)], x_ref.at[c, pl.ds(i * unit, unit)])
                for i, b in enumerate(blocks)
            ],
            in_sems.at[c],
        )
        for c in range(2)
    ]
    fill_tables(small, coarse_ref, fine_ref, tab_ref)
    for c in range(2):
        wait_all(arriving[c])
    real, imag = [x_ref[c].reshape(lanes, 2 * half) for c in range(2)]
    first = coarse_ref.shape[1] - 2
    wave_cos, wave_sin = [coarse_ref[i, first : first + 1] for i in range(2)]
    for p in range(2):
        if p == 0:
            values = real[:, :half] + real[:, half:], imag[:, :half] + imag[:, half:]
        else:
            odd_re, odd_im = real[:, :half] - real[:, half:], imag[:, :half] - imag[:, half:]
            values = odd_re * wave_cos - odd_im * wave_sin, odd_re * wave_sin + odd_im * wave_cos
        for c in range(2):
            high, low = split(values[c].T)
            cos_at = slice(c * lanes, (c + 1) * lanes)
            sin_at = slice((1 - c) * lanes, (2 - c) * lanes)
            for k, value in enumerate((high, high, low)):
                wide_ref[p, k * half : (k + 1) * half, cos_at] = value
                turned = value if c == 0 else -value
                wide_ref[p, (k + 3) * half : (k + 4) * half, sin_at] = turned
    parts, _, block, _ = stage_ref.shape
    out_lanes = 2 * lanes
    group = parts // 2
    count = half // 2

    def step(m, carry):
        at = pl.ds(pl.multiple_of(m * count, count), count)
        ch, sh = tab_ref[0, at], tab_ref[2, at]
        left = jnp.concatenate([ch, tab_ref[1, at], ch, sh, tab_ref[3, at], sh], axis=1)
        for p in range(2):
            product = dot_nn(left, wide_ref[p]).reshape(group, block // 2, out_lanes)
            for g in range(group):
                for i in range(out_lanes // 128):
                    to = pl.ds(p, block // 2, stride=2)
                    stage_ref[m * group + g, i, to, :] = product[g, :, i * 128 : (i + 1) * 128]
        send_group(stage_ref, out_ref, out_sems, m, group)
        return carry

    lax.fori_loop(0, 2, step, 0)
    if makes:
        pairs = zip(factors_hbm, (full_coarse_ref, full_fine_ref))
        small = copy_all(list(pairs), full_factor_sems)
        fill_tables(small, full_coarse_ref, full_fine_ref, full_ref)
        wait_all(copy_all([(full_ref.at[i], tab_out_ref.at[i]) for i in range(4)], full_sems))
    for m in range(2):
        wait_all(group_copies(stage_ref, out_ref, out_sems, m, group))


def inverse_rows(rho_hat, factors, full, flags, blocks):
    _, depth, local, width = rho_hat.shape
    half = factors[1].shape[2]
    block = factors[1].shape[1]
    parts = width // block
    unit = depth // 4
    planes = len(blocks) * unit
    lanes = planes * local
    out = (parts, 2 * lanes // 128, block, 128)
    scratch = [
        pltpu.VMEM((4, half, half), bf16),
        pltpu.VMEM((2, planes, local, width), f32),
        pltpu.VMEM((2, 6 * half, 2 * lanes), bf16),
        pltpu.VMEM(out, f32),
        pltpu.SemaphoreType.DMA((2, len(blocks))),
        pltpu.SemaphoreType.DMA((2, parts // 2)),
    ] + factor_scratch(factors)
    makes = full is not None
    body = lambda *refs: inverse_rows_body(blocks, makes, *refs)
    if makes:
        scratch += [pltpu.VMEM((4, width, width), bf16)] + factor_scratch(full)
        return call(
            body,
            [array(*out), jax.ShapeDtypeStruct((4, width, width), bf16)],
            10.0,
            grid=(1,),
            in_specs=[in_hbm] * 5 + [pl.BlockSpec(memory_space=pltpu.SMEM)],
            out_specs=[in_hbm] * 2,
            scratch_shapes=scratch + [pltpu.SemaphoreType.DMA((4,))],
            name="inverse_rows",
        )(rho_hat, *factors, *full, flags)
    return call(
        body,
        array(*out),
        10.0,
        grid=(1,),
        in_specs=[in_hbm] * 3,
        out_specs=in_hbm,
        scratch_shapes=scratch,
        name="inverse_rows",
    )(rho_hat, *factors)


def tile_copies(hbm_ref, in_ref, sems, t):
    group = in_ref.shape[0] // 4
    at = pl.ds(t * gather_tile, gather_tile)
    if not isinstance(t, int):
        at = pl.ds(pl.multiple_of(t * gather_tile, gather_tile), gather_tile)
    blocks = [pl.ds(g * group, group) for g in range(4)]
    return [
        pltpu.make_async_copy(hbm_ref.at[d, :, at], in_ref.at[d, :, at], sems.at[t, g])
        if len(in_ref.shape) == 4
        else pltpu.make_async_copy(hbm_ref.at[d, at], in_ref.at[d, at], sems.at[t, g])
        for g, d in enumerate(blocks)
    ]


def fetch_blocks(hbm_ref, in_ref, sems):
    for t in range(in_ref.shape[-2] // gather_tile):
        for copy in tile_copies(hbm_ref, in_ref, sems, t):
            copy.start()


def gather_blocks(hbm_ref, in_ref, sems, high_ref, low_ref, ways):
    parts, rows = in_ref.shape[0], in_ref.shape[-2]
    width = high_ref.shape[2]
    local = width // parts
    planes = high_ref.shape[1] // rows
    tile = gather_tile

    def load(p, at, block):
        if len(in_ref.shape) == 4:
            return in_ref[p, block, at]
        return in_ref[p, at, block * 128 : (block + 1) * 128]

    def gather_rows(t, carry):
        wait_all(tile_copies(hbm_ref, in_ref, sems, t))
        at = pl.ds(pl.multiple_of(t * tile, tile), tile)
        lane = lax.broadcasted_iota(jnp.int32, (tile, 128), 1)
        for piece in range(2 * planes):
            c, z = piece // planes, piece % planes
            first = piece * local
            block, offset = first // 128, first % 128
            turned = []
            for p in range(parts):
                value = load(p, at, block)
                if offset + local > 128:
                    after = load(p, at, block + 1)
                    value = jnp.where(lane < offset, after, value)
                turned.append(pltpu.roll(value, (p * (local // ways) - offset) % 128, 1))
            to = pl.ds(pl.multiple_of(z * rows + t * tile, tile), tile)
            for out in range(width // 128):
                way, within = out * ways // (width // 128), out % (width // 128 // ways)
                short = local // ways
                start = within * 128 // short
                value = turned[(start - way) % parts]
                for p in range(start + 1, parts):
                    edge = p * short - within * 128
                    if edge < 128:
                        value = jnp.where(lane < edge, value, turned[(p - way) % parts])
                high, low = split(value)
                high_ref[c, to, out * 128 : (out + 1) * 128] = high
                low_ref[c, to, out * 128 : (out + 1) * 128] = low
        return carry

    lax.fori_loop(0, rows // tile, gather_rows, 0)


def inverse_columns_body(sends, blocks_ref, coarse_hbm_ref, fine_hbm_ref, *refs):
    edge_ref, edge_sems, coarse_ref, fine_ref, factor_sems = refs[-5:]
    refs = refs[:-5]
    out_ref, head_ref, tail_ref = refs[:3]
    tab_ref, in_ref, stage_ref, high_ref, low_ref, in_sems, out_sems, send_sems = refs[-8:]
    planes, rows, width = stage_ref.shape
    small = copy_all([(coarse_hbm_ref, coarse_ref), (fine_hbm_ref, fine_ref)], factor_sems)
    fetch_blocks(blocks_ref, in_ref, in_sems)
    fill_tables(small, coarse_ref, fine_ref, tab_ref)
    gather_blocks(blocks_ref, in_ref, in_sems, high_ref, low_ref, 1)
    half = planes // 2

    def finish(z, carry):
        value = stage_ref[z]
        soft = jnp.maximum(value, 0.0) + jnp.log1p(jnp.exp(-jnp.abs(value)))
        stage_ref[z] = density_floor + density_scale * soft
        pltpu.make_async_copy(stage_ref.at[z], out_ref.at[z], out_sems.at[z]).start()
        return carry

    def step(m, carry):
        at = pl.ds(pl.multiple_of(m * half * rows, half * rows), half * rows)
        field = triple(dot_nn, high_ref[0, at], low_ref[0, at], tab_ref[0], tab_ref[1])
        field = field - triple(dot_nn, high_ref[1, at], low_ref[1, at], tab_ref[2], tab_ref[3])
        stage_ref[pl.ds(m * half, half)] = field.reshape(half, rows, width)
        lax.fori_loop(m * half, (m + 1) * half, finish, 0)
        return carry

    lax.fori_loop(0, 2, step, 0)
    leaving = [
        pltpu.make_async_copy(stage_ref.at[z], out_ref.at[z], out_sems.at[z]) for z in range(planes)
    ]
    for m in range(2 if sends else 0):
        first = m * (planes - reach)
        pairs = [(stage_ref.at[first + z], refs[3 + m].at[pl.ds(z * rows, rows)]) for z in range(reach)]
        leaving += copy_all(pairs, send_sems.at[m])
    for z in range(planes):
        at = slice(reach * z, reach * (z + 1))
        edge_ref[0, at] = stage_ref[z, :reach]
        edge_ref[1, at] = stage_ref[z, rows - reach :]
    leaving += copy_all([(edge_ref.at[0], head_ref), (edge_ref.at[1], tail_ref)], edge_sems)
    wait_all(leaving)


def inverse_columns(blocks, factors, sends):
    parts, _, rows, _ = blocks.shape
    lanes = blocks.shape[1] * blocks.shape[3]
    width = factors[0].shape[2]
    planes = lanes * parts // (2 * width)
    side = (reach * planes, width)
    slabs = 2 if sends else 0
    scratch = [
        pltpu.VMEM((4, width, width), bf16),
        pltpu.VMEM(blocks.shape, f32),
        pltpu.VMEM((planes, rows, width), f32),
        pltpu.VMEM((2, planes * rows, width), bf16),
        pltpu.VMEM((2, planes * rows, width), bf16),
        pltpu.SemaphoreType.DMA((rows // gather_tile, 4)),
        pltpu.SemaphoreType.DMA((planes,)),
        pltpu.SemaphoreType.DMA((2, reach)),
    ]
    edges = [pltpu.VMEM((2, *side), f32), pltpu.SemaphoreType.DMA((2,))]
    return call(
        lambda *refs: inverse_columns_body(sends, *refs),
        [array(planes, rows, width), array(*side), array(*side)]
        + [array(slab_rows(rows), width)] * slabs,
        7.0,
        grid=(1,),
        in_specs=[in_hbm] * 3,
        out_specs=[in_hbm] * (3 + slabs),
        scratch_shapes=scratch + edges + factor_scratch(factors),
        name="inverse_columns",
    )(blocks, *factors)


def shift(value, axis, up, ring):
    count = lax.axis_size(axis)
    pairs = [(i, (i + 1) % count) for i in range(count if ring else count - 1)]
    return lax.ppermute(value, axis, pairs if up else [(b, a) for a, b in pairs])


def slab_rows(rows):
    return reach * rows + -(-2 * reach * reach // 8) * 8


def halo_body(head_ref, tail_ref, low_ref, high_ref, down_ref, up_ref, edge_ref, sems):
    side = reach * reach
    held = head_ref.shape[0]
    copies = []
    for i, (first, out_ref) in enumerate(((0, down_ref), (held - side, up_ref))):
        edge_ref[i, :side] = head_ref[first : first + side]
        edge_ref[i, side : 2 * side] = tail_ref[first : first + side]
        count = edge_ref.shape[1]
        to = out_ref.at[pl.ds(out_ref.shape[0] - count, count)]
        copies += copy_all([(edge_ref.at[i], to)], sems.at[i])
    wait_all(copies)


def halo_slabs(low, high, head, tail):
    total, width = low.shape
    count = -(-2 * reach * reach // 8) * 8
    return call(
        halo_body,
        [array(total, width)] * 2,
        1.0,
        grid=(1,),
        in_specs=[whole(head.shape), whole(tail.shape), in_hbm, in_hbm],
        out_specs=[in_hbm] * 2,
        scratch_shapes=[pltpu.VMEM((2, count, width), f32), pltpu.SemaphoreType.DMA((2, 1))],
        input_output_aliases={2: 0, 3: 1},
        name="halo_slabs",
    )(head, tail, low, high)


def roll_x(value, by):
    return pltpu.roll(value, by % value.shape[-1], value.ndim - 1)


def energy_slopes(rho, sigma):
    two_a = 2.0 * correlation_scale
    b1, b2, b3, b4 = [two_a * term for term in correlation_terms]
    ratio = beta_value / gamma_value
    exchange = -0.75 * (3.0 / math.pi) ** (1.0 / 3.0)
    s_scale = 0.25 / (3.0 * math.pi**2) ** (2.0 / 3.0)
    t_scale = math.pi / (16.0 * (3.0 * math.pi**2) ** (1.0 / 3.0))
    radius_scale = (3.0 / (4.0 * math.pi)) ** (1.0 / 3.0)
    sixth = jnp.exp(jnp.log(rho) * (-1.0 / 6.0))
    inv = sixth * sixth
    inv2 = inv * inv
    inv4 = inv2 * inv2
    scaled_sigma = sigma * inv4
    stretch = 1.0 + (mu_value / kappa_value * s_scale) * scaled_sigma * inv4
    v = (ratio * t_scale) * scaled_sigma * (inv2 * inv)
    root = math.sqrt(radius_scale) * sixth
    denom = root * (b1 + root * (b2 + root * (b3 + root * b4)))
    denom_slope = root * (0.5 * b1 + root * (b2 + root * (1.5 * b3 + root * (2.0 * b4))))
    pair = denom * denom + denom
    recip = 1.0 / (stretch * pair)
    weight = recip * pair
    recip = recip * stretch
    x_rho = (rho * inv2) * (
        exchange * (4.0 / 3.0) * (1.0 + kappa_value)
        + weight
        * ((-4.0 * exchange * kappa_value) + (8.0 / 3.0 * exchange * kappa_value) * weight)
    )
    radius_part = (two_a * correlation_alpha * radius_scale) * inv
    linear = two_a + radius_part
    log_term = jnp.log(1.0 + (recip * denom + recip))
    uniform = -linear * log_term
    rho_uniform = (1.0 / 3.0) * (radius_part * log_term - linear * (recip * denom_slope))
    grown = jnp.exp(uniform * (-1.0 / gamma_value))
    x = grown - 1.0
    vx = v * x
    v2 = v * v
    lower = x * x + (vx + v2)
    upper = lower + vx * (x + v)
    both = 1.0 / (lower * upper)
    gradient = gamma_value * jnp.log(upper * (upper * both))
    h_part = (x + 2.0 * v) * (x * x) * (x * both)
    h_uniform = (v2 * both) * (v * (2.0 * x + v)) * grown
    d_rho = (
        (x_rho + uniform)
        + (gradient + rho_uniform * (1.0 - h_uniform))
        - (7.0 / 3.0 * gamma_value) * (v * h_part)
    )
    two_d_sigma = inv4 * (
        (2.0 * exchange * s_scale * mu_value) * (weight * weight)
        + (2.0 * t_scale * beta_value) * h_part
    )
    return d_rho, two_d_sigma


def potential_body(sources, groups, flag_ref, *refs):
    ext_ref, part_ref, smooth_ref, flat_ref, fx_ref, fy_ref, fz_ref = refs[-7:]
    count = 6 if groups == 2 else 4
    plane_refs = refs[: -count - 17]
    sides_hbm = plane_refs[-count:]
    tab_hbm_ref, out_ref, tab_ref, tab_sems, pot_ref, tall_ref, stage_ref = refs[-count - 17 : -count - 10]
    in_sems, out_sems, side_sems = refs[-count - 10 : -count - 7]
    side_refs = refs[-count - 7 : -7]
    planes, blocks, rows, _ = pot_ref.shape
    each = planes // groups
    sides = copy_all(
        [
            (hbm.at[pl.ds(hbm.shape[0] - ref.shape[0], ref.shape[0])], ref)
            for hbm, ref in zip(sides_hbm, side_refs)
        ],
        side_sems,
    )

    def plane_of(plane, at):
        ref = plane_refs[plane]
        return ref.at[at] if len(ref.shape) == 3 else ref.at[pl.ds(at * rows, rows)]

    arriving = copy_all(
        [
            (plane_of(plane, at), ext_ref.at[z, pl.ds(lead - 1, rows)])
            for z, (plane, at, *_) in enumerate(sources)
        ],
        in_sems,
    )
    slope = 1.0 / (2.0 * grid_step)
    tiles = rows // 8 + 1

    def at_end(flag):
        return pl.when(flag_ref[flag] == 1) if groups == 2 else lambda body: None

    wait_all(sides)
    for z, (_, _, head, head_row, tail, tail_row) in enumerate(sources):
        ext_ref[z, lead - 1 - reach : lead - 1] = side_refs[head][head_row : head_row + reach]
        after = side_refs[tail][tail_row : tail_row + reach]
        ext_ref[z, lead - 1 + rows : lead - 1 + rows + reach] = after
    wait_all(arriving)
    tables = load_tables(tab_hbm_ref, tab_ref, tab_sems)

    def widened(z, size, margin):
        return z + margin * (z // size) if groups > 1 else z

    @at_end(0)
    def _():
        ext_ref[reach - 1] = ext_ref[reach]

    @at_end(1)
    def _():
        ext_ref[ext_ref.shape[0] - reach] = ext_ref[ext_ref.shape[0] - reach - 1]

    def filter_depth(z, carry):
        w = widened(z, each + 4, 2)
        part_ref[z] = 0.25 * (ext_ref[w] + ext_ref[w + 2]) + 0.5 * ext_ref[w + 1]
        return carry

    lax.fori_loop(0, part_ref.shape[0], filter_depth, 0)

    def filter_plane(z, carry):
        for t in range(tiles):
            r = lead - 2 + 8 * t
            along_y = 0.25 * (part_ref[z, r - 2 : r + 6] + part_ref[z, r : r + 8]) + 0.5 * (
                part_ref[z, r - 1 : r + 7]
            )
            smooth_ref[z, r : r + 8] = (
                0.25 * (roll_x(along_y, 1) + roll_x(along_y, -1)) + 0.5 * along_y
            )
        return carry

    lax.fori_loop(0, part_ref.shape[0], filter_plane, 0)

    @at_end(0)
    def _():
        smooth_ref[1] = smooth_ref[2]

    @at_end(1)
    def _():
        smooth_ref[smooth_ref.shape[0] - 2] = smooth_ref[smooth_ref.shape[0] - 3]

    def local_terms(z, carry):
        w = widened(z, each + 2, 2)
        for t in range(tiles):
            r = lead - 1 + 8 * t
            center = smooth_ref[w + 1, r : r + 8]
            gx = (roll_x(center, -1) - roll_x(center, 1)) * slope
            gy = (smooth_ref[w + 1, r + 1 : r + 9] - smooth_ref[w + 1, r - 1 : r + 7]) * slope
            gz = (smooth_ref[w + 2, r : r + 8] - smooth_ref[w, r : r + 8]) * slope
            d_rho, two_d_sigma = energy_slopes(center, gx * gx + gy * gy + gz * gz)
            flat_ref[z, r : r + 8] = d_rho
            fx_ref[z, r : r + 8] = two_d_sigma * gx
            fy_ref[z, r : r + 8] = two_d_sigma * gy
            fz_ref[z, r : r + 8] = two_d_sigma * gz
        return carry

    lax.fori_loop(0, flat_ref.shape[0], local_terms, 0)

    @at_end(0)
    def _():
        fz_ref[0] = fz_ref[1]

    @at_end(1)
    def _():
        fz_ref[fz_ref.shape[0] - 1] = fz_ref[fz_ref.shape[0] - 2]

    def collect(z, carry):
        w = widened(z, each, 2)
        for t in range(rows // 8):
            r = lead + 8 * t
            here = slice(r, r + 8)
            fx = fx_ref[w + 1, here]
            along_x = (roll_x(fx, -1) - roll_x(fx, 1)) * slope
            along_y = (fy_ref[w + 1, r + 1 : r + 9] - fy_ref[w + 1, r - 1 : r + 7]) * slope
            along_z = (fz_ref[w + 2, here] - fz_ref[w, here]) * slope
            value = flat_ref[w + 1, here] - (along_x + along_y + along_z)
            for i in range(blocks):
                pot_ref[z, i, 8 * t : 8 * t + 8, :] = value[:, i * 128 : (i + 1) * 128]
        return carry

    lax.fori_loop(0, planes, collect, 0)
    wait_all(tables)
    forward_columns(pot_ref, tab_ref, tall_ref, stage_ref, out_ref, out_sems)


def forward_columns(x_ref, tab_ref, tall_ref, stage_ref, out_ref, out_sems):
    planes, blocks, rows, _ = x_ref.shape
    width = blocks * 128
    for i in range(blocks):
        pieces = [
            x_ref[z, i, pl.ds(p, rows // 2, stride=2), :] for z in range(planes) for p in range(2)
        ]
        high, low = split(jnp.concatenate(pieces, axis=0).T)
        for k, value in enumerate((high, high, low)):
            tall_ref[k * width + i * 128 : k * width + (i + 1) * 128] = value
    parts, block, out_lanes = stage_ref.shape
    group = parts // 2

    def step(m, carry):
        at = pl.ds(pl.multiple_of(m * group * block, group * block), group * block)
        ch, sh = tab_ref[0, at], tab_ref[2, at]
        real = dot_nn(jnp.concatenate([ch, tab_ref[1, at], ch], axis=1), tall_ref[...])
        imag = dot_nn(jnp.concatenate([sh, tab_ref[3, at], sh], axis=1), tall_ref[...])
        both = jnp.concatenate([real, -imag], axis=1)
        stage_ref[pl.ds(m * group, group)] = both.reshape(group, block, out_lanes)
        send_group(stage_ref, out_ref, out_sems, m, group)
        return carry

    lax.fori_loop(0, 2, step, 0)
    for m in range(2):
        wait_all(group_copies(stage_ref, out_ref, out_sems, m, group))


def potential_of(flags, planes, sides, sources, groups, tables, parts):
    rows, width = planes[0].shape[1:]
    tall = -(-(rows + lead + 8) // 8) * 8
    count = len(sources) - 2 * reach * groups
    lanes = count * rows
    out = (parts, width // parts, 2 * lanes)
    scratch = table_scratch(width) + [
        pltpu.VMEM((count, width // 128, rows, 128), f32),
        pltpu.VMEM((3 * width, lanes), bf16),
        pltpu.VMEM(out, f32),
        pltpu.SemaphoreType.DMA((len(sources),)),
        pltpu.SemaphoreType.DMA((2, parts // 2)),
        pltpu.SemaphoreType.DMA((len(sides),)),
    ]
    scratch += [pltpu.VMEM((min(side.shape[0], sides[0].shape[0]), width), f32) for side in sides]
    for margin in (6, 4, 4, 2, 2, 2, 2):
        scratch.append(pltpu.VMEM((count + margin * groups, tall, width), f32))
    return call(
        lambda *refs: potential_body(sources, groups, *refs),
        array(*out),
        20.0,
        52,
        grid=(1,),
        in_specs=[pl.BlockSpec(memory_space=pltpu.SMEM)]
        + [in_hbm] * len(planes)
        + [pl.BlockSpec(memory_space=pl.ANY)] * len(sides)
        + [in_hbm],
        out_specs=in_hbm,
        scratch_shapes=scratch,
        name="potential",
    )(flags, *planes, *sides, tables)


def forward_rows_body(starts, flag_ref, blocks_ref, coarse_hbm_ref, fine_hbm_ref, *refs):
    coarse_ref, fine_ref, factor_sems = refs[-3:]
    out_ref, tab_ref, wide_ref, in_ref, stage_ref, high_ref, low_ref, in_sems, out_sems = refs[-12:-3]
    _, planes, rows, width = stage_ref.shape
    small = copy_all([(coarse_hbm_ref, coarse_ref), (fine_hbm_ref, fine_ref)], factor_sems)
    fetch_blocks(blocks_ref, in_ref, in_sems)
    fill_tables(small, coarse_ref, fine_ref, tab_ref)
    length = tab_ref.shape[1]
    for k, part in enumerate((0, 0, 1)):
        re_at = slice(k * length, (k + 1) * length)
        im_at = slice((k + 3) * length, (k + 4) * length)
        wide_ref[re_at, :length], wide_ref[re_at, length:] = tab_ref[part], -tab_ref[2 + part]
        wide_ref[im_at, :length], wide_ref[im_at, length:] = tab_ref[2 + part], tab_ref[part]
    gather_blocks(blocks_ref, in_ref, in_sems, high_ref, low_ref, 2)
    last = coarse_ref.shape[1] - 1
    wave_cos, wave_sin = coarse_ref[0, last:], coarse_ref[1, last:]
    half = planes // 2

    def copies(c, m):
        to = starts[0] + m * (starts[1] - starts[0])
        return [
            pltpu.make_async_copy(stage_ref.at[c, z], out_ref.at[c, to + y], out_sems.at[c, z])
            for y, z in enumerate([m * half + y for y in range(half)])
        ]

    def step(m, carry):
        at = pl.ds(pl.multiple_of(m * half * rows, half * rows), half * rows)
        to = pl.ds(m * half, half)

        def product(way):
            lanes = slice(way * length, (way + 1) * length)
            pairs = [(high_ref[c, at, lanes], low_ref[c, at, lanes]) for c in range(2)]
            left = [value for high, low in pairs for value in (high, low, high)]
            both = dot_nn(jnp.concatenate(left, axis=1), wide_ref[...])
            return both[:, :length], both[:, length:]

        even = product(0)
        odd_re, odd_im = product(1)
        odd = odd_re * wave_cos - odd_im * wave_sin, odd_re * wave_sin + odd_im * wave_cos
        for c in range(2):
            shape = (half, rows, length)
            stage_ref[c, to, :, :length] = (even[c] + odd[c]).reshape(shape)
            stage_ref[c, to, :, length:] = (even[c] - odd[c]).reshape(shape)

        @pl.when(flag_ref[2] == 1)
        def _():
            tile = (8, 128)
            at_zero = (lax.broadcasted_iota(jnp.int32, tile, 0) == 0) & (
                lax.broadcasted_iota(jnp.int32, tile, 1) == 0
            )
            for c in range(2):
                for y in range(half):
                    z = m * half + y
                    corner = stage_ref[c, z, :8, :128]
                    stage_ref[c, z, :8, :128] = jnp.where(at_zero, 0.0, corner)

        for copy in copies(0, m) + copies(1, m):
            copy.start()
        return carry

    lax.fori_loop(0, 2, step, 0)
    for c in range(2):
        wait_all(copies(c, 0) + copies(c, 1))


def forward_rows(flags, blocks, factors, starts, depth, before):
    parts, rows, lanes = blocks.shape
    length = factors[0].shape[2]
    width = 2 * length
    planes = lanes * parts // (2 * width)
    earlier = [] if before is None else [before]
    scratch = [
        pltpu.VMEM((4, length, length), bf16),
        pltpu.VMEM((6 * length, width), bf16),
        pltpu.VMEM(blocks.shape, f32),
        pltpu.VMEM((2, planes, rows, width), f32),
        pltpu.VMEM((2, planes * rows, width), bf16),
        pltpu.VMEM((2, planes * rows, width), bf16),
        pltpu.SemaphoreType.DMA((rows // gather_tile, 4)),
        pltpu.SemaphoreType.DMA((2, planes)),
    ]
    return call(
        lambda *refs: forward_rows_body(starts, *refs),
        array(2, depth, rows, width),
        10.0,
        grid=(1,),
        in_specs=[pl.BlockSpec(memory_space=pltpu.SMEM)] + [in_hbm] * (3 + len(earlier)),
        out_specs=in_hbm,
        scratch_shapes=scratch + factor_scratch(factors),
        input_output_aliases={4: 0} if earlier else {},
        name="forward_rows",
    )(flags, blocks, *factors, *earlier)


def exchange(value):
    return lax.all_to_all(value, "py", 0, 0, tiled=True)


def on_device(rho_hat):
    parts = lax.axis_size("py")
    place_z, place_y = lax.axis_index("px"), lax.axis_index("py")
    flags = jnp.stack(
        [place_z == 0, place_z == lax.axis_size("px") - 1, place_y == 0]
    ).astype(jnp.int32)
    depth, width = rho_hat.shape[1], rho_hat.shape[3]
    unit = depth // 4
    block = width // parts
    factors = phase_factors(width, block, width)
    half_factors = phase_factors(width // 2, block, width)

    outer = exchange(inverse_rows(rho_hat, half_factors, None, None, (0, 3)))
    inner, tables = inverse_rows(rho_hat, half_factors, factors, flags, (1, 2))
    inner = exchange(inner)
    outer, head, tail, low_planes, high_planes = inverse_columns(outer, factors, True)
    outer_sides = shift(tail, "py", True, True), shift(head, "py", False, True)
    down, up = halo_slabs(low_planes, high_planes, *outer_sides)
    inner, down, up = lax.optimization_barrier((inner, down, up))
    inner, head, tail = inverse_columns(inner, factors, False)
    inner_sides = shift(tail, "py", True, True), shift(head, "py", False, True)

    down, up, _ = lax.optimization_barrier((down, up, head))
    below, above = shift(up, "px", True, False), shift(down, "px", False, False)

    def source(z):
        if unit <= z < depth - unit:
            row = reach * (z - unit)
            return 1, z - unit, 2, row, 3, row
        if 0 <= z < depth:
            at = z if z < unit else z - depth + 2 * unit
            return 0, at, 0, reach * at, 1, reach * at
        at = z + reach if z < 0 else z - depth
        side = 2 if z < 0 else 3
        return side, at, side + 2, reach * at, side + 2, reach * (reach + at)

    inside = [source(z) for z in range(unit - reach, depth - unit + reach)]
    outside = [source(z) for z in range(-reach, unit + reach)]
    outside += [source(z) for z in range(depth - unit - reach, depth + reach)]
    planes, sides = [outer, inner], [*outer_sides, *inner_sides]
    inner_waves = exchange(potential_of(flags, planes, sides, inside, 1, tables, parts))
    halo = [below, above]
    spectral = potential_of(flags, planes + halo, sides + halo, outside, 2, tables, parts)
    outer_waves = exchange(spectral)
    result = forward_rows(flags, inner_waves, half_factors, (unit, 2 * unit), depth, None)
    result = forward_rows(flags, outer_waves, half_factors, (0, depth - unit), depth, result)
    return result


def solution(mesh):
    return jax.shard_map(
        on_device,
        mesh=mesh,
        in_specs=(P(None, "px", "py", None),),
        out_specs=P(None, "px", "py", None),
        check_vma=False,
    )
```
